32 devices in a mesh: batch: 4 (over y, x), vocab: 8 (over z, core).
Axes of the slice: x: 2, y: 2, z: 4, core: 2. Of those that a mesh axis runs over, the one named last changes fastest.
Arguments:
- tokens: int32 [32768], P('batch'), may hold values from 0 to 51199
- targets: int32 [4096], P('batch'), may hold values from 0 to 51199
- segments: int32 [32768], P(('batch', 'vocab')), may hold values from 0 to 2, as said below
- counted: int32 [4096], P(('batch', 'vocab')), may hold values from 0 to 1023, as said below
- vocab_mask: int32 [51200], P('vocab'), may hold values 0 or 1
- step_count: int32 [1], replicated, may hold values from 2 to 20
- table: float32 [51200, 768], P('vocab', 'batch'), may hold values from -0.4375 to 0.4375
- table_moment: float32 [51200, 768], P('vocab', 'batch'), may hold values from -2.3841858e-06 to 2.3841858e-06
- table_square: float32 [51200, 768], P('vocab', 'batch'), may hold values from 2.1549823e-15 to 8.619929e-15
- attend: float32 [1, 768, 2304], P(None, 'batch'), may hold values from -0.21875 to 0.21875
- attend_moment: float32 [1, 768, 2304], P(None, 'batch'), may hold values from -4.7683716e-06 to 4.7683716e-06
- attend_square: float32 [1, 768, 2304], P(None, 'batch'), may hold values from 8.619929e-15 to 3.4479716e-14
- project: float32 [1, 768, 768], P(None, 'batch'), may hold values from -0.875 to 0.875
- project_moment: float32 [1, 768, 768], P(None, 'batch'), may hold values from -4.7683716e-06 to 4.7683716e-06
- project_square: float32 [1, 768, 768], P(None, 'batch'), may hold values from 8.619929e-15 to 3.4479716e-14
- expand: float32 [1, 768, 3072], P(None, 'batch'), may hold values from -0.21875 to 0.21875
- expand_moment: float32 [1, 768, 3072], P(None, 'batch'), may hold values from -4.7683716e-06 to 4.7683716e-06
- expand_square: float32 [1, 768, 3072], P(None, 'batch'), may hold values from 8.619929e-15 to 3.4479716e-14
- contract: float32 [1, 3072, 768], P(None, 'batch'), may hold values from -0.109375 to 0.109375
- contract_moment: float32 [1, 3072, 768], P(None, 'batch'), may hold values from -4.7683716e-06 to 4.7683716e-06
- contract_square: float32 [1, 3072, 768], P(None, 'batch'), may hold values from 8.619929e-15 to 3.4479716e-14
- gain: float32 [3, 768], P(None, 'batch'), may hold values from 0.5 to 1.5
- gain_moment: float32 [3, 768], P(None, 'batch'), may hold values from -2.2888184e-05 to 2.2888184e-05
- gain_square: float32 [3, 768], P(None, 'batch'), may hold values from 2.1549822e-13 to 8.619929e-13
- shift: float32 [3, 768], P(None, 'batch'), may hold values from -1 to 1
- shift_moment: float32 [3, 768], P(None, 'batch'), may hold values from -2.2888184e-05 to 2.2888184e-05
- shift_square: float32 [3, 768], P(None, 'batch'), may hold values from 2.1549822e-13 to 8.619929e-13
Outputs:
- loss: float32 [], replicated
- gradient_norm: float32 [], replicated
- table_after: float32 [51200, 768], P('vocab', 'batch')
- table_first: float32 [51200, 768], P('vocab', 'batch')
- table_second: float32 [51200, 768], P('vocab', 'batch')
- attend_after: float32 [1, 768, 2304], P(None, 'batch')
- attend_first: float32 [1, 768, 2304], P(None, 'batch')
- attend_second: float32 [1, 768, 2304], P(None, 'batch')
- project_after: float32 [1, 768, 768], P(None, 'batch')
- project_first: float32 [1, 768, 768], P(None, 'batch')
- project_second: float32 [1, 768, 768], P(None, 'batch')
- expand_after: float32 [1, 768, 3072], P(None, 'batch')
- expand_first: float32 [1, 768, 3072], P(None, 'batch')
- expand_second: float32 [1, 768, 3072], P(None, 'batch')
- contract_after: float32 [1, 3072, 768], P(None, 'batch')
- contract_first: float32 [1, 3072, 768], P(None, 'batch')
- contract_second: float32 [1, 3072, 768], P(None, 'batch')
- gain_after: float32 [3, 768], P(None, 'batch')
- gain_first: float32 [3, 768], P(None, 'batch')
- gain_second: float32 [3, 768], P(None, 'batch')
- shift_after: float32 [3, 768], P(None, 'batch')
- shift_first: float32 [3, 768], P(None, 'batch')
- shift_second: float32 [3, 768], P(None, 'batch')
The draws below stay inside these ranges and needn't reach their ends.
Inputs may be any that keep to these rules, and one draw needn't show every extreme that they name: Each sequence of 1024 tokens is cut into three segments, numbered 0, 1, 2 in order: one of 512 tokens and two of 256 tokens, in any order. Each sequence has 128 counted positions, the k-th among positions 8 k to 8 k + 7; the first is 0 and the last 1023.
All inputs are finite; a program needn't handle non-finite values. No bound on the sum of `vocab_mask` on one device may be relied on, other than what follows from the above.
Results may differ from the reference program's by a relative error of at most 0.022.
Values may be sent and summed in bfloat16 or wider, within the bound.
A program may use at most 448 MiB of HBM per device.

```python
import math
import jax
import jax.numpy as jnp
import numpy as np
from jax import lax

D = 768
H = 12
HD = 64
FF = 3072
VOCAB = 51200
NB = 256
SEG_UNIT = 256
SEG_BLOCKS = 4
LAYERS = 1
PICKS = 128
SEQ_LEN = 1024
TOKENS = 32768
NLN = 3
N_BATCH = 4


def draw_segments(key, part):
    count = TOKENS // SEQ_LEN
    longer = jax.random.randint(key, (count, 1), 0, 3)
    blocks = jnp.arange(SEG_BLOCKS, dtype=jnp.int32)[None, :]
    labels = blocks - (blocks > longer).astype(jnp.int32)
    return jnp.repeat(labels, SEG_UNIT, axis=1).reshape(TOKENS).astype(jnp.int32)


def draw_counted(key, part):
    count = TOKENS // SEQ_LEN
    stride = SEQ_LEN // PICKS
    offsets = jax.random.randint(jax.random.fold_in(key, 7), (count, PICKS), 0, stride)
    place = jnp.arange(PICKS, dtype=jnp.int32)[None, :]
    offsets = jnp.where(place == 0, 0, jnp.where(place == PICKS - 1, stride - 1, offsets))
    return (place * stride + offsets).reshape(count * PICKS).astype(jnp.int32)


def plant(values, own_key, low, largest):
    longest = values.shape.index(max(values.shape))
    spots = []
    for shift in (0, 1):
        where = [jax.random.randint(jax.random.fold_in(own_key, axis), (), 0, length) for axis, length in enumerate(values.shape)]
        where[longest] = (where[longest] + shift) % values.shape[longest]
        spots.append(tuple(where))
    return values.at[spots[0]].set(low).at[spots[1]].set(largest)


def steps_of(rng, dims, shards, least, top_value):
    factor_of, own = 1.0, jax.random.fold_in(rng, 6)
    for axis_at, parts in shards:
        heights = jnp.exp(jax.random.uniform(jax.random.fold_in(own, axis_at), (parts,), jnp.float32, least / len(shards), top_value / len(shards)))
        factor_of = factor_of * jnp.repeat(heights, dims[axis_at] // parts).reshape([-1 if axis == axis_at else 1 for axis in range(len(dims))])
    return factor_of


def cumulative_ranks(amount, slope):
    portions = [(1 << 20) // math.isqrt(rank ** slope) + 1 for rank in range(1, amount + 1)]
    deviation = 1 + sum(portions) // (1 << 30)
    return np.cumsum(np.array([max(1, weight // deviation) for weight in portions]))


def skewed_ids(rng, shape, number_of, slope):
    grid = cumulative_ranks(number_of, slope)
    lot = jax.random.randint(jax.random.fold_in(rng, 1), shape, 0, int(grid[number_of - 1]))
    standing = jnp.searchsorted(jnp.asarray(grid, jnp.int32), lot, side="right")
    return jax.random.permutation(jax.random.fold_in(rng, 2), number_of)[standing].astype(jnp.int32)


def bell_draw(rng, shape, width, limit, split=(), kind=jnp.bfloat16):
    values = jax.random.normal(rng, shape, jnp.float32) * width
    if len(split) > 0:
        values = steps_of(rng, shape, split, -0.22, 0.18) * values
    return jnp.clip(values, min=-limit, max=limit).astype(kind)


def setup_inputs(seed: int = 0) -> dict:
    seeds = jax.random.split(jax.random.key(seed), 28)
    return {
        "tokens": plant(skewed_ids(seeds[0], (TOKENS,), VOCAB, 0), jax.random.fold_in(seeds[0], 3), 0, VOCAB - 1).astype(jnp.int32),
        "targets": plant(skewed_ids(seeds[1], (TOKENS // SEQ_LEN * PICKS,), VOCAB, 0), jax.random.fold_in(seeds[1], 3), 0, VOCAB - 1).astype(jnp.int32),
        "segments": draw_segments(jax.random.fold_in(seeds[27], 71), 0),
        "counted": draw_counted(jax.random.fold_in(seeds[27], 71), 0),
        "vocab_mask": plant((jax.random.randint(seeds[4], (VOCAB,), 0, 16) < 15).astype(jnp.int32), jax.random.fold_in(seeds[4], 1), 0, 1),
        "step_count": jax.random.randint(seeds[5], (1,), 2, 21).astype(jnp.int32),
        "table": bell_draw(seeds[6], (VOCAB, D), (D // 4) ** -0.5, 0.4375, ((0, 8), (1, 4)), jnp.float32),
        "table_moment": bell_draw(seeds[7], (VOCAB, D), (0.111 * 0.01 / (LAYERS * (4 * D * D + 2 * D * FF) + VOCAB * D + 2 * NLN * D) ** 0.5), 2.384185791015625e-06, ((0, 8), (1, 4)), jnp.float32),
        "table_square": jnp.clip(jnp.exp(math.log(8.619929043555269e-15) - 1.3862944 * jax.random.uniform(seeds[8], (VOCAB, D), jnp.float32) ** steps_of(seeds[8], (VOCAB, D), ((0, 8), (1, 4)), -0.2, 0.2)), 2.1549822608888172e-15, 8.619929043555269e-15),
        "attend": bell_draw(seeds[9], (LAYERS, D, 3 * D), D ** -0.5, 0.21875, ((1, 4),), jnp.float32),
        "attend_moment": bell_draw(seeds[10], (LAYERS, D, 3 * D), (0.111 * 0.02 / (LAYERS * (4 * D * D + 2 * D * FF) + VOCAB * D + 2 * NLN * D) ** 0.5), 4.76837158203125e-06, ((1, 4),), jnp.float32),
        "attend_square": jnp.clip(jnp.exp(math.log(3.4479716174221076e-14) - 1.3862944 * jax.random.uniform(seeds[11], (LAYERS, D, 3 * D), jnp.float32) ** steps_of(seeds[11], (LAYERS, D, 3 * D), ((1, 4),), -0.2, 0.2)), 8.619929043555269e-15, 3.4479716174221076e-14),
        "project": bell_draw(seeds[12], (LAYERS, D, D), (D // 16) ** -0.5, 0.875, ((1, 4),), jnp.float32),
        "project_moment": bell_draw(seeds[13], (LAYERS, D, D), (0.111 * 0.02 / (LAYERS * (4 * D * D + 2 * D * FF) + VOCAB * D + 2 * NLN * D) ** 0.5), 4.76837158203125e-06, ((1, 4),), jnp.float32),
        "project_square": jnp.clip(jnp.exp(math.log(3.4479716174221076e-14) - 1.3862944 * jax.random.uniform(seeds[14], (LAYERS, D, D), jnp.float32) ** steps_of(seeds[14], (LAYERS, D, D), ((1, 4),), -0.2, 0.2)), 8.619929043555269e-15, 3.4479716174221076e-14),
        "expand": bell_draw(seeds[15], (LAYERS, D, FF), D ** -0.5, 0.21875, ((1, 4),), jnp.float32),
        "expand_moment": bell_draw(seeds[16], (LAYERS, D, FF), (0.111 * 0.02 / (LAYERS * (4 * D * D + 2 * D * FF) + VOCAB * D + 2 * NLN * D) ** 0.5), 4.76837158203125e-06, ((1, 4),), jnp.float32),
        "expand_square": jnp.clip(jnp.exp(math.log(3.4479716174221076e-14) - 1.3862944 * jax.random.uniform(seeds[17], (LAYERS, D, FF), jnp.float32) ** steps_of(seeds[17], (LAYERS, D, FF), ((1, 4),), -0.2, 0.2)), 8.619929043555269e-15, 3.4479716174221076e-14),
        "contract": bell_draw(seeds[18], (LAYERS, FF, D), FF ** -0.5, 0.109375, ((1, 4),), jnp.float32),
        "contract_moment": bell_draw(seeds[19], (LAYERS, FF, D), (0.111 * 0.02 / (LAYERS * (4 * D * D + 2 * D * FF) + VOCAB * D + 2 * NLN * D) ** 0.5), 4.76837158203125e-06, ((1, 4),), jnp.float32),
        "contract_square": jnp.clip(jnp.exp(math.log(3.4479716174221076e-14) - 1.3862944 * jax.random.uniform(seeds[20], (LAYERS, FF, D), jnp.float32) ** steps_of(seeds[20], (LAYERS, FF, D), ((1, 4),), -0.2, 0.2)), 8.619929043555269e-15, 3.4479716174221076e-14),
        "gain": jnp.clip(1.0 + 0.1 * jax.random.normal(seeds[21], (NLN, D), jnp.float32), 0.5, 1.5),
        "gain_moment": bell_draw(seeds[22], (NLN, D), (0.111 * 0.1 / (LAYERS * (4 * D * D + 2 * D * FF) + VOCAB * D + 2 * NLN * D) ** 0.5), 2.288818359375e-05, ((1, 4),), jnp.float32),
        "gain_square": jnp.clip(jnp.exp(math.log(8.619928772504726e-13) - 1.3862944 * jax.random.uniform(seeds[23], (NLN, D), jnp.float32) ** steps_of(seeds[23], (NLN, D), ((1, 4),), -0.2, 0.2)), 2.1549821931261814e-13, 8.619928772504726e-13),
        "shift": bell_draw(seeds[24], (NLN, D), 0.2, 1.0, ((1, 4),), jnp.float32),
        "shift_moment": bell_draw(seeds[25], (NLN, D), (0.111 * 0.1 / (LAYERS * (4 * D * D + 2 * D * FF) + VOCAB * D + 2 * NLN * D) ** 0.5), 2.288818359375e-05, ((1, 4),), jnp.float32),
        "shift_square": jnp.clip(jnp.exp(math.log(8.619928772504726e-13) - 1.3862944 * jax.random.uniform(seeds[26], (NLN, D), jnp.float32) ** steps_of(seeds[26], (NLN, D), ((1, 4),), -0.2, 0.2)), 2.1549821931261814e-13, 8.619928772504726e-13),
    }


HIGH = lax.Precision.HIGHEST
NORM_EPS = 1e-05
MAX_NORM = 0.02
LEARN_RATE = 0.04
NORM_RATE = 0.5
BETA_ONE = 0.9
BETA_TWO = 0.999
ADAM_EPS = 1e-08
DECAY = 0.1
NEG_BIG = -1e+30

@jax.custom_vjp
def low(v):
    return lax.optimization_barrier(v.astype(jnp.bfloat16)).astype(jnp.float32)

@jax.custom_vjp
def low_back(v):
    return v

def low_keep(v):
    return (low(v), None)

def low_pass(kept, grad):
    return (grad,)

def back_keep(v):
    return (v, None)

def back_low(kept, grad):
    return (low(grad),)
low.defvjp(low_keep, low_pass)
low_back.defvjp(back_keep, back_low)

def rounded(value):
    return low(low_back(value))

def layer_norm(value, gain, shift):
    centre = value - lax.optimization_barrier(jnp.mean(value, axis=-1, keepdims=True))
    spread = lax.optimization_barrier(jnp.mean(centre * centre, axis=-1, keepdims=True))
    return centre * lax.rsqrt(spread + NORM_EPS) * gain + shift

def memory_weights(segments):
    length = segments.shape[0]
    slots = SEG_BLOCKS - 2
    places = jnp.arange(length, dtype=jnp.int32)
    slot_ids = jnp.arange(slots, dtype=jnp.int32)
    inside = segments[None, :] == slot_ids[:, None]
    starts = lax.optimization_barrier(jnp.sum((segments[None, :] < slot_ids[:, None]).astype(jnp.int32), axis=1))
    counts = lax.optimization_barrier(jnp.sum(inside.astype(jnp.int32), axis=1))
    times = ((places[None, :] - starts[:, None]).astype(jnp.float32) + 0.5) / jnp.maximum(counts, 1)[:, None].astype(jnp.float32)
    centres = (jnp.arange(NB, dtype=jnp.float32) + 0.5) / NB
    offset = (times[:, None, :] - centres[None, :, None]) * NB
    basis = jnp.exp(-0.5 * offset * offset) * inside[:, None, :].astype(jnp.float32)
    total = lax.optimization_barrier(jnp.sum(basis, axis=2, keepdims=True)) + (counts == 0).astype(jnp.float32)[:, None, None]
    return (basis / total).reshape(slots * NB, length)

def run_sequence(embedded, segments, weights):
    attend, project, expand, contract, gain, shift = weights
    slots = SEG_BLOCKS - 2
    mixing = low(memory_weights(segments))
    key_seg = jnp.concatenate([jnp.repeat(jnp.arange(slots, dtype=jnp.int32) + 1, NB), segments])
    key_pos = jnp.concatenate([jnp.full((slots * NB,), -1, jnp.int32), jnp.arange(SEQ_LEN, dtype=jnp.int32)])
    places = jnp.arange(SEQ_LEN, dtype=jnp.int32)
    visible = (key_seg[None, :] == segments[:, None]) & (key_pos[None, :] <= places[:, None])
    state = embedded
    for layer in range(LAYERS):
        normed = low(layer_norm(state, gain[2 * layer], shift[2 * layer]))
        projected = rounded(jnp.dot(normed, attend[layer], precision=HIGH))
        memory = rounded(jnp.dot(mixing, normed, precision=HIGH))
        memory_kv = rounded(jnp.dot(memory, attend[layer][:, D:], precision=HIGH))
        queries = projected[:, :D].reshape(SEQ_LEN, H, HD)
        keys = jnp.concatenate([memory_kv[:, :D], projected[:, D:2 * D]]).reshape(-1, H, HD)
        values = jnp.concatenate([memory_kv[:, D:], projected[:, 2 * D:]]).reshape(-1, H, HD)
        scores = jnp.einsum('qhd,khd->hqk', queries, keys, precision=HIGH) * HD ** (-0.5)
        scores = low_back(jnp.where(visible[None], scores, NEG_BIG))
        probs = low(jax.nn.softmax(scores, axis=-1))
        mixed = rounded(jnp.einsum('hqk,khd->qhd', probs, values, precision=HIGH).reshape(SEQ_LEN, D))
        state = state + low_back(jnp.dot(mixed, project[layer], precision=HIGH))
        normed_two = low(layer_norm(state, gain[2 * layer + 1], shift[2 * layer + 1]))
        inner = low_back(jnp.dot(normed_two, expand[layer], precision=HIGH))
        active = low(jax.nn.gelu(inner, approximate=True))
        state = state + low_back(jnp.dot(active, contract[layer], precision=HIGH))
    return low(layer_norm(state, gain[2 * LAYERS], shift[2 * LAYERS]))

def reference(tokens, targets, segments, counted, vocab_mask, step_count, table, table_moment, table_square, attend, attend_moment, attend_square, project, project_moment, project_square, expand, expand_moment, expand_square, contract, contract_moment, contract_square, gain, gain_moment, gain_square, shift, shift_moment, shift_square):
    nseq = TOKENS // SEQ_LEN
    live = vocab_mask > 0
    valid = live[targets].astype(jnp.float32).reshape(N_BATCH, -1)
    counts = lax.optimization_barrier(jnp.sum(valid, axis=1))
    factor = (valid / (jnp.maximum(counts, 1.0)[:, None] * N_BATCH)).reshape(nseq, PICKS)
    seq_segments = segments.reshape(nseq, SEQ_LEN)
    seq_targets = targets.reshape(nseq, PICKS)
    seq_counted = counted.reshape(nseq, PICKS)

    def forward(table_f, attend_f, project_f, expand_f, contract_f, gain_f, shift_f):
        words = low(table_f)
        weights = (low(attend_f), low(project_f), low(expand_f), low(contract_f), low(gain_f), low(shift_f))
        embedded = low_back(jnp.take(words, tokens, axis=0)).reshape(nseq, SEQ_LEN, D)
        final = lax.map(jax.checkpoint(lambda pair: run_sequence(pair[0], pair[1], weights)), (embedded, seq_segments))
        chosen = jnp.take_along_axis(final, seq_counted[:, :, None], axis=1)

        def head(total, triple):
            rows, target, weight = triple
            logits = low_back(jnp.dot(rows, words.T, precision=HIGH))
            masked = jnp.where(live[None, :], logits, NEG_BIG)
            normal = jax.nn.logsumexp(masked, axis=-1)
            picked = jnp.take_along_axis(logits, target[:, None], axis=1)[:, 0]
            return (total + jnp.sum(weight * (normal - picked)), None)
        loss, unused = lax.scan(jax.checkpoint(head), jnp.zeros((), jnp.float32), (chosen, seq_targets, factor))
        return loss
    params = (table, attend, project, expand, contract, gain, shift)
    loss, pullback = jax.vjp(forward, *params)
    grads = pullback(jnp.ones_like(loss))
    gradient_norm = jnp.sqrt(sum((jnp.sum(item * item) for item in grads)))
    clip = jnp.minimum(1.0, MAX_NORM / (gradient_norm + 1e-06))
    count = step_count[0].astype(jnp.float32)

    def adamw(weight, moment, square, gradient, decay, rate):
        gradient = gradient * clip
        moment = BETA_ONE * moment + (1 - BETA_ONE) * gradient
        square = BETA_TWO * square + (1 - BETA_TWO) * gradient * gradient
        fixed_moment = moment / (1 - BETA_ONE ** count)
        fixed_square = square / (1 - BETA_TWO ** count)
        weight = weight - rate * (fixed_moment / (jnp.sqrt(fixed_square) + ADAM_EPS) + decay * weight)
        return (weight, moment, square)
    states = ((table_moment, table_square), (attend_moment, attend_square), (project_moment, project_square), (expand_moment, expand_square), (contract_moment, contract_square), (gain_moment, gain_square), (shift_moment, shift_square))
    decays = (DECAY, DECAY, DECAY, DECAY, DECAY, 0.0, 0.0)
    rates = (LEARN_RATE, LEARN_RATE, LEARN_RATE, LEARN_RATE, LEARN_RATE, NORM_RATE, NORM_RATE)
    results = [adamw(params[index], states[index][0], states[index][1], grads[index], decays[index], rates[index]) for index in range(7)]
    return (loss, gradient_norm, results[0][0], results[0][1], results[0][2], results[1][0], results[1][1], results[1][2], results[2][0], results[2][1], results[2][2], results[3][0], results[3][1], results[3][2], results[4][0], results[4][1], results[4][2], results[5][0], results[5][1], results[5][2], results[6][0], results[6][1], results[6][2])
```

```python
import functools
import math

import jax
import jax.numpy as jnp
from jax import lax
from jax.experimental import pallas as pl
from jax.experimental.pallas import tpu as pltpu
from jax.sharding import PartitionSpec as P

D = 768
H = 12
HD = 64
FF = 3072
NB = 256
SEG_BLOCKS = 4
SLOTS = SEG_BLOCKS - 2
SEQ_LEN = 1024
PICKS = 128
KEYS = SLOTS * NB + SEQ_LEN
BLK = 256
PAIR = 2 * HD
NPAIR = H // 2
EXTRA = 128

NORM_EPS = 1e-05
MAX_NORM = 0.02
LEARN_RATE = 0.04
NORM_RATE = 0.5
BETA_ONE = 0.9
BETA_TWO = 0.999
ADAM_EPS = 1e-08
DECAY = 0.1
NEG_BIG = -1e30
BF = jnp.bfloat16
FL = jnp.float32
I32 = jnp.int32
MESH = pl.DeviceIdType.MESH
SD = jax.ShapeDtypeStruct
VM = pl.BlockSpec(memory_space=pltpu.VMEM)
SM = pl.BlockSpec(memory_space=pltpu.SMEM)
HB = pl.BlockSpec(memory_space=pl.ANY)
LIMIT = 62 * 2**20


def nn(a, b):
    return lax.dot_general(a, b, (((1,), (0,)), ((), ())), preferred_element_type=FL)


def nt(a, b):
    return lax.dot_general(a, b, (((1,), (1,)), ((), ())), preferred_element_type=FL)


def iota(shape, axis):
    return lax.broadcasted_iota(I32, shape, axis)


def lanes(start, size):
    return pl.ds(pl.multiple_of(start, 128), size)


def chunk_of(rows, want):
    return want if rows % want == 0 else rows


def run(kernel, outs, scratch, ins, name, collective=None, flops=0, moved=0, out_specs=None, in_specs=None):
    return pl.pallas_call(
        kernel,
        out_shape=outs,
        in_specs=in_specs if in_specs is not None else [VM] * len(ins),
        out_specs=out_specs if out_specs is not None else [VM] * len(outs),
        scratch_shapes=scratch,
        compiler_params=pltpu.CompilerParams(
            vmem_limit_bytes=LIMIT,
            collective_id=collective,
            has_side_effects=collective is not None,
        ),
        cost_estimate=pl.CostEstimate(flops=flops, bytes_accessed=moved, transcendentals=0),
        name=name,
    )(*ins)


def send(source, target, out_sem, in_sem, device):
    return pltpu.make_async_remote_copy(
        src_ref=source, dst_ref=target, send_sem=out_sem, recv_sem=in_sem, device_id=device, device_id_type=MESH
    )


def meet(axes):
    barrier = pltpu.get_barrier_semaphore()
    count = 0
    for axis, size in axes:
        me = lax.axis_index(axis)

        def greet(step, carry, axis=axis, size=size, me=me):
            pl.semaphore_signal(barrier, inc=1, device_id={axis: lax.rem(me + step, size)}, device_id_type=MESH)
            return carry

        lax.fori_loop(1, size, greet, 0)
        count += size - 1
    pl.semaphore_wait(barrier, count)


def each(start, stop, body):
    def step(index, carry):
        body(index)
        return carry

    lax.fori_loop(start, stop, step, 0)


def embed_kernel(
    nb, nv, cap, part, round_ref, tok_ref, table_ref, x_ref, ids_ref, place_ref, most_ref, tok_ref_all,
    words, before, ranks, work, sent, got, spread, mixed, turned,
    tok_out, tok_in, row_out, row_in, mix_out, mix_in,
):
    b, v = lax.axis_index("batch"), lax.axis_index("vocab")
    width, rows = table_ref.shape
    shift = round_ref[0] * cap
    meet((("batch", nb), ("vocab", nv)))

    def tok_copy(step):
        return send(
            tok_ref, tok_ref_all.at[b], tok_out.at[step], tok_in.at[step], {"batch": lax.rem(b + step, nb)}
        )

    for step in range(1, nb):
        tok_copy(step).start()
    tok_ref_all[b] = tok_ref[...]
    words[...] = table_ref[...].astype(BF)
    before[...] = (iota((SEQ_LEN, SEQ_LEN), 0) < iota((SEQ_LEN, SEQ_LEN), 1)).astype(FL).astype(BF)
    for step in range(1, nb):
        tok_copy(step).wait()

    base = v * rows
    most = jnp.zeros((nv, 1), FL)
    for p in range(nb):
        ids = tok_ref_all[p]
        mine = (ids >= base) & (ids < base + rows)
        rank = nn(mine.astype(FL).astype(BF), before[...])
        ranks[p] = jnp.where(mine, rank.astype(I32) - shift, -1)
        for owner in range(nv):
            theirs = (ids >= owner * rows) & (ids < (owner + 1) * rows)
            most = jnp.maximum(most, jnp.sum(theirs.astype(FL), axis=1, keepdims=True))
    most_ref[...] = jnp.broadcast_to(jnp.max(most, axis=0, keepdims=True), most_ref.shape)

    def row_copy(step):
        return send(
            sent.at[step], got.at[v], row_out.at[step], row_in.at[step], {"vocab": lax.rem(v + step, nv)}
        )

    def build(turn):
        step = lax.rem(turn, nv)
        dest = lax.rem(v + step, nv)
        found = []
        for p in range(nb):
            pick = (iota((cap, SEQ_LEN), 0) == ranks[p, pl.ds(dest, 1), :]).astype(FL).astype(BF)
            local = tok_ref_all[p, pl.ds(dest, 1), :] - base
            line = iota((8, SEQ_LEN), 0)
            high, low = lax.shift_right_arithmetic(local, 7), lax.bitwise_and(local, 127)
            digits = jnp.where(line == 0, high, jnp.where(line == 1, low, 0)).astype(FL).astype(BF)
            both = nt(pick, digits)
            found.append((both[:, 0:1] * 128.0 + both[:, 1:2]).astype(I32))
        index = jnp.concatenate(found, axis=0)
        ids_ref[dest] = index
        work[...] = jnp.zeros_like(work)

        def piece(j):
            hot = (index - j * part == iota((nb * cap, part), 1)).astype(FL).astype(BF)
            work[...] += nt(hot, words[:, lanes(j * part, part)])

        each(0, rows // part, piece)
        block = work[...].T.astype(BF)

        @pl.when(step > 0)
        def _():
            sent[step] = block
            row_copy(step).start()

        @pl.when(step == 0)
        def _():
            got[v] = block

    each(1, nv + 1, build)

    keys = []
    for p in range(nb):
        ids = tok_ref_all[p, pl.ds(v, 1), :]
        owner = iota((nv, SEQ_LEN), 0)
        theirs = (ids >= owner * rows) & (ids < (owner + 1) * rows)
        rank = nn(theirs.astype(FL).astype(BF), before[...])
        place = jnp.sum(jnp.where(theirs, rank, 0.0), axis=0, keepdims=True).astype(I32) - shift
        holder = jnp.sum(jnp.where(theirs, owner.astype(FL), 0.0), axis=0, keepdims=True).astype(I32)
        line = iota((8, SEQ_LEN), 0)
        place_ref[p] = jnp.where(line == 0, holder, jnp.where(line == 1, place, 0))
        keys.append((holder, place))
        spread[p] = jnp.zeros((width, SEQ_LEN), FL)

    def take(turn):
        step = lax.rem(turn, nv)
        source = lax.rem(v - step + nv, nv)

        @pl.when(step > 0)
        def _():
            row_copy(step).wait()

        block = got[source]
        for p in range(nb):
            holder, place = keys[p]
            key = jnp.where(holder == source, place, -1)
            hot = (iota((cap, SEQ_LEN), 0) == key).astype(FL).astype(BF)
            spread[p] += nn(block[:, p * cap : (p + 1) * cap], hot)

    each(1, nv + 1, take)

    def mix_copy(step):
        return send(
            mixed.at[step], turned.at[b], mix_out.at[step], mix_in.at[step], {"batch": lax.rem(b + step, nb)}
        )

    for step in range(1, nb):
        mixed[step] = spread[lax.rem(b + step, nb)].astype(BF)
        mix_copy(step).start()
    turned[b] = spread[b].astype(BF)
    for step in range(1, nb):
        mix_copy(step).wait()
    x_ref[...] = turned[...].reshape(nb * width, SEQ_LEN).T


def embed(nb, nv, cap, turn, tok, table):
    width, rows = table.shape
    part = chunk_of(rows, 640)
    count = nb * cap
    outs = [
        SD((SEQ_LEN, D), BF),
        SD((nv, count, 1), I32),
        SD((nb, 8, SEQ_LEN), I32),
        SD((8, 128), FL),
        SD((nb, nv, SEQ_LEN), I32),
    ]
    dma = pltpu.SemaphoreType.DMA
    scratch = [
        pltpu.VMEM((width, rows), BF),
        pltpu.VMEM((SEQ_LEN, SEQ_LEN), BF),
        pltpu.VMEM((nb, nv, SEQ_LEN), I32),
        pltpu.VMEM((count, width), FL),
        pltpu.VMEM((nv, width, count), BF),
        pltpu.VMEM((nv, width, count), BF),
        pltpu.VMEM((nb, width, SEQ_LEN), FL),
        pltpu.VMEM((nb, width, SEQ_LEN), BF),
        pltpu.VMEM((nb, width, SEQ_LEN), BF),
        dma((nb,)), dma((nb,)), dma((nv,)), dma((nv,)), dma((nb,)), dma((nb,)),
    ]
    return run(
        functools.partial(embed_kernel, nb, nv, cap, part), outs, scratch, [turn, tok, table], "embed", 0,
        in_specs=[SM, VM, VM],
    )


def unembed_kernel(
    nb, nv, cap, part, x_ref, ids_ref, place_ref, out_ref,
    turned, parts, sent, got, mix_out, mix_in, row_out, row_in,
):
    b, v = lax.axis_index("batch"), lax.axis_index("vocab")
    width, rows = out_ref.shape
    meet((("batch", nb), ("vocab", nv)))
    turned[...] = x_ref[...].T.reshape(nb, width, SEQ_LEN)

    def mix_copy(step):
        other = lax.rem(b + step, nb)
        return send(turned.at[other], parts.at[b], mix_out.at[step], mix_in.at[step], {"batch": other})

    for step in range(1, nb):
        mix_copy(step).start()
    parts[b] = turned[b]
    for step in range(1, nb):
        mix_copy(step).wait()

    def row_copy(step):
        return send(
            sent.at[step], got.at[v], row_out.at[step], row_in.at[step], {"vocab": lax.rem(v + step, nv)}
        )

    def build(turn):
        step = lax.rem(turn, nv)
        owner = lax.rem(v + step, nv)
        blocks = []
        for p in range(nb):
            key = jnp.where(place_ref[p, 0:1, :] == owner, place_ref[p, 1:2, :], -1)
            hot = (iota((cap, SEQ_LEN), 0) == key).astype(FL).astype(BF)
            blocks.append(nt(parts[p], hot).astype(BF))
        block = jnp.concatenate(blocks, axis=1)

        @pl.when(step > 0)
        def _():
            sent[step] = block
            row_copy(step).start()

        @pl.when(step == 0)
        def _():
            got[v] = block

    each(1, nv + 1, build)
    out_ref[...] = jnp.zeros_like(out_ref)

    def take(step):
        source = lax.rem(v - step + nv, nv)

        @pl.when(step > 0)
        def _():
            row_copy(step).wait()

        block, index = got[source], ids_ref[source]

        def piece(j):
            hot = (index - j * part == iota((nb * cap, part), 1)).astype(FL).astype(BF)
            out_ref[:, lanes(j * part, part)] += nn(block, hot)

        each(0, rows // part, piece)

    each(0, nv, take)


def unembed(nb, nv, cap, width, rows, grad, ids, place):
    part = chunk_of(rows, 640)
    count = nb * cap
    dma = pltpu.SemaphoreType.DMA
    scratch = [
        pltpu.VMEM((nb, width, SEQ_LEN), BF),
        pltpu.VMEM((nb, width, SEQ_LEN), BF),
        pltpu.VMEM((nv, width, count), BF),
        pltpu.VMEM((nv, width, count), BF),
        dma((nb,)), dma((nb,)), dma((nv,)), dma((nv,)),
    ]
    return run(
        functools.partial(unembed_kernel, nb, nv, cap, part), [SD((width, rows), FL)], scratch,
        [grad, ids, place], "unembed", 2,
    )[0]


def later_slots(nv, cap, rows, every, turn):
    nb = every.shape[0]
    v = lax.axis_index("vocab")
    local = every - v * rows
    mine = (local >= 0) & (local < rows)
    rank = jnp.cumsum(mine.astype(I32), axis=-1) - 1 - turn * cap
    hot = (rank[:, :, None, :] == jnp.arange(cap)[None, None, :, None]) & mine[:, :, None, :]
    ids = jnp.sum(jnp.where(hot, local[:, :, None, :], 0), axis=-1)
    return jnp.transpose(ids, (1, 0, 2)).reshape(nv, nb * cap, 1)


def standard(value):
    centre = value - jnp.mean(value, axis=-1, keepdims=True)
    spread = jnp.mean(centre * centre, axis=-1, keepdims=True)
    scale = lax.rsqrt(spread + NORM_EPS)
    return centre * scale, scale


def norm_back(unit, scale, gain, upstream):
    inner = upstream * gain
    first = jnp.mean(inner, axis=-1, keepdims=True)
    second = jnp.mean(inner * unit, axis=-1, keepdims=True)
    grad = scale * (inner - first - unit * second)
    return grad, jnp.sum(upstream * unit, axis=0, keepdims=True), jnp.sum(upstream, axis=0, keepdims=True)


def head_lanes(value, head):
    lane = iota(value.shape, 1)
    keep = (lane < HD) if head == 0 else (lane >= HD)
    return jnp.where(keep, value, jnp.zeros_like(value))


def visible_keys(key_ref, query_ref):
    return (key_ref[:, 0:1] == query_ref[0:1, :]) & (key_ref[:, 1:2] <= query_ref[1:2, :])


def attend_kernel(
    x_ref, a_ref, mix_ref, pick_ref, key_ref, query_ref,
    hall_ref, kv_ref, q_ref, hq_ref, xq_ref, o_ref, lse_ref, norm_ref,
):
    norm_ref[...] = a_ref[:, 3 * D :].astype(FL).T[:8, :]
    gain, bias = norm_ref[0:1, :], norm_ref[3:4, :]

    def normalize(i):
        unit, _ = standard(x_ref[pl.ds(i * BLK, BLK), :].astype(FL))
        hall_ref[pl.ds(SLOTS * NB + i * BLK, BLK), :] = (unit * gain + bias).astype(BF)

    each(0, SEQ_LEN // BLK, normalize)
    normed = hall_ref[SLOTS * NB :, :]
    hall_ref[: SLOTS * NB, :] = nn(mix_ref[...], normed).astype(BF)

    def project(i):
        kv_ref[pl.ds(i * BLK, BLK), :] = nn(hall_ref[pl.ds(i * BLK, BLK), :], a_ref[:, D : 3 * D]).astype(BF)

    each(0, KEYS // BLK, project)
    pick = (pick_ref[...] == iota((PICKS, SEQ_LEN), 1)).astype(FL).astype(BF)
    hq_ref[...] = nn(pick, normed).astype(BF)
    xq_ref[...] = nn(pick, x_ref[...])
    q_ref[...] = nn(hq_ref[...], a_ref[:, :D]).astype(BF)
    visible = visible_keys(key_ref, query_ref)

    def attend(p):
        keys = kv_ref[:, lanes(p * PAIR, PAIR)]
        values = kv_ref[:, lanes(D + p * PAIR, PAIR)].T
        queries = q_ref[:, lanes(p * PAIR, PAIR)] * HD ** (-0.5)
        outs = []
        for head in range(2):
            scores = jnp.where(visible, nt(keys, head_lanes(queries, head)), NEG_BIG)
            peak = jnp.max(scores, axis=0, keepdims=True)
            expo = jnp.exp(scores - peak)
            total = jnp.sum(expo, axis=0, keepdims=True)
            probs = (expo * (1.0 / total)).astype(BF)
            outs.append(nn(values[head * HD : (head + 1) * HD, :], probs))
            lse_ref[p, head : head + 1, :] = peak + jnp.log(total)
        o_ref[:, lanes(p * PAIR, PAIR)] = jnp.concatenate(outs, axis=0).T.astype(BF)

    each(0, NPAIR, attend)


def feed_kernel(xq_ref, o_ref, p_ref, u_ref, c_ref, norm_ref, x1_ref, h2_ref, z_ref, act_ref, x2_ref, f_ref):
    x1 = xq_ref[...] + nn(o_ref[...], p_ref[...])
    x1_ref[...] = x1
    unit, _ = standard(x1)
    h2 = (unit * norm_ref[1:2, :] + norm_ref[4:5, :]).astype(BF)
    h2_ref[...] = h2
    x2_ref[...] = x1

    def piece(j):
        cut = lanes(j * D, D)
        z = nn(h2, u_ref[:, cut])
        z_ref[:, cut] = z
        act = jax.nn.gelu(z, approximate=True).astype(BF)
        act_ref[:, cut] = act
        x2_ref[...] += nn(act, c_ref[pl.ds(j * D, D), :])

    each(0, FF // D, piece)
    unit, _ = standard(x2_ref[...])
    f_ref[...] = (unit * norm_ref[2:3, :] + norm_ref[5:6, :]).astype(BF)


def feed_back_kernel(
    df_ref, x2_ref, x1_ref, h2_ref, z_ref, act_ref, o_ref, p_ref, u_ref, c_ref, norm_ref,
    dc_ref, du_ref, dp_ref, dx1_ref, do_ref, dnorm_ref, dh2,
):
    unit, scale = standard(x2_ref[...])
    dx2, gain_last, bias_last = norm_back(unit, scale, norm_ref[2:3, :], df_ref[...])
    dy = dx2.astype(BF)
    dh2[...] = jnp.zeros_like(dh2)
    h2t = h2_ref[...].T

    def piece(j):
        cut = lanes(j * D, D)
        dc_ref[pl.ds(j * D, D), :] = nn(act_ref[:, cut].T, dy).astype(BF)
        dact = nt(dy, c_ref[pl.ds(j * D, D), :])
        z = z_ref[:, cut]
        k = math.sqrt(2.0 / math.pi)
        t = jnp.tanh(k * (z + 0.044715 * z * z * z))
        slope = 0.5 * (1.0 + t) + 0.5 * z * (1.0 - t * t) * (k * (1.0 + 3 * 0.044715 * z * z))
        dz = (dact * slope).astype(BF)
        du_ref[:, cut] = nn(h2t, dz).astype(BF)
        dh2[...] += nt(dz, u_ref[:, cut])

    each(0, FF // D, piece)
    unit, scale = standard(x1_ref[...])
    dx1, gain_two, bias_two = norm_back(unit, scale, norm_ref[1:2, :], dh2[...])
    dx1 = dx1 + dx2
    dx1_ref[...] = dx1
    da = dx1.astype(BF)
    dp_ref[...] = nn(o_ref[...].T, da).astype(BF)
    do_ref[...] = nt(da, p_ref[...]).astype(BF)
    zero = jnp.zeros_like(gain_last)
    dnorm_ref[...] = jnp.concatenate([zero, gain_two, gain_last, zero, bias_two, bias_last, zero, zero], axis=0)


def attend_back_kernel(
    pos_ref, do_ref, q_ref, kv_ref, lse_ref, hall_ref, hq_ref, a_ref, x_ref, dx1_ref, mixt_ref, key_ref, query_ref,
    norm_ref, dnorm_ref, da_ref, dx_ref, dkv, dq, hallt, dh, dxin, dmem,
):
    visible = visible_keys(key_ref, query_ref)

    def attend(p):
        cut = lanes(p * PAIR, PAIR)
        keys = kv_ref[:, cut]
        values = kv_ref[:, lanes(D + p * PAIR, PAIR)]
        turned = keys.T
        queries = q_ref[:, cut] * HD ** (-0.5)
        grads = do_ref[:, cut]
        outs = []
        dk = dv = None
        for head in range(2):
            own, grad = head_lanes(queries, head), head_lanes(grads, head)
            scores = jnp.where(visible, nt(keys, own), NEG_BIG)
            probs = jnp.exp(scores - lse_ref[p, head : head + 1, :])
            dprobs = nt(values, grad)
            inner = jnp.sum(probs * dprobs, axis=0, keepdims=True)
            dscores = (probs * (dprobs - inner)).astype(BF)
            outs.append(nn(turned[head * HD : (head + 1) * HD, :], dscores))
            one, two = nn(dscores, own), nn(probs.astype(BF), grad)
            dk = one if head == 0 else dk + one
            dv = two if head == 0 else dv + two
        dq[:, cut] = (jnp.concatenate(outs, axis=0).T * HD ** (-0.5)).astype(BF)
        dkv[:, cut] = dk.astype(BF)
        dkv[:, lanes(D + p * PAIR, PAIR)] = dv.astype(BF)

    each(0, NPAIR, attend)
    da_ref[:, :D] = nn(hq_ref[...].T, dq[...]).astype(BF)

    def turn(i):
        hallt[:, lanes(i * BLK, BLK)] = hall_ref[pl.ds(i * BLK, BLK), :].T

    each(0, KEYS // BLK, turn)

    def weights(j):
        cut = lanes(j * BLK, BLK)
        da_ref[:, lanes(D + j * BLK, BLK)] = nn(hallt[...], dkv[:, cut]).astype(BF)

    each(0, 2 * D // BLK, weights)

    def memory(i):
        cut = pl.ds(i * BLK, BLK)
        dmem[cut, :] = nt(dkv[cut, :], a_ref[:, D : 3 * D]).astype(BF)

    each(0, SLOTS, memory)

    def local(i):
        cut = pl.ds(i * BLK, BLK)
        dh[cut, :] = nt(dkv[pl.ds(SLOTS * NB + i * BLK, BLK), :], a_ref[:, D : 3 * D]) + nn(mixt_ref[cut, :], dmem[...])

    each(0, SEQ_LEN // BLK, local)
    dxin[:PICKS, :] = nt(dq[...], a_ref[:, :D])

    def scatter_query(k):
        row = pl.ds(pos_ref[k], 1)
        dh[row, :] += dxin[pl.ds(k, 1), :]

    each(0, PICKS, scatter_query)
    gain = norm_ref[0:1, :]
    da_rows = [jnp.zeros((1, D), FL), jnp.zeros((1, D), FL)]

    def finish(i, carry):
        cut = pl.ds(i * BLK, BLK)
        unit, scale = standard(x_ref[cut, :].astype(FL))
        grad, dgain, dbias = norm_back(unit, scale, gain, dh[cut, :])
        dxin[cut, :] = grad
        return carry[0] + dgain, carry[1] + dbias

    dgain, dbias = lax.fori_loop(0, SEQ_LEN // BLK, finish, tuple(da_rows))

    def scatter_rest(k):
        row = pl.ds(pos_ref[k], 1)
        dxin[row, :] += dx1_ref[pl.ds(k, 1), :]

    each(0, PICKS, scatter_rest)
    dx_ref[...] = dxin[...].astype(BF)
    line = iota((8, D), 0)
    norms = dnorm_ref[...] + jnp.where(line == 0, dgain, jnp.where(line == 3, dbias, 0.0))
    tall = jnp.concatenate([norms, jnp.zeros((EXTRA - 8, D), FL)], axis=0)
    da_ref[:, 3 * D :] = tall.T.astype(BF)


def head_kernel(
    nb, nv, part, f_ref, w_ref, live_ref, target_ref, df_ref, dw_ref, loss_ref,
    fall, expo, block, mine, stats, ft, grad_sum, coef, df, half, far_got, out,
    near_out, near_in, far_out, far_in, stat_out, stat_in, pair_out, pair_in, sum_out, sum_in, dw_sem,
):
    v = lax.axis_index("vocab")
    rows = w_ref.shape[1]
    total_rows = nv * PICKS
    core, chip, chips = lax.rem(v, 2), v // 2, nv // 2
    sibling = {"vocab": v + 1 - 2 * core}
    base = v * rows
    pieces = rows // part
    depth = min(2, pieces)
    meet((("vocab", nv),))

    def peer(step):
        return {"vocab": lax.rem(chip + step, chips) * 2 + core}

    def far_copy(step):
        return send(f_ref, fall.at[v], far_out.at[step], far_in.at[step], peer(step))

    def near_copy(step):
        slot = lax.rem(chip - step + chips, chips) * 2 + core
        return send(fall.at[slot], fall.at[slot], near_out.at[step], near_in.at[step], sibling)

    fall[v] = f_ref[...]
    near_copy(0).start()
    each(1, chips, lambda step: far_copy(step).start())

    def logits(step):
        @pl.when(step > 0)
        def _():
            far_copy(step).wait_recv()
            near_copy(step).start()

        near_copy(step).wait_recv()
        source = lax.rem(chip - step + chips, chips)
        start = pl.multiple_of(source * 2 * PICKS, 2 * PICKS)
        features = fall[pl.ds(source * 2, 2)].reshape(2 * PICKS, D)
        target = target_ref[pl.ds(start, 2 * PICKS), :] - base

        def score(j, peak):
            cut = lanes(j * part, part)
            value = nn(features, w_ref[:, cut])
            block[:, cut] = value
            return jnp.maximum(
                peak, jnp.max(jnp.where(live_ref[0:1, cut] > 0, value, NEG_BIG), axis=1, keepdims=True)
            )

        peak = lax.fori_loop(0, pieces, score, jnp.full((2 * PICKS, 1), NEG_BIG, FL))

        def count(j, carry):
            total, picked, valid = carry
            cut = lanes(j * part, part)
            value = block[:, cut]
            live = live_ref[0:1, cut] > 0
            hot = target - j * part == iota((2 * PICKS, part), 1)
            e = jnp.where(live, jnp.exp(value - peak), 0.0)
            expo[pl.ds(start, 2 * PICKS), cut] = e.astype(BF)
            total = total + jnp.sum(e, axis=1, keepdims=True)
            picked = picked + jnp.sum(jnp.where(hot, value, 0.0), axis=1, keepdims=True)
            valid = valid + jnp.sum(jnp.where(hot & live, 1.0, 0.0), axis=1, keepdims=True)
            return total, picked, valid

        zero = jnp.zeros((2 * PICKS, 1), FL)
        total, picked, valid = lax.fori_loop(0, pieces, count, (zero, zero, zero))
        lane = iota((2 * PICKS, 128), 1)
        wide = jnp.where(lane == 0, peak, jnp.where(lane == 1, total, jnp.where(lane == 2, picked, valid)))
        mine[:, pl.ds(start, 2 * PICKS)] = wide.T[:8, :]

    each(0, chips, logits)

    def stat_copy(step):
        return send(mine, stats.at[v], stat_out.at[step], stat_in.at[step], {"vocab": lax.rem(v + step, nv)})

    each(1, nv, lambda step: stat_copy(step).start())
    stats[v] = mine[...]
    for i in range(total_rows // 256 if pieces > 1 else 0):
        ft[:, i * 256 : (i + 1) * 256] = fall[2 * i : 2 * i + 2].reshape(256, D).T
    each(1, nv, lambda step: stat_copy(step).wait())
    start = jnp.full((1, total_rows), NEG_BIG, FL)
    peak = lax.fori_loop(0, nv, lambda u, top: jnp.maximum(top, stats[u, 0:1, :]), start)

    def combine(u, carry):
        scale = jnp.exp(stats[u, 0:1, :] - peak)
        return (
            carry[0] + stats[u, 1:2, :] * scale, carry[1] + stats[u, 2:3, :], carry[2] + stats[u, 3:4, :],
        )

    zero = jnp.zeros((1, total_rows), FL)
    total, picked, valid = lax.fori_loop(0, nv, combine, (zero, zero, zero))
    lse = peak + jnp.log(jnp.maximum(total, 1e-37))
    weight = valid / (jnp.maximum(jnp.sum(valid, axis=1, keepdims=True), 1.0) * nb)
    loss = jnp.sum(weight * (lse - picked), axis=1, keepdims=True)
    loss_ref[...] = jnp.broadcast_to(loss, loss_ref.shape)
    alpha = weight * jnp.exp(mine[0:1, :] - lse)
    line = iota((128, 256), 0)
    for i in range(total_rows // 256):
        cut = slice(i * 256, (i + 1) * 256)
        coef[cut, :] = jnp.where(line == 0, alpha[:, cut], weight[:, cut]).T

    tall = min(total_rows, 1024 if pieces > 1 else 256)
    shards_tall = tall // PICKS
    df[...] = jnp.zeros_like(df)

    def out_copy(j):
        return pltpu.make_async_copy(
            out.at[lax.rem(j, depth)], dw_ref.at[:, lanes(j * part, part)], dw_sem.at[lax.rem(j, depth)]
        )

    def gradients(j):
        cut = lanes(j * part, part)
        words = w_ref[:, cut]

        @pl.when(j >= depth)
        def _():
            out_copy(j - depth).wait()

        def strip(t):
            start = t * tall if total_rows == tall else pl.multiple_of(t * tall, tall)
            here = pl.ds(start, tall)
            hot = target_ref[here, :] - base - j * part == iota((tall, part), 1)
            two = coef[here, :]
            value = two[:, 0:1] * expo[here, cut].astype(FL) - jnp.where(hot, two[:, 1:2], 0.0)
            dlogits = value.astype(BF)
            df[here, :] += nt(dlogits, words)
            if pieces > 1:
                turned = ft[:, pl.ds(start, tall)]
            else:
                turned = fall[pl.ds(t * shards_tall, shards_tall)].reshape(tall, D).T
            for r in range(0, D, D // 3):
                more = nn(turned[r : r + D // 3, :], dlogits)
                if total_rows == tall:
                    out[lax.rem(j, depth), r : r + D // 3, :] = more.astype(BF)
                else:
                    grad_sum[r : r + D // 3, :] += more

        if total_rows == tall:
            strip(0)
        else:
            grad_sum[...] = jnp.zeros_like(grad_sum)
            each(0, total_rows // tall, strip)
            for r in range(0, D, D // 3):
                out[lax.rem(j, depth), r : r + D // 3, :] = grad_sum[r : r + D // 3, :].astype(BF)
        out_copy(j).start()

    each(0, pieces, gradients)

    def shard(index):
        return pl.ds(pl.multiple_of(index * PICKS, PICKS), PICKS)

    def pair_copy(k):
        source = df.at[shard(2 * k + 1 - core), :] if pieces > 1 else fall.at[k]
        return send(source, half.at[k], pair_out.at[k], pair_in.at[k], sibling)

    near_copy(0).wait_send()

    def drain(step):
        far_copy(step).wait_send()
        near_copy(step).wait_send()

    each(1, chips, drain)

    def swap(k):
        if pieces == 1:
            fall[k] = df[shard(2 * k + 1 - core), :].astype(BF)
        pair_copy(k).start()

    each(0, chips, swap)

    def sum_copy(step):
        return send(fall.at[chips + step], far_got.at[step], sum_out.at[step], sum_in.at[step], peer(step))

    def pass_on(turn):
        step = lax.rem(turn, chips)
        k = lax.rem(chip + step, chips)
        pair_copy(k).wait()
        value = df[shard(2 * k + core), :] + half[k].astype(FL)

        @pl.when(step > 0)
        def _():
            fall[chips + step] = value.astype(BF)
            sum_copy(step).start()

        @pl.when(step == 0)
        def _():
            df_ref[...] = value

    each(1, chips + 1, pass_on)

    def collect(step):
        sum_copy(step).wait()
        df_ref[...] += far_got[step].astype(FL)

    each(1, chips, collect)
    for j in range(pieces - depth, pieces):
        out_copy(j).wait()


def head(nb, nv, features, words, live, targets):
    rows = words.shape[1]
    part = chunk_of(rows, 640)
    total_rows = nv * PICKS
    chips = nv // 2
    dma = pltpu.SemaphoreType.DMA
    scratch = [
        pltpu.VMEM((nv, PICKS, D), BF),
        pltpu.VMEM((total_rows, rows), BF),
        pltpu.VMEM((2 * PICKS, rows), FL),
        pltpu.VMEM((8, total_rows), FL),
        pltpu.VMEM((nv, 8, total_rows), FL),
        pltpu.VMEM((D, total_rows) if rows > part else (8, 128), BF),
        pltpu.VMEM((8, 128) if rows > part else (D, part), FL),
        pltpu.VMEM((total_rows, 128), FL),
        pltpu.VMEM((total_rows, D), FL),
        pltpu.VMEM((chips, PICKS, D), FL if rows > part else BF),
        pltpu.VMEM((chips, PICKS, D), BF),
        pltpu.VMEM((min(2, rows // part), D, part), BF),
        dma((chips,)), dma((chips,)), dma((chips,)), dma((chips,)), dma((nv,)), dma((nv,)),
        dma((chips,)), dma((chips,)), dma((chips,)), dma((chips,)), dma((2,)),
    ]
    return run(
        functools.partial(head_kernel, nb, nv, part),
        [SD((PICKS, D), FL), SD((D, rows), BF), SD((8, 128), FL)],
        scratch,
        [features, words, live, targets],
        "head",
        1,
        out_specs=[VM, HB, VM],
    )


def memory_weights(segments):
    length = segments.shape[0]
    places = jnp.arange(length, dtype=I32)
    slot_ids = jnp.arange(SLOTS, dtype=I32)
    inside = segments[None, :] == slot_ids[:, None]
    starts = jnp.sum((segments[None, :] < slot_ids[:, None]).astype(I32), axis=1)
    counts = jnp.sum(inside.astype(I32), axis=1)
    times = ((places[None, :] - starts[:, None]).astype(FL) + 0.5) / jnp.maximum(counts, 1)[:, None].astype(FL)
    centres = (jnp.arange(NB, dtype=FL) + 0.5) / NB
    offset = (times[:, None, :] - centres[None, :, None]) * NB
    basis = jnp.exp(-0.5 * offset * offset) * inside[:, None, :].astype(FL)
    total = jnp.sum(basis, axis=2, keepdims=True) + (counts == 0).astype(FL)[:, None, None]
    return (basis / total).reshape(SLOTS * NB, length)


def adamw(weight, moment, square, gradient, clip, count, decay, rate):
    gradient = gradient * clip
    moment = BETA_ONE * moment + (1 - BETA_ONE) * gradient
    square = BETA_TWO * square + (1 - BETA_TWO) * gradient * gradient
    fixed_moment = moment / (1 - BETA_ONE**count)
    fixed_square = square / (1 - BETA_TWO**count)
    weight = weight - rate * (fixed_moment / (jnp.sqrt(fixed_square) + ADAM_EPS) + decay * weight)
    return (weight, moment, square)


def slot_size(nv):
    mean = SEQ_LEN // nv
    return -(-(mean + int(5.5 * math.sqrt(mean))) // 32) * 32


def shards(
    nb, nv,
    tokens, targets, segments, counted, vocab_mask, step_count,
    table, table_moment, table_square,
    attend, attend_moment, attend_square,
    project, project_moment, project_square,
    expand, expand_moment, expand_square,
    contract, contract_moment, contract_square,
    gain, gain_moment, gain_square,
    shift, shift_moment, shift_square,
):
    rows, width = table.shape
    cap = slot_size(nv)
    table_t = table.T
    norms = jnp.concatenate([gain, shift], axis=0)
    packed = jnp.concatenate([attend[0], norms.T, jnp.zeros((width, EXTRA - 6), FL)], axis=1).astype(BF)
    a_all = lax.all_gather(packed, "batch", axis=0, tiled=True)
    p_all = lax.all_gather(project[0].astype(BF), "batch", axis=0, tiled=True)
    u_all = lax.all_gather(expand[0].astype(BF), "batch", axis=0, tiled=True)
    c_all = lax.all_gather(contract[0].astype(BF), "batch", axis=0, tiled=True)
    words = lax.all_gather(table_t.astype(BF), "batch", axis=0, tiled=True)

    mixing = memory_weights(segments).astype(BF)
    mixing_t = mixing.T
    key_seg = jnp.concatenate([jnp.repeat(jnp.arange(SLOTS, dtype=I32) + 1, NB), segments])
    key_pos = jnp.concatenate([jnp.full((SLOTS * NB,), -1, I32), jnp.arange(SEQ_LEN, dtype=I32)])
    keys = jnp.stack([key_seg, key_pos], axis=1)
    query_blk = counted // BLK
    query_seg = functools.reduce(
        lambda seg, i: jnp.where(query_blk == i, segments[i * BLK], seg), range(1, SEQ_LEN // BLK), jnp.broadcast_to(segments[0], counted.shape)
    )
    queries = jnp.concatenate([query_seg[None], counted[None], jnp.zeros((6, PICKS), I32)], axis=0)

    tok = tokens.reshape(nv, SEQ_LEN)
    x, ids, place, most, every = embed(nb, nv, cap, jnp.zeros((1,), I32), tok, table_t)
    turns = (most[0, 0].astype(I32) + cap - 1) // cap

    def more_rows(state):
        turn, total = state
        return turn + 1, total + embed(nb, nv, cap, turn[None], tok, table_t)[0]

    x = lax.while_loop(lambda state: state[0] < turns, more_rows, (jnp.int32(1), x))[1]

    hall, kv, q, hq, xq, mixed, lse, norm_rows = run(
        attend_kernel,
        [
            SD((KEYS, D), BF), SD((KEYS, 2 * D), BF), SD((PICKS, D), BF), SD((PICKS, D), BF), SD((PICKS, D), FL),
            SD((PICKS, D), BF), SD((NPAIR, 2, PICKS), FL), SD((8, D), FL),
        ],
        [],
        [x, a_all, mixing, counted[:, None], keys, queries],
        "attend", flops=7 * 10**9, moved=20 * 10**6,
    )
    x1, h2, z, act, x2, features = run(
        feed_kernel,
        [
            SD((PICKS, D), FL), SD((PICKS, D), BF), SD((PICKS, FF), FL), SD((PICKS, FF), BF), SD((PICKS, D), FL),
            SD((PICKS, D), BF),
        ],
        [],
        [xq, mixed, p_all, u_all, c_all, norm_rows],
        "feed", flops=2 * 10**9, moved=15 * 10**6,
    )
    df, dw, loss_block = head(nb, nv, features, words, vocab_mask[None, :], targets[:, None])
    loss_part = loss_block[0, 0]
    dw_sum = lax.psum_scatter(dw, "batch", scatter_dimension=0, tiled=True)

    dc, du, dp, dx1, dmixed, dnorm = run(
        feed_back_kernel,
        [
            SD((FF, D), BF), SD((D, FF), BF), SD((D, D), BF), SD((PICKS, D), FL), SD((PICKS, D), BF), SD((8, D), FL),
        ],
        [pltpu.VMEM((PICKS, D), FL)],
        [df, x2, x1, h2, z, act, mixed, p_all, u_all, c_all, norm_rows],
        "feed_back", flops=4 * 10**9, moved=30 * 10**6,
    )
    da, dx = run(
        attend_back_kernel,
        [SD((D, 3 * D + EXTRA), BF), SD((SEQ_LEN, D), BF)],
        [
            pltpu.VMEM((KEYS, 2 * D), BF), pltpu.VMEM((PICKS, D), BF), pltpu.VMEM((D, KEYS), BF),
            pltpu.VMEM((SEQ_LEN, D), FL), pltpu.VMEM((SEQ_LEN, D), FL), pltpu.VMEM((SLOTS * NB, D), BF),
        ],
        [counted, dmixed, q, kv, lse, hall, hq, a_all, x, dx1, mixing_t, keys, queries, norm_rows, dnorm],
        "attend_back", flops=12 * 10**9, moved=25 * 10**6,
        in_specs=[SM] + [VM] * 14,
    )
    sums = [
        lax.psum(lax.psum_scatter(item, "batch", scatter_dimension=0, tiled=True), "vocab").astype(FL)
        for item in (dc, du, dp, da)
    ]
    extra = unembed(nb, nv, cap, width, rows, dx, ids, place)

    def more_grads(state):
        turn, total = state
        later = later_slots(nv, cap, rows, every, turn)
        return turn + 1, total + unembed(
            nb, nv, cap, width, rows, dx, later, place - jnp.array([0, 1, 0, 0, 0, 0, 0, 0], I32)[None, :, None] * (turn * cap)
        )

    extra = lax.while_loop(lambda state: state[0] < turns, more_grads, (jnp.int32(1), extra))[1]

    grad_table = dw_sum.astype(FL) + extra
    grad_c, grad_u, grad_p, grad_a = sums
    grad_norms = grad_a[:, 3 * D : 3 * D + 6].T
    grad_a = grad_a[:, : 3 * D]
    at_root = (lax.axis_index("vocab") == 0).astype(FL)
    owned = sum(jnp.sum(item * item) for item in (grad_a, grad_p, grad_u, grad_c, grad_norms))
    squares, loss = lax.psum(
        (jnp.sum(grad_table * grad_table) + at_root * owned, at_root * loss_part), ("batch", "vocab")
    )
    gradient_norm = jnp.sqrt(squares)
    clip = jnp.minimum(1.0, MAX_NORM / (gradient_norm + 1e-06))
    count = step_count[0].astype(FL)

    def update(weight, moment, square, gradient, decay=DECAY, rate=LEARN_RATE):
        return adamw(weight, moment, square, gradient, clip, count, decay, rate)

    table_out = [item.T for item in update(table_t, table_moment.T, table_square.T, grad_table)]
    attend_out = update(attend, attend_moment, attend_square, grad_a[None])
    project_out = update(project, project_moment, project_square, grad_p[None])
    expand_out = update(expand, expand_moment, expand_square, grad_u[None])
    contract_out = update(contract, contract_moment, contract_square, grad_c[None])
    gain_out = update(gain, gain_moment, gain_square, grad_norms[:3], 0.0, NORM_RATE)
    shift_out = update(shift, shift_moment, shift_square, grad_norms[3:], 0.0, NORM_RATE)
    return (
        loss, gradient_norm, *table_out, *attend_out, *project_out, *expand_out, *contract_out, *gain_out, *shift_out,
    )


def solution(mesh):
    nb, nv = mesh.shape["batch"], mesh.shape["vocab"]
    both, split, middle, last = P(("batch", "vocab")), P("vocab", "batch"), P(None, "batch", None), P(None, "batch")
    state = (split,) * 3 + (middle,) * 12 + (last,) * 6
    return jax.shard_map(
        functools.partial(shards, nb, nv),
        mesh=mesh,
        in_specs=(P("batch"), P("batch"), both, both, P("vocab"), P()) + state,
        out_specs=(P(), P()) + state,
        check_vma=False,
    )
```

```python
import functools
import math

import jax
import jax.numpy as jnp
from jax import lax
from jax.experimental import pallas as pl
from jax.experimental.pallas import tpu as pltpu
from jax.sharding import PartitionSpec as P

D = 768
H = 12
HD = 64
FF = 3072
NB = 256
SEG_BLOCKS = 4
SLOTS = SEG_BLOCKS - 2
SEQ_LEN = 1024
PICKS = 128
KEYS = SLOTS * NB + SEQ_LEN
BLK = 256
PAIR = 2 * HD
NPAIR = H // 2
EXTRA = 256
WIDE = (3 * D + EXTRA, D, FF, D)

NORM_EPS = 1e-05
MAX_NORM = 0.02
LEARN_RATE = 0.04
NORM_RATE = 0.5
BETA_ONE = 0.9
BETA_TWO = 0.999
ADAM_EPS = 1e-08
DECAY = 0.1
NEG_BIG = -1e30
BF = jnp.bfloat16
FL = jnp.float32
I32 = jnp.int32
MESH = pl.DeviceIdType.MESH
SD = jax.ShapeDtypeStruct
VM = pl.BlockSpec(memory_space=pltpu.VMEM)
SM = pl.BlockSpec(memory_space=pltpu.SMEM)
HB = pl.BlockSpec(memory_space=pl.ANY)
LIMIT = 62 * 2**20


def nn(a, b):
    return lax.dot_general(a, b, (((1,), (0,)), ((), ())), preferred_element_type=FL)


def nt(a, b):
    return lax.dot_general(a, b, (((1,), (1,)), ((), ())), preferred_element_type=FL)


def iota(shape, axis):
    return lax.broadcasted_iota(I32, shape, axis)


def lanes(start, size):
    return pl.ds(pl.multiple_of(start, 128), size)


def chunk_of(rows, want):
    return want if rows % want == 0 else rows


def run(kernel, outs, scratch, ins, name, collective=None, flops=0, moved=0, out_specs=None, in_specs=None):
    return pl.pallas_call(
        kernel,
        out_shape=outs,
        in_specs=in_specs if in_specs is not None else [VM] * len(ins),
        out_specs=out_specs if out_specs is not None else [VM] * len(outs),
        scratch_shapes=scratch,
        compiler_params=pltpu.CompilerParams(
            vmem_limit_bytes=LIMIT,
            collective_id=collective,
            has_side_effects=collective is not None,
        ),
        cost_estimate=pl.CostEstimate(flops=flops, bytes_accessed=moved, transcendentals=0),
        name=name,
    )(*ins)


def send(source, target, out_sem, in_sem, device):
    return pltpu.make_async_remote_copy(
        src_ref=source, dst_ref=target, send_sem=out_sem, recv_sem=in_sem, device_id=device, device_id_type=MESH
    )


def meet(axes):
    barrier = pltpu.get_barrier_semaphore()
    count = 0
    for axis, size in axes:
        me = lax.axis_index(axis)

        def greet(step, carry, axis=axis, size=size, me=me):
            pl.semaphore_signal(barrier, inc=1, device_id={axis: lax.rem(me + step, size)}, device_id_type=MESH)
            return carry

        lax.fori_loop(1, size, greet, 0)
        count += size - 1
    pl.semaphore_wait(barrier, count)


def each(start, stop, body):
    def step(index, carry):
        body(index)
        return carry

    lax.fori_loop(start, stop, step, 0)


def embed_kernel(
    nb, nv, cap, part, first, *refs
):
    round_ref, tok_ref, table_ref = refs[:3]
    shards, refs = (refs[3:7], refs[7:]) if first else ((), refs[3:])
    x_ref, ids_ref, place_ref, most_ref, tok_ref_all = refs[:5]
    wholes, refs = (refs[5:9], refs[9:]) if first else ((), refs[5:])
    words, before, ranks, work, sent, got, spread, mixed, turned = refs[:9]
    tok_out, tok_in, row_out, row_in, mix_out, mix_in = refs[9:15]
    b, v = lax.axis_index("batch"), lax.axis_index("vocab")
    width, rows = table_ref.shape
    shift = round_ref[0] * cap
    meet((("batch", nb), ("vocab", nv)))
    gather = WeightGather(nb, shards, wholes, *refs[15:20]) if first else None

    def tok_copy(step):
        return send(
            tok_ref, tok_ref_all.at[b], tok_out.at[step], tok_in.at[step], {"batch": lax.rem(b + step, nb)}
        )

    for step in range(1, nb):
        tok_copy(step).start()
    if first:
        gather.start()
    tok_ref_all[b] = tok_ref[...]
    words[...] = table_ref[...].astype(BF)
    before[...] = (iota((SEQ_LEN, SEQ_LEN), 0) < iota((SEQ_LEN, SEQ_LEN), 1)).astype(FL).astype(BF)
    for step in range(1, nb):
        tok_copy(step).wait()

    base = v * rows
    most = jnp.zeros((nv, 1), FL)
    for p in range(nb):
        ids = tok_ref_all[p]
        mine = (ids >= base) & (ids < base + rows)
        rank = nn(mine.astype(FL).astype(BF), before[...])
        ranks[p] = jnp.where(mine, rank.astype(I32) - shift, -1)
        for owner in range(nv):
            theirs = (ids >= owner * rows) & (ids < (owner + 1) * rows)
            most = jnp.maximum(most, jnp.sum(theirs.astype(FL), axis=1, keepdims=True))
    most_ref[...] = jnp.broadcast_to(jnp.max(most, axis=0, keepdims=True), most_ref.shape)

    def row_copy(step):
        return send(
            sent.at[step], got.at[v], row_out.at[step], row_in.at[step], {"vocab": lax.rem(v + step, nv)}
        )

    def build(turn):
        step = lax.rem(turn, nv)
        dest = lax.rem(v + step, nv)
        found = []
        for p in range(nb):
            pick = (iota((cap, SEQ_LEN), 0) == ranks[p, pl.ds(dest, 1), :]).astype(FL).astype(BF)
            local = tok_ref_all[p, pl.ds(dest, 1), :] - base
            line = iota((8, SEQ_LEN), 0)
            high, low = lax.shift_right_arithmetic(local, 7), lax.bitwise_and(local, 127)
            digits = jnp.where(line == 0, high, jnp.where(line == 1, low, 0)).astype(FL).astype(BF)
            both = nt(pick, digits)
            found.append((both[:, 0:1] * 128.0 + both[:, 1:2]).astype(I32))
        index = jnp.concatenate(found, axis=0)
        ids_ref[dest] = index
        work[...] = jnp.zeros_like(work)

        def piece(j):
            hot = (index - j * part == iota((nb * cap, part), 1)).astype(FL).astype(BF)
            work[...] += nt(hot, words[:, lanes(j * part, part)])

        each(0, rows // part, piece)
        block = work[...].T.astype(BF)

        @pl.when(step > 0)
        def _():
            sent[step] = block
            row_copy(step).start()

        @pl.when(step == 0)
        def _():
            got[v] = block

    each(1, nv + 1, build)
    if first:
        gather.pass_on()

    keys = []
    for p in range(nb):
        ids = tok_ref_all[p, pl.ds(v, 1), :]
        owner = iota((nv, SEQ_LEN), 0)
        theirs = (ids >= owner * rows) & (ids < (owner + 1) * rows)
        rank = nn(theirs.astype(FL).astype(BF), before[...])
        place = jnp.sum(jnp.where(theirs, rank, 0.0), axis=0, keepdims=True).astype(I32) - shift
        holder = jnp.sum(jnp.where(theirs, owner.astype(FL), 0.0), axis=0, keepdims=True).astype(I32)
        line = iota((8, SEQ_LEN), 0)
        place_ref[p] = jnp.where(line == 0, holder, jnp.where(line == 1, place, 0))
        keys.append((holder, place))
        spread[p] = jnp.zeros((width, SEQ_LEN), FL)

    def take(turn):
        step = lax.rem(turn, nv)
        source = lax.rem(v - step + nv, nv)

        @pl.when(step > 0)
        def _():
            row_copy(step).wait()

        block = got[source]
        for p in range(nb):
            holder, place = keys[p]
            key = jnp.where(holder == source, place, -1)
            hot = (iota((cap, SEQ_LEN), 0) == key).astype(FL).astype(BF)
            spread[p] += nn(block[:, p * cap : (p + 1) * cap], hot)

    each(1, nv + 1, take)

    def mix_copy(step):
        return send(
            mixed.at[step], turned.at[b], mix_out.at[step], mix_in.at[step], {"batch": lax.rem(b + step, nb)}
        )

    for step in range(1, nb):
        mixed[step] = spread[lax.rem(b + step, nb)].astype(BF)
        mix_copy(step).start()
    turned[b] = spread[b].astype(BF)
    for step in range(1, nb):
        mix_copy(step).wait()
    x_ref[...] = turned[...].reshape(nb * width, SEQ_LEN).T
    if first:
        gather.finish()


class WeightGather:
    def __init__(self, nb, shards, wholes, own_sem, out_sem, in_sem, pair_out, pair_in):
        self.nb, self.shards, self.wholes = nb, shards, wholes
        self.own_sem, self.out_sem, self.in_sem, self.pair_out, self.pair_in = own_sem, out_sem, in_sem, pair_out, pair_in
        self.b, v = lax.axis_index("batch"), lax.axis_index("vocab")
        self.core = lax.rem(v, 2)
        self.sibling = {"vocab": v + 1 - 2 * self.core}

    def flip(self, bits):
        b = self.b
        low, high = lax.rem(b, 2), b // 2
        return (high if bits < 2 else 1 - high) * 2 + (low if bits % 2 == 0 else 1 - low)

    def place(self, w, owner, top, size):
        rows, cols = self.shards[w].shape
        first = pl.multiple_of(owner * rows + top, 16)
        return self.wholes[w].at[pl.ds(first, size), lanes(self.core * (cols // 2), cols // 2)]

    def routes(self, w):
        rows = self.shards[w].shape[0]
        if self.nb == 4:
            half = rows // 2
            return [
                (self.b, 0, rows, self.flip(1), self.flip(1)),
                (self.b, 0, rows, self.flip(2), self.flip(2)),
                (self.flip(1), 0, half, self.flip(2), self.flip(3)),
                (self.flip(2), half, half, self.flip(1), self.flip(3)),
            ]
        others = [lax.rem(self.b + step, self.nb) for step in range(1, self.nb)]
        came = [lax.rem(self.b - step + self.nb, self.nb) for step in range(1, self.nb)]
        return [(self.b, 0, rows, other, source) for other, source in zip(others, came)]

    def own_copy(self, w):
        rows = self.shards[w].shape[0]
        first = pl.multiple_of(self.b * rows, 16)
        return pltpu.make_async_copy(self.shards[w], self.wholes[w].at[pl.ds(first, rows), :], self.own_sem.at[w])

    def copy(self, w, k):
        owner, top, size, device, _ = self.routes(w)[k]
        cols = self.shards[w].shape[1]
        if self.nb == 4 and k >= 2:
            source = self.place(w, owner, top, size)
        else:
            source = self.shards[w].at[:, lanes(self.core * (cols // 2), cols // 2)]
        target = self.place(w, owner, top, size)
        return send(source, target, self.out_sem.at[w, k], self.in_sem.at[w, k], {"batch": device})

    def pair(self, w, k):
        _, top, size, _, arrived = self.routes(w)[k]
        ref = self.place(w, arrived, top, size)
        return send(ref, ref, self.pair_out.at[w, k], self.pair_in.at[w, k], self.sibling)

    def start(self):
        for w in range(4):
            for k in range(2 if self.nb == 4 else self.nb - 1):
                self.copy(w, k).start()
        for w in range(4):
            self.own_copy(w).start()

    def pass_on(self):
        if self.nb != 4:
            return
        for w in range(4):
            for k in range(2):
                self.copy(w, k).wait_recv()
                self.copy(w, k + 2).start()
                self.pair(w, k).start()

    def finish(self):
        for w in range(4):
            for k in range(2 if self.nb == 4 else 0, len(self.routes(w))):
                self.copy(w, k).wait_recv()
                self.pair(w, k).start()
        for w in range(4):
            self.own_copy(w).wait()
            for k in range(len(self.routes(w))):
                self.copy(w, k).wait_send()
                self.pair(w, k).wait()


def embed(nb, nv, cap, turn, tok, table, shards=()):
    width, rows = table.shape
    part = chunk_of(rows, 640)
    count = nb * cap
    outs = [
        SD((SEQ_LEN, D), BF),
        SD((nv, count, 1), I32),
        SD((nb, 8, SEQ_LEN), I32),
        SD((8, 128), FL),
        SD((nb, nv, SEQ_LEN), I32),
    ]
    first = len(shards) > 0
    outs += [SD((nb * item.shape[0], item.shape[1]), BF) for item in shards]
    dma = pltpu.SemaphoreType.DMA
    scratch = [
        pltpu.VMEM((width, rows), BF),
        pltpu.VMEM((SEQ_LEN, SEQ_LEN), BF),
        pltpu.VMEM((nb, nv, SEQ_LEN), I32),
        pltpu.VMEM((count, width), FL),
        pltpu.VMEM((nv, width, count), BF),
        pltpu.VMEM((nv, width, count), BF),
        pltpu.VMEM((nb, width, SEQ_LEN), FL),
        pltpu.VMEM((nb, width, SEQ_LEN), BF),
        pltpu.VMEM((nb, width, SEQ_LEN), BF),
        dma((nb,)), dma((nb,)), dma((nv,)), dma((nv,)), dma((nb,)), dma((nb,)),
    ]
    if first:
        scratch += [dma((4,)), dma((4, 4)), dma((4, 4)), dma((4, 4)), dma((4, 4))]
    return run(
        functools.partial(embed_kernel, nb, nv, cap, part, first), outs, scratch, [turn, tok, table, *shards],
        "embed" if first else "embed_more", 0 if first else 3,
        in_specs=[SM, VM, VM] + [HB] * len(shards), out_specs=[VM] * 5 + [HB] * len(shards),
    )


class GradientSum:
    def __init__(self, nb, nv, grads, sums, refs):
        self.nb, self.nv, self.grads, self.sums = nb, nv, grads, sums
        self.own, self.near, self.shard, self.total = refs[0:4], refs[4:8], refs[8:12], refs[12:16]
        self.bits, self.result = refs[16:20], refs[20:24]
        (self.load_sem, self.pair_out, self.pair_in, self.mix_out, self.mix_in, self.cut_out, self.cut_in,
         self.all_out, self.all_in, self.last_out, self.last_in, self.store_sem) = refs[24:36]
        self.b, v = lax.axis_index("batch"), lax.axis_index("vocab")
        self.core, self.chip, self.chips = lax.rem(v, 2), v // 2, nv // 2
        self.sibling = {"vocab": v + 1 - 2 * self.core}

    def half(self, w, core):
        cols = self.grads[w].shape[1] // 2
        return lanes(core * cols, cols)

    def load(self, w):
        return pltpu.make_async_copy(self.grads[w].at[:, self.half(w, self.core)], self.own[w], self.load_sem.at[w])

    def pair(self, w):
        source = self.grads[w].at[:, self.half(w, 1 - self.core)]
        return send(source, self.near[w], self.pair_out.at[w], self.pair_in.at[w], self.sibling)

    def start(self):
        for w in range(4):
            self.pair(w).start()
            self.load(w).start()

    def mix(self, w, step):
        other = lax.rem(self.b + step, self.nb)
        rows = self.own[w].shape[0] // self.nb
        source = self.own[w].at[pl.ds(pl.multiple_of(other * rows, 16), rows), :]
        return send(source, self.shard[w].at[step], self.mix_out.at[w, step], self.mix_in.at[w, step], {"batch": other})

    def scatter(self):
        for w in range(4):
            self.load(w).wait()
            self.pair(w).wait()
            rows = self.own[w].shape[0] // self.nb

            def add(i, w=w, rows=rows):
                cut = pl.ds(pl.multiple_of(i * rows, 16), rows)
                self.own[w][cut, :] = (self.own[w][cut, :].astype(FL) + self.near[w][cut, :].astype(FL)).astype(BF)

            each(0, self.nb, add)
            for step in range(1, self.nb):
                self.mix(w, step).start()

    def pieces(self, w):
        rows = self.total[w].shape[0]
        count = max(n for n in range(1, self.chips + 1) if rows % (16 * n) == 0)
        return count, rows // count

    def peer(self, step):
        other = lax.rem(self.chip + step, self.chips)
        return other, {"vocab": other * 2 + self.core}

    def cut(self, w, step):
        other, device = self.peer(step)
        size = self.pieces(w)[1]
        source = self.total[w].at[pl.ds(pl.multiple_of(other * size, 16), size), :]
        return send(source, self.bits[w].at[step], self.cut_out.at[w, step], self.cut_in.at[w, step], device)

    def back(self, w, step):
        size = self.pieces(w)[1]
        place = self.result[w].at[pl.ds(pl.multiple_of(self.chip * size, 16), size), :]
        return send(place, place, self.all_out.at[w, step], self.all_in.at[w, step], self.peer(step)[1])

    def back_recv(self, w, step):
        source = lax.rem(self.chip - step + self.chips, self.chips)
        size = self.pieces(w)[1]
        place = self.result[w].at[pl.ds(pl.multiple_of(source * size, 16), size), :]
        return send(place, place, self.all_out.at[w, step], self.all_in.at[w, step], self.peer(step)[1])

    def reduce(self):
        for w in range(4):
            rows = self.total[w].shape[0]
            for step in range(1, self.nb):
                self.mix(w, step).wait()
            here = pl.ds(pl.multiple_of(self.b * rows, 16), rows)
            value = self.own[w][here, :].astype(FL)
            for step in range(1, self.nb):
                value = value + self.shard[w][step].astype(FL)
            self.total[w][...] = value.astype(BF)
            count = self.pieces(w)[0]

            def go(step, w=w, count=count):
                @pl.when(self.peer(step)[0] < count)
                def _():
                    self.cut(w, step).start()

            each(1, self.chips, go)

    def collect(self):
        for w in range(4):
            count, size = self.pieces(w)
            mine = pl.ds(pl.multiple_of(self.chip * size, 16), size)

            @pl.when(self.chip < count)
            def _(w=w, mine=mine):
                def add(step, value):
                    self.cut(w, step).wait_recv()
                    return value + self.bits[w][step].astype(FL)

                value = lax.fori_loop(1, self.chips, add, self.total[w][mine, :].astype(FL))
                self.result[w][mine, :] = value.astype(BF)
                each(1, self.chips, lambda step: self.back(w, step).start())

            def sent(step, w=w, count=count):
                @pl.when(self.peer(step)[0] < count)
                def _():
                    self.cut(w, step).wait_send()

            each(1, self.chips, sent)

    def last(self, w):
        return send(
            self.result[w], self.sums[w].at[:, self.half(w, self.core)], self.last_out.at[w], self.last_in.at[w], self.sibling
        )

    def store(self, w):
        return pltpu.make_async_copy(self.result[w], self.sums[w].at[:, self.half(w, self.core)], self.store_sem.at[w])

    def finish(self):
        for w in range(4):
            count = self.pieces(w)[0]

            def got(step, w=w, count=count):
                @pl.when(lax.rem(self.chip - step + self.chips, self.chips) < count)
                def _():
                    self.back_recv(w, step).wait_recv()

            each(1, self.chips, got)
            self.last(w).start()
            self.store(w).start()
        for w in range(4):
            count = self.pieces(w)[0]

            @pl.when(self.chip < count)
            def _(w=w):
                each(1, self.chips, lambda step: self.back(w, step).wait_send())

            self.store(w).wait()
            self.last(w).wait_send()
            other = self.sums[w].at[:, self.half(w, 1 - self.core)]
            send(other, other, self.last_out.at[w], self.last_in.at[w], self.sibling).wait_recv()


def gradient_scratch(nb, nv, grads):
    chips = nv // 2
    halves = [(item.shape[0], item.shape[1] // 2) for item in grads]
    shards = [(rows // nb, cols) for rows, cols in halves]
    sizes = [rows // max(n for n in range(1, chips + 1) if rows % (16 * n) == 0) for rows, _ in shards]
    dma = pltpu.SemaphoreType.DMA
    return (
        [pltpu.VMEM(item, BF) for item in halves] * 2
        + [pltpu.VMEM((nb, *item), BF) for item in shards]
        + [pltpu.VMEM(item, BF) for item in shards]
        + [pltpu.VMEM((chips, size, item[1]), BF) for size, item in zip(sizes, shards)]
        + [pltpu.VMEM(item, BF) for item in shards]
        + [dma((4,)), dma((4,)), dma((4,)), dma((4, nb)), dma((4, nb)), dma((4, chips)), dma((4, chips))]
        + [dma((4, chips)), dma((4, chips)), dma((4,)), dma((4,)), dma((4,))]
    )


def unembed_kernel(nb, nv, cap, part, first, *refs):
    x_ref, ids_ref, place_ref = refs[:3]
    grads, refs = (refs[3:7], refs[7:]) if first else ((), refs[3:])
    out_ref = refs[0]
    sums, refs = (refs[1:5], refs[5:]) if first else ((), refs[1:])
    turned, parts, sent, got, mix_out, mix_in, row_out, row_in = refs[:8]
    layer = GradientSum(nb, nv, grads, sums, refs[8:]) if first else None
    b, v = lax.axis_index("batch"), lax.axis_index("vocab")
    width, rows = out_ref.shape
    meet((("batch", nb), ("vocab", nv)))
    turned[...] = x_ref[...].T.reshape(nb, width, SEQ_LEN)

    def mix_copy(step):
        other = lax.rem(b + step, nb)
        return send(turned.at[other], parts.at[b], mix_out.at[step], mix_in.at[step], {"batch": other})

    for step in range(1, nb):
        mix_copy(step).start()
    if first:
        layer.start()
    parts[b] = turned[b]
    for step in range(1, nb):
        mix_copy(step).wait()

    def row_copy(step):
        return send(
            sent.at[step], got.at[v], row_out.at[step], row_in.at[step], {"vocab": lax.rem(v + step, nv)}
        )

    def build(turn):
        step = lax.rem(turn, nv)
        owner = lax.rem(v + step, nv)
        blocks = []
        for p in range(nb):
            key = jnp.where(place_ref[p, 0:1, :] == owner, place_ref[p, 1:2, :], -1)
            hot = (iota((cap, SEQ_LEN), 0) == key).astype(FL).astype(BF)
            blocks.append(nt(parts[p], hot).astype(BF))
        block = jnp.concatenate(blocks, axis=1)

        @pl.when(step > 0)
        def _():
            sent[step] = block
            row_copy(step).start()

        @pl.when(step == 0)
        def _():
            got[v] = block

    each(1, nv + 1, build)
    if first:
        layer.scatter()
    out_ref[...] = jnp.zeros_like(out_ref)

    def take(step):
        source = lax.rem(v - step + nv, nv)

        @pl.when(step > 0)
        def _():
            row_copy(step).wait()

        block, index = got[source], ids_ref[source]

        def piece(j):
            hot = (index - j * part == iota((nb * cap, part), 1)).astype(FL).astype(BF)
            out_ref[:, lanes(j * part, part)] += nn(block, hot)

        each(0, rows // part, piece)

    each(0, nv // 2, take)
    if first:
        layer.reduce()
    each(nv // 2, nv, take)
    if first:
        layer.collect()
        layer.finish()


def unembed(nb, nv, cap, width, rows, grad, ids, place, grads=()):
    part = chunk_of(rows, 640)
    count = nb * cap
    dma = pltpu.SemaphoreType.DMA
    scratch = [
        pltpu.VMEM((nb, width, SEQ_LEN), BF),
        pltpu.VMEM((nb, width, SEQ_LEN), BF),
        pltpu.VMEM((nv, width, count), BF),
        pltpu.VMEM((nv, width, count), BF),
        dma((nb,)), dma((nb,)), dma((nv,)), dma((nv,)),
    ]
    first = len(grads) > 0
    if first:
        scratch += gradient_scratch(nb, nv, grads)
    return run(
        functools.partial(unembed_kernel, nb, nv, cap, part, first),
        [SD((width, rows), FL)] + [SD((item.shape[0] // nb, item.shape[1]), BF) for item in grads],
        scratch,
        [grad, ids, place, *grads],
        "unembed" if first else "unembed_more",
        2 if first else 4,
        in_specs=[VM] * 3 + [HB] * len(grads),
        out_specs=[VM] + [HB] * len(grads),
    )


def later_slots(nv, cap, rows, every, turn):
    nb = every.shape[0]
    v = lax.axis_index("vocab")
    local = every - v * rows
    mine = (local >= 0) & (local < rows)
    rank = jnp.cumsum(mine.astype(I32), axis=-1) - 1 - turn * cap
    hot = (rank[:, :, None, :] == jnp.arange(cap)[None, None, :, None]) & mine[:, :, None, :]
    ids = jnp.sum(jnp.where(hot, local[:, :, None, :], 0), axis=-1)
    return jnp.transpose(ids, (1, 0, 2)).reshape(nv, nb * cap, 1)


def standard(value):
    centre = value - jnp.mean(value, axis=-1, keepdims=True)
    spread = jnp.mean(centre * centre, axis=-1, keepdims=True)
    scale = lax.rsqrt(spread + NORM_EPS)
    return centre * scale, scale


def norm_back(unit, scale, gain, upstream):
    inner = upstream * gain
    first = jnp.mean(inner, axis=-1, keepdims=True)
    second = jnp.mean(inner * unit, axis=-1, keepdims=True)
    grad = scale * (inner - first - unit * second)
    return grad, jnp.sum(upstream * unit, axis=0, keepdims=True), jnp.sum(upstream, axis=0, keepdims=True)


def head_lanes(value, head):
    lane = iota(value.shape, 1)
    keep = (lane < HD) if head == 0 else (lane >= HD)
    return jnp.where(keep, value, jnp.zeros_like(value))


def visible_keys(key_ref, query_ref):
    return (key_ref[:, 0:1] == query_ref[0:1, :]) & (key_ref[:, 1:2] <= query_ref[1:2, :])


def memory_weights(segments, slot):
    length = segments.shape[1]
    inside = (segments == slot).astype(FL)
    start = jnp.sum((segments < slot).astype(FL), axis=1, keepdims=True)
    count = jnp.sum(inside, axis=1, keepdims=True)
    times = (iota((1, length), 1).astype(FL) - start + 0.5) / jnp.maximum(count, 1.0)
    centres = (iota((NB, 1), 0).astype(FL) + 0.5) / NB
    offset = (times - centres) * NB
    basis = jnp.exp(-0.5 * offset * offset) * inside
    total = jnp.sum(basis, axis=1, keepdims=True) + (count == 0.0).astype(FL)
    return basis / total


def attend_kernel(
    x_ref, a_ref, seg_ref, pick_ref, key_ref, query_ref,
    hall_ref, kv_ref, q_ref, hq_ref, xq_ref, o_ref, lse_ref, norm_ref, mixt_ref,
):
    norm_ref[...] = a_ref[:, 3 * D : 3 * D + 128].astype(FL).T[:8, :]
    gain, bias = norm_ref[0:1, :], norm_ref[3:4, :]

    def normalize(i):
        unit, _ = standard(x_ref[pl.ds(i * BLK, BLK), :].astype(FL))
        hall_ref[pl.ds(SLOTS * NB + i * BLK, BLK), :] = (unit * gain + bias).astype(BF)

    each(0, SEQ_LEN // BLK, normalize)
    normed = hall_ref[SLOTS * NB :, :]
    for slot in range(SLOTS):
        mixing = memory_weights(seg_ref[...], slot).astype(BF)
        hall_ref[slot * NB : (slot + 1) * NB, :] = nn(mixing, normed).astype(BF)
        mixt_ref[:, slot * NB : (slot + 1) * NB] = mixing.T

    def project(i):
        kv_ref[pl.ds(i * BLK, BLK), :] = nn(hall_ref[pl.ds(i * BLK, BLK), :], a_ref[:, D : 3 * D]).astype(BF)

    each(0, KEYS // BLK, project)
    pick = (pick_ref[...] == iota((PICKS, SEQ_LEN), 1)).astype(FL).astype(BF)
    hq_ref[...] = nn(pick, normed).astype(BF)
    xq_ref[...] = nn(pick, x_ref[...])
    q_ref[...] = nn(hq_ref[...], a_ref[:, :D]).astype(BF)
    visible = visible_keys(key_ref, query_ref)

    def attend(p):
        keys = kv_ref[:, lanes(p * PAIR, PAIR)]
        values = kv_ref[:, lanes(D + p * PAIR, PAIR)].T
        queries = q_ref[:, lanes(p * PAIR, PAIR)] * HD ** (-0.5)
        outs = []
        for head in range(2):
            scores = jnp.where(visible, nt(keys, head_lanes(queries, head)), NEG_BIG)
            peak = jnp.max(scores, axis=0, keepdims=True)
            expo = jnp.exp(scores - peak)
            total = jnp.sum(expo, axis=0, keepdims=True)
            probs = (expo * (1.0 / total)).astype(BF)
            outs.append(nn(values[head * HD : (head + 1) * HD, :], probs))
            lse_ref[p, head : head + 1, :] = peak + jnp.log(total)
        o_ref[:, lanes(p * PAIR, PAIR)] = jnp.concatenate(outs, axis=0).T.astype(BF)

    each(0, NPAIR, attend)


def feed_kernel(xq_ref, o_ref, p_ref, u_ref, c_ref, norm_ref, x1_ref, h2_ref, z_ref, act_ref, x2_ref, f_ref):
    x1 = xq_ref[...] + nn(o_ref[...], p_ref[...])
    x1_ref[...] = x1
    unit, _ = standard(x1)
    h2 = (unit * norm_ref[1:2, :] + norm_ref[4:5, :]).astype(BF)
    h2_ref[...] = h2
    x2_ref[...] = x1

    def piece(j):
        cut = lanes(j * D, D)
        z = nn(h2, u_ref[:, cut])
        z_ref[:, cut] = z
        act = jax.nn.gelu(z, approximate=True).astype(BF)
        act_ref[:, cut] = act
        x2_ref[...] += nn(act, c_ref[pl.ds(j * D, D), :])

    each(0, FF // D, piece)
    unit, _ = standard(x2_ref[...])
    f_ref[...] = (unit * norm_ref[2:3, :] + norm_ref[5:6, :]).astype(BF)


def feed_back_kernel(
    df_ref, x2_ref, x1_ref, h2_ref, z_ref, act_ref, o_ref, p_ref, u_ref, c_ref, norm_ref,
    dc_ref, du_ref, dp_ref, dx1_ref, do_ref, dnorm_ref, dh2,
):
    unit, scale = standard(x2_ref[...])
    dx2, gain_last, bias_last = norm_back(unit, scale, norm_ref[2:3, :], df_ref[...])
    dy = dx2.astype(BF)
    dh2[...] = jnp.zeros_like(dh2)
    h2t = h2_ref[...].T

    def piece(j):
        cut = lanes(j * D, D)
        dc_ref[pl.ds(j * D, D), :] = nn(act_ref[:, cut].T, dy).astype(BF)
        dact = nt(dy, c_ref[pl.ds(j * D, D), :])
        z = z_ref[:, cut]
        k = math.sqrt(2.0 / math.pi)
        t = jnp.tanh(k * (z + 0.044715 * z * z * z))
        slope = 0.5 * (1.0 + t) + 0.5 * z * (1.0 - t * t) * (k * (1.0 + 3 * 0.044715 * z * z))
        dz = (dact * slope).astype(BF)
        du_ref[:, cut] = nn(h2t, dz).astype(BF)
        dh2[...] += nt(dz, u_ref[:, cut])

    each(0, FF // D, piece)
    unit, scale = standard(x1_ref[...])
    dx1, gain_two, bias_two = norm_back(unit, scale, norm_ref[1:2, :], dh2[...])
    dx1 = dx1 + dx2
    dx1_ref[...] = dx1
    da = dx1.astype(BF)
    dp_ref[...] = nn(o_ref[...].T, da).astype(BF)
    do_ref[...] = nt(da, p_ref[...]).astype(BF)
    zero = jnp.zeros_like(gain_last)
    dnorm_ref[...] = jnp.concatenate([zero, gain_two, gain_last, zero, bias_two, bias_last, zero, zero], axis=0)


def attend_back_kernel(
    pos_ref, do_ref, q_ref, kv_ref, lse_ref, hall_ref, hq_ref, a_ref, x_ref, dx1_ref, mixt_ref, key_ref, query_ref,
    norm_ref, dnorm_ref, da_ref, dx_ref, dkv, dq, hallt, dh, dxin, dmem,
):
    visible = visible_keys(key_ref, query_ref)

    def attend(p):
        cut = lanes(p * PAIR, PAIR)
        keys = kv_ref[:, cut]
        values = kv_ref[:, lanes(D + p * PAIR, PAIR)]
        turned = keys.T
        queries = q_ref[:, cut] * HD ** (-0.5)
        grads = do_ref[:, cut]
        outs = []
        dk = dv = None
        for head in range(2):
            own, grad = head_lanes(queries, head), head_lanes(grads, head)
            scores = jnp.where(visible, nt(keys, own), NEG_BIG)
            probs = jnp.exp(scores - lse_ref[p, head : head + 1, :])
            dprobs = nt(values, grad)
            inner = jnp.sum(probs * dprobs, axis=0, keepdims=True)
            dscores = (probs * (dprobs - inner)).astype(BF)
            outs.append(nn(turned[head * HD : (head + 1) * HD, :], dscores))
            one, two = nn(dscores, own), nn(probs.astype(BF), grad)
            dk = one if head == 0 else dk + one
            dv = two if head == 0 else dv + two
        dq[:, cut] = (jnp.concatenate(outs, axis=0).T * HD ** (-0.5)).astype(BF)
        dkv[:, cut] = dk.astype(BF)
        dkv[:, lanes(D + p * PAIR, PAIR)] = dv.astype(BF)

    each(0, NPAIR, attend)
    da_ref[:, :D] = nn(hq_ref[...].T, dq[...]).astype(BF)

    def turn(i):
        hallt[:, lanes(i * BLK, BLK)] = hall_ref[pl.ds(i * BLK, BLK), :].T

    each(0, KEYS // BLK, turn)

    def weights(j):
        cut = lanes(j * BLK, BLK)
        da_ref[:, lanes(D + j * BLK, BLK)] = nn(hallt[...], dkv[:, cut]).astype(BF)

    each(0, 2 * D // BLK, weights)

    def memory(i):
        cut = pl.ds(i * BLK, BLK)
        dmem[cut, :] = nt(dkv[cut, :], a_ref[:, D : 3 * D]).astype(BF)

    each(0, SLOTS, memory)

    def local(i):
        cut = pl.ds(i * BLK, BLK)
        dh[cut, :] = nt(dkv[pl.ds(SLOTS * NB + i * BLK, BLK), :], a_ref[:, D : 3 * D]) + nn(mixt_ref[cut, :], dmem[...])

    each(0, SEQ_LEN // BLK, local)
    dxin[:PICKS, :] = nt(dq[...], a_ref[:, :D])

    def scatter_query(k):
        row = pl.ds(pos_ref[k], 1)
        dh[row, :] += dxin[pl.ds(k, 1), :]

    each(0, PICKS, scatter_query)
    gain = norm_ref[0:1, :]
    da_rows = [jnp.zeros((1, D), FL), jnp.zeros((1, D), FL)]

    def finish(i, carry):
        cut = pl.ds(i * BLK, BLK)
        unit, scale = standard(x_ref[cut, :].astype(FL))
        grad, dgain, dbias = norm_back(unit, scale, gain, dh[cut, :])
        dxin[cut, :] = grad
        return carry[0] + dgain, carry[1] + dbias

    dgain, dbias = lax.fori_loop(0, SEQ_LEN // BLK, finish, tuple(da_rows))

    def scatter_rest(k):
        row = pl.ds(pos_ref[k], 1)
        dxin[row, :] += dx1_ref[pl.ds(k, 1), :]

    each(0, PICKS, scatter_rest)
    dx_ref[...] = dxin[...].astype(BF)
    line = iota((8, D), 0)
    norms = dnorm_ref[...] + jnp.where(line == 0, dgain, jnp.where(line == 3, dbias, 0.0))
    tall = jnp.concatenate([norms, jnp.zeros((EXTRA - 8, D), FL)], axis=0)
    da_ref[:, 3 * D :] = tall.T.astype(BF)


def head_kernel(
    nb, nv, part, f_ref, w_ref, live_ref, target_ref, df_ref, dw_ref, loss_ref,
    fall, expo, block, mine, stats, ft, grad_sum, coef, df, half, far_got, out,
    near_out, near_in, far_out, far_in, stat_out, stat_in, pair_out, pair_in, sum_out, sum_in, dw_sem,
):
    v = lax.axis_index("vocab")
    rows = w_ref.shape[1]
    total_rows = nv * PICKS
    core, chip, chips = lax.rem(v, 2), v // 2, nv // 2
    sibling = {"vocab": v + 1 - 2 * core}
    base = v * rows
    pieces = rows // part
    depth = min(2, pieces)
    meet((("vocab", nv),))

    def peer(step):
        return {"vocab": lax.rem(chip + step, chips) * 2 + core}

    def far_copy(step):
        return send(f_ref, fall.at[v], far_out.at[step], far_in.at[step], peer(step))

    def near_copy(step):
        slot = lax.rem(chip - step + chips, chips) * 2 + core
        return send(fall.at[slot], fall.at[slot], near_out.at[step], near_in.at[step], sibling)

    fall[v] = f_ref[...]
    near_copy(0).start()
    each(1, chips, lambda step: far_copy(step).start())

    def logits(step):
        @pl.when(step > 0)
        def _():
            far_copy(step).wait_recv()
            near_copy(step).start()

        near_copy(step).wait_recv()
        source = lax.rem(chip - step + chips, chips)
        start = pl.multiple_of(source * 2 * PICKS, 2 * PICKS)
        features = fall[pl.ds(source * 2, 2)].reshape(2 * PICKS, D)
        target = target_ref[pl.ds(start, 2 * PICKS), :] - base

        def score(j, peak):
            cut = lanes(j * part, part)
            value = nn(features, w_ref[:, cut])
            block[:, cut] = value
            return jnp.maximum(
                peak, jnp.max(jnp.where(live_ref[0:1, cut] > 0, value, NEG_BIG), axis=1, keepdims=True)
            )

        peak = lax.fori_loop(0, pieces, score, jnp.full((2 * PICKS, 1), NEG_BIG, FL))

        def count(j, carry):
            total, picked, valid = carry
            cut = lanes(j * part, part)
            value = block[:, cut]
            live = live_ref[0:1, cut] > 0
            hot = target - j * part == iota((2 * PICKS, part), 1)
            e = jnp.where(live, jnp.exp(value - peak), 0.0)
            expo[pl.ds(start, 2 * PICKS), cut] = e.astype(BF)
            total = total + jnp.sum(e, axis=1, keepdims=True)
            picked = picked + jnp.sum(jnp.where(hot, value, 0.0), axis=1, keepdims=True)
            valid = valid + jnp.sum(jnp.where(hot & live, 1.0, 0.0), axis=1, keepdims=True)
            return total, picked, valid

        zero = jnp.zeros((2 * PICKS, 1), FL)
        total, picked, valid = lax.fori_loop(0, pieces, count, (zero, zero, zero))
        lane = iota((2 * PICKS, 128), 1)
        wide = jnp.where(lane == 0, peak, jnp.where(lane == 1, total, jnp.where(lane == 2, picked, valid)))
        mine[:, pl.ds(start, 2 * PICKS)] = wide.T[:8, :]

    each(0, chips, logits)

    def stat_copy(step):
        return send(mine, stats.at[v], stat_out.at[step], stat_in.at[step], {"vocab": lax.rem(v + step, nv)})

    each(1, nv, lambda step: stat_copy(step).start())
    stats[v] = mine[...]
    for i in range(total_rows // 256 if pieces > 1 else 0):
        ft[:, i * 256 : (i + 1) * 256] = fall[2 * i : 2 * i + 2].reshape(256, D).T
    each(1, nv, lambda step: stat_copy(step).wait())
    start = jnp.full((1, total_rows), NEG_BIG, FL)
    peak = lax.fori_loop(0, nv, lambda u, top: jnp.maximum(top, stats[u, 0:1, :]), start)

    def combine(u, carry):
        scale = jnp.exp(stats[u, 0:1, :] - peak)
        return (
            carry[0] + stats[u, 1:2, :] * scale, carry[1] + stats[u, 2:3, :], carry[2] + stats[u, 3:4, :],
        )

    zero = jnp.zeros((1, total_rows), FL)
    total, picked, valid = lax.fori_loop(0, nv, combine, (zero, zero, zero))
    lse = peak + jnp.log(jnp.maximum(total, 1e-37))
    weight = valid / (jnp.maximum(jnp.sum(valid, axis=1, keepdims=True), 1.0) * nb)
    loss = jnp.sum(weight * (lse - picked), axis=1, keepdims=True)
    loss_ref[...] = jnp.broadcast_to(loss, loss_ref.shape)
    alpha = weight * jnp.exp(mine[0:1, :] - lse)
    line = iota((128, 256), 0)
    for i in range(total_rows // 256):
        cut = slice(i * 256, (i + 1) * 256)
        coef[cut, :] = jnp.where(line == 0, alpha[:, cut], weight[:, cut]).T

    tall = min(total_rows, 1024 if pieces > 1 else 256)
    shards_tall = tall // PICKS
    df[...] = jnp.zeros_like(df)

    def out_copy(j):
        return pltpu.make_async_copy(
            out.at[lax.rem(j, depth)], dw_ref.at[:, lanes(j * part, part)], dw_sem.at[lax.rem(j, depth)]
        )

    def gradients(j):
        cut = lanes(j * part, part)
        words = w_ref[:, cut]

        @pl.when(j >= depth)
        def _():
            out_copy(j - depth).wait()

        def strip(t):
            start = t * tall if total_rows == tall else pl.multiple_of(t * tall, tall)
            here = pl.ds(start, tall)
            hot = target_ref[here, :] - base - j * part == iota((tall, part), 1)
            two = coef[here, :]
            value = two[:, 0:1] * expo[here, cut].astype(FL) - jnp.where(hot, two[:, 1:2], 0.0)
            dlogits = value.astype(BF)
            df[here, :] += nt(dlogits, words)
            if pieces > 1:
                turned = ft[:, pl.ds(start, tall)]
            else:
                turned = fall[pl.ds(t * shards_tall, shards_tall)].reshape(tall, D).T
            for r in range(0, D, D // 3):
                more = nn(turned[r : r + D // 3, :], dlogits)
                if total_rows == tall:
                    out[lax.rem(j, depth), r : r + D // 3, :] = more.astype(BF)
                else:
                    grad_sum[r : r + D // 3, :] += more

        if total_rows == tall:
            strip(0)
        else:
            grad_sum[...] = jnp.zeros_like(grad_sum)
            each(0, total_rows // tall, strip)
            for r in range(0, D, D // 3):
                out[lax.rem(j, depth), r : r + D // 3, :] = grad_sum[r : r + D // 3, :].astype(BF)
        out_copy(j).start()

    each(0, pieces, gradients)

    def shard(index):
        return pl.ds(pl.multiple_of(index * PICKS, PICKS), PICKS)

    def pair_copy(k):
        source = df.at[shard(2 * k + 1 - core), :] if pieces > 1 else fall.at[k]
        return send(source, half.at[k], pair_out.at[k], pair_in.at[k], sibling)

    near_copy(0).wait_send()

    def drain(step):
        far_copy(step).wait_send()
        near_copy(step).wait_send()

    each(1, chips, drain)

    def swap(k):
        if pieces == 1:
            fall[k] = df[shard(2 * k + 1 - core), :].astype(BF)
        pair_copy(k).start()

    each(0, chips, swap)

    def sum_copy(step):
        return send(fall.at[chips + step], far_got.at[step], sum_out.at[step], sum_in.at[step], peer(step))

    def pass_on(turn):
        step = lax.rem(turn, chips)
        k = lax.rem(chip + step, chips)
        pair_copy(k).wait()
        value = df[shard(2 * k + core), :] + half[k].astype(FL)

        @pl.when(step > 0)
        def _():
            fall[chips + step] = value.astype(BF)
            sum_copy(step).start()

        @pl.when(step == 0)
        def _():
            df_ref[...] = value

    each(1, chips + 1, pass_on)

    def collect(step):
        sum_copy(step).wait()
        df_ref[...] += far_got[step].astype(FL)

    each(1, chips, collect)
    for j in range(pieces - depth, pieces):
        out_copy(j).wait()


def head(nb, nv, features, words, live, targets):
    rows = words.shape[1]
    part = chunk_of(rows, 640)
    total_rows = nv * PICKS
    chips = nv // 2
    dma = pltpu.SemaphoreType.DMA
    scratch = [
        pltpu.VMEM((nv, PICKS, D), BF),
        pltpu.VMEM((total_rows, rows), BF),
        pltpu.VMEM((2 * PICKS, rows), FL),
        pltpu.VMEM((8, total_rows), FL),
        pltpu.VMEM((nv, 8, total_rows), FL),
        pltpu.VMEM((D, total_rows) if rows > part else (8, 128), BF),
        pltpu.VMEM((8, 128) if rows > part else (D, part), FL),
        pltpu.VMEM((total_rows, 128), FL),
        pltpu.VMEM((total_rows, D), FL),
        pltpu.VMEM((chips, PICKS, D), FL if rows > part else BF),
        pltpu.VMEM((chips, PICKS, D), BF),
        pltpu.VMEM((min(2, rows // part), D, part), BF),
        dma((chips,)), dma((chips,)), dma((chips,)), dma((chips,)), dma((nv,)), dma((nv,)),
        dma((chips,)), dma((chips,)), dma((chips,)), dma((chips,)), dma((2,)),
    ]
    return run(
        functools.partial(head_kernel, nb, nv, part),
        [SD((PICKS, D), FL), SD((D, rows), BF), SD((8, 128), FL)],
        scratch,
        [features, words, live, targets],
        "head",
        1,
        out_specs=[VM, HB, VM],
    )


def adamw(weight, moment, square, gradient, clip, count, decay, rate):
    gradient = gradient * clip
    moment = BETA_ONE * moment + (1 - BETA_ONE) * gradient
    square = BETA_TWO * square + (1 - BETA_TWO) * gradient * gradient
    fixed_moment = moment / (1 - BETA_ONE**count)
    fixed_square = square / (1 - BETA_TWO**count)
    weight = weight - rate * (fixed_moment / (jnp.sqrt(fixed_square) + ADAM_EPS) + decay * weight)
    return (weight, moment, square)


def slot_size(nv):
    mean = SEQ_LEN // nv
    return -(-(mean + int(5.5 * math.sqrt(mean))) // 32) * 32


def shards(
    nb, nv,
    tokens, targets, segments, counted, vocab_mask, step_count,
    table, table_moment, table_square,
    attend, attend_moment, attend_square,
    project, project_moment, project_square,
    expand, expand_moment, expand_square,
    contract, contract_moment, contract_square,
    gain, gain_moment, gain_square,
    shift, shift_moment, shift_square,
):
    rows, width = table.shape
    cap = slot_size(nv)
    table_t = table.T
    norms = jnp.concatenate([gain, shift], axis=0)
    packed = jnp.concatenate([attend[0], norms.T, jnp.zeros((width, EXTRA - 6), FL)], axis=1).astype(BF)
    pieces = (packed, project[0].astype(BF), expand[0].astype(BF), contract[0].astype(BF))
    words = lax.all_gather(table_t.astype(BF), "batch", axis=0, tiled=True)

    key_seg = jnp.concatenate([jnp.repeat(jnp.arange(SLOTS, dtype=I32) + 1, NB), segments])
    key_pos = jnp.concatenate([jnp.full((SLOTS * NB,), -1, I32), jnp.arange(SEQ_LEN, dtype=I32)])
    keys = jnp.stack([key_seg, key_pos], axis=1)
    query_blk = counted // BLK
    query_seg = functools.reduce(
        lambda seg, i: jnp.where(query_blk == i, segments[i * BLK], seg), range(1, SEQ_LEN // BLK), jnp.broadcast_to(segments[0], counted.shape)
    )
    queries = jnp.concatenate([query_seg[None], counted[None], jnp.zeros((6, PICKS), I32)], axis=0)

    tok = tokens.reshape(nv, SEQ_LEN)
    x, ids, place, most, every, a_all, p_all, u_all, c_all = embed(
        nb, nv, cap, jnp.zeros((1,), I32), tok, table_t, pieces
    )
    turns = (most[0, 0].astype(I32) + cap - 1) // cap

    def more_rows(state):
        turn, total = state
        return turn + 1, total + embed(nb, nv, cap, turn[None], tok, table_t)[0]

    x = lax.while_loop(lambda state: state[0] < turns, more_rows, (jnp.int32(1), x))[1]

    hall, kv, q, hq, xq, mixed, lse, norm_rows, mixing_t = run(
        attend_kernel,
        [
            SD((KEYS, D), BF), SD((KEYS, 2 * D), BF), SD((PICKS, D), BF), SD((PICKS, D), BF), SD((PICKS, D), FL),
            SD((PICKS, D), BF), SD((NPAIR, 2, PICKS), FL), SD((8, D), FL), SD((SEQ_LEN, SLOTS * NB), BF),
        ],
        [],
        [x, a_all, segments[None, :], counted[:, None], keys, queries],
        "attend", flops=7 * 10**9, moved=20 * 10**6,
    )
    x1, h2, z, act, x2, features = run(
        feed_kernel,
        [
            SD((PICKS, D), FL), SD((PICKS, D), BF), SD((PICKS, FF), FL), SD((PICKS, FF), BF), SD((PICKS, D), FL),
            SD((PICKS, D), BF),
        ],
        [],
        [xq, mixed, p_all, u_all, c_all, norm_rows],
        "feed", flops=2 * 10**9, moved=15 * 10**6,
    )
    df, dw, loss_block = head(nb, nv, features, words, vocab_mask[None, :], targets[:, None])
    loss_part = loss_block[0, 0]
    dw_sum = lax.psum_scatter(dw, "batch", scatter_dimension=0, tiled=True)

    dc, du, dp, dx1, dmixed, dnorm = run(
        feed_back_kernel,
        [
            SD((FF, D), BF), SD((D, FF), BF), SD((D, D), BF), SD((PICKS, D), FL), SD((PICKS, D), BF), SD((8, D), FL),
        ],
        [pltpu.VMEM((PICKS, D), FL)],
        [df, x2, x1, h2, z, act, mixed, p_all, u_all, c_all, norm_rows],
        "feed_back", flops=4 * 10**9, moved=30 * 10**6,
    )
    da, dx = run(
        attend_back_kernel,
        [SD((D, 3 * D + EXTRA), BF), SD((SEQ_LEN, D), BF)],
        [
            pltpu.VMEM((KEYS, 2 * D), BF), pltpu.VMEM((PICKS, D), BF), pltpu.VMEM((D, KEYS), BF),
            pltpu.VMEM((SEQ_LEN, D), FL), pltpu.VMEM((SEQ_LEN, D), FL), pltpu.VMEM((SLOTS * NB, D), BF),
        ],
        [counted, dmixed, q, kv, lse, hall, hq, a_all, x, dx1, mixing_t, keys, queries, norm_rows, dnorm],
        "attend_back", flops=12 * 10**9, moved=25 * 10**6,
        in_specs=[SM] + [VM] * 14,
    )
    extra, *sums = unembed(nb, nv, cap, width, rows, dx, ids, place, (da, dp, du, dc))
    sums = [item.astype(FL) for item in sums]

    def more_grads(state):
        turn, total = state
        later = later_slots(nv, cap, rows, every, turn)
        return turn + 1, total + unembed(
            nb, nv, cap, width, rows, dx, later, place - jnp.array([0, 1, 0, 0, 0, 0, 0, 0], I32)[None, :, None] * (turn * cap)
        )[0]

    extra = lax.while_loop(lambda state: state[0] < turns, more_grads, (jnp.int32(1), extra))[1]

    grad_table = dw_sum.astype(FL) + extra
    grad_a, grad_p, grad_u, grad_c = sums
    grad_norms = grad_a[:, 3 * D : 3 * D + 6].T
    grad_a = grad_a[:, : 3 * D]
    at_root = (lax.axis_index("vocab") == 0).astype(FL)
    owned = sum(jnp.sum(item * item) for item in (grad_a, grad_p, grad_u, grad_c, grad_norms))
    squares, loss = lax.psum(
        (jnp.sum(grad_table * grad_table) + at_root * owned, at_root * loss_part), ("batch", "vocab")
    )
    gradient_norm = jnp.sqrt(squares)
    clip = jnp.minimum(1.0, MAX_NORM / (gradient_norm + 1e-06))
    count = step_count[0].astype(FL)

    def update(weight, moment, square, gradient, decay=DECAY, rate=LEARN_RATE):
        return adamw(weight, moment, square, gradient, clip, count, decay, rate)

    table_out = [item.T for item in update(table_t, table_moment.T, table_square.T, grad_table)]
    attend_out = update(attend, attend_moment, attend_square, grad_a[None])
    project_out = update(project, project_moment, project_square, grad_p[None])
    expand_out = update(expand, expand_moment, expand_square, grad_u[None])
    contract_out = update(contract, contract_moment, contract_square, grad_c[None])
    gain_out = update(gain, gain_moment, gain_square, grad_norms[:3], 0.0, NORM_RATE)
    shift_out = update(shift, shift_moment, shift_square, grad_norms[3:], 0.0, NORM_RATE)
    return (
        loss, gradient_norm, *table_out, *attend_out, *project_out, *expand_out, *contract_out, *gain_out, *shift_out,
    )


def solution(mesh):
    nb, nv = mesh.shape["batch"], mesh.shape["vocab"]
    both, split, middle, last = P(("batch", "vocab")), P("vocab", "batch"), P(None, "batch", None), P(None, "batch")
    state = (split,) * 3 + (middle,) * 12 + (last,) * 6
    return jax.shard_map(
        functools.partial(shards, nb, nv),
        mesh=mesh,
        in_specs=(P("batch"), P("batch"), both, both, P("vocab"), P()) + state,
        out_specs=(P(), P()) + state,
        check_vma=False,
    )
```

```python
import functools
import math

import jax
import jax.numpy as jnp
from jax import lax
from jax.experimental import pallas as pl
from jax.experimental.pallas import tpu as pltpu
from jax.sharding import PartitionSpec as P

D = 768
H = 12
HD = 64
FF = 3072
NB = 256
SEG_BLOCKS = 4
SLOTS = SEG_BLOCKS - 2
SEQ_LEN = 1024
PICKS = 128
KEYS = SLOTS * NB + SEQ_LEN
BLK = 256
PAIR = 2 * HD
NPAIR = H // 2
EXTRA = 256
WIDE = (3 * D + EXTRA, D, FF, D)

NORM_EPS = 1e-05
MAX_NORM = 0.02
LEARN_RATE = 0.04
NORM_RATE = 0.5
BETA_ONE = 0.9
BETA_TWO = 0.999
ADAM_EPS = 1e-08
DECAY = 0.1
NEG_BIG = -1e30
BF = jnp.bfloat16
FL = jnp.float32
I32 = jnp.int32
MESH = pl.DeviceIdType.MESH
SD = jax.ShapeDtypeStruct
VM = pl.BlockSpec(memory_space=pltpu.VMEM)
SM = pl.BlockSpec(memory_space=pltpu.SMEM)
HB = pl.BlockSpec(memory_space=pl.ANY)
LIMIT = 62 * 2**20


def nn(a, b):
    return lax.dot_general(a, b, (((1,), (0,)), ((), ())), preferred_element_type=FL)


def nt(a, b):
    return lax.dot_general(a, b, (((1,), (1,)), ((), ())), preferred_element_type=FL)


def iota(shape, axis):
    return lax.broadcasted_iota(I32, shape, axis)


def lanes(start, size):
    return pl.ds(pl.multiple_of(start, 128), size)


def chunk_of(rows, want):
    return want if rows % want == 0 else rows


def run(kernel, outs, scratch, ins, name, collective=None, flops=0, moved=0, out_specs=None, in_specs=None):
    return pl.pallas_call(
        kernel,
        out_shape=outs,
        in_specs=in_specs if in_specs is not None else [VM] * len(ins),
        out_specs=out_specs if out_specs is not None else [VM] * len(outs),
        scratch_shapes=scratch,
        compiler_params=pltpu.CompilerParams(
            vmem_limit_bytes=LIMIT,
            collective_id=collective,
            has_side_effects=collective is not None,
        ),
        cost_estimate=pl.CostEstimate(flops=flops, bytes_accessed=moved, transcendentals=0),
        name=name,
    )(*ins)


def send(source, target, out_sem, in_sem, device):
    return pltpu.make_async_remote_copy(
        src_ref=source, dst_ref=target, send_sem=out_sem, recv_sem=in_sem, device_id=device, device_id_type=MESH
    )


def meet(axes):
    barrier = pltpu.get_barrier_semaphore()
    count = 0
    for axis, size in axes:
        me = lax.axis_index(axis)

        def greet(step, carry, axis=axis, size=size, me=me):
            pl.semaphore_signal(barrier, inc=1, device_id={axis: lax.rem(me + step, size)}, device_id_type=MESH)
            return carry

        lax.fori_loop(1, size, greet, 0)
        count += size - 1
    pl.semaphore_wait(barrier, count)


def each(start, stop, body):
    def step(index, carry):
        body(index)
        return carry

    lax.fori_loop(start, stop, step, 0)


def embed_kernel(
    nb, nv, cap, part, first, *refs
):
    round_ref, tok_ref, table_ref = refs[:3]
    shards, refs = (refs[3:7], refs[7:]) if first else ((), refs[3:])
    x_ref, ids_ref, place_ref, most_ref, tok_ref_all = refs[:5]
    wholes, refs = (refs[5:9], refs[9:]) if first else ((), refs[5:])
    words, before, ranks, work, sent, got, spread, mixed, turned = refs[:9]
    tok_out, tok_in, row_out, row_in, mix_out, mix_in = refs[9:15]
    b, v = lax.axis_index("batch"), lax.axis_index("vocab")
    width, rows = table_ref.shape
    shift = round_ref[0] * cap
    meet((("batch", nb), ("vocab", nv)))
    gather = WeightGather(nb, shards, wholes, *refs[15:20]) if first else None

    def tok_copy(step):
        return send(
            tok_ref, tok_ref_all.at[b], tok_out.at[step], tok_in.at[step], {"batch": lax.rem(b + step, nb)}
        )

    for step in range(1, nb):
        tok_copy(step).start()
    if first:
        gather.start()
    tok_ref_all[b] = tok_ref[...]
    words[...] = table_ref[...].astype(BF)
    before[...] = (iota((SEQ_LEN, SEQ_LEN), 0) < iota((SEQ_LEN, SEQ_LEN), 1)).astype(FL).astype(BF)
    for step in range(1, nb):
        tok_copy(step).wait()

    base = v * rows
    most = jnp.zeros((nv, 1), FL)
    for p in range(nb):
        ids = tok_ref_all[p]
        mine = (ids >= base) & (ids < base + rows)
        rank = nn(mine.astype(FL).astype(BF), before[...])
        ranks[p] = jnp.where(mine, rank.astype(I32) - shift, -1)
        for owner in range(nv):
            theirs = (ids >= owner * rows) & (ids < (owner + 1) * rows)
            most = jnp.maximum(most, jnp.sum(theirs.astype(FL), axis=1, keepdims=True))
    most_ref[...] = jnp.broadcast_to(jnp.max(most, axis=0, keepdims=True), most_ref.shape)

    def row_copy(step):
        return send(
            sent.at[step], got.at[v], row_out.at[step], row_in.at[step], {"vocab": lax.rem(v + step, nv)}
        )

    def build(turn):
        step = lax.rem(turn, nv)
        dest = lax.rem(v + step, nv)
        found = []
        for p in range(nb):
            pick = (iota((cap, SEQ_LEN), 0) == ranks[p, pl.ds(dest, 1), :]).astype(FL).astype(BF)
            local = tok_ref_all[p, pl.ds(dest, 1), :] - base
            line = iota((8, SEQ_LEN), 0)
            high, low = lax.shift_right_arithmetic(local, 7), lax.bitwise_and(local, 127)
            digits = jnp.where(line == 0, high, jnp.where(line == 1, low, 0)).astype(FL).astype(BF)
            both = nt(pick, digits)
            found.append((both[:, 0:1] * 128.0 + both[:, 1:2]).astype(I32))
        index = jnp.concatenate(found, axis=0)
        ids_ref[dest] = index
        work[...] = jnp.zeros_like(work)

        def piece(j):
            hot = (index - j * part == iota((nb * cap, part), 1)).astype(FL).astype(BF)
            work[...] += nt(hot, words[:, lanes(j * part, part)])

        each(0, rows // part, piece)
        block = work[...].T.astype(BF)

        @pl.when(step > 0)
        def _():
            sent[step] = block
            row_copy(step).start()

        @pl.when(step == 0)
        def _():
            got[v] = block

    each(1, nv + 1, build)
    if first:
        gather.pass_on()

    keys = []
    for p in range(nb):
        ids = tok_ref_all[p, pl.ds(v, 1), :]
        owner = iota((nv, SEQ_LEN), 0)
        theirs = (ids >= owner * rows) & (ids < (owner + 1) * rows)
        rank = nn(theirs.astype(FL).astype(BF), before[...])
        place = jnp.sum(jnp.where(theirs, rank, 0.0), axis=0, keepdims=True).astype(I32) - shift
        holder = jnp.sum(jnp.where(theirs, owner.astype(FL), 0.0), axis=0, keepdims=True).astype(I32)
        line = iota((8, SEQ_LEN), 0)
        place_ref[p] = jnp.where(line == 0, holder, jnp.where(line == 1, place, 0))
        keys.append((holder, place))
        spread[p] = jnp.zeros((width, SEQ_LEN), FL)

    def take(turn):
        step = lax.rem(turn, nv)
        source = lax.rem(v - step + nv, nv)

        @pl.when(step > 0)
        def _():
            row_copy(step).wait()

        block = got[source]
        for p in range(nb):
            holder, place = keys[p]
            key = jnp.where(holder == source, place, -1)
            hot = (iota((cap, SEQ_LEN), 0) == key).astype(FL).astype(BF)
            spread[p] += nn(block[:, p * cap : (p + 1) * cap], hot)

    each(1, nv + 1, take)

    def mix_copy(step):
        return send(
            mixed.at[step], turned.at[b], mix_out.at[step], mix_in.at[step], {"batch": lax.rem(b + step, nb)}
        )

    for step in range(1, nb):
        mixed[step] = spread[lax.rem(b + step, nb)].astype(BF)
        mix_copy(step).start()
    turned[b] = spread[b].astype(BF)
    for step in range(1, nb):
        mix_copy(step).wait()
    x_ref[...] = turned[...].reshape(nb * width, SEQ_LEN).T
    if first:
        gather.finish()


class WeightGather:
    def __init__(self, nb, shards, wholes, own_sem, out_sem, in_sem, pair_out, pair_in):
        self.nb, self.shards, self.wholes = nb, shards, wholes
        self.own_sem, self.out_sem, self.in_sem, self.pair_out, self.pair_in = own_sem, out_sem, in_sem, pair_out, pair_in
        self.b, v = lax.axis_index("batch"), lax.axis_index("vocab")
        self.core = lax.rem(v, 2)
        self.sibling = {"vocab": v + 1 - 2 * self.core}

    def flip(self, bits):
        b = self.b
        low, high = lax.rem(b, 2), b // 2
        return (high if bits < 2 else 1 - high) * 2 + (low if bits % 2 == 0 else 1 - low)

    def place(self, w, owner, top, size):
        rows, cols = self.shards[w].shape
        first = pl.multiple_of(owner * rows + top, 16)
        return self.wholes[w].at[pl.ds(first, size), lanes(self.core * (cols // 2), cols // 2)]

    def routes(self, w):
        rows = self.shards[w].shape[0]
        if self.nb == 4:
            half = rows // 2
            return [
                (self.b, 0, rows, self.flip(1), self.flip(1)),
                (self.b, 0, rows, self.flip(2), self.flip(2)),
                (self.flip(1), 0, half, self.flip(2), self.flip(3)),
                (self.flip(2), half, half, self.flip(1), self.flip(3)),
            ]
        others = [lax.rem(self.b + step, self.nb) for step in range(1, self.nb)]
        came = [lax.rem(self.b - step + self.nb, self.nb) for step in range(1, self.nb)]
        return [(self.b, 0, rows, other, source) for other, source in zip(others, came)]

    def own_copy(self, w):
        rows = self.shards[w].shape[0]
        first = pl.multiple_of(self.b * rows, 16)
        return pltpu.make_async_copy(self.shards[w], self.wholes[w].at[pl.ds(first, rows), :], self.own_sem.at[w])

    def copy(self, w, k):
        owner, top, size, device, _ = self.routes(w)[k]
        cols = self.shards[w].shape[1]
        if self.nb == 4 and k >= 2:
            source = self.place(w, owner, top, size)
        else:
            source = self.shards[w].at[:, lanes(self.core * (cols // 2), cols // 2)]
        target = self.place(w, owner, top, size)
        return send(source, target, self.out_sem.at[w, k], self.in_sem.at[w, k], {"batch": device})

    def pair(self, w, k):
        _, top, size, _, arrived = self.routes(w)[k]
        ref = self.place(w, arrived, top, size)
        return send(ref, ref, self.pair_out.at[w, k], self.pair_in.at[w, k], self.sibling)

    def start(self):
        for w in range(4):
            for k in range(2 if self.nb == 4 else self.nb - 1):
                self.copy(w, k).start()
        for w in range(4):
            self.own_copy(w).start()

    def pass_on(self):
        if self.nb != 4:
            return
        for w in range(4):
            for k in range(2):
                self.copy(w, k).wait_recv()
                self.copy(w, k + 2).start()
                self.pair(w, k).start()

    def finish(self):
        for w in range(4):
            for k in range(2 if self.nb == 4 else 0, len(self.routes(w))):
                self.copy(w, k).wait_recv()
                self.pair(w, k).start()
        for w in range(4):
            self.own_copy(w).wait()
            for k in range(len(self.routes(w))):
                self.copy(w, k).wait_send()
                self.pair(w, k).wait()


def embed(nb, nv, cap, turn, tok, table, shards=()):
    width, rows = table.shape
    part = chunk_of(rows, 640)
    count = nb * cap
    outs = [
        SD((SEQ_LEN, D), BF),
        SD((nv, count, 1), I32),
        SD((nb, 8, SEQ_LEN), I32),
        SD((8, 128), FL),
        SD((nb, nv, SEQ_LEN), I32),
    ]
    first = len(shards) > 0
    outs += [SD((nb * item.shape[0], item.shape[1]), BF) for item in shards]
    dma = pltpu.SemaphoreType.DMA
    scratch = [
        pltpu.VMEM((width, rows), BF),
        pltpu.VMEM((SEQ_LEN, SEQ_LEN), BF),
        pltpu.VMEM((nb, nv, SEQ_LEN), I32),
        pltpu.VMEM((count, width), FL),
        pltpu.VMEM((nv, width, count), BF),
        pltpu.VMEM((nv, width, count), BF),
        pltpu.VMEM((nb, width, SEQ_LEN), FL),
        pltpu.VMEM((nb, width, SEQ_LEN), BF),
        pltpu.VMEM((nb, width, SEQ_LEN), BF),
        dma((nb,)), dma((nb,)), dma((nv,)), dma((nv,)), dma((nb,)), dma((nb,)),
    ]
    if first:
        scratch += [dma((4,)), dma((4, 4)), dma((4, 4)), dma((4, 4)), dma((4, 4))]
    return run(
        functools.partial(embed_kernel, nb, nv, cap, part, first), outs, scratch, [turn, tok, table, *shards],
        "embed" if first else "embed_more", 0 if first else 3,
        in_specs=[SM, VM, VM] + [HB] * len(shards), out_specs=[VM] * 5 + [HB] * len(shards),
    )


class GradientSum:
    def __init__(self, nb, nv, grads, sums, refs):
        self.nb, self.nv, self.grads, self.sums = nb, nv, grads, sums
        self.own, self.near, self.shard, self.total = refs[0:4], refs[4:8], refs[8:12], refs[12:16]
        self.bits, self.result = refs[16:20], refs[20:24]
        (self.load_sem, self.pair_out, self.pair_in, self.mix_out, self.mix_in, self.cut_out, self.cut_in,
         self.all_out, self.all_in, self.last_out, self.last_in, self.store_sem) = refs[24:36]
        self.b, v = lax.axis_index("batch"), lax.axis_index("vocab")
        self.core, self.chip, self.chips = lax.rem(v, 2), v // 2, nv // 2
        self.sibling = {"vocab": v + 1 - 2 * self.core}

    def half(self, w, core):
        cols = self.grads[w].shape[1] // 2
        return lanes(core * cols, cols)

    def load(self, w):
        return pltpu.make_async_copy(self.grads[w].at[:, self.half(w, self.core)], self.own[w], self.load_sem.at[w])

    def pair(self, w):
        source = self.grads[w].at[:, self.half(w, 1 - self.core)]
        return send(source, self.near[w], self.pair_out.at[w], self.pair_in.at[w], self.sibling)

    def start(self):
        for w in range(4):
            self.pair(w).start()
            self.load(w).start()

    def mix(self, w, step):
        other = lax.rem(self.b + step, self.nb)
        rows = self.own[w].shape[0] // self.nb
        source = self.own[w].at[pl.ds(pl.multiple_of(other * rows, 16), rows), :]
        return send(source, self.shard[w].at[step], self.mix_out.at[w, step], self.mix_in.at[w, step], {"batch": other})

    def scatter(self):
        for w in range(4):
            self.load(w).wait()
            self.pair(w).wait()
            rows = self.own[w].shape[0] // self.nb

            def add(i, w=w, rows=rows):
                cut = pl.ds(pl.multiple_of(i * rows, 16), rows)
                self.own[w][cut, :] = (self.own[w][cut, :].astype(FL) + self.near[w][cut, :].astype(FL)).astype(BF)

            each(0, self.nb, add)
            for step in range(1, self.nb):
                self.mix(w, step).start()

    def pieces(self, w):
        rows = self.total[w].shape[0]
        count = max(n for n in range(1, self.chips + 1) if rows % (16 * n) == 0)
        return count, rows // count

    def peer(self, step):
        other = lax.rem(self.chip + step, self.chips)
        return other, {"vocab": other * 2 + self.core}

    def cut(self, w, step):
        other, device = self.peer(step)
        size = self.pieces(w)[1]
        source = self.total[w].at[pl.ds(pl.multiple_of(other * size, 16), size), :]
        return send(source, self.bits[w].at[step], self.cut_out.at[w, step], self.cut_in.at[w, step], device)

    def back(self, w, step):
        size = self.pieces(w)[1]
        place = self.result[w].at[pl.ds(pl.multiple_of(self.chip * size, 16), size), :]
        return send(place, place, self.all_out.at[w, step], self.all_in.at[w, step], self.peer(step)[1])

    def back_recv(self, w, step):
        source = lax.rem(self.chip - step + self.chips, self.chips)
        size = self.pieces(w)[1]
        place = self.result[w].at[pl.ds(pl.multiple_of(source * size, 16), size), :]
        return send(place, place, self.all_out.at[w, step], self.all_in.at[w, step], self.peer(step)[1])

    def reduce(self):
        for w in range(4):
            rows = self.total[w].shape[0]
            for step in range(1, self.nb):
                self.mix(w, step).wait()
            here = pl.ds(pl.multiple_of(self.b * rows, 16), rows)
            value = self.own[w][here, :].astype(FL)
            for step in range(1, self.nb):
                value = value + self.shard[w][step].astype(FL)
            self.total[w][...] = value.astype(BF)
            count = self.pieces(w)[0]

            def go(step, w=w, count=count):
                @pl.when(self.peer(step)[0] < count)
                def _():
                    self.cut(w, step).start()

            each(1, self.chips, go)

    def collect(self):
        for w in range(4):
            count, size = self.pieces(w)
            mine = pl.ds(pl.multiple_of(self.chip * size, 16), size)

            @pl.when(self.chip < count)
            def _(w=w, mine=mine):
                def add(step, value):
                    self.cut(w, step).wait_recv()
                    return value + self.bits[w][step].astype(FL)

                value = lax.fori_loop(1, self.chips, add, self.total[w][mine, :].astype(FL))
                self.result[w][mine, :] = value.astype(BF)
                each(1, self.chips, lambda step: self.back(w, step).start())

            def sent(step, w=w, count=count):
                @pl.when(self.peer(step)[0] < count)
                def _():
                    self.cut(w, step).wait_send()

            each(1, self.chips, sent)

    def last(self, w):
        return send(
            self.result[w], self.sums[w].at[:, self.half(w, self.core)], self.last_out.at[w], self.last_in.at[w], self.sibling
        )

    def store(self, w):
        return pltpu.make_async_copy(self.result[w], self.sums[w].at[:, self.half(w, self.core)], self.store_sem.at[w])

    def finish(self):
        for w in range(4):
            count = self.pieces(w)[0]

            def got(step, w=w, count=count):
                @pl.when(lax.rem(self.chip - step + self.chips, self.chips) < count)
                def _():
                    self.back_recv(w, step).wait_recv()

            each(1, self.chips, got)
            self.last(w).start()
            self.store(w).start()
        for w in range(4):
            count = self.pieces(w)[0]

            @pl.when(self.chip < count)
            def _(w=w):
                each(1, self.chips, lambda step: self.back(w, step).wait_send())

            self.store(w).wait()
            self.last(w).wait_send()
            other = self.sums[w].at[:, self.half(w, 1 - self.core)]
            send(other, other, self.last_out.at[w], self.last_in.at[w], self.sibling).wait_recv()


def gradient_scratch(nb, nv, grads):
    chips = nv // 2
    halves = [(item.shape[0], item.shape[1] // 2) for item in grads]
    shards = [(rows // nb, cols) for rows, cols in halves]
    sizes = [rows // max(n for n in range(1, chips + 1) if rows % (16 * n) == 0) for rows, _ in shards]
    dma = pltpu.SemaphoreType.DMA
    return (
        [pltpu.VMEM(item, BF) for item in halves] * 2
        + [pltpu.VMEM((nb, *item), BF) for item in shards]
        + [pltpu.VMEM(item, BF) for item in shards]
        + [pltpu.VMEM((chips, size, item[1]), BF) for size, item in zip(sizes, shards)]
        + [pltpu.VMEM(item, BF) for item in shards]
        + [dma((4,)), dma((4,)), dma((4,)), dma((4, nb)), dma((4, nb)), dma((4, chips)), dma((4, chips))]
        + [dma((4, chips)), dma((4, chips)), dma((4,)), dma((4,)), dma((4,))]
    )


def unembed_kernel(nb, nv, cap, part, first, *refs):
    x_ref, ids_ref, place_ref = refs[:3]
    grads, refs = (refs[3:7], refs[7:]) if first else ((), refs[3:])
    out_ref = refs[0]
    sums, refs = (refs[1:5], refs[5:]) if first else ((), refs[1:])
    turned, parts, sent, got, mix_out, mix_in, row_out, row_in = refs[:8]
    layer = GradientSum(nb, nv, grads, sums, refs[8:]) if first else None
    b, v = lax.axis_index("batch"), lax.axis_index("vocab")
    width, rows = out_ref.shape
    meet((("batch", nb), ("vocab", nv)))
    turned[...] = x_ref[...].T.reshape(nb, width, SEQ_LEN)

    def mix_copy(step):
        other = lax.rem(b + step, nb)
        return send(turned.at[other], parts.at[b], mix_out.at[step], mix_in.at[step], {"batch": other})

    for step in range(1, nb):
        mix_copy(step).start()
    if first:
        layer.start()
    parts[b] = turned[b]
    for step in range(1, nb):
        mix_copy(step).wait()

    def row_copy(step):
        return send(
            sent.at[step], got.at[v], row_out.at[step], row_in.at[step], {"vocab": lax.rem(v + step, nv)}
        )

    def build(turn):
        step = lax.rem(turn, nv)
        owner = lax.rem(v + step, nv)
        blocks = []
        for p in range(nb):
            key = jnp.where(place_ref[p, 0:1, :] == owner, place_ref[p, 1:2, :], -1)
            hot = (iota((cap, SEQ_LEN), 0) == key).astype(FL).astype(BF)
            blocks.append(nt(parts[p], hot).astype(BF))
        block = jnp.concatenate(blocks, axis=1)

        @pl.when(step > 0)
        def _():
            sent[step] = block
            row_copy(step).start()

        @pl.when(step == 0)
        def _():
            got[v] = block

    each(1, nv + 1, build)
    if first:
        layer.scatter()
    out_ref[...] = jnp.zeros_like(out_ref)

    def take(step):
        source = lax.rem(v - step + nv, nv)

        @pl.when(step > 0)
        def _():
            row_copy(step).wait()

        block, index = got[source], ids_ref[source]

        def piece(j):
            hot = (index - j * part == iota((nb * cap, part), 1)).astype(FL).astype(BF)
            out_ref[:, lanes(j * part, part)] += nn(block, hot)

        each(0, rows // part, piece)

    each(0, nv // 2, take)
    if first:
        layer.reduce()
    each(nv // 2, nv, take)
    if first:
        layer.collect()
        layer.finish()


def unembed(nb, nv, cap, width, rows, grad, ids, place, grads=()):
    part = chunk_of(rows, 640)
    count = nb * cap
    dma = pltpu.SemaphoreType.DMA
    scratch = [
        pltpu.VMEM((nb, width, SEQ_LEN), BF),
        pltpu.VMEM((nb, width, SEQ_LEN), BF),
        pltpu.VMEM((nv, width, count), BF),
        pltpu.VMEM((nv, width, count), BF),
        dma((nb,)), dma((nb,)), dma((nv,)), dma((nv,)),
    ]
    first = len(grads) > 0
    if first:
        scratch += gradient_scratch(nb, nv, grads)
    return run(
        functools.partial(unembed_kernel, nb, nv, cap, part, first),
        [SD((width, rows), FL)] + [SD((item.shape[0] // nb, item.shape[1]), BF) for item in grads],
        scratch,
        [grad, ids, place, *grads],
        "unembed" if first else "unembed_more",
        2 if first else 4,
        in_specs=[VM] * 3 + [HB] * len(grads),
        out_specs=[VM] + [HB] * len(grads),
    )


def later_slots(nv, cap, rows, every, turn):
    nb = every.shape[0]
    v = lax.axis_index("vocab")
    local = every - v * rows
    mine = (local >= 0) & (local < rows)
    rank = jnp.cumsum(mine.astype(I32), axis=-1) - 1 - turn * cap
    hot = (rank[:, :, None, :] == jnp.arange(cap)[None, None, :, None]) & mine[:, :, None, :]
    ids = jnp.sum(jnp.where(hot, local[:, :, None, :], 0), axis=-1)
    return jnp.transpose(ids, (1, 0, 2)).reshape(nv, nb * cap, 1)


def standard(value):
    centre = value - jnp.mean(value, axis=-1, keepdims=True)
    spread = jnp.mean(centre * centre, axis=-1, keepdims=True)
    scale = lax.rsqrt(spread + NORM_EPS)
    return centre * scale, scale


def norm_back(unit, scale, gain, upstream):
    inner = upstream * gain
    first = jnp.mean(inner, axis=-1, keepdims=True)
    second = jnp.mean(inner * unit, axis=-1, keepdims=True)
    grad = scale * (inner - first - unit * second)
    return grad, jnp.sum(upstream * unit, axis=0, keepdims=True), jnp.sum(upstream, axis=0, keepdims=True)


def head_lanes(value, head):
    lane = iota(value.shape, 1)
    keep = (lane < HD) if head == 0 else (lane >= HD)
    return jnp.where(keep, value, jnp.zeros_like(value))


def visible_keys(seg_ref, pos_ref):
    position = pos_ref[...]
    block = position // BLK
    marks = [seg_ref[:, i * BLK : i * BLK + 1] for i in range(SEQ_LEN // BLK)]
    segment = jnp.zeros_like(position)
    for i, mark in enumerate(marks):
        segment = jnp.where(block == i, mark, segment)
    row = iota((BLK, PICKS), 0)
    parts = [jnp.broadcast_to(segment == slot + 1, (NB, PICKS)) for slot in range(SLOTS)]
    parts += [(segment == mark) & (row + i * BLK <= position) for i, mark in enumerate(marks)]
    return parts


def masked(visible, scores):
    return jnp.concatenate(
        [jnp.where(keep, scores[i * BLK : (i + 1) * BLK, :], NEG_BIG) for i, keep in enumerate(visible)], axis=0
    )


def memory_weights(segments, slot):
    length = segments.shape[1]
    inside = (segments == slot).astype(FL)
    start = jnp.sum((segments < slot).astype(FL), axis=1, keepdims=True)
    count = jnp.sum(inside, axis=1, keepdims=True)
    times = (iota((1, length), 1).astype(FL) - start + 0.5) / jnp.maximum(count, 1.0)
    centres = (iota((NB, 1), 0).astype(FL) + 0.5) / NB
    offset = (times - centres) * NB
    basis = jnp.exp(-0.5 * offset * offset) * inside
    total = jnp.sum(basis, axis=1, keepdims=True) + (count == 0.0).astype(FL)
    return basis / total


def attend_kernel(
    x_ref, a_ref, seg_ref, pos_ref,
    hall_ref, kv_ref, q_ref, hq_ref, xq_ref, o_ref, lse_ref, norm_ref, mixt_ref,
):
    norm_ref[...] = a_ref[:, 3 * D : 3 * D + 128].astype(FL).T[:8, :]
    gain, bias = norm_ref[0:1, :], norm_ref[3:4, :]

    def normalize(i):
        unit, _ = standard(x_ref[pl.ds(i * BLK, BLK), :].astype(FL))
        hall_ref[pl.ds(SLOTS * NB + i * BLK, BLK), :] = (unit * gain + bias).astype(BF)

    each(0, SEQ_LEN // BLK, normalize)
    normed = hall_ref[SLOTS * NB :, :]
    for slot in range(SLOTS):
        mixing = memory_weights(seg_ref[...], slot).astype(BF)
        hall_ref[slot * NB : (slot + 1) * NB, :] = nn(mixing, normed).astype(BF)
        mixt_ref[:, slot * NB : (slot + 1) * NB] = mixing.T

    def project(i):
        kv_ref[pl.ds(i * BLK, BLK), :] = nn(hall_ref[pl.ds(i * BLK, BLK), :], a_ref[:, D : 3 * D]).astype(BF)

    each(0, KEYS // BLK, project)
    pick = (pos_ref[...] == iota((SEQ_LEN, PICKS), 0)).astype(FL).astype(BF).T
    hq_ref[...] = nn(pick, normed).astype(BF)
    xq_ref[...] = nn(pick, x_ref[...])
    q_ref[...] = nn(hq_ref[...], a_ref[:, :D]).astype(BF)
    visible = visible_keys(seg_ref, pos_ref)

    def attend(p):
        keys = kv_ref[:, lanes(p * PAIR, PAIR)]
        values = kv_ref[:, lanes(D + p * PAIR, PAIR)].T
        queries = q_ref[:, lanes(p * PAIR, PAIR)] * HD ** (-0.5)
        outs = []
        for head in range(2):
            scores = masked(visible, nt(keys, head_lanes(queries, head)))
            peak = jnp.max(scores, axis=0, keepdims=True)
            expo = jnp.exp(scores - peak)
            total = jnp.sum(expo, axis=0, keepdims=True)
            probs = (expo * (1.0 / total)).astype(BF)
            outs.append(nn(values[head * HD : (head + 1) * HD, :], probs))
            lse_ref[p, head : head + 1, :] = peak + jnp.log(total)
        o_ref[:, lanes(p * PAIR, PAIR)] = jnp.concatenate(outs, axis=0).T.astype(BF)

    each(0, NPAIR, attend)


def feed_kernel(xq_ref, o_ref, p_ref, u_ref, c_ref, norm_ref, x1_ref, h2_ref, z_ref, act_ref, x2_ref, f_ref):
    x1 = xq_ref[...] + nn(o_ref[...], p_ref[...])
    x1_ref[...] = x1
    unit, _ = standard(x1)
    h2 = (unit * norm_ref[1:2, :] + norm_ref[4:5, :]).astype(BF)
    h2_ref[...] = h2
    x2_ref[...] = x1

    def piece(j):
        cut = lanes(j * D, D)
        z = nn(h2, u_ref[:, cut])
        z_ref[:, cut] = z
        act = jax.nn.gelu(z, approximate=True).astype(BF)
        act_ref[:, cut] = act
        x2_ref[...] += nn(act, c_ref[pl.ds(j * D, D), :])

    each(0, FF // D, piece)
    unit, _ = standard(x2_ref[...])
    f_ref[...] = (unit * norm_ref[2:3, :] + norm_ref[5:6, :]).astype(BF)


def feed_back_kernel(
    df_ref, x2_ref, x1_ref, h2_ref, z_ref, act_ref, o_ref, p_ref, u_ref, c_ref, norm_ref,
    dc_ref, du_ref, dp_ref, dx1_ref, do_ref, dnorm_ref, dh2,
):
    unit, scale = standard(x2_ref[...])
    dx2, gain_last, bias_last = norm_back(unit, scale, norm_ref[2:3, :], df_ref[...])
    dy = dx2.astype(BF)
    dh2[...] = jnp.zeros_like(dh2)
    h2t = h2_ref[...].T

    def piece(j):
        cut = lanes(j * D, D)
        dc_ref[pl.ds(j * D, D), :] = nn(act_ref[:, cut].T, dy).astype(BF)
        dact = nt(dy, c_ref[pl.ds(j * D, D), :])
        z = z_ref[:, cut]
        k = math.sqrt(2.0 / math.pi)
        t = jnp.tanh(k * (z + 0.044715 * z * z * z))
        slope = 0.5 * (1.0 + t) + 0.5 * z * (1.0 - t * t) * (k * (1.0 + 3 * 0.044715 * z * z))
        dz = (dact * slope).astype(BF)
        du_ref[:, cut] = nn(h2t, dz).astype(BF)
        dh2[...] += nt(dz, u_ref[:, cut])

    each(0, FF // D, piece)
    unit, scale = standard(x1_ref[...])
    dx1, gain_two, bias_two = norm_back(unit, scale, norm_ref[1:2, :], dh2[...])
    dx1 = dx1 + dx2
    dx1_ref[...] = dx1
    da = dx1.astype(BF)
    dp_ref[...] = nn(o_ref[...].T, da).astype(BF)
    do_ref[...] = nt(da, p_ref[...]).astype(BF)
    zero = jnp.zeros_like(gain_last)
    dnorm_ref[...] = jnp.concatenate([zero, gain_two, gain_last, zero, bias_two, bias_last, zero, zero], axis=0)


def attend_back_kernel(
    pos_ref, do_ref, q_ref, kv_ref, lse_ref, hall_ref, hq_ref, a_ref, x_ref, dx1_ref, mixt_ref, seg_ref, row_ref,
    norm_ref, dnorm_ref, da_ref, dx_ref, dkv, dq, hallt, dh, dxin, dmem,
):
    visible = visible_keys(seg_ref, row_ref)

    def attend(p):
        cut = lanes(p * PAIR, PAIR)
        keys = kv_ref[:, cut]
        values = kv_ref[:, lanes(D + p * PAIR, PAIR)]
        turned = keys.T
        queries = q_ref[:, cut] * HD ** (-0.5)
        grads = do_ref[:, cut]
        outs = []
        dk = dv = None
        for head in range(2):
            own, grad = head_lanes(queries, head), head_lanes(grads, head)
            scores = masked(visible, nt(keys, own))
            probs = jnp.exp(scores - lse_ref[p, head : head + 1, :])
            dprobs = nt(values, grad)
            inner = jnp.sum(probs * dprobs, axis=0, keepdims=True)
            dscores = (probs * (dprobs - inner)).astype(BF)
            outs.append(nn(turned[head * HD : (head + 1) * HD, :], dscores))
            one, two = nn(dscores, own), nn(probs.astype(BF), grad)
            dk = one if head == 0 else dk + one
            dv = two if head == 0 else dv + two
        dq[:, cut] = (jnp.concatenate(outs, axis=0).T * HD ** (-0.5)).astype(BF)
        dkv[:, cut] = dk.astype(BF)
        dkv[:, lanes(D + p * PAIR, PAIR)] = dv.astype(BF)

    each(0, NPAIR, attend)
    da_ref[:, :D] = nn(hq_ref[...].T, dq[...]).astype(BF)

    def turn(i):
        hallt[:, lanes(i * BLK, BLK)] = hall_ref[pl.ds(i * BLK, BLK), :].T

    each(0, KEYS // BLK, turn)

    def weights(j):
        cut = lanes(j * BLK, BLK)
        da_ref[:, lanes(D + j * BLK, BLK)] = nn(hallt[...], dkv[:, cut]).astype(BF)

    each(0, 2 * D // BLK, weights)

    def memory(i):
        cut = pl.ds(i * BLK, BLK)
        dmem[cut, :] = nt(dkv[cut, :], a_ref[:, D : 3 * D]).astype(BF)

    each(0, SLOTS, memory)

    def local(i):
        cut = pl.ds(i * BLK, BLK)
        dh[cut, :] = nt(dkv[pl.ds(SLOTS * NB + i * BLK, BLK), :], a_ref[:, D : 3 * D]) + nn(mixt_ref[cut, :], dmem[...])

    each(0, SEQ_LEN // BLK, local)
    dxin[:PICKS, :] = nt(dq[...], a_ref[:, :D])

    def scatter_query(k):
        row = pl.ds(pos_ref[k], 1)
        dh[row, :] += dxin[pl.ds(k, 1), :]

    each(0, PICKS, scatter_query)
    gain = norm_ref[0:1, :]
    da_rows = [jnp.zeros((1, D), FL), jnp.zeros((1, D), FL)]

    def finish(i, carry):
        cut = pl.ds(i * BLK, BLK)
        unit, scale = standard(x_ref[cut, :].astype(FL))
        grad, dgain, dbias = norm_back(unit, scale, gain, dh[cut, :])
        dxin[cut, :] = grad
        return carry[0] + dgain, carry[1] + dbias

    dgain, dbias = lax.fori_loop(0, SEQ_LEN // BLK, finish, tuple(da_rows))

    def scatter_rest(k):
        row = pl.ds(pos_ref[k], 1)
        dxin[row, :] += dx1_ref[pl.ds(k, 1), :]

    each(0, PICKS, scatter_rest)
    dx_ref[...] = dxin[...].astype(BF)
    line = iota((8, D), 0)
    norms = dnorm_ref[...] + jnp.where(line == 0, dgain, jnp.where(line == 3, dbias, 0.0))
    tall = jnp.concatenate([norms, jnp.zeros((EXTRA - 8, D), FL)], axis=0)
    da_ref[:, 3 * D :] = tall.T.astype(BF)


def head_kernel(
    nb, nv, part, f_ref, w_ref, live_ref, target_ref, df_ref, dw_ref, loss_ref,
    fall, expo, block, mine, stats, ft, grad_sum, coef, df, half, far_got, out,
    near_out, near_in, far_out, far_in, stat_out, stat_in, pair_out, pair_in, sum_out, sum_in, dw_sem,
):
    v = lax.axis_index("vocab")
    rows = w_ref.shape[1]
    total_rows = nv * PICKS
    core, chip, chips = lax.rem(v, 2), v // 2, nv // 2
    sibling = {"vocab": v + 1 - 2 * core}
    base = v * rows
    pieces = rows // part
    depth = min(2, pieces)
    meet((("vocab", nv),))

    def peer(step):
        return {"vocab": lax.rem(chip + step, chips) * 2 + core}

    def far_copy(step):
        return send(f_ref, fall.at[v], far_out.at[step], far_in.at[step], peer(step))

    def near_copy(step):
        slot = lax.rem(chip - step + chips, chips) * 2 + core
        return send(fall.at[slot], fall.at[slot], near_out.at[step], near_in.at[step], sibling)

    fall[v] = f_ref[...]
    near_copy(0).start()
    each(1, chips, lambda step: far_copy(step).start())

    def logits(step):
        @pl.when(step > 0)
        def _():
            far_copy(step).wait_recv()
            near_copy(step).start()

        near_copy(step).wait_recv()
        source = lax.rem(chip - step + chips, chips)
        start = pl.multiple_of(source * 2 * PICKS, 2 * PICKS)
        features = fall[pl.ds(source * 2, 2)].reshape(2 * PICKS, D)
        target = target_ref[pl.ds(start, 2 * PICKS), :] - base

        def score(j, peak):
            cut = lanes(j * part, part)
            value = nn(features, w_ref[:, cut])
            block[:, cut] = value
            return jnp.maximum(
                peak, jnp.max(jnp.where(live_ref[0:1, cut] > 0, value, NEG_BIG), axis=1, keepdims=True)
            )

        peak = lax.fori_loop(0, pieces, score, jnp.full((2 * PICKS, 1), NEG_BIG, FL))

        def count(j, carry):
            total, picked, valid = carry
            cut = lanes(j * part, part)
            value = block[:, cut]
            live = live_ref[0:1, cut] > 0
            hot = target - j * part == iota((2 * PICKS, part), 1)
            e = jnp.where(live, jnp.exp(value - peak), 0.0)
            expo[pl.ds(start, 2 * PICKS), cut] = e.astype(BF)
            total = total + jnp.sum(e, axis=1, keepdims=True)
            picked = picked + jnp.sum(jnp.where(hot, value, 0.0), axis=1, keepdims=True)
            valid = valid + jnp.sum(jnp.where(hot & live, 1.0, 0.0), axis=1, keepdims=True)
            return total, picked, valid

        zero = jnp.zeros((2 * PICKS, 1), FL)
        total, picked, valid = lax.fori_loop(0, pieces, count, (zero, zero, zero))
        lane = iota((2 * PICKS, 128), 1)
        wide = jnp.where(lane == 0, peak, jnp.where(lane == 1, total, jnp.where(lane == 2, picked, valid)))
        mine[:, pl.ds(start, 2 * PICKS)] = wide.T[:8, :]

    each(0, chips, logits)

    def stat_copy(step):
        return send(mine, stats.at[v], stat_out.at[step], stat_in.at[step], {"vocab": lax.rem(v + step, nv)})

    each(1, nv, lambda step: stat_copy(step).start())
    stats[v] = mine[...]
    for i in range(total_rows // 256 if pieces > 1 else 0):
        ft[:, i * 256 : (i + 1) * 256] = fall[2 * i : 2 * i + 2].reshape(256, D).T
    each(1, nv, lambda step: stat_copy(step).wait())
    start = jnp.full((1, total_rows), NEG_BIG, FL)
    peak = lax.fori_loop(0, nv, lambda u, top: jnp.maximum(top, stats[u, 0:1, :]), start)

    def combine(u, carry):
        scale = jnp.exp(stats[u, 0:1, :] - peak)
        return (
            carry[0] + stats[u, 1:2, :] * scale, carry[1] + stats[u, 2:3, :], carry[2] + stats[u, 3:4, :],
        )

    zero = jnp.zeros((1, total_rows), FL)
    total, picked, valid = lax.fori_loop(0, nv, combine, (zero, zero, zero))
    lse = peak + jnp.log(jnp.maximum(total, 1e-37))
    weight = valid / (jnp.maximum(jnp.sum(valid, axis=1, keepdims=True), 1.0) * nb)
    loss = jnp.sum(weight * (lse - picked), axis=1, keepdims=True)
    loss_ref[...] = jnp.broadcast_to(loss, loss_ref.shape)
    alpha = weight * jnp.exp(mine[0:1, :] - lse)
    line = iota((128, 256), 0)
    for i in range(total_rows // 256):
        cut = slice(i * 256, (i + 1) * 256)
        coef[cut, :] = jnp.where(line == 0, alpha[:, cut], weight[:, cut]).T

    tall = min(total_rows, 1024 if pieces > 1 else 256)
    shards_tall = tall // PICKS
    df[...] = jnp.zeros_like(df)

    def out_copy(j):
        return pltpu.make_async_copy(
            out.at[lax.rem(j, depth)], dw_ref.at[:, lanes(j * part, part)], dw_sem.at[lax.rem(j, depth)]
        )

    def gradients(j):
        cut = lanes(j * part, part)
        words = w_ref[:, cut]

        @pl.when(j >= depth)
        def _():
            out_copy(j - depth).wait()

        def strip(t):
            start = t * tall if total_rows == tall else pl.multiple_of(t * tall, tall)
            here = pl.ds(start, tall)
            hot = target_ref[here, :] - base - j * part == iota((tall, part), 1)
            two = coef[here, :]
            value = two[:, 0:1] * expo[here, cut].astype(FL) - jnp.where(hot, two[:, 1:2], 0.0)
            dlogits = value.astype(BF)
            df[here, :] += nt(dlogits, words)
            if pieces > 1:
                turned = ft[:, pl.ds(start, tall)]
            else:
                turned = fall[pl.ds(t * shards_tall, shards_tall)].reshape(tall, D).T
            for r in range(0, D, D // 3):
                more = nn(turned[r : r + D // 3, :], dlogits)
                if total_rows == tall:
                    out[lax.rem(j, depth), r : r + D // 3, :] = more.astype(BF)
                else:
                    grad_sum[r : r + D // 3, :] += more

        if total_rows == tall:
            strip(0)
        else:
            grad_sum[...] = jnp.zeros_like(grad_sum)
            each(0, total_rows // tall, strip)
            for r in range(0, D, D // 3):
                out[lax.rem(j, depth), r : r + D // 3, :] = grad_sum[r : r + D // 3, :].astype(BF)
        out_copy(j).start()

    each(0, pieces, gradients)

    def shard(index):
        return pl.ds(pl.multiple_of(index * PICKS, PICKS), PICKS)

    def pair_copy(k):
        source = df.at[shard(2 * k + 1 - core), :] if pieces > 1 else fall.at[k]
        return send(source, half.at[k], pair_out.at[k], pair_in.at[k], sibling)

    near_copy(0).wait_send()

    def drain(step):
        far_copy(step).wait_send()
        near_copy(step).wait_send()

    each(1, chips, drain)

    def swap(k):
        if pieces == 1:
            fall[k] = df[shard(2 * k + 1 - core), :].astype(BF)
        pair_copy(k).start()

    each(0, chips, swap)

    def sum_copy(step):
        return send(fall.at[chips + step], far_got.at[step], sum_out.at[step], sum_in.at[step], peer(step))

    def pass_on(turn):
        step = lax.rem(turn, chips)
        k = lax.rem(chip + step, chips)
        pair_copy(k).wait()
        value = df[shard(2 * k + core), :] + half[k].astype(FL)

        @pl.when(step > 0)
        def _():
            fall[chips + step] = value.astype(BF)
            sum_copy(step).start()

        @pl.when(step == 0)
        def _():
            df_ref[...] = value

    each(1, chips + 1, pass_on)

    def collect(step):
        sum_copy(step).wait()
        df_ref[...] += far_got[step].astype(FL)

    each(1, chips, collect)
    for j in range(pieces - depth, pieces):
        out_copy(j).wait()


def head(nb, nv, features, words, live, targets):
    rows = words.shape[1]
    part = chunk_of(rows, 640)
    total_rows = nv * PICKS
    chips = nv // 2
    dma = pltpu.SemaphoreType.DMA
    scratch = [
        pltpu.VMEM((nv, PICKS, D), BF),
        pltpu.VMEM((total_rows, rows), BF),
        pltpu.VMEM((2 * PICKS, rows), FL),
        pltpu.VMEM((8, total_rows), FL),
        pltpu.VMEM((nv, 8, total_rows), FL),
        pltpu.VMEM((D, total_rows) if rows > part else (8, 128), BF),
        pltpu.VMEM((8, 128) if rows > part else (D, part), FL),
        pltpu.VMEM((total_rows, 128), FL),
        pltpu.VMEM((total_rows, D), FL),
        pltpu.VMEM((chips, PICKS, D), FL if rows > part else BF),
        pltpu.VMEM((chips, PICKS, D), BF),
        pltpu.VMEM((min(2, rows // part), D, part), BF),
        dma((chips,)), dma((chips,)), dma((chips,)), dma((chips,)), dma((nv,)), dma((nv,)),
        dma((chips,)), dma((chips,)), dma((chips,)), dma((chips,)), dma((2,)),
    ]
    return run(
        functools.partial(head_kernel, nb, nv, part),
        [SD((PICKS, D), FL), SD((D, rows), BF), SD((8, 128), FL)],
        scratch,
        [features, words, live, targets],
        "head",
        1,
        out_specs=[VM, HB, VM],
    )


def norm_kernel(
    nb, nv, extra_ref, dw_ref, a_ref, p_ref, u_ref, c_ref, loss_ref, out_ref,
    mine, near, lines, vocab_out, vocab_in, batch_out, batch_in,
):
    b, v = lax.axis_index("batch"), lax.axis_index("vocab")
    meet((("batch", nb), ("vocab", nv)))

    def squares(refs, part):
        cols = refs[0].shape[1]

        def add(j, total):
            value = refs[0][:, lanes(j * part, part)].astype(FL)
            for ref in refs[1:]:
                value = value + ref[:, lanes(j * part, part)].astype(FL)
            return total + jnp.sum(value * value, axis=0, keepdims=True)

        line = lax.fori_loop(0, cols // part, add, jnp.zeros((1, part), FL))
        return jnp.sum(line, axis=1, keepdims=True)

    own = squares((extra_ref, dw_ref), chunk_of(dw_ref.shape[1], 640))
    layer = squares((a_ref,), 512) + squares((p_ref,), 384) + squares((u_ref,), 512) + squares((c_ref,), 384)
    own = own + jnp.where(v == 0, layer, jnp.zeros_like(layer))
    line = iota((8, 128), 0)
    mine[...] = jnp.where(line == 0, own, jnp.where((line == 1) & (v == 0), loss_ref[...], 0.0))

    def vocab_copy(step):
        return send(mine, near.at[v], vocab_out.at[step], vocab_in.at[step], {"vocab": lax.rem(v + step, nv)})

    each(1, nv, lambda step: vocab_copy(step).start())
    near[v] = mine[...]
    each(1, nv, lambda step: vocab_copy(step).wait())
    mine[...] = lax.fori_loop(0, nv, lambda u, total: total + near[u], jnp.zeros((8, 128), FL))

    def batch_copy(step):
        return send(mine, lines.at[b], batch_out.at[step], batch_in.at[step], {"batch": lax.rem(b + step, nb)})

    each(1, nb, lambda step: batch_copy(step).start())
    lines[b] = mine[...]
    each(1, nb, lambda step: batch_copy(step).wait())
    out_ref[...] = lax.fori_loop(0, nb, lambda u, total: total + lines[u], jnp.zeros((8, 128), FL))


def norm(nb, nv, extra, dw, sums, loss):
    dma = pltpu.SemaphoreType.DMA
    return run(
        functools.partial(norm_kernel, nb, nv),
        [SD((8, 128), FL)],
        [
            pltpu.VMEM((8, 128), FL), pltpu.VMEM((nv, 8, 128), FL), pltpu.VMEM((nb, 8, 128), FL),
            dma((nv,)), dma((nv,)), dma((nb,)), dma((nb,)),
        ],
        [extra, dw, *sums, loss],
        "norm",
        5,
    )[0]


def adamw(weight, moment, square, gradient, clip, count, decay, rate):
    gradient = gradient * clip
    moment = BETA_ONE * moment + (1 - BETA_ONE) * gradient
    square = BETA_TWO * square + (1 - BETA_TWO) * gradient * gradient
    fixed_moment = moment / (1 - BETA_ONE**count)
    fixed_square = square / (1 - BETA_TWO**count)
    weight = weight - rate * (fixed_moment / (jnp.sqrt(fixed_square) + ADAM_EPS) + decay * weight)
    return (weight, moment, square)


def slot_size(nv):
    mean = SEQ_LEN // nv
    return -(-(mean + int(5.5 * math.sqrt(mean))) // 32) * 32


def shards(
    nb, nv,
    tokens, targets, segments, counted, vocab_mask, step_count,
    table, table_moment, table_square,
    attend, attend_moment, attend_square,
    project, project_moment, project_square,
    expand, expand_moment, expand_square,
    contract, contract_moment, contract_square,
    gain, gain_moment, gain_square,
    shift, shift_moment, shift_square,
):
    rows, width = table.shape
    cap = slot_size(nv)
    table_t = table.T
    norms = jnp.concatenate([gain, shift], axis=0)
    packed = jnp.concatenate([attend[0], norms.T, jnp.zeros((width, EXTRA - 6), FL)], axis=1).astype(BF)
    pieces = (packed, project[0].astype(BF), expand[0].astype(BF), contract[0].astype(BF))
    words = lax.all_gather(table_t.astype(BF), "batch", axis=0, tiled=True)

    seg_row, pos_row = segments[None, :], counted[None, :]
    tok = tokens.reshape(nv, SEQ_LEN)
    x, ids, place, most, every, a_all, p_all, u_all, c_all = embed(
        nb, nv, cap, jnp.zeros((1,), I32), tok, table_t, pieces
    )
    turns = (most[0, 0].astype(I32) + cap - 1) // cap

    def more_rows(state):
        turn, total = state
        return turn + 1, total + embed(nb, nv, cap, turn[None], tok, table_t)[0]

    x = lax.cond(
        turns > 1,
        lambda x: lax.while_loop(lambda state: state[0] < turns, more_rows, (jnp.int32(1), x))[1],
        lambda x: x,
        x,
    )

    hall, kv, q, hq, xq, mixed, lse, norm_rows, mixing_t = run(
        attend_kernel,
        [
            SD((KEYS, D), BF), SD((KEYS, 2 * D), BF), SD((PICKS, D), BF), SD((PICKS, D), BF), SD((PICKS, D), FL),
            SD((PICKS, D), BF), SD((NPAIR, 2, PICKS), FL), SD((8, D), FL), SD((SEQ_LEN, SLOTS * NB), BF),
        ],
        [],
        [x, a_all, seg_row, pos_row],
        "attend", flops=7 * 10**9, moved=20 * 10**6,
    )
    x1, h2, z, act, x2, features = run(
        feed_kernel,
        [
            SD((PICKS, D), FL), SD((PICKS, D), BF), SD((PICKS, FF), FL), SD((PICKS, FF), BF), SD((PICKS, D), FL),
            SD((PICKS, D), BF),
        ],
        [],
        [xq, mixed, p_all, u_all, c_all, norm_rows],
        "feed", flops=2 * 10**9, moved=15 * 10**6,
    )
    df, dw, loss_block = head(nb, nv, features, words, vocab_mask[None, :], targets[:, None])
    dw_sum = lax.psum_scatter(dw, "batch", scatter_dimension=0, tiled=True)

    dc, du, dp, dx1, dmixed, dnorm = run(
        feed_back_kernel,
        [
            SD((FF, D), BF), SD((D, FF), BF), SD((D, D), BF), SD((PICKS, D), FL), SD((PICKS, D), BF), SD((8, D), FL),
        ],
        [pltpu.VMEM((PICKS, D), FL)],
        [df, x2, x1, h2, z, act, mixed, p_all, u_all, c_all, norm_rows],
        "feed_back", flops=4 * 10**9, moved=30 * 10**6,
    )
    da, dx = run(
        attend_back_kernel,
        [SD((D, 3 * D + EXTRA), BF), SD((SEQ_LEN, D), BF)],
        [
            pltpu.VMEM((KEYS, 2 * D), BF), pltpu.VMEM((PICKS, D), BF), pltpu.VMEM((D, KEYS), BF),
            pltpu.VMEM((SEQ_LEN, D), FL), pltpu.VMEM((SEQ_LEN, D), FL), pltpu.VMEM((SLOTS * NB, D), BF),
        ],
        [counted, dmixed, q, kv, lse, hall, hq, a_all, x, dx1, mixing_t, seg_row, pos_row, norm_rows, dnorm],
        "attend_back", flops=12 * 10**9, moved=25 * 10**6,
        in_specs=[SM] + [VM] * 14,
    )
    extra, *sums = unembed(nb, nv, cap, width, rows, dx, ids, place, (da, dp, du, dc))

    def more_grads(state):
        turn, total = state
        later = later_slots(nv, cap, rows, every, turn)
        return turn + 1, total + unembed(
            nb, nv, cap, width, rows, dx, later, place - jnp.array([0, 1, 0, 0, 0, 0, 0, 0], I32)[None, :, None] * (turn * cap)
        )[0]

    extra = lax.cond(
        turns > 1,
        lambda extra: lax.while_loop(lambda state: state[0] < turns, more_grads, (jnp.int32(1), extra))[1],
        lambda extra: extra,
        extra,
    )

    totals = norm(nb, nv, extra, dw_sum, sums, loss_block)
    grad_table = dw_sum.astype(FL) + extra
    grad_a, grad_p, grad_u, grad_c = (item.astype(FL) for item in sums)
    grad_norms = grad_a[:, 3 * D : 3 * D + 6].T
    grad_a = grad_a[:, : 3 * D]
    squares, loss = totals[0, 0], totals[1, 0]
    gradient_norm = jnp.sqrt(squares)
    clip = jnp.minimum(1.0, MAX_NORM / (gradient_norm + 1e-06))
    count = step_count[0].astype(FL)

    def update(weight, moment, square, gradient, decay=DECAY, rate=LEARN_RATE):
        return adamw(weight, moment, square, gradient, clip, count, decay, rate)

    table_out = [item.T for item in update(table_t, table_moment.T, table_square.T, grad_table)]
    attend_out = update(attend, attend_moment, attend_square, grad_a[None])
    project_out = update(project, project_moment, project_square, grad_p[None])
    expand_out = update(expand, expand_moment, expand_square, grad_u[None])
    contract_out = update(contract, contract_moment, contract_square, grad_c[None])
    gain_out = update(gain, gain_moment, gain_square, grad_norms[:3], 0.0, NORM_RATE)
    shift_out = update(shift, shift_moment, shift_square, grad_norms[3:], 0.0, NORM_RATE)
    return (
        loss, gradient_norm, *table_out, *attend_out, *project_out, *expand_out, *contract_out, *gain_out, *shift_out,
    )


def solution(mesh):
    nb, nv = mesh.shape["batch"], mesh.shape["vocab"]
    both, split, middle, last = P(("batch", "vocab")), P("vocab", "batch"), P(None, "batch", None), P(None, "batch")
    state = (split,) * 3 + (middle,) * 12 + (last,) * 6
    return jax.shard_map(
        functools.partial(shards, nb, nv),
        mesh=mesh,
        in_specs=(P("batch"), P("batch"), both, both, P("vocab"), P()) + state,
        out_specs=(P(), P()) + state,
        check_vma=False,
    )
```

```python
import functools
import math

import jax
import jax.numpy as jnp
from jax import lax
from jax.experimental import pallas as pl
from jax.experimental.pallas import tpu as pltpu
from jax.sharding import PartitionSpec as P

D = 768
H = 12
HD = 64
FF = 3072
NB = 256
SEG_BLOCKS = 4
SLOTS = SEG_BLOCKS - 2
SEQ_LEN = 1024
PICKS = 128
KEYS = SLOTS * NB + SEQ_LEN
BLK = 256
PAIR = 2 * HD
NPAIR = H // 2
EXTRA = 256
WIDE = (3 * D + EXTRA, D, FF, D)

NORM_EPS = 1e-05
MAX_NORM = 0.02
LEARN_RATE = 0.04
NORM_RATE = 0.5
BETA_ONE = 0.9
BETA_TWO = 0.999
ADAM_EPS = 1e-08
DECAY = 0.1
NEG_BIG = -1e30
BF = jnp.bfloat16
FL = jnp.float32
I32 = jnp.int32
MESH = pl.DeviceIdType.MESH
SD = jax.ShapeDtypeStruct
VM = pl.BlockSpec(memory_space=pltpu.VMEM)
SM = pl.BlockSpec(memory_space=pltpu.SMEM)
HB = pl.BlockSpec(memory_space=pl.ANY)
LIMIT = 62 * 2**20


def nn(a, b):
    return lax.dot_general(a, b, (((1,), (0,)), ((), ())), preferred_element_type=FL)


def nt(a, b):
    return lax.dot_general(a, b, (((1,), (1,)), ((), ())), preferred_element_type=FL)


def iota(shape, axis):
    return lax.broadcasted_iota(I32, shape, axis)


def lanes(start, size):
    return pl.ds(pl.multiple_of(start, 128), size)


def chunk_of(rows, want):
    return want if rows % want == 0 else rows


def run(kernel, outs, scratch, ins, name, collective=None, flops=0, moved=0, out_specs=None, in_specs=None):
    return pl.pallas_call(
        kernel,
        out_shape=outs,
        in_specs=in_specs if in_specs is not None else [VM] * len(ins),
        out_specs=out_specs if out_specs is not None else [VM] * len(outs),
        scratch_shapes=scratch,
        compiler_params=pltpu.CompilerParams(
            vmem_limit_bytes=LIMIT,
            collective_id=collective,
            has_side_effects=collective is not None,
        ),
        cost_estimate=pl.CostEstimate(flops=flops, bytes_accessed=moved, transcendentals=0),
        name=name,
    )(*ins)


def send(source, target, out_sem, in_sem, device):
    return pltpu.make_async_remote_copy(
        src_ref=source, dst_ref=target, send_sem=out_sem, recv_sem=in_sem, device_id=device, device_id_type=MESH
    )


def meet(axes):
    barrier = pltpu.get_barrier_semaphore()
    count = 0
    for axis, size in axes:
        me = lax.axis_index(axis)

        def greet(step, carry, axis=axis, size=size, me=me):
            pl.semaphore_signal(barrier, inc=1, device_id={axis: lax.rem(me + step, size)}, device_id_type=MESH)
            return carry

        lax.fori_loop(1, size, greet, 0)
        count += size - 1
    pl.semaphore_wait(barrier, count)


def each(start, stop, body):
    def step(index, carry):
        body(index)
        return carry

    lax.fori_loop(start, stop, step, 0)


def embed_kernel(
    nb, nv, cap, part, rows, first, split, *refs
):
    round_ref, tok_ref, words = refs[:3]
    shards, refs = (refs[3:7], refs[7:]) if first else ((), refs[3:])
    target_ref, refs = (refs[0], refs[1:]) if split else (None, refs)
    x_ref, ids_ref, place_ref, most_ref, tok_ref_all = refs[:5]
    wholes, refs = (refs[5:9], refs[9:]) if first else ((), refs[5:])
    (quarter_ref, target_all), refs = (refs[:2], refs[2:]) if split else ((None, None), refs)
    before, ranks, work, sent, got, spread, mixed, turned = refs[:8]
    tok_out, tok_in, row_out, row_in, mix_out, mix_in = refs[8:14]
    b, v = lax.axis_index("batch"), lax.axis_index("vocab")
    width = words.shape[0]
    shift = round_ref[0] * cap
    meet((("batch", nb), ("vocab", nv)))
    gather = WeightGather(nb, shards, wholes, *refs[14:19]) if first else None
    quarter_out, quarter_in, quarter_own, target_out, target_in = refs[19:24] if split else [None] * 5

    def tok_copy(step):
        return send(
            tok_ref, tok_ref_all.at[b], tok_out.at[step], tok_in.at[step], {"batch": lax.rem(b + step, nb)}
        )

    for step in range(1, nb):
        tok_copy(step).start()

    def target_copy(step):
        return send(
            target_ref, target_all.at[b], target_out.at[step], target_in.at[step], {"batch": lax.rem(b + step, nb)}
        )

    def quarter(owner):
        return words.at[:, lanes(owner * (words.shape[1] // nb), words.shape[1] // nb)]

    def quarter_copy(step):
        other = lax.rem(b + step, nb)
        place = quarter_ref.at[pl.ds(pl.multiple_of(b * width, 16), width), :]
        return send(quarter(other), place, quarter_out.at[step], quarter_in.at[step], {"batch": other})

    def quarter_keep():
        place = quarter_ref.at[pl.ds(pl.multiple_of(b * width, 16), width), :]
        return pltpu.make_async_copy(quarter(b), place, quarter_own.at[0])

    if split:
        target_all[b] = target_ref[...]
        for step in range(1, nb):
            target_copy(step).start()
    if first:
        gather.start()
    if split:
        quarter_keep().start()
    tok_ref_all[b] = tok_ref[...]
    before[...] = (iota((SEQ_LEN, SEQ_LEN), 0) < iota((SEQ_LEN, SEQ_LEN), 1)).astype(FL).astype(BF)
    for step in range(1, nb):
        tok_copy(step).wait()

    base = v * rows
    most = jnp.zeros((nv, 1), FL)
    for p in range(nb):
        ids = tok_ref_all[p]
        mine = (ids >= base) & (ids < base + rows)
        rank = nn(mine.astype(FL).astype(BF), before[...])
        ranks[p] = jnp.where(mine, rank.astype(I32) - shift, -1)
        for owner in range(nv):
            theirs = (ids >= owner * rows) & (ids < (owner + 1) * rows)
            most = jnp.maximum(most, jnp.sum(theirs.astype(FL), axis=1, keepdims=True))
    most_ref[...] = jnp.broadcast_to(jnp.max(most, axis=0, keepdims=True), most_ref.shape)

    def row_copy(step):
        return send(
            sent.at[step], got.at[v], row_out.at[step], row_in.at[step], {"vocab": lax.rem(v + step, nv)}
        )

    def build(turn):
        step = lax.rem(turn, nv)
        dest = lax.rem(v + step, nv)
        found = []
        for p in range(nb):
            pick = (iota((cap, SEQ_LEN), 0) == ranks[p, pl.ds(dest, 1), :]).astype(FL).astype(BF)
            local = tok_ref_all[p, pl.ds(dest, 1), :] - base
            line = iota((8, SEQ_LEN), 0)
            high, low = lax.shift_right_arithmetic(local, 7), lax.bitwise_and(local, 127)
            digits = jnp.where(line == 0, high, jnp.where(line == 1, low, 0)).astype(FL).astype(BF)
            both = nt(pick, digits)
            found.append((both[:, 0:1] * 128.0 + both[:, 1:2]).astype(I32))
        index = jnp.concatenate(found, axis=0)
        ids_ref[dest] = index
        work[...] = jnp.zeros_like(work)

        def piece(j):
            hot = (index - j * part == iota((nb * cap, part), 1)).astype(FL).astype(BF)
            work[...] += nt(hot, words[:, lanes(j * part, part)])

        each(0, rows // part, piece)
        block = work[...].T.astype(BF)

        @pl.when(step > 0)
        def _():
            sent[step] = block
            row_copy(step).start()

        @pl.when(step == 0)
        def _():
            got[v] = block

    each(1, nv + 1, build)
    if first:
        gather.pass_on()
    if split:
        for step in range(1, nb):
            quarter_copy(step).start()

    keys = []
    for p in range(nb):
        ids = tok_ref_all[p, pl.ds(v, 1), :]
        owner = iota((nv, SEQ_LEN), 0)
        theirs = (ids >= owner * rows) & (ids < (owner + 1) * rows)
        rank = nn(theirs.astype(FL).astype(BF), before[...])
        place = jnp.sum(jnp.where(theirs, rank, 0.0), axis=0, keepdims=True).astype(I32) - shift
        holder = jnp.sum(jnp.where(theirs, owner.astype(FL), 0.0), axis=0, keepdims=True).astype(I32)
        line = iota((8, SEQ_LEN), 0)
        place_ref[p] = jnp.where(line == 0, holder, jnp.where(line == 1, place, 0))
        keys.append((holder, place))
        spread[p] = jnp.zeros((width, SEQ_LEN), FL)

    def take(turn):
        step = lax.rem(turn, nv)
        source = lax.rem(v - step + nv, nv)

        @pl.when(step > 0)
        def _():
            row_copy(step).wait()

        block = got[source]
        for p in range(nb):
            holder, place = keys[p]
            key = jnp.where(holder == source, place, -1)
            hot = (iota((cap, SEQ_LEN), 0) == key).astype(FL).astype(BF)
            spread[p] += nn(block[:, p * cap : (p + 1) * cap], hot)

    each(1, nv + 1, take)

    def mix_copy(step):
        return send(
            mixed.at[step], turned.at[b], mix_out.at[step], mix_in.at[step], {"batch": lax.rem(b + step, nb)}
        )

    for step in range(1, nb):
        mixed[step] = spread[lax.rem(b + step, nb)].astype(BF)
        mix_copy(step).start()
    turned[b] = spread[b].astype(BF)
    for step in range(1, nb):
        mix_copy(step).wait()
    x_ref[...] = turned[...].reshape(nb * width, SEQ_LEN).T
    if first:
        gather.finish()
    if split:
        quarter_keep().wait()
        for step in range(1, nb):
            target_copy(step).wait()
            quarter_copy(step).wait()


class WeightGather:
    def __init__(self, nb, shards, wholes, own_sem, out_sem, in_sem, pair_out, pair_in):
        self.nb, self.shards, self.wholes = nb, shards, wholes
        self.own_sem, self.out_sem, self.in_sem, self.pair_out, self.pair_in = own_sem, out_sem, in_sem, pair_out, pair_in
        self.b, v = lax.axis_index("batch"), lax.axis_index("vocab")
        self.core = lax.rem(v, 2)
        self.sibling = {"vocab": v + 1 - 2 * self.core}

    def flip(self, bits):
        b = self.b
        low, high = lax.rem(b, 2), b // 2
        return (high if bits < 2 else 1 - high) * 2 + (low if bits % 2 == 0 else 1 - low)

    def place(self, w, owner, top, size):
        rows, cols = self.shards[w].shape
        first = pl.multiple_of(owner * rows + top, 16)
        return self.wholes[w].at[pl.ds(first, size), lanes(self.core * (cols // 2), cols // 2)]

    def routes(self, w):
        rows = self.shards[w].shape[0]
        if self.nb == 4:
            half = rows // 2
            return [
                (self.b, 0, rows, self.flip(1), self.flip(1)),
                (self.b, 0, rows, self.flip(2), self.flip(2)),
                (self.flip(1), 0, half, self.flip(2), self.flip(3)),
                (self.flip(2), half, half, self.flip(1), self.flip(3)),
            ]
        others = [lax.rem(self.b + step, self.nb) for step in range(1, self.nb)]
        came = [lax.rem(self.b - step + self.nb, self.nb) for step in range(1, self.nb)]
        return [(self.b, 0, rows, other, source) for other, source in zip(others, came)]

    def own_copy(self, w):
        rows = self.shards[w].shape[0]
        first = pl.multiple_of(self.b * rows, 16)
        return pltpu.make_async_copy(self.shards[w], self.wholes[w].at[pl.ds(first, rows), :], self.own_sem.at[w])

    def copy(self, w, k):
        owner, top, size, device, _ = self.routes(w)[k]
        cols = self.shards[w].shape[1]
        if self.nb == 4 and k >= 2:
            source = self.place(w, owner, top, size)
        else:
            source = self.shards[w].at[:, lanes(self.core * (cols // 2), cols // 2)]
        target = self.place(w, owner, top, size)
        return send(source, target, self.out_sem.at[w, k], self.in_sem.at[w, k], {"batch": device})

    def pair(self, w, k):
        _, top, size, _, arrived = self.routes(w)[k]
        ref = self.place(w, arrived, top, size)
        return send(ref, ref, self.pair_out.at[w, k], self.pair_in.at[w, k], self.sibling)

    def start(self):
        for w in range(4):
            for k in range(2 if self.nb == 4 else self.nb - 1):
                self.copy(w, k).start()
        for w in range(4):
            self.own_copy(w).start()

    def pass_on(self):
        if self.nb != 4:
            return
        for w in range(4):
            for k in range(2):
                self.copy(w, k).wait_recv()
                self.copy(w, k + 2).start()
                self.pair(w, k).start()

    def finish(self):
        for w in range(4):
            for k in range(2 if self.nb == 4 else 0, len(self.routes(w))):
                self.copy(w, k).wait_recv()
                self.pair(w, k).start()
        for w in range(4):
            self.own_copy(w).wait()
            for k in range(len(self.routes(w))):
                self.copy(w, k).wait_send()
                self.pair(w, k).wait()


def embed(nb, nv, cap, rows, turn, tok, table, shards=(), targets=None):
    width = table.shape[0]
    split = targets is not None
    part = chunk_of(rows, 640)
    count = nb * cap
    outs = [
        SD((SEQ_LEN, D), BF),
        SD((nv, count, 1), I32),
        SD((nb, 8, SEQ_LEN), I32),
        SD((8, 128), FL),
        SD((nb, nv, SEQ_LEN), I32),
    ]
    first = len(shards) > 0
    outs += [SD((nb * item.shape[0], item.shape[1]), BF) for item in shards]
    if split:
        outs += [SD((D, table.shape[1] // nb), BF), SD((nb, *targets.shape), I32)]
    dma = pltpu.SemaphoreType.DMA
    scratch = [
        pltpu.VMEM((SEQ_LEN, SEQ_LEN), BF),
        pltpu.VMEM((nb, nv, SEQ_LEN), I32),
        pltpu.VMEM((count, width), FL),
        pltpu.VMEM((nv, width, count), BF),
        pltpu.VMEM((nv, width, count), BF),
        pltpu.VMEM((nb, width, SEQ_LEN), FL),
        pltpu.VMEM((nb, width, SEQ_LEN), BF),
        pltpu.VMEM((nb, width, SEQ_LEN), BF),
        dma((nb,)), dma((nb,)), dma((nv,)), dma((nv,)), dma((nb,)), dma((nb,)),
    ]
    if first:
        scratch += [dma((4,)), dma((4, 4)), dma((4, 4)), dma((4, 4)), dma((4, 4))]
    if split:
        scratch += [dma((nb,)), dma((nb,)), dma((1,)), dma((nb,)), dma((nb,))]
    extra = [targets] if split else []
    return run(
        functools.partial(embed_kernel, nb, nv, cap, part, rows, first, split), outs, scratch,
        [turn, tok, table, *shards, *extra],
        "embed" if first else "embed_more", 0 if first else 3,
        in_specs=[SM, VM, VM] + [HB] * len(shards) + [VM] * len(extra),
        out_specs=[VM] * 5 + [HB] * len(shards) + ([HB, VM] if split else []),
    )


class GradientSum:
    def __init__(self, nb, nv, grads, sums, refs):
        self.nb, self.nv, self.grads, self.sums = nb, nv, grads, sums
        self.own, self.near, self.shard, self.total = refs[0:4], refs[4:8], refs[8:12], refs[12:16]
        self.bits, self.result = refs[16:20], refs[20:24]
        (self.load_sem, self.pair_out, self.pair_in, self.mix_out, self.mix_in, self.cut_out, self.cut_in,
         self.all_out, self.all_in, self.last_out, self.last_in, self.store_sem) = refs[24:36]
        self.b, v = lax.axis_index("batch"), lax.axis_index("vocab")
        self.core, self.chip, self.chips = lax.rem(v, 2), v // 2, nv // 2
        self.sibling = {"vocab": v + 1 - 2 * self.core}

    def half(self, w, core):
        cols = self.grads[w].shape[1] // 2
        return lanes(core * cols, cols)

    def load(self, w):
        return pltpu.make_async_copy(self.grads[w].at[:, self.half(w, self.core)], self.own[w], self.load_sem.at[w])

    def pair(self, w):
        source = self.grads[w].at[:, self.half(w, 1 - self.core)]
        return send(source, self.near[w], self.pair_out.at[w], self.pair_in.at[w], self.sibling)

    def start(self):
        for w in (2, 3, 0, 1):
            self.pair(w).start()
            self.load(w).start()

    def mix(self, w, step):
        other = lax.rem(self.b + step, self.nb)
        rows = self.own[w].shape[0] // self.nb
        source = self.own[w].at[pl.ds(pl.multiple_of(other * rows, 16), rows), :]
        return send(source, self.shard[w].at[step], self.mix_out.at[w, step], self.mix_in.at[w, step], {"batch": other})

    def scatter(self, w):
        self.load(w).wait()
        self.pair(w).wait()
        rows = self.own[w].shape[0] // self.nb

        def add(i, w=w, rows=rows):
            cut = pl.ds(pl.multiple_of(i * rows, 16), rows)
            self.own[w][cut, :] = (self.own[w][cut, :].astype(FL) + self.near[w][cut, :].astype(FL)).astype(BF)

        each(0, self.nb, add)
        for step in range(1, self.nb):
            self.mix(w, step).start()

    def pieces(self, w):
        rows = self.total[w].shape[0]
        count = max(n for n in range(1, self.chips + 1) if rows % (16 * n) == 0)
        return count, rows // count

    def peer(self, step):
        other = lax.rem(self.chip + step, self.chips)
        return other, {"vocab": other * 2 + self.core}

    def cut(self, w, step):
        other, device = self.peer(step)
        size = self.pieces(w)[1]
        source = self.total[w].at[pl.ds(pl.multiple_of(other * size, 16), size), :]
        return send(source, self.bits[w].at[step], self.cut_out.at[w, step], self.cut_in.at[w, step], device)

    def back(self, w, step):
        size = self.pieces(w)[1]
        place = self.result[w].at[pl.ds(pl.multiple_of(self.chip * size, 16), size), :]
        return send(place, place, self.all_out.at[w, step], self.all_in.at[w, step], self.peer(step)[1])

    def back_recv(self, w, step):
        source = lax.rem(self.chip - step + self.chips, self.chips)
        size = self.pieces(w)[1]
        place = self.result[w].at[pl.ds(pl.multiple_of(source * size, 16), size), :]
        return send(place, place, self.all_out.at[w, step], self.all_in.at[w, step], self.peer(step)[1])

    def reduce(self, w):
        rows = self.total[w].shape[0]
        for step in range(1, self.nb):
            self.mix(w, step).wait()
        here = pl.ds(pl.multiple_of(self.b * rows, 16), rows)
        value = self.own[w][here, :].astype(FL)
        for step in range(1, self.nb):
            value = value + self.shard[w][step].astype(FL)
        self.total[w][...] = value.astype(BF)
        count = self.pieces(w)[0]

        def go(step, w=w, count=count):
            @pl.when(self.peer(step)[0] < count)
            def _():
                self.cut(w, step).start()

        each(1, self.chips, go)

    def collect(self, w):
        count, size = self.pieces(w)
        mine = pl.ds(pl.multiple_of(self.chip * size, 16), size)

        @pl.when(self.chip < count)
        def _(w=w, mine=mine):
            def add(step, value):
                self.cut(w, step).wait_recv()
                return value + self.bits[w][step].astype(FL)

            value = lax.fori_loop(1, self.chips, add, self.total[w][mine, :].astype(FL))
            self.result[w][mine, :] = value.astype(BF)
            each(1, self.chips, lambda step: self.back(w, step).start())

        def sent(step, w=w, count=count):
            @pl.when(self.peer(step)[0] < count)
            def _():
                self.cut(w, step).wait_send()

        each(1, self.chips, sent)

    def last(self, w):
        return send(
            self.result[w], self.sums[w].at[:, self.half(w, self.core)], self.last_out.at[w], self.last_in.at[w], self.sibling
        )

    def store(self, w):
        return pltpu.make_async_copy(self.result[w], self.sums[w].at[:, self.half(w, self.core)], self.store_sem.at[w])

    def finish(self):
        for w in range(4):
            count = self.pieces(w)[0]

            def got(step, w=w, count=count):
                @pl.when(lax.rem(self.chip - step + self.chips, self.chips) < count)
                def _():
                    self.back_recv(w, step).wait_recv()

            each(1, self.chips, got)
            self.last(w).start()
            self.store(w).start()
        for w in range(4):
            count = self.pieces(w)[0]

            @pl.when(self.chip < count)
            def _(w=w):
                each(1, self.chips, lambda step: self.back(w, step).wait_send())

            self.store(w).wait()
            self.last(w).wait_send()
            other = self.sums[w].at[:, self.half(w, 1 - self.core)]
            send(other, other, self.last_out.at[w], self.last_in.at[w], self.sibling).wait_recv()


def gradient_scratch(nb, nv, grads):
    chips = nv // 2
    halves = [(item.shape[0], item.shape[1] // 2) for item in grads]
    shards = [(rows // nb, cols) for rows, cols in halves]
    sizes = [rows // max(n for n in range(1, chips + 1) if rows % (16 * n) == 0) for rows, _ in shards]
    dma = pltpu.SemaphoreType.DMA
    return (
        [pltpu.VMEM(item, BF) for item in halves] * 2
        + [pltpu.VMEM((nb, *item), BF) for item in shards]
        + [pltpu.VMEM(item, BF) for item in shards]
        + [pltpu.VMEM((chips, size, item[1]), BF) for size, item in zip(sizes, shards)]
        + [pltpu.VMEM(item, BF) for item in shards]
        + [dma((4,)), dma((4,)), dma((4,)), dma((4, nb)), dma((4, nb)), dma((4, chips)), dma((4, chips))]
        + [dma((4, chips)), dma((4, chips)), dma((4,)), dma((4,)), dma((4,))]
    )


def unembed_kernel(nb, nv, cap, part, first, split, *refs):
    x_ref, ids_ref, place_ref = refs[:3]
    grads, refs = (refs[3:7], refs[7:]) if first else ((), refs[3:])
    quarter_ref, refs = (refs[0], refs[1:]) if split else (None, refs)
    out_ref = refs[0]
    sums, refs = (refs[1:5], refs[5:]) if first else ((), refs[1:])
    dw_ref, refs = (refs[0], refs[1:]) if split else (None, refs)
    (quarter_out, quarter_in, quarter_own), refs = (refs[:3], refs[3:]) if split else ([None] * 3, refs)
    turned, parts, sent, got, mix_out, mix_in, row_out, row_in = refs[:8]
    layer = GradientSum(nb, nv, grads, sums, refs[8:]) if first else None
    b, v = lax.axis_index("batch"), lax.axis_index("vocab")
    width, rows = out_ref.shape
    meet((("batch", nb), ("vocab", nv)))
    turned[...] = x_ref[...].T.reshape(nb, width, SEQ_LEN)

    def mix_copy(step):
        other = lax.rem(b + step, nb)
        return send(turned.at[other], parts.at[b], mix_out.at[step], mix_in.at[step], {"batch": other})

    for step in range(1, nb):
        mix_copy(step).start()
    if first:
        layer.start()
    parts[b] = turned[b]
    for step in range(1, nb):
        mix_copy(step).wait()

    def quarter_place():
        size = quarter_ref.shape[1]
        return dw_ref.at[:, lanes(b * size, size)]

    def quarter_copy(step):
        other = lax.rem(b + step, nb)
        source = quarter_ref.at[pl.ds(pl.multiple_of(other * width, 16), width), :]
        return send(source, quarter_place(), quarter_out.at[step], quarter_in.at[step], {"batch": other})

    def quarter_keep():
        source = quarter_ref.at[pl.ds(pl.multiple_of(b * width, 16), width), :]
        return pltpu.make_async_copy(source, quarter_place(), quarter_own.at[0])

    def row_copy(step):
        return send(
            sent.at[step], got.at[v], row_out.at[step], row_in.at[step], {"vocab": lax.rem(v + step, nv)}
        )

    def build(turn):
        step = lax.rem(turn, nv)
        owner = lax.rem(v + step, nv)
        blocks = []
        for p in range(nb):
            key = jnp.where(place_ref[p, 0:1, :] == owner, place_ref[p, 1:2, :], -1)
            hot = (iota((cap, SEQ_LEN), 0) == key).astype(FL).astype(BF)
            blocks.append(nt(parts[p], hot).astype(BF))
        block = jnp.concatenate(blocks, axis=1)

        @pl.when(step > 0)
        def _():
            sent[step] = block
            row_copy(step).start()

        @pl.when(step == 0)
        def _():
            got[v] = block

    if first:
        layer.scatter(2)
    each(1, nv + 1, build)
    if first:
        layer.scatter(3)
    if split:
        quarter_keep().start()
    out_ref[...] = jnp.zeros_like(out_ref)

    def take(step):
        source = lax.rem(v - step + nv, nv)

        @pl.when(step > 0)
        def _():
            row_copy(step).wait()

        block, index = got[source], ids_ref[source]

        def piece(j):
            hot = (index - j * part == iota((nb * cap, part), 1)).astype(FL).astype(BF)
            out_ref[:, lanes(j * part, part)] += nn(block, hot)

        each(0, rows // part, piece)

    if first:
        quarter = nv // 4
        each(0, quarter, take)
        layer.reduce(2)
        layer.scatter(0)
        each(quarter, 2 * quarter, take)
        layer.reduce(3)
        layer.scatter(1)
        if split:
            for step in range(1, nb):
                quarter_copy(step).start()
        each(2 * quarter, 3 * quarter, take)
        layer.collect(2)
        each(3 * quarter, nv, take)
        layer.collect(3)
        for w in (0, 1):
            layer.reduce(w)
        for w in (0, 1):
            layer.collect(w)
        layer.finish()
        if split:
            quarter_keep().wait()
            for step in range(1, nb):
                quarter_copy(step).wait()
    else:
        each(0, nv, take)


def unembed(nb, nv, cap, width, rows, grad, ids, place, grads=(), quarter=None):
    part = chunk_of(rows, 640)
    count = nb * cap
    dma = pltpu.SemaphoreType.DMA
    scratch = [
        pltpu.VMEM((nb, width, SEQ_LEN), BF),
        pltpu.VMEM((nb, width, SEQ_LEN), BF),
        pltpu.VMEM((nv, width, count), BF),
        pltpu.VMEM((nv, width, count), BF),
        dma((nb,)), dma((nb,)), dma((nv,)), dma((nv,)),
    ]
    first, split = len(grads) > 0, quarter is not None
    if split:
        scratch = [dma((nb,)), dma((nb,)), dma((1,))] + scratch
    if first:
        scratch += gradient_scratch(nb, nv, grads)
    outs = [SD((width, rows), FL)] + [SD((item.shape[0] // nb, item.shape[1]), BF) for item in grads]
    extra = [quarter] if split else []
    if split:
        outs.append(SD((width, nb * quarter.shape[1]), BF))
    return run(
        functools.partial(unembed_kernel, nb, nv, cap, part, first, split),
        outs,
        scratch,
        [grad, ids, place, *grads, *extra],
        "unembed" if first else "unembed_more",
        2 if first else 4,
        in_specs=[VM] * 3 + [HB] * (len(grads) + len(extra)),
        out_specs=[VM] + [HB] * (len(grads) + len(extra)),
    )


def later_slots(nv, cap, rows, every, turn):
    nb = every.shape[0]
    v = lax.axis_index("vocab")
    local = every - v * rows
    mine = (local >= 0) & (local < rows)
    rank = jnp.cumsum(mine.astype(I32), axis=-1) - 1 - turn * cap
    hot = (rank[:, :, None, :] == jnp.arange(cap)[None, None, :, None]) & mine[:, :, None, :]
    ids = jnp.sum(jnp.where(hot, local[:, :, None, :], 0), axis=-1)
    return jnp.transpose(ids, (1, 0, 2)).reshape(nv, nb * cap, 1)


def standard(value):
    centre = value - jnp.mean(value, axis=-1, keepdims=True)
    spread = jnp.mean(centre * centre, axis=-1, keepdims=True)
    scale = lax.rsqrt(spread + NORM_EPS)
    return centre * scale, scale


def norm_back(unit, scale, gain, upstream):
    inner = upstream * gain
    first = jnp.mean(inner, axis=-1, keepdims=True)
    second = jnp.mean(inner * unit, axis=-1, keepdims=True)
    grad = scale * (inner - first - unit * second)
    return grad, jnp.sum(upstream * unit, axis=0, keepdims=True), jnp.sum(upstream, axis=0, keepdims=True)


def head_lanes(value, head):
    lane = iota(value.shape, 1)
    keep = (lane < HD) if head == 0 else (lane >= HD)
    return jnp.where(keep, value, jnp.zeros_like(value))


def visible_keys(seg_ref, pos_ref):
    position = pos_ref[...]
    block = position // BLK
    marks = [seg_ref[:, i * BLK : i * BLK + 1] for i in range(SEQ_LEN // BLK)]
    segment = jnp.zeros_like(position)
    for i, mark in enumerate(marks):
        segment = jnp.where(block == i, mark, segment)
    row = iota((BLK, PICKS), 0)
    parts = [jnp.broadcast_to(segment == slot + 1, (NB, PICKS)) for slot in range(SLOTS)]
    parts += [(segment == mark) & (row + i * BLK <= position) for i, mark in enumerate(marks)]
    return parts


def masked(visible, scores):
    return jnp.concatenate(
        [jnp.where(keep, scores[i * BLK : (i + 1) * BLK, :], NEG_BIG) for i, keep in enumerate(visible)], axis=0
    )


def memory_weights(segments, slot):
    length = segments.shape[1]
    inside = (segments == slot).astype(FL)
    start = jnp.sum((segments < slot).astype(FL), axis=1, keepdims=True)
    count = jnp.sum(inside, axis=1, keepdims=True)
    times = (iota((1, length), 1).astype(FL) - start + 0.5) / jnp.maximum(count, 1.0)
    centres = (iota((NB, 1), 0).astype(FL) + 0.5) / NB
    offset = (times - centres) * NB
    basis = jnp.exp(-0.5 * offset * offset) * inside
    total = jnp.sum(basis, axis=1, keepdims=True) + (count == 0.0).astype(FL)
    return basis / total


def attend_kernel(
    x_ref, a_ref, seg_ref, pos_ref,
    hall_ref, kv_ref, q_ref, hq_ref, xq_ref, o_ref, lse_ref, norm_ref, mixt_ref,
):
    norm_ref[...] = a_ref[:, 3 * D : 3 * D + 128].astype(FL).T[:8, :]
    gain, bias = norm_ref[0:1, :], norm_ref[3:4, :]

    def normalize(i):
        unit, _ = standard(x_ref[pl.ds(i * BLK, BLK), :].astype(FL))
        hall_ref[pl.ds(SLOTS * NB + i * BLK, BLK), :] = (unit * gain + bias).astype(BF)

    each(0, SEQ_LEN // BLK, normalize)
    normed = hall_ref[SLOTS * NB :, :]
    for slot in range(SLOTS):
        mixing = memory_weights(seg_ref[...], slot).astype(BF)
        hall_ref[slot * NB : (slot + 1) * NB, :] = nn(mixing, normed).astype(BF)
        mixt_ref[:, slot * NB : (slot + 1) * NB] = mixing.T

    def project(i):
        kv_ref[pl.ds(i * BLK, BLK), :] = nn(hall_ref[pl.ds(i * BLK, BLK), :], a_ref[:, D : 3 * D]).astype(BF)

    each(0, KEYS // BLK, project)
    pick = (pos_ref[...] == iota((SEQ_LEN, PICKS), 0)).astype(FL).astype(BF).T
    hq_ref[...] = nn(pick, normed).astype(BF)
    xq_ref[...] = nn(pick, x_ref[...])
    q_ref[...] = nn(hq_ref[...], a_ref[:, :D]).astype(BF)
    visible = visible_keys(seg_ref, pos_ref)

    def attend(p):
        keys = kv_ref[:, lanes(p * PAIR, PAIR)]
        values = kv_ref[:, lanes(D + p * PAIR, PAIR)].T
        queries = q_ref[:, lanes(p * PAIR, PAIR)] * HD ** (-0.5)
        outs = []
        for head in range(2):
            scores = masked(visible, nt(keys, head_lanes(queries, head)))
            peak = jnp.max(scores, axis=0, keepdims=True)
            expo = jnp.exp(scores - peak)
            total = jnp.sum(expo, axis=0, keepdims=True)
            probs = (expo * (1.0 / total)).astype(BF)
            outs.append(nn(values[head * HD : (head + 1) * HD, :], probs))
            lse_ref[p, head : head + 1, :] = peak + jnp.log(total)
        o_ref[:, lanes(p * PAIR, PAIR)] = jnp.concatenate(outs, axis=0).T.astype(BF)

    each(0, NPAIR, attend)


def feed_kernel(xq_ref, o_ref, p_ref, u_ref, c_ref, norm_ref, x1_ref, h2_ref, z_ref, act_ref, x2_ref, f_ref):
    x1 = xq_ref[...] + nn(o_ref[...], p_ref[...])
    x1_ref[...] = x1
    unit, _ = standard(x1)
    h2 = (unit * norm_ref[1:2, :] + norm_ref[4:5, :]).astype(BF)
    h2_ref[...] = h2
    x2_ref[...] = x1

    def piece(j):
        cut = lanes(j * D, D)
        z = nn(h2, u_ref[:, cut])
        z_ref[:, cut] = z
        act = jax.nn.gelu(z, approximate=True).astype(BF)
        act_ref[:, cut] = act
        x2_ref[...] += nn(act, c_ref[pl.ds(j * D, D), :])

    each(0, FF // D, piece)
    unit, _ = standard(x2_ref[...])
    f_ref[...] = (unit * norm_ref[2:3, :] + norm_ref[5:6, :]).astype(BF)


def feed_back_kernel(
    df_ref, x2_ref, x1_ref, h2_ref, z_ref, act_ref, o_ref, p_ref, u_ref, c_ref, norm_ref,
    dc_ref, du_ref, dp_ref, dx1_ref, do_ref, dnorm_ref, dh2,
):
    unit, scale = standard(x2_ref[...])
    dx2, gain_last, bias_last = norm_back(unit, scale, norm_ref[2:3, :], df_ref[...])
    dy = dx2.astype(BF)
    dh2[...] = jnp.zeros_like(dh2)
    h2t = h2_ref[...].T

    def piece(j):
        cut = lanes(j * D, D)
        dc_ref[pl.ds(j * D, D), :] = nn(act_ref[:, cut].T, dy).astype(BF)
        dact = nt(dy, c_ref[pl.ds(j * D, D), :])
        z = z_ref[:, cut]
        k = math.sqrt(2.0 / math.pi)
        t = jnp.tanh(k * (z + 0.044715 * z * z * z))
        slope = 0.5 * (1.0 + t) + 0.5 * z * (1.0 - t * t) * (k * (1.0 + 3 * 0.044715 * z * z))
        dz = (dact * slope).astype(BF)
        du_ref[:, cut] = nn(h2t, dz).astype(BF)
        dh2[...] += nt(dz, u_ref[:, cut])

    each(0, FF // D, piece)
    unit, scale = standard(x1_ref[...])
    dx1, gain_two, bias_two = norm_back(unit, scale, norm_ref[1:2, :], dh2[...])
    dx1 = dx1 + dx2
    dx1_ref[...] = dx1
    da = dx1.astype(BF)
    dp_ref[...] = nn(o_ref[...].T, da).astype(BF)
    do_ref[...] = nt(da, p_ref[...]).astype(BF)
    zero = jnp.zeros_like(gain_last)
    dnorm_ref[...] = jnp.concatenate([zero, gain_two, gain_last, zero, bias_two, bias_last, zero, zero], axis=0)


def attend_back_kernel(
    pos_ref, do_ref, q_ref, kv_ref, lse_ref, hall_ref, hq_ref, a_ref, x_ref, dx1_ref, mixt_ref, seg_ref, row_ref,
    norm_ref, dnorm_ref, da_ref, dx_ref, dkv, dq, hallt, dh, dxin, dmem,
):
    visible = visible_keys(seg_ref, row_ref)

    def attend(p):
        cut = lanes(p * PAIR, PAIR)
        keys = kv_ref[:, cut]
        values = kv_ref[:, lanes(D + p * PAIR, PAIR)]
        turned = keys.T
        queries = q_ref[:, cut] * HD ** (-0.5)
        grads = do_ref[:, cut]
        outs = []
        dk = dv = None
        for head in range(2):
            own, grad = head_lanes(queries, head), head_lanes(grads, head)
            scores = masked(visible, nt(keys, own))
            probs = jnp.exp(scores - lse_ref[p, head : head + 1, :])
            dprobs = nt(values, grad)
            inner = jnp.sum(probs * dprobs, axis=0, keepdims=True)
            dscores = (probs * (dprobs - inner)).astype(BF)
            outs.append(nn(turned[head * HD : (head + 1) * HD, :], dscores))
            one, two = nn(dscores, own), nn(probs.astype(BF), grad)
            dk = one if head == 0 else dk + one
            dv = two if head == 0 else dv + two
        dq[:, cut] = (jnp.concatenate(outs, axis=0).T * HD ** (-0.5)).astype(BF)
        dkv[:, cut] = dk.astype(BF)
        dkv[:, lanes(D + p * PAIR, PAIR)] = dv.astype(BF)

    each(0, NPAIR, attend)
    da_ref[:, :D] = nn(hq_ref[...].T, dq[...]).astype(BF)

    def turn(i):
        hallt[:, lanes(i * BLK, BLK)] = hall_ref[pl.ds(i * BLK, BLK), :].T

    each(0, KEYS // BLK, turn)

    def weights(j):
        cut = lanes(j * BLK, BLK)
        da_ref[:, lanes(D + j * BLK, BLK)] = nn(hallt[...], dkv[:, cut]).astype(BF)

    each(0, 2 * D // BLK, weights)

    def memory(i):
        cut = pl.ds(i * BLK, BLK)
        dmem[cut, :] = nt(dkv[cut, :], a_ref[:, D : 3 * D]).astype(BF)

    each(0, SLOTS, memory)

    def local(i):
        cut = pl.ds(i * BLK, BLK)
        dh[cut, :] = nt(dkv[pl.ds(SLOTS * NB + i * BLK, BLK), :], a_ref[:, D : 3 * D]) + nn(mixt_ref[cut, :], dmem[...])

    each(0, SEQ_LEN // BLK, local)
    dxin[:PICKS, :] = nt(dq[...], a_ref[:, :D])

    def scatter_query(k):
        row = pl.ds(pos_ref[k], 1)
        dh[row, :] += dxin[pl.ds(k, 1), :]

    each(0, PICKS, scatter_query)
    gain = norm_ref[0:1, :]
    da_rows = [jnp.zeros((1, D), FL), jnp.zeros((1, D), FL)]

    def finish(i, carry):
        cut = pl.ds(i * BLK, BLK)
        unit, scale = standard(x_ref[cut, :].astype(FL))
        grad, dgain, dbias = norm_back(unit, scale, gain, dh[cut, :])
        dxin[cut, :] = grad
        return carry[0] + dgain, carry[1] + dbias

    dgain, dbias = lax.fori_loop(0, SEQ_LEN // BLK, finish, tuple(da_rows))

    def scatter_rest(k):
        row = pl.ds(pos_ref[k], 1)
        dxin[row, :] += dx1_ref[pl.ds(k, 1), :]

    each(0, PICKS, scatter_rest)
    dx_ref[...] = dxin[...].astype(BF)
    line = iota((8, D), 0)
    norms = dnorm_ref[...] + jnp.where(line == 0, dgain, jnp.where(line == 3, dbias, 0.0))
    tall = jnp.concatenate([norms, jnp.zeros((EXTRA - 8, D), FL)], axis=0)
    da_ref[:, 3 * D :] = tall.T.astype(BF)


def head_kernel(
    nb, nv, part, f_ref, w_ref, live_ref, target_ref, df_ref, dw_ref, loss_ref,
    fall, expo, block, mine, stats, ft, grad_sum, coef, df, half, far_got, out,
    near_out, near_in, far_out, far_in, stat_out, stat_in, pair_out, pair_in, sum_out, sum_in, dw_sem,
):
    v = lax.axis_index("vocab")
    rows = w_ref.shape[1]
    total_rows = nv * PICKS
    core, chip, chips = lax.rem(v, 2), v // 2, nv // 2
    sibling = {"vocab": v + 1 - 2 * core}
    base = v * rows
    pieces = rows // part
    depth = min(2, pieces)
    meet((("vocab", nv),))

    def peer(step):
        return {"vocab": lax.rem(chip + step, chips) * 2 + core}

    def far_copy(step):
        return send(f_ref, fall.at[v], far_out.at[step], far_in.at[step], peer(step))

    def near_copy(step):
        slot = lax.rem(chip - step + chips, chips) * 2 + core
        return send(fall.at[slot], fall.at[slot], near_out.at[step], near_in.at[step], sibling)

    fall[v] = f_ref[...]
    near_copy(0).start()
    each(1, chips, lambda step: far_copy(step).start())

    def logits(step):
        @pl.when(step > 0)
        def _():
            far_copy(step).wait_recv()
            near_copy(step).start()

        near_copy(step).wait_recv()
        source = lax.rem(chip - step + chips, chips)
        start = pl.multiple_of(source * 2 * PICKS, 2 * PICKS)
        features = fall[pl.ds(source * 2, 2)].reshape(2 * PICKS, D)
        target = target_ref[pl.ds(start, 2 * PICKS), :] - base

        def score(j, peak):
            cut = lanes(j * part, part)
            value = nn(features, w_ref[:, cut])
            block[:, cut] = value
            return jnp.maximum(
                peak, jnp.max(jnp.where(live_ref[0:1, cut] > 0, value, NEG_BIG), axis=1, keepdims=True)
            )

        peak = lax.fori_loop(0, pieces, score, jnp.full((2 * PICKS, 1), NEG_BIG, FL))

        def count(j, carry):
            total, picked, valid = carry
            cut = lanes(j * part, part)
            value = block[:, cut]
            live = live_ref[0:1, cut] > 0
            hot = target - j * part == iota((2 * PICKS, part), 1)
            e = jnp.where(live, jnp.exp(value - peak), 0.0)
            expo[pl.ds(start, 2 * PICKS), cut] = e.astype(BF)
            total = total + jnp.sum(e, axis=1, keepdims=True)
            picked = picked + jnp.sum(jnp.where(hot, value, 0.0), axis=1, keepdims=True)
            valid = valid + jnp.sum(jnp.where(hot & live, 1.0, 0.0), axis=1, keepdims=True)
            return total, picked, valid

        zero = jnp.zeros((2 * PICKS, 1), FL)
        total, picked, valid = lax.fori_loop(0, pieces, count, (zero, zero, zero))
        lane = iota((2 * PICKS, 128), 1)
        wide = jnp.where(lane == 0, peak, jnp.where(lane == 1, total, jnp.where(lane == 2, picked, valid)))
        mine[:, pl.ds(start, 2 * PICKS)] = wide.T[:8, :]

    each(0, chips, logits)

    def stat_copy(step):
        return send(mine, stats.at[v], stat_out.at[step], stat_in.at[step], {"vocab": lax.rem(v + step, nv)})

    each(1, nv, lambda step: stat_copy(step).start())
    stats[v] = mine[...]
    for i in range(total_rows // 256 if pieces > 1 else 0):
        ft[:, i * 256 : (i + 1) * 256] = fall[2 * i : 2 * i + 2].reshape(256, D).T
    each(1, nv, lambda step: stat_copy(step).wait())
    start = jnp.full((1, total_rows), NEG_BIG, FL)
    peak = lax.fori_loop(0, nv, lambda u, top: jnp.maximum(top, stats[u, 0:1, :]), start)

    def combine(u, carry):
        scale = jnp.exp(stats[u, 0:1, :] - peak)
        return (
            carry[0] + stats[u, 1:2, :] * scale, carry[1] + stats[u, 2:3, :], carry[2] + stats[u, 3:4, :],
        )

    zero = jnp.zeros((1, total_rows), FL)
    total, picked, valid = lax.fori_loop(0, nv, combine, (zero, zero, zero))
    lse = peak + jnp.log(jnp.maximum(total, 1e-37))
    weight = valid / (jnp.maximum(jnp.sum(valid, axis=1, keepdims=True), 1.0) * nb)
    loss = jnp.sum(weight * (lse - picked), axis=1, keepdims=True)
    loss_ref[...] = jnp.broadcast_to(loss, loss_ref.shape)
    alpha = weight * jnp.exp(mine[0:1, :] - lse)
    line = iota((128, 256), 0)
    for i in range(total_rows // 256):
        cut = slice(i * 256, (i + 1) * 256)
        coef[cut, :] = jnp.where(line == 0, alpha[:, cut], weight[:, cut]).T

    tall = min(total_rows, 1024 if pieces > 1 else 256)
    shards_tall = tall // PICKS
    df[...] = jnp.zeros_like(df)

    def out_copy(j):
        return pltpu.make_async_copy(
            out.at[lax.rem(j, depth)], dw_ref.at[:, lanes(j * part, part)], dw_sem.at[lax.rem(j, depth)]
        )

    def gradients(j):
        cut = lanes(j * part, part)
        words = w_ref[:, cut]

        @pl.when(j >= depth)
        def _():
            out_copy(j - depth).wait()

        def strip(t):
            start = t * tall if total_rows == tall else pl.multiple_of(t * tall, tall)
            here = pl.ds(start, tall)
            hot = target_ref[here, :] - base - j * part == iota((tall, part), 1)
            two = coef[here, :]
            value = two[:, 0:1] * expo[here, cut].astype(FL) - jnp.where(hot, two[:, 1:2], 0.0)
            dlogits = value.astype(BF)
            df[here, :] += nt(dlogits, words)
            if pieces > 1:
                turned = ft[:, pl.ds(start, tall)]
            else:
                turned = fall[pl.ds(t * shards_tall, shards_tall)].reshape(tall, D).T
            for r in range(0, D, D // 3):
                more = nn(turned[r : r + D // 3, :], dlogits)
                if total_rows == tall:
                    out[lax.rem(j, depth), r : r + D // 3, :] = more.astype(BF)
                else:
                    grad_sum[r : r + D // 3, :] += more

        if total_rows == tall:
            strip(0)
        else:
            grad_sum[...] = jnp.zeros_like(grad_sum)
            each(0, total_rows // tall, strip)
            for r in range(0, D, D // 3):
                out[lax.rem(j, depth), r : r + D // 3, :] = grad_sum[r : r + D // 3, :].astype(BF)
        out_copy(j).start()

    each(0, pieces, gradients)

    def shard(index):
        return pl.ds(pl.multiple_of(index * PICKS, PICKS), PICKS)

    def pair_copy(k):
        source = df.at[shard(2 * k + 1 - core), :] if pieces > 1 else fall.at[k]
        return send(source, half.at[k], pair_out.at[k], pair_in.at[k], sibling)

    near_copy(0).wait_send()

    def drain(step):
        far_copy(step).wait_send()
        near_copy(step).wait_send()

    each(1, chips, drain)

    def swap(k):
        if pieces == 1:
            fall[k] = df[shard(2 * k + 1 - core), :].astype(BF)
        pair_copy(k).start()

    each(0, chips, swap)

    def sum_copy(step):
        return send(fall.at[chips + step], far_got.at[step], sum_out.at[step], sum_in.at[step], peer(step))

    def pass_on(turn):
        step = lax.rem(turn, chips)
        k = lax.rem(chip + step, chips)
        pair_copy(k).wait()
        value = df[shard(2 * k + core), :] + half[k].astype(FL)

        @pl.when(step > 0)
        def _():
            fall[chips + step] = value.astype(BF)
            sum_copy(step).start()

        @pl.when(step == 0)
        def _():
            df_ref[...] = value

    each(1, chips + 1, pass_on)

    def collect(step):
        sum_copy(step).wait()
        df_ref[...] += far_got[step].astype(FL)

    each(1, chips, collect)
    for j in range(pieces - depth, pieces):
        out_copy(j).wait()


def head(nb, nv, features, words, live, targets):
    rows = words.shape[1]
    part = chunk_of(rows, 640)
    total_rows = nv * PICKS
    chips = nv // 2
    dma = pltpu.SemaphoreType.DMA
    scratch = [
        pltpu.VMEM((nv, PICKS, D), BF),
        pltpu.VMEM((total_rows, rows), BF),
        pltpu.VMEM((2 * PICKS, rows), FL),
        pltpu.VMEM((8, total_rows), FL),
        pltpu.VMEM((nv, 8, total_rows), FL),
        pltpu.VMEM((D, total_rows) if rows > part else (8, 128), BF),
        pltpu.VMEM((8, 128) if rows > part else (D, part), FL),
        pltpu.VMEM((total_rows, 128), FL),
        pltpu.VMEM((total_rows, D), FL),
        pltpu.VMEM((chips, PICKS, D), FL if rows > part else BF),
        pltpu.VMEM((chips, PICKS, D), BF),
        pltpu.VMEM((min(2, rows // part), D, part), BF),
        dma((chips,)), dma((chips,)), dma((chips,)), dma((chips,)), dma((nv,)), dma((nv,)),
        dma((chips,)), dma((chips,)), dma((chips,)), dma((chips,)), dma((2,)),
    ]
    return run(
        functools.partial(head_kernel, nb, nv, part),
        [SD((PICKS, D), FL), SD((D, rows), BF), SD((8, 128), FL)],
        scratch,
        [features, words, live, targets],
        "head",
        1,
        out_specs=[VM, HB, VM],
    )


def wide_head_kernel(
    nb, nv, block_rows, f_ref, w_ref, live_ref, target_ref, df_ref, dw_ref, loss_ref,
    fall, ft, expo, words_sum, mine, first_got, merged, second_got, tile, third_got, tiles, coef, group, half, handed, mix_got,
    far_sum, far_got,
    z_out, z_in, mix_out, mix_in, near_out, near_in, s_out, s_in, pair_out, pair_in, give_out, give_in, sum_out, sum_in,
):
    b, v = lax.axis_index("batch"), lax.axis_index("vocab")
    rows = w_ref.shape[1]
    core, chip, chips = lax.rem(v, 2), v // 2, nv // 2
    sibling = {"vocab": v + 1 - 2 * core}
    base = v * block_rows + b * rows
    live = live_ref[:, lanes(b * rows, rows)] > 0
    span = nv * PICKS
    meet((("batch", nb), ("vocab", nv)))

    def peer(step):
        return {"vocab": lax.rem(chip + step, chips) * 2 + core}

    def other(step):
        return {"batch": lax.rem(b + step, nb)}

    def slot(s, k):
        return lax.rem(b - s + nb, nb) * nv + lax.rem(chip - k + chips, chips) * 2 + core

    def z_copy(k):
        return send(f_ref, fall.at[b * nv + v], z_out.at[k], z_in.at[k], peer(k))

    def mix_copy(s, k):
        place = fall.at[slot(0, k)]
        return send(place, place, mix_out.at[k, s], mix_in.at[k, s], other(s))

    def near_copy(s, k):
        place = fall.at[slot(s, k)]
        return send(place, place, near_out.at[k, s], near_in.at[k, s], sibling)

    def arrive(s, k):
        if s == 0:

            @pl.when(k > 0)
            def _():
                z_copy(k).wait_recv()

            each(1, nb, lambda t: mix_copy(t, k).start())
        else:
            mix_copy(s, k).wait_recv()
        near_copy(s, k).start()

    fall[b * nv + v] = f_ref[...]
    each(1, chips, lambda k: z_copy(k).start())
    arrive(0, 0)

    def logits(s, k):
        near_copy(s, k).wait_recv()
        p, c = lax.rem(b - s + nb, nb), lax.rem(chip - k + chips, chips)
        first = p * nv + c * 2
        start = pl.multiple_of(first * PICKS, 2 * PICKS)
        features = fall[pl.ds(first, 2)].reshape(2 * PICKS, D)
        ft[:, pl.ds(start, 2 * PICKS)] = features.T
        line = target_ref[p, :, pl.ds(pl.multiple_of(c * 2 * PICKS, 2 * PICKS), 2 * PICKS)].astype(FL)
        target = jnp.broadcast_to(line, (128, 2 * PICKS)).T[:, 0:1].astype(I32) - base
        value = nn(features, w_ref[...])
        peak = jnp.max(jnp.where(live, value, NEG_BIG), axis=1, keepdims=True)
        hot = target == iota((2 * PICKS, rows), 1)
        e = jnp.where(live, jnp.exp(value - peak), 0.0)
        expo[pl.ds(start, 2 * PICKS), :] = e.astype(BF)
        total = jnp.sum(e, axis=1, keepdims=True)
        picked = jnp.sum(jnp.where(hot, value, 0.0), axis=1, keepdims=True)
        valid = jnp.sum(jnp.where(hot & live, 1.0, 0.0), axis=1, keepdims=True)
        lane = iota((2 * PICKS, 128), 1)
        wide = jnp.where(lane == 0, peak, jnp.where(lane == 1, total, jnp.where(lane == 2, picked, valid))).T
        mine[c * 2, p] = wide[:8, :PICKS]
        mine[c * 2 + 1, p] = wide[:8, PICKS:]

    for s in range(nb):

        def one(k, s=s):
            @pl.when(k + 1 < chips)
            def _():
                arrive(s, k + 1)

            if s + 1 < nb:

                @pl.when(k + 1 == chips)
                def _():
                    arrive(s + 1, 0)

            logits(s, k)

        each(0, chips, one)

    def merge(read, count):
        peak = lax.fori_loop(
            0, count, lambda u, top: jnp.maximum(top, read(u)[0:1, :]), jnp.full((1, PICKS), NEG_BIG, FL)
        )

        def add(u, carry):
            one = read(u)
            return carry[0] + one[1:2, :] * jnp.exp(one[0:1, :] - peak), carry[1] + one[2:3, :], carry[2] + one[3:4, :]

        zero = jnp.zeros((1, PICKS), FL)
        return (peak, *lax.fori_loop(0, count, add, (zero, zero, zero)))

    def tile_of(rows_of):
        line = iota((8, PICKS), 0)
        value = jnp.zeros((8, PICKS), FL)
        for i, row in enumerate(rows_of):
            value = jnp.where(line == i, row, value)
        return value

    def first_copy(t):
        u = lax.rem(v + t, nv)
        return send(mine.at[u], first_got.at[v], s_out.at[0, t], s_in.at[0, t], {"vocab": u})

    each(1, nv, lambda t: first_copy(t).start())
    first_got[v] = mine[v]
    each(1, nv, lambda t: first_copy(t).wait())
    for p in range(nb):
        merged[p] = tile_of(merge(lambda u, p=p: first_got[u, p], nv))

    def second_copy(t):
        return send(merged.at[lax.rem(b + t, nb)], second_got.at[b], s_out.at[1, t], s_in.at[1, t], other(t))

    each(1, nb, lambda t: second_copy(t).start())
    second_got[b] = merged[b]
    each(1, nb, lambda t: second_copy(t).wait())
    peak, total, picked, valid = merge(lambda u: second_got[u], nb)
    tile[...] = tile_of((peak + jnp.log(jnp.maximum(total, 1e-37)), picked, valid))

    def third_copy(t):
        return send(tile, third_got.at[b], s_out.at[2, t], s_in.at[2, t], other(t))

    each(1, nb, lambda t: third_copy(t).start())
    third_got[b] = tile[...]
    each(1, nb, lambda t: third_copy(t).wait())

    def last_copy(t):
        return send(third_got, tiles.at[v], s_out.at[3, t], s_in.at[3, t], {"vocab": lax.rem(v + t, nv)})

    each(1, nv, lambda t: last_copy(t).start())
    tiles[v] = third_got[...]
    each(1, nv, lambda t: last_copy(t).wait())

    def coefficients(p):
        count = lax.fori_loop(0, nv, lambda u, total: total + tiles[u, p, 2:3, :], jnp.zeros((1, PICKS), FL))
        share = 1.0 / (jnp.maximum(jnp.sum(count, axis=1, keepdims=True), 1.0) * nb)

        def spread(c, loss):
            rows_of = []
            for side in range(2):
                u = c * 2 + side
                lse, picked, valid = (tiles[u, p, i : i + 1, :] for i in range(3))
                weight = valid * share
                loss = loss + weight * (lse - picked)
                rows_of.append((weight * jnp.exp(mine[u, p, 0:1, :] - lse), weight))
            line = iota((128, 2 * PICKS), 0)
            alpha = jnp.concatenate([rows_of[0][0], rows_of[1][0]], axis=1)
            weight = jnp.concatenate([rows_of[0][1], rows_of[1][1]], axis=1)
            start = pl.multiple_of(p * span + c * 2 * PICKS, 2 * PICKS)
            coef[pl.ds(start, 2 * PICKS), :] = jnp.where(line == 0, alpha, weight).T
            return loss

        loss = lax.fori_loop(0, chips, spread, jnp.zeros((1, PICKS), FL))

        @pl.when(p == b)
        def _():
            loss_ref[...] = jnp.broadcast_to(jnp.sum(loss, axis=1, keepdims=True), loss_ref.shape)

    each(0, nb, coefficients)

    def shard(k, side):
        return pl.ds(pl.multiple_of((2 * k + side) * PICKS, PICKS), PICKS)

    def pair_copy(s, k):
        return send(handed.at[s, k], half.at[s, k], pair_out.at[s, k], pair_in.at[s, k], sibling)

    def give_copy(s):
        return send(handed.at[s], mix_got.at[s], give_out.at[s], give_in.at[s], other(s))

    def exchange(s):
        def add(k):
            pair_copy(s, k).wait()
            handed[s, k] = (group[shard(k, core), :] + half[s, k].astype(FL)).astype(BF)

        each(0, chips, add)
        if s > 0:
            give_copy(s).start()

    for s in list(range(1, nb)) + [0]:
        p = lax.rem(b + s, nb)

        def strip(c, p=p):
            start = pl.multiple_of(p * span + c * 2 * PICKS, 2 * PICKS)
            here = pl.ds(start, 2 * PICKS)
            line = target_ref[p, :, pl.ds(pl.multiple_of(c * 2 * PICKS, 2 * PICKS), 2 * PICKS)].astype(FL)
            target = jnp.broadcast_to(line, (128, 2 * PICKS)).T[:, 0:1].astype(I32) - base
            two = coef[here, :]
            hot = target == iota((2 * PICKS, rows), 1)
            value = two[:, 0:1] * expo[here, :].astype(FL) - jnp.where(hot, two[:, 1:2], 0.0)
            expo[here, :] = value.astype(BF)

        each(0, chips, strip)
        def features_grad(i, p=p):
            here = pl.ds(pl.multiple_of(i * 512, 512), 512)
            group[here, :] = nt(expo[pl.ds(pl.multiple_of(p * span + i * 512, 512), 512), :], w_ref[...])

        each(0, span // 512, features_grad)

        def swap(k, s=s):
            handed[s, k] = group[shard(k, 1 - core), :].astype(BF)
            pair_copy(s, k).start()

        each(0, chips, swap)
        exchange(s)

    words_sum[...] = jnp.zeros_like(words_sum)

    def words_grad(i):
        cut = lanes(i * 512, 512)
        words_sum[...] += nn(ft[:, cut], expo[cut, :])

    each(0, nb * span // 512, words_grad)
    dw_ref[...] = words_sum[...].astype(BF)

    for s in range(1, nb):
        give_copy(s).wait()

    def total_of(k):
        value = handed[0, k].astype(FL)
        for s in range(1, nb):
            value = value + mix_got[s, k].astype(FL)
        return value

    def sum_copy(t):
        return send(far_sum.at[t], far_got.at[t], sum_out.at[t], sum_in.at[t], peer(t))

    def pass_on(t):
        far_sum[t] = total_of(lax.rem(chip + t, chips)).astype(BF)
        sum_copy(t).start()

    each(1, chips, pass_on)
    df_ref[...] = total_of(chip)

    def collect(t):
        sum_copy(t).wait()
        df_ref[...] += far_got[t].astype(FL)

    each(1, chips, collect)
    each(1, chips, lambda k: z_copy(k).wait_send())
    for s in range(nb):
        each(0, chips, lambda k, s=s: near_copy(s, k).wait_send())
        if s > 0:
            each(0, chips, lambda k, s=s: mix_copy(s, k).wait_send())


def wide_head(nb, nv, block_rows, features, words, live, targets):
    rows = words.shape[1]
    tokens = nb * nv * PICKS
    chips = nv // 2
    dma = pltpu.SemaphoreType.DMA
    most = max(nb, nv)
    scratch = [
        pltpu.VMEM((nb * nv, PICKS, D), BF),
        pltpu.VMEM((D, tokens), BF),
        pltpu.VMEM((tokens, rows), BF),
        pltpu.VMEM((D, rows), FL),
        pltpu.VMEM((nv, nb, 8, PICKS), FL),
        pltpu.VMEM((nv, nb, 8, PICKS), FL),
        pltpu.VMEM((nb, 8, PICKS), FL),
        pltpu.VMEM((nb, 8, PICKS), FL),
        pltpu.VMEM((8, PICKS), FL),
        pltpu.VMEM((nb, 8, PICKS), FL),
        pltpu.VMEM((nv, nb, 8, PICKS), FL),
        pltpu.VMEM((tokens, 128), FL),
        pltpu.VMEM((nv * PICKS, D), FL),
        pltpu.VMEM((nb, chips, PICKS, D), BF),
        pltpu.VMEM((nb, chips, PICKS, D), BF),
        pltpu.VMEM((nb, chips, PICKS, D), BF),
        pltpu.VMEM((chips, PICKS, D), BF),
        pltpu.VMEM((chips, PICKS, D), BF),
        dma((chips,)), dma((chips,)), dma((chips, nb)), dma((chips, nb)), dma((chips, nb)), dma((chips, nb)),
        dma((4, most)), dma((4, most)), dma((nb, chips)), dma((nb, chips)), dma((nb,)), dma((nb,)),
        dma((chips,)), dma((chips,)),
    ]
    return run(
        functools.partial(wide_head_kernel, nb, nv, block_rows),
        [SD((PICKS, D), FL), SD((D, rows), BF), SD((8, 128), FL)],
        scratch,
        [features, words, live, targets],
        "wide_head",
        1,
    )


def norm_kernel(
    nb, nv, extra_ref, dw_ref, a_ref, p_ref, u_ref, c_ref, loss_ref, out_ref,
    mine, near, lines, vocab_out, vocab_in, batch_out, batch_in,
):
    b, v = lax.axis_index("batch"), lax.axis_index("vocab")
    meet((("batch", nb), ("vocab", nv)))

    def squares(refs, part):
        cols = refs[0].shape[1]

        def add(j, total):
            value = refs[0][:, lanes(j * part, part)].astype(FL)
            for ref in refs[1:]:
                value = value + ref[:, lanes(j * part, part)].astype(FL)
            return total + jnp.sum(value * value, axis=0, keepdims=True)

        line = lax.fori_loop(0, cols // part, add, jnp.zeros((1, part), FL))
        return jnp.sum(line, axis=1, keepdims=True)

    own = squares((extra_ref, dw_ref), chunk_of(extra_ref.shape[1], 640))
    layer = squares((a_ref,), 512) + squares((p_ref,), 384) + squares((u_ref,), 512) + squares((c_ref,), 384)
    own = own + jnp.where(v == 0, layer, jnp.zeros_like(layer))
    line = iota((8, 128), 0)
    mine[...] = jnp.where(line == 0, own, jnp.where((line == 1) & (v == 0), loss_ref[...], 0.0))

    def vocab_copy(step):
        return send(mine, near.at[v], vocab_out.at[step], vocab_in.at[step], {"vocab": lax.rem(v + step, nv)})

    each(1, nv, lambda step: vocab_copy(step).start())
    near[v] = mine[...]
    each(1, nv, lambda step: vocab_copy(step).wait())
    mine[...] = lax.fori_loop(0, nv, lambda u, total: total + near[u], jnp.zeros((8, 128), FL))

    def batch_copy(step):
        return send(mine, lines.at[b], batch_out.at[step], batch_in.at[step], {"batch": lax.rem(b + step, nb)})

    each(1, nb, lambda step: batch_copy(step).start())
    lines[b] = mine[...]
    each(1, nb, lambda step: batch_copy(step).wait())
    out_ref[...] = lax.fori_loop(0, nb, lambda u, total: total + lines[u], jnp.zeros((8, 128), FL))


def norm(nb, nv, extra, dw, sums, loss):
    dma = pltpu.SemaphoreType.DMA
    return run(
        functools.partial(norm_kernel, nb, nv),
        [SD((8, 128), FL)],
        [
            pltpu.VMEM((8, 128), FL), pltpu.VMEM((nv, 8, 128), FL), pltpu.VMEM((nb, 8, 128), FL),
            dma((nv,)), dma((nv,)), dma((nb,)), dma((nb,)),
        ],
        [extra, dw, *sums, loss],
        "norm",
        5,
    )[0]


def adamw(weight, moment, square, gradient, clip, count, decay, rate):
    gradient = gradient * clip
    moment = BETA_ONE * moment + (1 - BETA_ONE) * gradient
    square = BETA_TWO * square + (1 - BETA_TWO) * gradient * gradient
    fixed_moment = moment / (1 - BETA_ONE**count)
    fixed_square = square / (1 - BETA_TWO**count)
    weight = weight - rate * (fixed_moment / (jnp.sqrt(fixed_square) + ADAM_EPS) + decay * weight)
    return (weight, moment, square)


def slot_size(nv):
    mean = SEQ_LEN // nv
    return -(-(mean + int(5.5 * math.sqrt(mean))) // 32) * 32


def shards(
    nb, nv,
    tokens, targets, segments, counted, vocab_mask, step_count,
    table, table_moment, table_square,
    attend, attend_moment, attend_square,
    project, project_moment, project_square,
    expand, expand_moment, expand_square,
    contract, contract_moment, contract_square,
    gain, gain_moment, gain_square,
    shift, shift_moment, shift_square,
):
    rows, width = table.shape
    cap = slot_size(nv)
    table_t = table.T
    norms = jnp.concatenate([gain, shift], axis=0)
    packed = jnp.concatenate([attend[0], norms.T, jnp.zeros((width, EXTRA - 6), FL)], axis=1).astype(BF)
    pieces = (packed, project[0].astype(BF), expand[0].astype(BF), contract[0].astype(BF))
    split = nb * nv * PICKS <= 4096
    rounded = table_t.astype(BF)
    quarter = -(-rows // (nb * 128)) * 128
    if split:
        rounded = jnp.pad(rounded, ((0, 0), (0, nb * quarter - rows)))
    else:
        words = lax.all_gather(rounded, "batch", axis=0, tiled=True)

    seg_row, pos_row = segments[None, :], counted[None, :]
    tok = tokens.reshape(nv, SEQ_LEN)
    x, ids, place, most, every, a_all, p_all, u_all, c_all, *rest = embed(
        nb, nv, cap, rows, jnp.zeros((1,), I32), tok, rounded, pieces, targets[None, :] if split else None
    )
    turns = (most[0, 0].astype(I32) + cap - 1) // cap

    def more_rows(state):
        turn, total = state
        return turn + 1, total + embed(nb, nv, cap, rows, turn[None], tok, rounded)[0]

    x = lax.while_loop(lambda state: state[0] < turns, more_rows, (jnp.int32(1), x))[1]

    hall, kv, q, hq, xq, mixed, lse, norm_rows, mixing_t = run(
        attend_kernel,
        [
            SD((KEYS, D), BF), SD((KEYS, 2 * D), BF), SD((PICKS, D), BF), SD((PICKS, D), BF), SD((PICKS, D), FL),
            SD((PICKS, D), BF), SD((NPAIR, 2, PICKS), FL), SD((8, D), FL), SD((SEQ_LEN, SLOTS * NB), BF),
        ],
        [],
        [x, a_all, seg_row, pos_row],
        "attend", flops=7 * 10**9, moved=20 * 10**6,
    )
    x1, h2, z, act, x2, features = run(
        feed_kernel,
        [
            SD((PICKS, D), FL), SD((PICKS, D), BF), SD((PICKS, FF), FL), SD((PICKS, FF), BF), SD((PICKS, D), FL),
            SD((PICKS, D), BF),
        ],
        [],
        [xq, mixed, p_all, u_all, c_all, norm_rows],
        "feed", flops=2 * 10**9, moved=15 * 10**6,
    )
    if split:
        live = jnp.pad(vocab_mask, (0, nb * quarter - rows))[None, :]
        df, dw, loss_block = wide_head(nb, nv, rows, features, rest[0], live, rest[1])
    else:
        df, dw, loss_block = head(nb, nv, features, words, vocab_mask[None, :], targets[:, None])
        dw_sum = lax.psum_scatter(dw, "batch", scatter_dimension=0, tiled=True)

    dc, du, dp, dx1, dmixed, dnorm = run(
        feed_back_kernel,
        [
            SD((FF, D), BF), SD((D, FF), BF), SD((D, D), BF), SD((PICKS, D), FL), SD((PICKS, D), BF), SD((8, D), FL),
        ],
        [pltpu.VMEM((PICKS, D), FL)],
        [df, x2, x1, h2, z, act, mixed, p_all, u_all, c_all, norm_rows],
        "feed_back", flops=4 * 10**9, moved=30 * 10**6,
    )
    da, dx = run(
        attend_back_kernel,
        [SD((D, 3 * D + EXTRA), BF), SD((SEQ_LEN, D), BF)],
        [
            pltpu.VMEM((KEYS, 2 * D), BF), pltpu.VMEM((PICKS, D), BF), pltpu.VMEM((D, KEYS), BF),
            pltpu.VMEM((SEQ_LEN, D), FL), pltpu.VMEM((SEQ_LEN, D), FL), pltpu.VMEM((SLOTS * NB, D), BF),
        ],
        [counted, dmixed, q, kv, lse, hall, hq, a_all, x, dx1, mixing_t, seg_row, pos_row, norm_rows, dnorm],
        "attend_back", flops=12 * 10**9, moved=25 * 10**6,
        in_specs=[SM] + [VM] * 14,
    )
    extra, *sums = unembed(nb, nv, cap, width, rows, dx, ids, place, (da, dp, du, dc), dw if split else None)
    if split:
        dw_sum = sums.pop()

    def more_grads(state):
        turn, total = state
        later = later_slots(nv, cap, rows, every, turn)
        return turn + 1, total + unembed(
            nb, nv, cap, width, rows, dx, later, place - jnp.array([0, 1, 0, 0, 0, 0, 0, 0], I32)[None, :, None] * (turn * cap)
        )[0]

    extra = lax.while_loop(lambda state: state[0] < turns, more_grads, (jnp.int32(1), extra))[1]

    totals = norm(nb, nv, extra, dw_sum, sums, loss_block)
    grad_table = dw_sum[:, :rows].astype(FL) + extra
    grad_a, grad_p, grad_u, grad_c = (item.astype(FL) for item in sums)
    grad_norms = grad_a[:, 3 * D : 3 * D + 6].T
    grad_a = grad_a[:, : 3 * D]
    squares, loss = totals[0, 0], totals[1, 0]
    gradient_norm = jnp.sqrt(squares)
    clip = jnp.minimum(1.0, MAX_NORM / (gradient_norm + 1e-06))
    count = step_count[0].astype(FL)

    def update(weight, moment, square, gradient, decay=DECAY, rate=LEARN_RATE):
        return adamw(weight, moment, square, gradient, clip, count, decay, rate)

    table_out = [item.T for item in update(table_t, table_moment.T, table_square.T, grad_table)]
    attend_out = update(attend, attend_moment, attend_square, grad_a[None])
    project_out = update(project, project_moment, project_square, grad_p[None])
    expand_out = update(expand, expand_moment, expand_square, grad_u[None])
    contract_out = update(contract, contract_moment, contract_square, grad_c[None])
    gain_out = update(gain, gain_moment, gain_square, grad_norms[:3], 0.0, NORM_RATE)
    shift_out = update(shift, shift_moment, shift_square, grad_norms[3:], 0.0, NORM_RATE)
    return (
        loss, gradient_norm, *table_out, *attend_out, *project_out, *expand_out, *contract_out, *gain_out, *shift_out,
    )


def solution(mesh):
    nb, nv = mesh.shape["batch"], mesh.shape["vocab"]
    both, split, middle, last = P(("batch", "vocab")), P("vocab", "batch"), P(None, "batch", None), P(None, "batch")
    state = (split,) * 3 + (middle,) * 12 + (last,) * 6
    return jax.shard_map(
        functools.partial(shards, nb, nv),
        mesh=mesh,
        in_specs=(P("batch"), P("batch"), both, both, P("vocab"), P()) + state,
        out_specs=(P(), P()) + state,
        check_vma=False,
    )
```

```python
import functools
import math

import jax
import jax.numpy as jnp
from jax import lax
from jax.experimental import pallas as pl
from jax.experimental.pallas import tpu as pltpu
from jax.sharding import PartitionSpec as P

D = 768
H = 12
HD = 64
FF = 3072
NB = 256
SEG_BLOCKS = 4
SLOTS = SEG_BLOCKS - 2
SEQ_LEN = 1024
PICKS = 128
KEYS = SLOTS * NB + SEQ_LEN
BLK = 256
PAIR = 2 * HD
NPAIR = H // 2
EXTRA = 256
WIDE = (3 * D + EXTRA, D, FF, D)

NORM_EPS = 1e-05
MAX_NORM = 0.02
LEARN_RATE = 0.04
NORM_RATE = 0.5
BETA_ONE = 0.9
BETA_TWO = 0.999
ADAM_EPS = 1e-08
DECAY = 0.1
NEG_BIG = -1e30
BF = jnp.bfloat16
FL = jnp.float32
I32 = jnp.int32
MESH = pl.DeviceIdType.MESH
SD = jax.ShapeDtypeStruct
VM = pl.BlockSpec(memory_space=pltpu.VMEM)
SM = pl.BlockSpec(memory_space=pltpu.SMEM)
HB = pl.BlockSpec(memory_space=pl.ANY)
LIMIT = 62 * 2**20


def nn(a, b):
    return lax.dot_general(a, b, (((1,), (0,)), ((), ())), preferred_element_type=FL)


def nt(a, b):
    return lax.dot_general(a, b, (((1,), (1,)), ((), ())), preferred_element_type=FL)


def iota(shape, axis):
    return lax.broadcasted_iota(I32, shape, axis)


def lanes(start, size):
    return pl.ds(pl.multiple_of(start, 128), size)


def chunk_of(rows, want):
    return want if rows % want == 0 else rows


def run(kernel, outs, scratch, ins, name, collective=None, flops=0, moved=0, out_specs=None, in_specs=None):
    return pl.pallas_call(
        kernel,
        out_shape=outs,
        in_specs=in_specs if in_specs is not None else [VM] * len(ins),
        out_specs=out_specs if out_specs is not None else [VM] * len(outs),
        scratch_shapes=scratch,
        compiler_params=pltpu.CompilerParams(
            vmem_limit_bytes=LIMIT,
            collective_id=collective,
            has_side_effects=collective is not None,
        ),
        cost_estimate=pl.CostEstimate(flops=flops, bytes_accessed=moved, transcendentals=0),
        name=name,
    )(*ins)


def send(source, target, out_sem, in_sem, device):
    return pltpu.make_async_remote_copy(
        src_ref=source, dst_ref=target, send_sem=out_sem, recv_sem=in_sem, device_id=device, device_id_type=MESH
    )


def meet(axes):
    barrier = pltpu.get_barrier_semaphore()
    count = 0
    for axis, size in axes:
        me = lax.axis_index(axis)

        def greet(step, carry, axis=axis, size=size, me=me):
            pl.semaphore_signal(barrier, inc=1, device_id={axis: lax.rem(me + step, size)}, device_id_type=MESH)
            return carry

        lax.fori_loop(1, size, greet, 0)
        count += size - 1
    pl.semaphore_wait(barrier, count)


def each(start, stop, body):
    def step(index, carry):
        body(index)
        return carry

    lax.fori_loop(start, stop, step, 0)


def embed_kernel(
    nb, nv, cap, part, rows, first, split, *refs
):
    round_ref, tok_ref, words = refs[:3]
    shards, refs = (refs[3:5], refs[5:]) if first else ((), refs[3:])
    target_ref, refs = (refs[0], refs[1:]) if split else (None, refs)
    x_ref, ids_ref, place_ref, most_ref, tok_ref_all = refs[:5]
    wholes, refs = (refs[5:7], refs[7:]) if first else ((), refs[5:])
    (quarter_ref, target_all), refs = (refs[:2], refs[2:]) if split else ((None, None), refs)
    before, ranks, work, sent, got, spread, mixed, turned = refs[:8]
    tok_out, tok_in, row_out, row_in, mix_out, mix_in = refs[8:14]
    b, v = lax.axis_index("batch"), lax.axis_index("vocab")
    width = words.shape[0]
    shift = round_ref[0] * cap
    meet((("batch", nb), ("vocab", nv)))
    gather = WeightGather(nb, shards, wholes, *refs[14:19]) if first else None
    quarter_out, quarter_in, quarter_own, target_out, target_in = refs[19:24] if split else [None] * 5

    def tok_copy(step):
        return send(
            tok_ref, tok_ref_all.at[b], tok_out.at[step], tok_in.at[step], {"batch": lax.rem(b + step, nb)}
        )

    for step in range(1, nb):
        tok_copy(step).start()

    def target_copy(step):
        return send(
            target_ref, target_all.at[b], target_out.at[step], target_in.at[step], {"batch": lax.rem(b + step, nb)}
        )

    def quarter(owner):
        return words.at[:, lanes(owner * (words.shape[1] // nb), words.shape[1] // nb)]

    def quarter_copy(step):
        other = lax.rem(b + step, nb)
        place = quarter_ref.at[pl.ds(pl.multiple_of(b * width, 16), width), :]
        return send(quarter(other), place, quarter_out.at[step], quarter_in.at[step], {"batch": other})

    def quarter_keep():
        place = quarter_ref.at[pl.ds(pl.multiple_of(b * width, 16), width), :]
        return pltpu.make_async_copy(quarter(b), place, quarter_own.at[0])

    if split:
        target_all[b] = target_ref[...]
        for step in range(1, nb):
            target_copy(step).start()
    if first:
        gather.start()
    if split:
        quarter_keep().start()
    tok_ref_all[b] = tok_ref[...]
    before[...] = (iota((SEQ_LEN, SEQ_LEN), 0) < iota((SEQ_LEN, SEQ_LEN), 1)).astype(FL).astype(BF)
    for step in range(1, nb):
        tok_copy(step).wait()

    base = v * rows
    most = jnp.zeros((nv, 1), FL)
    for p in range(nb):
        ids = tok_ref_all[p]
        mine = (ids >= base) & (ids < base + rows)
        rank = nn(mine.astype(FL).astype(BF), before[...])
        ranks[p] = jnp.where(mine, rank.astype(I32) - shift, -1)
        for owner in range(nv):
            theirs = (ids >= owner * rows) & (ids < (owner + 1) * rows)
            most = jnp.maximum(most, jnp.sum(theirs.astype(FL), axis=1, keepdims=True))
    most_ref[0] = jnp.max(most).astype(I32)

    def row_copy(step):
        return send(
            sent.at[step], got.at[v], row_out.at[step], row_in.at[step], {"vocab": lax.rem(v + step, nv)}
        )

    def build(turn):
        step = lax.rem(turn, nv)
        dest = lax.rem(v + step, nv)
        found = []
        for p in range(nb):
            pick = (iota((cap, SEQ_LEN), 0) == ranks[p, pl.ds(dest, 1), :]).astype(FL).astype(BF)
            local = tok_ref_all[p, pl.ds(dest, 1), :] - base
            line = iota((8, SEQ_LEN), 0)
            high, low = lax.shift_right_arithmetic(local, 7), lax.bitwise_and(local, 127)
            digits = jnp.where(line == 0, high, jnp.where(line == 1, low, 0)).astype(FL).astype(BF)
            both = nt(pick, digits)
            found.append((both[:, 0:1] * 128.0 + both[:, 1:2]).astype(I32))
        index = jnp.concatenate(found, axis=0)
        ids_ref[dest] = index
        work[...] = jnp.zeros_like(work)

        def piece(j):
            hot = (index - j * part == iota((nb * cap, part), 1)).astype(FL).astype(BF)
            work[...] += nt(hot, words[:, lanes(j * part, part)])

        each(0, rows // part, piece)
        block = work[...].T.astype(BF)

        @pl.when(step > 0)
        def _():
            sent[step] = block
            row_copy(step).start()

        @pl.when(step == 0)
        def _():
            got[v] = block

    each(1, nv // 2 + 1, build)
    if first:
        gather.pass_on()
    if split:
        for step in range(1, nb):
            quarter_copy(step).start()
    each(nv // 2 + 1, nv + 1, build)

    keys = []
    for p in range(nb):
        ids = tok_ref_all[p, pl.ds(v, 1), :]
        owner = iota((nv, SEQ_LEN), 0)
        theirs = (ids >= owner * rows) & (ids < (owner + 1) * rows)
        rank = nn(theirs.astype(FL).astype(BF), before[...])
        place = jnp.sum(jnp.where(theirs, rank, 0.0), axis=0, keepdims=True).astype(I32) - shift
        holder = jnp.sum(jnp.where(theirs, owner.astype(FL), 0.0), axis=0, keepdims=True).astype(I32)
        line = iota((8, SEQ_LEN), 0)
        place_ref[p] = jnp.where(line == 0, holder, jnp.where(line == 1, place, 0))
        keys.append((holder, place))
        spread[p] = jnp.zeros((width, SEQ_LEN), FL)

    def take(turn):
        step = lax.rem(turn, nv)
        source = lax.rem(v - step + nv, nv)

        @pl.when(step > 0)
        def _():
            row_copy(step).wait()

        block = got[source]
        for p in range(nb):
            holder, place = keys[p]
            key = jnp.where(holder == source, place, -1)
            hot = (iota((cap, SEQ_LEN), 0) == key).astype(FL).astype(BF)
            spread[p] += nn(block[:, p * cap : (p + 1) * cap], hot)

    each(1, nv + 1, take)

    def mix_copy(step):
        return send(
            mixed.at[step], turned.at[b], mix_out.at[step], mix_in.at[step], {"batch": lax.rem(b + step, nb)}
        )

    for step in range(1, nb):
        mixed[step] = spread[lax.rem(b + step, nb)].astype(BF)
        mix_copy(step).start()
    turned[b] = spread[b].astype(BF)
    for step in range(1, nb):
        mix_copy(step).wait()
    x_ref[...] = turned[...].reshape(nb * width, SEQ_LEN).T
    if first:
        gather.finish()
    if split:
        quarter_keep().wait()
        for step in range(1, nb):
            target_copy(step).wait()
            quarter_copy(step).wait()


def weight_semaphores(count):
    return [pltpu.SemaphoreType.DMA((count,))] + [pltpu.SemaphoreType.DMA((count, 4))] * 4


class WeightGather:
    def __init__(self, nb, shards, wholes, own_sem, out_sem, in_sem, pair_out, pair_in):
        self.nb, self.shards, self.wholes = nb, shards, wholes
        self.own_sem, self.out_sem, self.in_sem, self.pair_out, self.pair_in = own_sem, out_sem, in_sem, pair_out, pair_in
        self.b, v = lax.axis_index("batch"), lax.axis_index("vocab")
        self.core = lax.rem(v, 2)
        self.sibling = {"vocab": v + 1 - 2 * self.core}

    def flip(self, bits):
        b = self.b
        low, high = lax.rem(b, 2), b // 2
        return (high if bits < 2 else 1 - high) * 2 + (low if bits % 2 == 0 else 1 - low)

    def place(self, w, owner, top, size):
        rows, cols = self.shards[w].shape
        first = pl.multiple_of(owner * rows + top, 16)
        return self.wholes[w].at[pl.ds(first, size), lanes(self.core * (cols // 2), cols // 2)]

    def routes(self, w):
        rows = self.shards[w].shape[0]
        if self.nb == 4:
            half = rows // 2
            return [
                (self.b, 0, rows, self.flip(1), self.flip(1)),
                (self.b, 0, rows, self.flip(2), self.flip(2)),
                (self.flip(1), 0, half, self.flip(2), self.flip(3)),
                (self.flip(2), half, half, self.flip(1), self.flip(3)),
            ]
        others = [lax.rem(self.b + step, self.nb) for step in range(1, self.nb)]
        came = [lax.rem(self.b - step + self.nb, self.nb) for step in range(1, self.nb)]
        return [(self.b, 0, rows, other, source) for other, source in zip(others, came)]

    def own_copy(self, w):
        rows = self.shards[w].shape[0]
        first = pl.multiple_of(self.b * rows, 16)
        return pltpu.make_async_copy(self.shards[w], self.wholes[w].at[pl.ds(first, rows), :], self.own_sem.at[w])

    def copy(self, w, k):
        owner, top, size, device, _ = self.routes(w)[k]
        cols = self.shards[w].shape[1]
        if self.nb == 4 and k >= 2:
            source = self.place(w, owner, top, size)
        else:
            source = self.shards[w].at[:, lanes(self.core * (cols // 2), cols // 2)]
        target = self.place(w, owner, top, size)
        return send(source, target, self.out_sem.at[w, k], self.in_sem.at[w, k], {"batch": device})

    def pair(self, w, k):
        _, top, size, _, arrived = self.routes(w)[k]
        ref = self.place(w, arrived, top, size)
        return send(ref, ref, self.pair_out.at[w, k], self.pair_in.at[w, k], self.sibling)

    def start(self):
        for w in range(len(self.shards)):
            for k in range(2 if self.nb == 4 else self.nb - 1):
                self.copy(w, k).start()
        for w in range(len(self.shards)):
            self.own_copy(w).start()

    def pass_on(self):
        if self.nb != 4:
            return
        for w in range(len(self.shards)):
            for k in range(2):
                self.copy(w, k).wait_recv()
                self.copy(w, k + 2).start()
                self.pair(w, k).start()

    def finish(self):
        for w in range(len(self.shards)):
            for k in range(2 if self.nb == 4 else 0, len(self.routes(w))):
                self.copy(w, k).wait_recv()
                self.pair(w, k).start()
        for w in range(len(self.shards)):
            self.own_copy(w).wait()
            for k in range(len(self.routes(w))):
                self.copy(w, k).wait_send()
                self.pair(w, k).wait()


def embed(nb, nv, cap, rows, turn, tok, table, shards=(), targets=None):
    width = table.shape[0]
    split = targets is not None
    part = chunk_of(rows, 640)
    count = nb * cap
    outs = [
        SD((SEQ_LEN, D), BF),
        SD((nv, count, 1), I32),
        SD((nb, 8, SEQ_LEN), I32),
        SD((1,), I32),
        SD((nb, nv, SEQ_LEN), I32),
    ]
    first = len(shards) > 0
    outs += [SD((nb * item.shape[0], item.shape[1]), BF) for item in shards]
    if split:
        outs += [SD((D, table.shape[1] // nb), BF), SD((nb, *targets.shape), I32)]
    dma = pltpu.SemaphoreType.DMA
    scratch = [
        pltpu.VMEM((SEQ_LEN, SEQ_LEN), BF),
        pltpu.VMEM((nb, nv, SEQ_LEN), I32),
        pltpu.VMEM((count, width), FL),
        pltpu.VMEM((nv, width, count), BF),
        pltpu.VMEM((nv, width, count), BF),
        pltpu.VMEM((nb, width, SEQ_LEN), FL),
        pltpu.VMEM((nb, width, SEQ_LEN), BF),
        pltpu.VMEM((nb, width, SEQ_LEN), BF),
        dma((nb,)), dma((nb,)), dma((nv,)), dma((nv,)), dma((nb,)), dma((nb,)),
    ]
    if first:
        scratch += weight_semaphores(len(shards))
    if split:
        scratch += [dma((nb,)), dma((nb,)), dma((1,)), dma((nb,)), dma((nb,))]
    extra = [targets] if split else []
    return run(
        functools.partial(embed_kernel, nb, nv, cap, part, rows, first, split), outs, scratch,
        [turn, tok, table, *shards, *extra],
        "embed" if first else "embed_more", 0 if first else 3,
        in_specs=[SM, VM, VM] + [HB] * len(shards) + [VM] * len(extra),
        out_specs=[VM] * 3 + [SM, VM] + [HB] * len(shards) + ([HB, VM] if split else []),
    )


class GradientSum:
    def __init__(self, nb, nv, grads, refs, totals=None, sums=None):
        self.nb, self.nv, self.grads, self.sums = nb, nv, grads, sums
        self.todo = [w for w, item in enumerate(grads) if item is not None]
        take = iter(refs)
        spread = lambda keys: {w: next(take) for w in keys}
        everything = range(len(grads))
        self.own, self.near, self.shard = spread(self.todo), spread(self.todo), spread(self.todo)
        if sums is not None:
            self.total = spread(self.todo)
            self.total.update(totals)
            self.bits, self.result = spread(everything), spread(everything)
        else:
            self.total = totals
        self.load_sem, self.pair_out, self.pair_in, self.mix_out, self.mix_in = (next(take) for _ in range(5))
        if sums is not None:
            (self.cut_out, self.cut_in, self.all_out, self.all_in, self.last_out, self.last_in,
             self.store_sem) = take
        self.b, v = lax.axis_index("batch"), lax.axis_index("vocab")
        self.core, self.chip, self.chips = lax.rem(v, 2), v // 2, nv // 2
        self.sibling = {"vocab": v + 1 - 2 * self.core}

    def half(self, w, core):
        cols = self.total[w].shape[1]
        return lanes(core * cols, cols)

    def load(self, w):
        return pltpu.make_async_copy(self.grads[w].at[:, self.half(w, self.core)], self.own[w], self.load_sem.at[w])

    def pair(self, w):
        source = self.grads[w].at[:, self.half(w, 1 - self.core)]
        return send(source, self.near[w], self.pair_out.at[w], self.pair_in.at[w], self.sibling)

    def start(self):
        for w in sorted(self.todo, reverse=True):
            self.pair(w).start()
            self.load(w).start()

    def mix(self, w, step):
        other = lax.rem(self.b + step, self.nb)
        rows = self.own[w].shape[0] // self.nb
        source = self.own[w].at[pl.ds(pl.multiple_of(other * rows, 16), rows), :]
        return send(source, self.shard[w].at[step], self.mix_out.at[w, step], self.mix_in.at[w, step], {"batch": other})

    def scatter(self, w):
        self.load(w).wait()
        self.pair(w).wait()
        rows = self.own[w].shape[0] // self.nb

        def add(i, w=w, rows=rows):
            cut = pl.ds(pl.multiple_of(i * rows, 16), rows)
            self.own[w][cut, :] = (self.own[w][cut, :].astype(FL) + self.near[w][cut, :].astype(FL)).astype(BF)

        each(0, self.nb, add)
        for step in range(1, self.nb):
            self.mix(w, step).start()

    def pieces(self, w):
        rows = self.total[w].shape[0]
        count = max(n for n in range(1, self.chips + 1) if rows % (16 * n) == 0)
        return count, rows // count

    def peer(self, step):
        other = lax.rem(self.chip + step, self.chips)
        return other, {"vocab": other * 2 + self.core}

    def cut(self, w, step):
        other, device = self.peer(step)
        size = self.pieces(w)[1]
        source = self.total[w].at[pl.ds(pl.multiple_of(other * size, 16), size), :]
        return send(source, self.bits[w].at[step], self.cut_out.at[w, step], self.cut_in.at[w, step], device)

    def back(self, w, step):
        size = self.pieces(w)[1]
        place = self.result[w].at[pl.ds(pl.multiple_of(self.chip * size, 16), size), :]
        return send(place, place, self.all_out.at[w, step], self.all_in.at[w, step], self.peer(step)[1])

    def back_recv(self, w, step):
        source = lax.rem(self.chip - step + self.chips, self.chips)
        size = self.pieces(w)[1]
        place = self.result[w].at[pl.ds(pl.multiple_of(source * size, 16), size), :]
        return send(place, place, self.all_out.at[w, step], self.all_in.at[w, step], self.peer(step)[1])

    def gather(self, w):
        rows = self.total[w].shape[0]
        for step in range(1, self.nb):
            self.mix(w, step).wait()
        here = pl.ds(pl.multiple_of(self.b * rows, 16), rows)
        value = self.own[w][here, :].astype(FL)
        for step in range(1, self.nb):
            value = value + self.shard[w][step].astype(FL)
        self.total[w][...] = value.astype(BF)

    def reduce(self, w):
        if w in self.todo:
            self.gather(w)
        count = self.pieces(w)[0]

        def go(step):
            @pl.when(self.peer(step)[0] < count)
            def _():
                self.cut(w, step).start()

        each(1, self.chips, go)

    def collect(self, w):
        count, size = self.pieces(w)
        mine = pl.ds(pl.multiple_of(self.chip * size, 16), size)

        @pl.when(self.chip < count)
        def _(w=w, mine=mine):
            def add(step, value):
                self.cut(w, step).wait_recv()
                return value + self.bits[w][step].astype(FL)

            value = lax.fori_loop(1, self.chips, add, self.total[w][mine, :].astype(FL))
            self.result[w][mine, :] = value.astype(BF)
            each(1, self.chips, lambda step: self.back(w, step).start())

        def sent(step, w=w, count=count):
            @pl.when(self.peer(step)[0] < count)
            def _():
                self.cut(w, step).wait_send()

        each(1, self.chips, sent)

    def last(self, w):
        return send(
            self.result[w], self.sums[w].at[:, self.half(w, self.core)], self.last_out.at[w], self.last_in.at[w], self.sibling
        )

    def store(self, w):
        return pltpu.make_async_copy(self.result[w], self.sums[w].at[:, self.half(w, self.core)], self.store_sem.at[w])

    def finish(self):
        for w in range(4):
            count = self.pieces(w)[0]

            def got(step, w=w, count=count):
                @pl.when(lax.rem(self.chip - step + self.chips, self.chips) < count)
                def _():
                    self.back_recv(w, step).wait_recv()

            each(1, self.chips, got)
            self.last(w).start()
            self.store(w).start()
        for w in range(4):
            count = self.pieces(w)[0]

            @pl.when(self.chip < count)
            def _(w=w):
                each(1, self.chips, lambda step: self.back(w, step).wait_send())

            self.store(w).wait()
            self.last(w).wait_send()
            other = self.sums[w].at[:, self.half(w, 1 - self.core)]
            send(other, other, self.last_out.at[w], self.last_in.at[w], self.sibling).wait_recv()


def gradient_scratch(nb, nv, shapes, todo, whole=True):
    chips = nv // 2
    halves = [(rows, cols // 2) for rows, cols in shapes]
    shards = [(rows // nb, cols) for rows, cols in halves]
    sizes = [rows // max(n for n in range(1, chips + 1) if rows % (16 * n) == 0) for rows, _ in shards]
    dma = pltpu.SemaphoreType.DMA
    count = len(shapes)
    refs = [pltpu.VMEM(halves[w], BF) for w in todo] * 2 + [pltpu.VMEM((nb, *shards[w]), BF) for w in todo]
    if whole:
        refs += [pltpu.VMEM(shards[w], BF) for w in todo]
        refs += [pltpu.VMEM((chips, size, item[1]), BF) for size, item in zip(sizes, shards)]
        refs += [pltpu.VMEM(item, BF) for item in shards]
    refs += [dma((count,)), dma((count,)), dma((count,)), dma((count, nb)), dma((count, nb))]
    if whole:
        refs += [dma((count, chips))] * 4 + [dma((count,))] * 3
    return refs


def unembed_kernel(nb, nv, cap, part, first, split, *refs):
    x_ref, ids_ref, place_ref = refs[:3]
    grads, refs = (refs[3:7], refs[7:]) if first else ((), refs[3:])
    if first:
        totals, grads = {2: grads[2]}, (grads[0], grads[1], None, grads[3])
    quarter_ref, refs = (refs[0], refs[1:]) if split else (None, refs)
    out_ref = refs[0]
    sums, refs = (refs[1:5], refs[5:]) if first else ((), refs[1:])
    dw_ref, refs = (refs[0], refs[1:]) if split else (None, refs)
    (quarter_out, quarter_in, quarter_own), refs = (refs[:3], refs[3:]) if split else ([None] * 3, refs)
    turned, parts, sent, got, mix_out, mix_in, row_out, row_in = refs[:8]
    layer = GradientSum(nb, nv, grads, refs[8:], totals, sums) if first else None
    b, v = lax.axis_index("batch"), lax.axis_index("vocab")
    width, rows = out_ref.shape
    meet((("batch", nb), ("vocab", nv)))
    turned[...] = x_ref[...].T.reshape(nb, width, SEQ_LEN)

    def mix_copy(step):
        other = lax.rem(b + step, nb)
        return send(turned.at[other], parts.at[b], mix_out.at[step], mix_in.at[step], {"batch": other})

    for step in range(1, nb):
        mix_copy(step).start()
    if first:
        layer.start()
        layer.reduce(2)
    parts[b] = turned[b]
    for step in range(1, nb):
        mix_copy(step).wait()

    def quarter_place():
        size = quarter_ref.shape[1]
        return dw_ref.at[:, lanes(b * size, size)]

    def quarter_copy(step):
        other = lax.rem(b + step, nb)
        source = quarter_ref.at[pl.ds(pl.multiple_of(other * width, 16), width), :]
        return send(source, quarter_place(), quarter_out.at[step], quarter_in.at[step], {"batch": other})

    def quarter_keep():
        source = quarter_ref.at[pl.ds(pl.multiple_of(b * width, 16), width), :]
        return pltpu.make_async_copy(source, quarter_place(), quarter_own.at[0])

    def row_copy(step):
        return send(
            sent.at[step], got.at[v], row_out.at[step], row_in.at[step], {"vocab": lax.rem(v + step, nv)}
        )

    def build(turn):
        step = lax.rem(turn, nv)
        owner = lax.rem(v + step, nv)
        blocks = []
        for p in range(nb):
            key = jnp.where(place_ref[p, 0:1, :] == owner, place_ref[p, 1:2, :], -1)
            hot = (iota((cap, SEQ_LEN), 0) == key).astype(FL).astype(BF)
            blocks.append(nt(parts[p], hot).astype(BF))
        block = jnp.concatenate(blocks, axis=1)

        @pl.when(step > 0)
        def _():
            sent[step] = block
            row_copy(step).start()

        @pl.when(step == 0)
        def _():
            got[v] = block

    if first:
        layer.scatter(3)
    each(1, nv // 2 + 1, build)
    if first:
        layer.collect(2)
    each(nv // 2 + 1, nv + 1, build)
    if first:
        layer.scatter(0)
    if split:
        quarter_keep().start()
    out_ref[...] = jnp.zeros_like(out_ref)

    def take(step):
        source = lax.rem(v - step + nv, nv)

        @pl.when(step > 0)
        def _():
            row_copy(step).wait()

        block, index = got[source], ids_ref[source]

        def piece(j):
            hot = (index - j * part == iota((nb * cap, part), 1)).astype(FL).astype(BF)
            out_ref[:, lanes(j * part, part)] += nn(block, hot)

        each(0, rows // part, piece)

    if first:
        quarter = nv // 4
        each(0, quarter, take)
        layer.reduce(3)
        layer.scatter(1)
        if split:
            for step in range(1, nb):
                quarter_copy(step).start()
        each(quarter, 2 * quarter, take)
        layer.reduce(0)
        each(2 * quarter, 3 * quarter, take)
        layer.collect(3)
        layer.reduce(1)
        each(3 * quarter, nv, take)
        layer.collect(0)
        layer.collect(1)
        layer.finish()
        if split:
            quarter_keep().wait()
            for step in range(1, nb):
                quarter_copy(step).wait()
    else:
        each(0, nv, take)


def unembed(nb, nv, cap, width, rows, grad, ids, place, grads=(), quarter=None):
    part = chunk_of(rows, 640)
    count = nb * cap
    dma = pltpu.SemaphoreType.DMA
    scratch = [
        pltpu.VMEM((nb, width, SEQ_LEN), BF),
        pltpu.VMEM((nb, width, SEQ_LEN), BF),
        pltpu.VMEM((nv, width, count), BF),
        pltpu.VMEM((nv, width, count), BF),
        dma((nb,)), dma((nb,)), dma((nv,)), dma((nv,)),
    ]
    first, split = len(grads) > 0, quarter is not None
    if split:
        scratch = [dma((nb,)), dma((nb,)), dma((1,))] + scratch
    if first:
        shapes = [item.shape if w != 2 else (nb * item.shape[0], 2 * item.shape[1]) for w, item in enumerate(grads)]
        scratch += gradient_scratch(nb, nv, shapes, (0, 1, 3))
    outs = [SD((width, rows), FL)] + [SD((item[0] // nb, item[1]), BF) for item in (shapes if first else ())]
    extra = [quarter] if split else []
    if split:
        outs.append(SD((width, nb * quarter.shape[1]), BF))
    return run(
        functools.partial(unembed_kernel, nb, nv, cap, part, first, split),
        outs,
        scratch,
        [grad, ids, place, *grads, *extra],
        "unembed" if first else "unembed_more",
        2 if first else 4,
        in_specs=[VM] * 3 + ([HB, HB, VM, HB] if first else []) + [HB] * len(extra),
        out_specs=[VM] + [HB] * (len(grads) + len(extra)),
    )


def later_slots(nv, cap, rows, every, turn):
    nb = every.shape[0]
    v = lax.axis_index("vocab")
    local = every - v * rows
    mine = (local >= 0) & (local < rows)
    rank = jnp.cumsum(mine.astype(I32), axis=-1) - 1 - turn * cap
    hot = (rank[:, :, None, :] == jnp.arange(cap)[None, None, :, None]) & mine[:, :, None, :]
    ids = jnp.sum(jnp.where(hot, local[:, :, None, :], 0), axis=-1)
    return jnp.transpose(ids, (1, 0, 2)).reshape(nv, nb * cap, 1)


def standard(value):
    centre = value - jnp.mean(value, axis=-1, keepdims=True)
    spread = jnp.mean(centre * centre, axis=-1, keepdims=True)
    scale = lax.rsqrt(spread + NORM_EPS)
    return centre * scale, scale


def norm_back(unit, scale, gain, upstream):
    inner = upstream * gain
    first = jnp.mean(inner, axis=-1, keepdims=True)
    second = jnp.mean(inner * unit, axis=-1, keepdims=True)
    grad = scale * (inner - first - unit * second)
    return grad, jnp.sum(upstream * unit, axis=0, keepdims=True), jnp.sum(upstream, axis=0, keepdims=True)


def head_lanes(value, head):
    lane = iota(value.shape, 1)
    keep = (lane < HD) if head == 0 else (lane >= HD)
    return jnp.where(keep, value, jnp.zeros_like(value))


def visible_keys(seg_ref, pos_ref):
    position = pos_ref[...]
    block = position // BLK
    marks = [seg_ref[:, i * BLK : i * BLK + 1] for i in range(SEQ_LEN // BLK)]
    segment = jnp.zeros_like(position)
    for i, mark in enumerate(marks):
        segment = jnp.where(block == i, mark, segment)
    row = iota((BLK, PICKS), 0)
    parts = [jnp.broadcast_to(segment == slot + 1, (NB, PICKS)) for slot in range(SLOTS)]
    parts += [(segment == mark) & (row + i * BLK <= position) for i, mark in enumerate(marks)]
    return parts


def masked(visible, scores):
    return jnp.concatenate(
        [jnp.where(keep, scores[i * BLK : (i + 1) * BLK, :], NEG_BIG) for i, keep in enumerate(visible)], axis=0
    )


def memory_weights(segments, slot):
    length = segments.shape[1]
    inside = (segments == slot).astype(FL)
    start = jnp.sum((segments < slot).astype(FL), axis=1, keepdims=True)
    count = jnp.sum(inside, axis=1, keepdims=True)
    times = (iota((1, length), 1).astype(FL) - start + 0.5) / jnp.maximum(count, 1.0)
    centres = (iota((NB, 1), 0).astype(FL) + 0.5) / NB
    offset = (times - centres) * NB
    basis = jnp.exp(-0.5 * offset * offset) * inside
    total = jnp.sum(basis, axis=1, keepdims=True) + (count == 0.0).astype(FL)
    return basis / total


def attend_kernel(
    nb, nv, x_ref, a_ref, seg_ref, pos_ref, p_ref, c_ref,
    hall_ref, kv_ref, q_ref, hq_ref, xq_ref, o_ref, lse_ref, norm_ref, mixt_ref, p_all, c_all, *sems,
):
    meet((("batch", nb), ("vocab", nv)))
    gather = WeightGather(nb, (p_ref, c_ref), (p_all, c_all), *sems)
    gather.start()
    norm_ref[...] = a_ref[:, 3 * D : 3 * D + 128].astype(FL).T[:8, :]
    gain, bias = norm_ref[0:1, :], norm_ref[3:4, :]

    def normalize(i):
        unit, _ = standard(x_ref[pl.ds(i * BLK, BLK), :].astype(FL))
        hall_ref[pl.ds(SLOTS * NB + i * BLK, BLK), :] = (unit * gain + bias).astype(BF)

    each(0, SEQ_LEN // BLK, normalize)
    normed = hall_ref[SLOTS * NB :, :]
    for slot in range(SLOTS):
        mixing = memory_weights(seg_ref[...], slot).astype(BF)
        hall_ref[slot * NB : (slot + 1) * NB, :] = nn(mixing, normed).astype(BF)
        mixt_ref[:, slot * NB : (slot + 1) * NB] = mixing.T

    def project(i):
        kv_ref[pl.ds(i * BLK, BLK), :] = nn(hall_ref[pl.ds(i * BLK, BLK), :], a_ref[:, D : 3 * D]).astype(BF)

    each(0, KEYS // BLK, project)
    pick = (pos_ref[...] == iota((SEQ_LEN, PICKS), 0)).astype(FL).astype(BF).T
    hq_ref[...] = nn(pick, normed).astype(BF)
    xq_ref[...] = nn(pick, x_ref[...])
    q_ref[...] = nn(hq_ref[...], a_ref[:, :D]).astype(BF)
    visible = visible_keys(seg_ref, pos_ref)

    def attend(p):
        keys = kv_ref[:, lanes(p * PAIR, PAIR)]
        values = kv_ref[:, lanes(D + p * PAIR, PAIR)].T
        queries = q_ref[:, lanes(p * PAIR, PAIR)] * HD ** (-0.5)
        outs = []
        for head in range(2):
            scores = masked(visible, nt(keys, head_lanes(queries, head)))
            peak = jnp.max(scores, axis=0, keepdims=True)
            expo = jnp.exp(scores - peak)
            total = jnp.sum(expo, axis=0, keepdims=True)
            probs = (expo * (1.0 / total)).astype(BF)
            outs.append(nn(values[head * HD : (head + 1) * HD, :], probs))
            lse_ref[p, head : head + 1, :] = peak + jnp.log(total)
        o_ref[:, lanes(p * PAIR, PAIR)] = jnp.concatenate(outs, axis=0).T.astype(BF)

    gather.pass_on()
    each(0, NPAIR, attend)
    gather.finish()


def feed_kernel(xq_ref, o_ref, p_ref, u_ref, c_ref, norm_ref, x1_ref, h2_ref, z_ref, act_ref, x2_ref, f_ref):
    x1 = xq_ref[...] + nn(o_ref[...], p_ref[...])
    x1_ref[...] = x1
    unit, _ = standard(x1)
    h2 = (unit * norm_ref[1:2, :] + norm_ref[4:5, :]).astype(BF)
    h2_ref[...] = h2
    x2_ref[...] = x1

    def piece(j):
        cut = lanes(j * D, D)
        z = nn(h2, u_ref[:, cut])
        z_ref[:, cut] = z
        act = jax.nn.gelu(z, approximate=True).astype(BF)
        act_ref[:, cut] = act
        x2_ref[...] += nn(act, c_ref[pl.ds(j * D, D), :])

    each(0, FF // D, piece)
    unit, _ = standard(x2_ref[...])
    f_ref[...] = (unit * norm_ref[2:3, :] + norm_ref[5:6, :]).astype(BF)


def feed_back_kernel(
    df_ref, x2_ref, x1_ref, h2_ref, z_ref, act_ref, o_ref, p_ref, u_ref, c_ref, norm_ref,
    dc_ref, du_ref, dp_ref, dx1_ref, do_ref, dnorm_ref, dh2,
):
    unit, scale = standard(x2_ref[...])
    dx2, gain_last, bias_last = norm_back(unit, scale, norm_ref[2:3, :], df_ref[...])
    dy = dx2.astype(BF)
    dh2[...] = jnp.zeros_like(dh2)
    h2t = h2_ref[...].T

    def piece(j):
        cut = lanes(j * D, D)
        dc_ref[pl.ds(j * D, D), :] = nn(act_ref[:, cut].T, dy).astype(BF)
        dact = nt(dy, c_ref[pl.ds(j * D, D), :])
        z = z_ref[:, cut]
        k = math.sqrt(2.0 / math.pi)
        t = jnp.tanh(k * (z + 0.044715 * z * z * z))
        slope = 0.5 * (1.0 + t) + 0.5 * z * (1.0 - t * t) * (k * (1.0 + 3 * 0.044715 * z * z))
        dz = (dact * slope).astype(BF)
        du_ref[:, cut] = nn(h2t, dz).astype(BF)
        dh2[...] += nt(dz, u_ref[:, cut])

    each(0, FF // D, piece)
    unit, scale = standard(x1_ref[...])
    dx1, gain_two, bias_two = norm_back(unit, scale, norm_ref[1:2, :], dh2[...])
    dx1 = dx1 + dx2
    dx1_ref[...] = dx1
    da = dx1.astype(BF)
    dp_ref[...] = nn(o_ref[...].T, da).astype(BF)
    do_ref[...] = nt(da, p_ref[...]).astype(BF)
    zero = jnp.zeros_like(gain_last)
    dnorm_ref[...] = jnp.concatenate([zero, gain_two, gain_last, zero, bias_two, bias_last, zero, zero], axis=0)


def attend_back_kernel(
    nb, nv, do_ref, q_ref, kv_ref, lse_ref, hall_ref, hq_ref, a_ref, x_ref, dx1_ref, mixt_ref, seg_ref, row_ref,
    norm_ref, dnorm_ref, du_ref, da_ref, dx_ref, du_sum, dkv, dq, hallt, dh, dxin, dmem, sel, *refs,
):
    meet((("batch", nb), ("vocab", nv)))
    layer = GradientSum(nb, nv, (du_ref,), refs, {0: du_sum})
    layer.start()
    visible = visible_keys(seg_ref, row_ref)

    def attend(p):
        cut = lanes(p * PAIR, PAIR)
        keys = kv_ref[:, cut]
        values = kv_ref[:, lanes(D + p * PAIR, PAIR)]
        turned = keys.T
        queries = q_ref[:, cut] * HD ** (-0.5)
        grads = do_ref[:, cut]
        outs = []
        dk = dv = None
        for head in range(2):
            own, grad = head_lanes(queries, head), head_lanes(grads, head)
            scores = masked(visible, nt(keys, own))
            probs = jnp.exp(scores - lse_ref[p, head : head + 1, :])
            dprobs = nt(values, grad)
            inner = jnp.sum(probs * dprobs, axis=0, keepdims=True)
            dscores = (probs * (dprobs - inner)).astype(BF)
            outs.append(nn(turned[head * HD : (head + 1) * HD, :], dscores))
            one, two = nn(dscores, own), nn(probs.astype(BF), grad)
            dk = one if head == 0 else dk + one
            dv = two if head == 0 else dv + two
        dq[:, cut] = (jnp.concatenate(outs, axis=0).T * HD ** (-0.5)).astype(BF)
        dkv[:, cut] = dk.astype(BF)
        dkv[:, lanes(D + p * PAIR, PAIR)] = dv.astype(BF)

    each(0, NPAIR // 2, attend)
    layer.scatter(0)
    each(NPAIR // 2, NPAIR, attend)
    da_ref[:, :D] = nn(hq_ref[...].T, dq[...]).astype(BF)

    def turn(i):
        hallt[:, lanes(i * BLK, BLK)] = hall_ref[pl.ds(i * BLK, BLK), :].T

    each(0, KEYS // BLK, turn)

    def weights(j):
        cut = lanes(j * BLK, BLK)
        da_ref[:, lanes(D + j * BLK, BLK)] = nn(hallt[...], dkv[:, cut]).astype(BF)

    each(0, 2 * D // BLK, weights)

    def memory(i):
        cut = pl.ds(i * BLK, BLK)
        dmem[cut, :] = nt(dkv[cut, :], a_ref[:, D : 3 * D]).astype(BF)

    each(0, SLOTS, memory)

    def local(i):
        cut = pl.ds(i * BLK, BLK)
        dh[cut, :] = nt(dkv[pl.ds(SLOTS * NB + i * BLK, BLK), :], a_ref[:, D : 3 * D]) + nn(mixt_ref[cut, :], dmem[...])

    each(0, SEQ_LEN // BLK, local)
    put = (row_ref[...] == iota((SEQ_LEN, PICKS), 0)).astype(FL).astype(BF)

    def scatter(target, value):
        for _ in range(3):
            part = value.astype(BF)
            value = value - part.astype(FL)

            def add(i, part=part):
                cut = pl.ds(i * BLK, BLK)
                target[cut, :] += nn(sel[cut, :], part)

            each(0, SEQ_LEN // BLK, add)

    sel[...] = put
    scatter(dh, nt(dq[...], a_ref[:, :D]))
    gain = norm_ref[0:1, :]
    da_rows = [jnp.zeros((1, D), FL), jnp.zeros((1, D), FL)]

    def finish(i, carry):
        cut = pl.ds(i * BLK, BLK)
        unit, scale = standard(x_ref[cut, :].astype(FL))
        grad, dgain, dbias = norm_back(unit, scale, gain, dh[cut, :])
        dxin[cut, :] = grad
        return carry[0] + dgain, carry[1] + dbias

    dgain, dbias = lax.fori_loop(0, SEQ_LEN // BLK, finish, tuple(da_rows))

    scatter(dxin, dx1_ref[...])
    dx_ref[...] = dxin[...].astype(BF)
    line = iota((8, D), 0)
    norms = dnorm_ref[...] + jnp.where(line == 0, dgain, jnp.where(line == 3, dbias, 0.0))
    tall = jnp.concatenate([norms, jnp.zeros((EXTRA - 8, D), FL)], axis=0)
    da_ref[:, 3 * D :] = tall.T.astype(BF)
    layer.gather(0)


def head_kernel(
    nb, nv, part, f_ref, w_ref, live_ref, target_ref, df_ref, dw_ref, loss_ref,
    fall, expo, block, mine, stats, ft, grad_sum, coef, df, half, far_got, out,
    near_out, near_in, far_out, far_in, stat_out, stat_in, pair_out, pair_in, sum_out, sum_in, dw_sem,
):
    v = lax.axis_index("vocab")
    rows = w_ref.shape[1]
    total_rows = nv * PICKS
    core, chip, chips = lax.rem(v, 2), v // 2, nv // 2
    sibling = {"vocab": v + 1 - 2 * core}
    base = v * rows
    pieces = rows // part
    depth = min(2, pieces)
    meet((("vocab", nv),))

    def peer(step):
        return {"vocab": lax.rem(chip + step, chips) * 2 + core}

    def far_copy(step):
        return send(f_ref, fall.at[v], far_out.at[step], far_in.at[step], peer(step))

    def near_copy(step):
        slot = lax.rem(chip - step + chips, chips) * 2 + core
        return send(fall.at[slot], fall.at[slot], near_out.at[step], near_in.at[step], sibling)

    fall[v] = f_ref[...]
    near_copy(0).start()
    each(1, chips, lambda step: far_copy(step).start())

    def logits(step):
        @pl.when(step > 0)
        def _():
            far_copy(step).wait_recv()
            near_copy(step).start()

        near_copy(step).wait_recv()
        source = lax.rem(chip - step + chips, chips)
        start = pl.multiple_of(source * 2 * PICKS, 2 * PICKS)
        features = fall[pl.ds(source * 2, 2)].reshape(2 * PICKS, D)
        target = target_ref[pl.ds(start, 2 * PICKS), :] - base

        def score(j, peak):
            cut = lanes(j * part, part)
            value = nn(features, w_ref[:, cut])
            block[:, cut] = value
            return jnp.maximum(
                peak, jnp.max(jnp.where(live_ref[0:1, cut] > 0, value, NEG_BIG), axis=1, keepdims=True)
            )

        peak = lax.fori_loop(0, pieces, score, jnp.full((2 * PICKS, 1), NEG_BIG, FL))

        def count(j, carry):
            total, picked, valid = carry
            cut = lanes(j * part, part)
            value = block[:, cut]
            live = live_ref[0:1, cut] > 0
            hot = target - j * part == iota((2 * PICKS, part), 1)
            e = jnp.where(live, jnp.exp(value - peak), 0.0)
            expo[pl.ds(start, 2 * PICKS), cut] = e.astype(BF)
            total = total + jnp.sum(e, axis=1, keepdims=True)
            picked = picked + jnp.sum(jnp.where(hot, value, 0.0), axis=1, keepdims=True)
            valid = valid + jnp.sum(jnp.where(hot & live, 1.0, 0.0), axis=1, keepdims=True)
            return total, picked, valid

        zero = jnp.zeros((2 * PICKS, 1), FL)
        total, picked, valid = lax.fori_loop(0, pieces, count, (zero, zero, zero))
        lane = iota((2 * PICKS, 128), 1)
        wide = jnp.where(lane == 0, peak, jnp.where(lane == 1, total, jnp.where(lane == 2, picked, valid)))
        mine[:, pl.ds(start, 2 * PICKS)] = wide.T[:8, :]

    each(0, chips, logits)

    def stat_copy(step):
        return send(mine, stats.at[v], stat_out.at[step], stat_in.at[step], {"vocab": lax.rem(v + step, nv)})

    each(1, nv, lambda step: stat_copy(step).start())
    stats[v] = mine[...]
    for i in range(total_rows // 256 if pieces > 1 else 0):
        ft[:, i * 256 : (i + 1) * 256] = fall[2 * i : 2 * i + 2].reshape(256, D).T
    each(1, nv, lambda step: stat_copy(step).wait())
    start = jnp.full((1, total_rows), NEG_BIG, FL)
    peak = lax.fori_loop(0, nv, lambda u, top: jnp.maximum(top, stats[u, 0:1, :]), start)

    def combine(u, carry):
        scale = jnp.exp(stats[u, 0:1, :] - peak)
        return (
            carry[0] + stats[u, 1:2, :] * scale, carry[1] + stats[u, 2:3, :], carry[2] + stats[u, 3:4, :],
        )

    zero = jnp.zeros((1, total_rows), FL)
    total, picked, valid = lax.fori_loop(0, nv, combine, (zero, zero, zero))
    lse = peak + jnp.log(jnp.maximum(total, 1e-37))
    weight = valid / (jnp.maximum(jnp.sum(valid, axis=1, keepdims=True), 1.0) * nb)
    loss = jnp.sum(weight * (lse - picked), axis=1, keepdims=True)
    loss_ref[...] = jnp.broadcast_to(loss, loss_ref.shape)
    alpha = weight * jnp.exp(mine[0:1, :] - lse)
    line = iota((128, 256), 0)
    for i in range(total_rows // 256):
        cut = slice(i * 256, (i + 1) * 256)
        coef[cut, :] = jnp.where(line == 0, alpha[:, cut], weight[:, cut]).T

    tall = min(total_rows, 1024 if pieces > 1 else 256)
    shards_tall = tall // PICKS
    df[...] = jnp.zeros_like(df)

    def out_copy(j):
        return pltpu.make_async_copy(
            out.at[lax.rem(j, depth)], dw_ref.at[:, lanes(j * part, part)], dw_sem.at[lax.rem(j, depth)]
        )

    def gradients(j):
        cut = lanes(j * part, part)
        words = w_ref[:, cut]

        @pl.when(j >= depth)
        def _():
            out_copy(j - depth).wait()

        def strip(t):
            start = t * tall if total_rows == tall else pl.multiple_of(t * tall, tall)
            here = pl.ds(start, tall)
            hot = target_ref[here, :] - base - j * part == iota((tall, part), 1)
            two = coef[here, :]
            value = two[:, 0:1] * expo[here, cut].astype(FL) - jnp.where(hot, two[:, 1:2], 0.0)
            dlogits = value.astype(BF)
            df[here, :] += nt(dlogits, words)
            if pieces > 1:
                turned = ft[:, pl.ds(start, tall)]
            else:
                turned = fall[pl.ds(t * shards_tall, shards_tall)].reshape(tall, D).T
            for r in range(0, D, D // 3):
                more = nn(turned[r : r + D // 3, :], dlogits)
                if total_rows == tall:
                    out[lax.rem(j, depth), r : r + D // 3, :] = more.astype(BF)
                else:
                    grad_sum[r : r + D // 3, :] += more

        if total_rows == tall:
            strip(0)
        else:
            grad_sum[...] = jnp.zeros_like(grad_sum)
            each(0, total_rows // tall, strip)
            for r in range(0, D, D // 3):
                out[lax.rem(j, depth), r : r + D // 3, :] = grad_sum[r : r + D // 3, :].astype(BF)
        out_copy(j).start()

    each(0, pieces, gradients)

    def shard(index):
        return pl.ds(pl.multiple_of(index * PICKS, PICKS), PICKS)

    def pair_copy(k):
        source = df.at[shard(2 * k + 1 - core), :] if pieces > 1 else fall.at[k]
        return send(source, half.at[k], pair_out.at[k], pair_in.at[k], sibling)

    near_copy(0).wait_send()

    def drain(step):
        far_copy(step).wait_send()
        near_copy(step).wait_send()

    each(1, chips, drain)

    def swap(k):
        if pieces == 1:
            fall[k] = df[shard(2 * k + 1 - core), :].astype(BF)
        pair_copy(k).start()

    each(0, chips, swap)

    def sum_copy(step):
        return send(fall.at[chips + step], far_got.at[step], sum_out.at[step], sum_in.at[step], peer(step))

    def pass_on(turn):
        step = lax.rem(turn, chips)
        k = lax.rem(chip + step, chips)
        pair_copy(k).wait()
        value = df[shard(2 * k + core), :] + half[k].astype(FL)

        @pl.when(step > 0)
        def _():
            fall[chips + step] = value.astype(BF)
            sum_copy(step).start()

        @pl.when(step == 0)
        def _():
            df_ref[...] = value

    each(1, chips + 1, pass_on)

    def collect(step):
        sum_copy(step).wait()
        df_ref[...] += far_got[step].astype(FL)

    each(1, chips, collect)
    for j in range(pieces - depth, pieces):
        out_copy(j).wait()


def head(nb, nv, features, words, live, targets):
    rows = words.shape[1]
    part = chunk_of(rows, 640)
    total_rows = nv * PICKS
    chips = nv // 2
    dma = pltpu.SemaphoreType.DMA
    scratch = [
        pltpu.VMEM((nv, PICKS, D), BF),
        pltpu.VMEM((total_rows, rows), BF),
        pltpu.VMEM((2 * PICKS, rows), FL),
        pltpu.VMEM((8, total_rows), FL),
        pltpu.VMEM((nv, 8, total_rows), FL),
        pltpu.VMEM((D, total_rows) if rows > part else (8, 128), BF),
        pltpu.VMEM((8, 128) if rows > part else (D, part), FL),
        pltpu.VMEM((total_rows, 128), FL),
        pltpu.VMEM((total_rows, D), FL),
        pltpu.VMEM((chips, PICKS, D), FL if rows > part else BF),
        pltpu.VMEM((chips, PICKS, D), BF),
        pltpu.VMEM((min(2, rows // part), D, part), BF),
        dma((chips,)), dma((chips,)), dma((chips,)), dma((chips,)), dma((nv,)), dma((nv,)),
        dma((chips,)), dma((chips,)), dma((chips,)), dma((chips,)), dma((2,)),
    ]
    return run(
        functools.partial(head_kernel, nb, nv, part),
        [SD((PICKS, D), FL), SD((D, rows), BF), SD((8, 128), FL)],
        scratch,
        [features, words, live, targets],
        "head",
        1,
        out_specs=[VM, HB, VM],
    )


def wide_head_kernel(
    nb, nv, block_rows, f_ref, w_ref, live_ref, target_ref, df_ref, dw_ref, loss_ref,
    fall, ft, expo, words_sum, mine, first_got, merged, second_got, tile, third_got, tiles, coef, group, half, handed, mix_got,
    far_sum, far_got,
    z_out, z_in, mix_out, mix_in, near_out, near_in, s_out, s_in, pair_out, pair_in, give_out, give_in, sum_out, sum_in,
):
    b, v = lax.axis_index("batch"), lax.axis_index("vocab")
    rows = w_ref.shape[1]
    core, chip, chips = lax.rem(v, 2), v // 2, nv // 2
    sibling = {"vocab": v + 1 - 2 * core}
    base = v * block_rows + b * rows
    live = live_ref[:, lanes(b * rows, rows)] > 0
    span = nv * PICKS
    meet((("batch", nb), ("vocab", nv)))

    def column(line):
        line = jnp.where(line < (v + 1) * block_rows, line - base, -1).astype(FL)
        return jnp.broadcast_to(line, (128, 2 * PICKS)).T[:, 0:1].astype(I32)

    def peer(step):
        return {"vocab": lax.rem(chip + step, chips) * 2 + core}

    def other(step):
        return {"batch": lax.rem(b + step, nb)}

    def slot(s, k):
        return lax.rem(b - s + nb, nb) * nv + lax.rem(chip - k + chips, chips) * 2 + core

    def z_copy(k):
        return send(f_ref, fall.at[b * nv + v], z_out.at[k], z_in.at[k], peer(k))

    def mix_copy(s, k):
        place = fall.at[slot(0, k)]
        return send(place, place, mix_out.at[k, s], mix_in.at[k, s], other(s))

    def near_copy(s, k):
        place = fall.at[slot(s, k)]
        return send(place, place, near_out.at[k, s], near_in.at[k, s], sibling)

    def arrive(s, k):
        if s == 0:

            @pl.when(k > 0)
            def _():
                z_copy(k).wait_recv()

            each(1, nb, lambda t: mix_copy(t, k).start())
        else:
            mix_copy(s, k).wait_recv()
        near_copy(s, k).start()

    fall[b * nv + v] = f_ref[...]
    each(1, chips, lambda k: z_copy(k).start())
    arrive(0, 0)

    def logits(s, k):
        near_copy(s, k).wait_recv()
        p, c = lax.rem(b - s + nb, nb), lax.rem(chip - k + chips, chips)
        first = p * nv + c * 2
        start = pl.multiple_of(first * PICKS, 2 * PICKS)
        features = fall[pl.ds(first, 2)].reshape(2 * PICKS, D)
        ft[:, pl.ds(start, 2 * PICKS)] = features.T
        line = target_ref[p, :, pl.ds(pl.multiple_of(c * 2 * PICKS, 2 * PICKS), 2 * PICKS)]
        target = column(line)
        value = nn(features, w_ref[...])
        value = jnp.where(live, value, NEG_BIG)
        peak = jnp.maximum(jnp.max(value, axis=1, keepdims=True), 0.1 * NEG_BIG)
        e = jnp.exp(value - peak)
        expo[pl.ds(start, 2 * PICKS), :] = e.astype(BF)
        total = jnp.sum(e, axis=1, keepdims=True)
        picked = jnp.sum(jnp.where(target == iota((2 * PICKS, rows), 1), value, 0.0), axis=1, keepdims=True)
        lane = iota((2 * PICKS, 128), 1)
        wide = jnp.where(lane == 0, peak, jnp.where(lane == 1, total, picked)).T
        mine[c * 2, p] = wide[:8, :PICKS]
        mine[c * 2 + 1, p] = wide[:8, PICKS:]

    for s in range(nb):

        def one(k, s=s):
            @pl.when(k + 1 < chips)
            def _():
                arrive(s, k + 1)

            if s + 1 < nb:

                @pl.when(k + 1 == chips)
                def _():
                    arrive(s + 1, 0)

            logits(s, k)

        each(0, chips, one)

    def merge(read, count):
        peak = lax.fori_loop(
            0, count, lambda u, top: jnp.maximum(top, read(u)[0:1, :]), jnp.full((1, PICKS), NEG_BIG, FL)
        )

        def add(u, carry):
            one = read(u)
            return carry[0] + one[1:2, :] * jnp.exp(one[0:1, :] - peak), carry[1] + one[2:3, :]

        zero = jnp.zeros((1, PICKS), FL)
        return (peak, *lax.fori_loop(0, count, add, (zero, zero)))

    def tile_of(rows_of):
        line = iota((8, PICKS), 0)
        value = jnp.zeros((8, PICKS), FL)
        for i, row in enumerate(rows_of):
            value = jnp.where(line == i, row, value)
        return value

    def first_copy(t):
        u = lax.rem(v + t, nv)
        return send(mine.at[u], first_got.at[v], s_out.at[0, t], s_in.at[0, t], {"vocab": u})

    each(1, nv, lambda t: first_copy(t).start())
    first_got[v] = mine[v]
    each(1, nv, lambda t: first_copy(t).wait())
    for p in range(nb):
        merged[p] = tile_of(merge(lambda u, p=p: first_got[u, p], nv))

    def second_copy(t):
        return send(merged.at[lax.rem(b + t, nb)], second_got.at[b], s_out.at[1, t], s_in.at[1, t], other(t))

    each(1, nb, lambda t: second_copy(t).start())
    second_got[b] = merged[b]
    each(1, nb, lambda t: second_copy(t).wait())
    peak, total, picked = merge(lambda u: second_got[u], nb)
    valid = (picked > 0.5 * NEG_BIG).astype(FL)
    tile[...] = tile_of((peak + jnp.log(jnp.maximum(total, 1e-37)), picked, valid))

    def third_copy(t):
        return send(tile, third_got.at[b], s_out.at[2, t], s_in.at[2, t], other(t))

    each(1, nb, lambda t: third_copy(t).start())
    third_got[b] = tile[...]
    each(1, nb, lambda t: third_copy(t).wait())

    def last_copy(t):
        return send(third_got, tiles.at[v], s_out.at[3, t], s_in.at[3, t], {"vocab": lax.rem(v + t, nv)})

    each(1, nv, lambda t: last_copy(t).start())
    tiles[v] = third_got[...]
    each(1, nv, lambda t: last_copy(t).wait())

    def coefficients(p):
        count = lax.fori_loop(0, nv, lambda u, total: total + tiles[u, p, 2:3, :], jnp.zeros((1, PICKS), FL))
        share = 1.0 / (jnp.maximum(jnp.sum(count, axis=1, keepdims=True), 1.0) * nb)

        def spread(c, loss):
            rows_of = []
            for side in range(2):
                u = c * 2 + side
                lse, picked, valid = (tiles[u, p, i : i + 1, :] for i in range(3))
                weight = valid * share
                loss = loss + weight * (lse - picked)
                rows_of.append((weight * jnp.exp(mine[u, p, 0:1, :] - lse), weight))
            line = iota((128, 2 * PICKS), 0)
            alpha = jnp.concatenate([rows_of[0][0], rows_of[1][0]], axis=1)
            weight = jnp.concatenate([rows_of[0][1], rows_of[1][1]], axis=1)
            start = pl.multiple_of(p * span + c * 2 * PICKS, 2 * PICKS)
            coef[pl.ds(start, 2 * PICKS), :] = jnp.where(line == 0, alpha, weight).T
            return loss

        loss = lax.fori_loop(0, chips, spread, jnp.zeros((1, PICKS), FL))

        @pl.when(p == b)
        def _():
            loss_ref[...] = jnp.broadcast_to(jnp.sum(loss, axis=1, keepdims=True), loss_ref.shape)

    each(0, nb, coefficients)

    def shard(k, side):
        return pl.ds(pl.multiple_of((2 * k + side) * PICKS, PICKS), PICKS)

    def pair_copy(s, k):
        return send(handed.at[s, k], half.at[s, k], pair_out.at[s, k], pair_in.at[s, k], sibling)

    def give_copy(s):
        return send(handed.at[s], mix_got.at[s], give_out.at[s], give_in.at[s], other(s))

    def exchange(s):
        def add(k):
            pair_copy(s, k).wait()
            handed[s, k] = (group[s % 2, shard(k, core), :] + half[s, k].astype(FL)).astype(BF)

        each(0, chips, add)
        if s > 0:
            give_copy(s).start()

    for s in list(range(1, nb)) + [0]:
        p = lax.rem(b + s, nb)

        def strip(c, p=p):
            start = pl.multiple_of(p * span + c * 2 * PICKS, 2 * PICKS)
            here = pl.ds(start, 2 * PICKS)
            line = target_ref[p, :, pl.ds(pl.multiple_of(c * 2 * PICKS, 2 * PICKS), 2 * PICKS)]
            target = column(line)
            two = coef[here, :]
            hot = target == iota((2 * PICKS, rows), 1)
            value = two[:, 0:1] * expo[here, :].astype(FL) - jnp.where(hot, two[:, 1:2], 0.0)
            expo[here, :] = value.astype(BF)

        each(0, chips, strip)
        def features_grad(i, p=p, s=s):
            here = pl.ds(pl.multiple_of(i * 512, 512), 512)
            group[s % 2, here, :] = nt(expo[pl.ds(pl.multiple_of(p * span + i * 512, 512), 512), :], w_ref[...])

        each(0, span // 512, features_grad)

        def swap(k, s=s):
            handed[s, k] = group[s % 2, shard(k, 1 - core), :].astype(BF)
            pair_copy(s, k).start()

        if s != 1:
            exchange(s - 1 if s > 0 else nb - 1)
        each(0, chips, swap)

    words_sum[...] = jnp.zeros_like(words_sum)

    def words_grad(i):
        cut = lanes(i * 512, 512)
        words_sum[...] += nn(ft[:, cut], expo[cut, :])

    each(0, 1, words_grad)
    exchange(0)
    each(1, nb * span // 512, words_grad)
    dw_ref[...] = words_sum[...].astype(BF)

    for s in range(1, nb):
        give_copy(s).wait()

    def total_of(k):
        value = handed[0, k].astype(FL)
        for s in range(1, nb):
            value = value + mix_got[s, k].astype(FL)
        return value

    def sum_copy(t):
        return send(far_sum.at[t], far_got.at[t], sum_out.at[t], sum_in.at[t], peer(t))

    def pass_on(t):
        far_sum[t] = total_of(lax.rem(chip + t, chips)).astype(BF)
        sum_copy(t).start()

    each(1, chips, pass_on)
    df_ref[...] = total_of(chip)

    def collect(t):
        sum_copy(t).wait()
        df_ref[...] += far_got[t].astype(FL)

    each(1, chips, collect)
    each(1, chips, lambda k: z_copy(k).wait_send())
    for s in range(nb):
        each(0, chips, lambda k, s=s: near_copy(s, k).wait_send())
        if s > 0:
            each(0, chips, lambda k, s=s: mix_copy(s, k).wait_send())


def wide_head(nb, nv, block_rows, features, words, live, targets):
    rows = words.shape[1]
    tokens = nb * nv * PICKS
    chips = nv // 2
    dma = pltpu.SemaphoreType.DMA
    most = max(nb, nv)
    scratch = [
        pltpu.VMEM((nb * nv, PICKS, D), BF),
        pltpu.VMEM((D, tokens), BF),
        pltpu.VMEM((tokens, rows), BF),
        pltpu.VMEM((D, rows), FL),
        pltpu.VMEM((nv, nb, 8, PICKS), FL),
        pltpu.VMEM((nv, nb, 8, PICKS), FL),
        pltpu.VMEM((nb, 8, PICKS), FL),
        pltpu.VMEM((nb, 8, PICKS), FL),
        pltpu.VMEM((8, PICKS), FL),
        pltpu.VMEM((nb, 8, PICKS), FL),
        pltpu.VMEM((nv, nb, 8, PICKS), FL),
        pltpu.VMEM((tokens, 128), FL),
        pltpu.VMEM((2, nv * PICKS, D), FL),
        pltpu.VMEM((nb, chips, PICKS, D), BF),
        pltpu.VMEM((nb, chips, PICKS, D), BF),
        pltpu.VMEM((nb, chips, PICKS, D), BF),
        pltpu.VMEM((chips, PICKS, D), BF),
        pltpu.VMEM((chips, PICKS, D), BF),
        dma((chips,)), dma((chips,)), dma((chips, nb)), dma((chips, nb)), dma((chips, nb)), dma((chips, nb)),
        dma((4, most)), dma((4, most)), dma((nb, chips)), dma((nb, chips)), dma((nb,)), dma((nb,)),
        dma((chips,)), dma((chips,)),
    ]
    return run(
        functools.partial(wide_head_kernel, nb, nv, block_rows),
        [SD((PICKS, D), FL), SD((D, rows), BF), SD((8, 128), FL)],
        scratch,
        [features, words, live, targets],
        "wide_head",
        1,
    )


def norm_kernel(
    nb, nv, extra_ref, dw_ref, a_ref, p_ref, u_ref, c_ref, loss_ref, out_ref,
    mine, near, lines, vocab_out, vocab_in, batch_out, batch_in,
):
    b, v = lax.axis_index("batch"), lax.axis_index("vocab")
    meet((("batch", nb), ("vocab", nv)))

    def squares(refs, part):
        cols = refs[0].shape[1]

        def add(j, total):
            value = refs[0][:, lanes(j * part, part)].astype(FL)
            for ref in refs[1:]:
                value = value + ref[:, lanes(j * part, part)].astype(FL)
            return total + jnp.sum(value * value, axis=0, keepdims=True)

        line = lax.fori_loop(0, cols // part, add, jnp.zeros((1, part), FL))
        return jnp.sum(line, axis=1, keepdims=True)

    own = squares((extra_ref, dw_ref), chunk_of(extra_ref.shape[1], 640))
    layer = squares((a_ref,), 512) + squares((p_ref,), 384) + squares((u_ref,), 512) + squares((c_ref,), 384)
    own = own + jnp.where(v == 0, layer, jnp.zeros_like(layer))
    line = iota((8, 128), 0)
    mine[...] = jnp.where(line == 0, own, jnp.where((line == 1) & (v == 0), loss_ref[...], 0.0))

    def vocab_copy(step):
        return send(mine, near.at[v], vocab_out.at[step], vocab_in.at[step], {"vocab": lax.rem(v + step, nv)})

    each(1, nv, lambda step: vocab_copy(step).start())
    near[v] = mine[...]
    each(1, nv, lambda step: vocab_copy(step).wait())
    mine[...] = lax.fori_loop(0, nv, lambda u, total: total + near[u], jnp.zeros((8, 128), FL))

    def batch_copy(step):
        return send(mine, lines.at[b], batch_out.at[step], batch_in.at[step], {"batch": lax.rem(b + step, nb)})

    each(1, nb, lambda step: batch_copy(step).start())
    lines[b] = mine[...]
    each(1, nb, lambda step: batch_copy(step).wait())
    out_ref[...] = lax.fori_loop(0, nb, lambda u, total: total + lines[u], jnp.zeros((8, 128), FL))


def norm(nb, nv, extra, dw, sums, loss):
    dma = pltpu.SemaphoreType.DMA
    return run(
        functools.partial(norm_kernel, nb, nv),
        [SD((8, 128), FL)],
        [
            pltpu.VMEM((8, 128), FL), pltpu.VMEM((nv, 8, 128), FL), pltpu.VMEM((nb, 8, 128), FL),
            dma((nv,)), dma((nv,)), dma((nb,)), dma((nb,)),
        ],
        [extra, dw, *sums, loss],
        "norm",
        5,
    )[0]


def adamw(weight, moment, square, gradient, clip, count, decay, rate):
    gradient = gradient * clip
    moment = BETA_ONE * moment + (1 - BETA_ONE) * gradient
    square = BETA_TWO * square + (1 - BETA_TWO) * gradient * gradient
    fixed_moment = moment / (1 - BETA_ONE**count)
    fixed_square = square / (1 - BETA_TWO**count)
    weight = weight - rate * (fixed_moment / (jnp.sqrt(fixed_square) + ADAM_EPS) + decay * weight)
    return (weight, moment, square)


def slot_size(nv):
    mean = SEQ_LEN // nv
    return -(-(mean + int(5.5 * math.sqrt(mean))) // 32) * 32


def shards(
    nb, nv,
    tokens, targets, segments, counted, vocab_mask, step_count,
    table, table_moment, table_square,
    attend, attend_moment, attend_square,
    project, project_moment, project_square,
    expand, expand_moment, expand_square,
    contract, contract_moment, contract_square,
    gain, gain_moment, gain_square,
    shift, shift_moment, shift_square,
):
    rows, width = table.shape
    cap = slot_size(nv)
    table_t = table.T
    norms = jnp.concatenate([gain, shift], axis=0)
    packed = jnp.concatenate([attend[0], norms.T, jnp.zeros((width, EXTRA - 6), FL)], axis=1).astype(BF)
    pieces = (packed, project[0].astype(BF), expand[0].astype(BF), contract[0].astype(BF))
    split = nb * nv * PICKS <= 4096
    rounded = table_t.astype(BF)
    quarter = -(-rows // (nb * 128)) * 128
    if split:
        rounded = jnp.pad(rounded, ((0, 0), (0, nb * quarter - rows)))
    else:
        words = lax.all_gather(rounded, "batch", axis=0, tiled=True)

    seg_row, pos_row = segments[None, :], counted[None, :]
    tok = tokens.reshape(nv, SEQ_LEN)
    x, ids, place, most, every, a_all, u_all, *rest = embed(
        nb, nv, cap, rows, jnp.zeros((1,), I32), tok, rounded, (pieces[0], pieces[2]),
        targets[None, :] if split else None,
    )
    turns = (most[0] + cap - 1) // cap

    def more_rows(state):
        turn, total = state
        return turn + 1, total + embed(nb, nv, cap, rows, turn[None], tok, rounded)[0]

    x = lax.while_loop(lambda state: state[0] < turns, more_rows, (jnp.int32(1), x))[1]

    hall, kv, q, hq, xq, mixed, lse, norm_rows, mixing_t, p_all, c_all = run(
        functools.partial(attend_kernel, nb, nv),
        [
            SD((KEYS, D), BF), SD((KEYS, 2 * D), BF), SD((PICKS, D), BF), SD((PICKS, D), BF), SD((PICKS, D), FL),
            SD((PICKS, D), BF), SD((NPAIR, 2, PICKS), FL), SD((8, D), FL), SD((SEQ_LEN, SLOTS * NB), BF),
            SD((D, D), BF), SD((FF, D), BF),
        ],
        weight_semaphores(2),
        [x, a_all, seg_row, pos_row, pieces[1], pieces[3]],
        "attend", 6, flops=7 * 10**9, moved=20 * 10**6,
        in_specs=[VM] * 4 + [HB] * 2, out_specs=[VM] * 9 + [HB] * 2,
    )
    x1, h2, z, act, x2, features = run(
        feed_kernel,
        [
            SD((PICKS, D), FL), SD((PICKS, D), BF), SD((PICKS, FF), FL), SD((PICKS, FF), BF), SD((PICKS, D), FL),
            SD((PICKS, D), BF),
        ],
        [],
        [xq, mixed, p_all, u_all, c_all, norm_rows],
        "feed", flops=2 * 10**9, moved=15 * 10**6,
    )
    if split:
        live = jnp.pad(vocab_mask, (0, nb * quarter - rows))[None, :]
        df, dw, loss_block = wide_head(nb, nv, rows, features, rest[0], live, rest[1])
    else:
        df, dw, loss_block = head(nb, nv, features, words, vocab_mask[None, :], targets[:, None])
        dw_sum = lax.psum_scatter(dw, "batch", scatter_dimension=0, tiled=True)

    dc, du, dp, dx1, dmixed, dnorm = run(
        feed_back_kernel,
        [
            SD((FF, D), BF), SD((D, FF), BF), SD((D, D), BF), SD((PICKS, D), FL), SD((PICKS, D), BF), SD((8, D), FL),
        ],
        [pltpu.VMEM((PICKS, D), FL)],
        [df, x2, x1, h2, z, act, mixed, p_all, u_all, c_all, norm_rows],
        "feed_back", flops=4 * 10**9, moved=30 * 10**6,
    )
    da, dx, du_sum = run(
        functools.partial(attend_back_kernel, nb, nv),
        [SD((D, 3 * D + EXTRA), BF), SD((SEQ_LEN, D), BF), SD((width, FF // 2), BF)],
        [
            pltpu.VMEM((KEYS, 2 * D), BF), pltpu.VMEM((PICKS, D), BF), pltpu.VMEM((D, KEYS), BF),
            pltpu.VMEM((SEQ_LEN, D), FL), pltpu.VMEM((SEQ_LEN, D), FL), pltpu.VMEM((SLOTS * NB, D), BF),
            pltpu.VMEM((SEQ_LEN, PICKS), BF), *gradient_scratch(nb, nv, [du.shape], (0,), False),
        ],
        [dmixed, q, kv, lse, hall, hq, a_all, x, dx1, mixing_t, seg_row, pos_row, norm_rows, dnorm, du],
        "attend_back", 7, flops=12 * 10**9, moved=25 * 10**6,
        in_specs=[VM] * 14 + [HB],
    )
    extra, *sums = unembed(nb, nv, cap, width, rows, dx, ids, place, (da, dp, du_sum, dc), dw if split else None)
    if split:
        dw_sum = sums.pop()

    def more_grads(state):
        turn, total = state
        later = later_slots(nv, cap, rows, every, turn)
        return turn + 1, total + unembed(
            nb, nv, cap, width, rows, dx, later, place - jnp.array([0, 1, 0, 0, 0, 0, 0, 0], I32)[None, :, None] * (turn * cap)
        )[0]

    extra = lax.while_loop(lambda state: state[0] < turns, more_grads, (jnp.int32(1), extra))[1]

    totals = norm(nb, nv, extra, dw_sum, sums, loss_block)
    grad_table = dw_sum[:, :rows].astype(FL) + extra
    grad_a, grad_p, grad_u, grad_c = (item.astype(FL) for item in sums)
    grad_norms = grad_a[:, 3 * D : 3 * D + 6].T
    grad_a = grad_a[:, : 3 * D]
    squares, loss = totals[0, 0], totals[1, 0]
    gradient_norm = jnp.sqrt(squares)
    clip = jnp.minimum(1.0, MAX_NORM / (gradient_norm + 1e-06))
    count = step_count[0].astype(FL)

    def update(weight, moment, square, gradient, decay=DECAY, rate=LEARN_RATE):
        return adamw(weight, moment, square, gradient, clip, count, decay, rate)

    table_out = [item.T for item in update(table_t, table_moment.T, table_square.T, grad_table)]
    attend_out = update(attend, attend_moment, attend_square, grad_a[None])
    project_out = update(project, project_moment, project_square, grad_p[None])
    expand_out = update(expand, expand_moment, expand_square, grad_u[None])
    contract_out = update(contract, contract_moment, contract_square, grad_c[None])
    gain_out = update(gain, gain_moment, gain_square, grad_norms[:3], 0.0, NORM_RATE)
    shift_out = update(shift, shift_moment, shift_square, grad_norms[3:], 0.0, NORM_RATE)
    return (
        loss, gradient_norm, *table_out, *attend_out, *project_out, *expand_out, *contract_out, *gain_out, *shift_out,
    )


def solution(mesh):
    nb, nv = mesh.shape["batch"], mesh.shape["vocab"]
    both, split, middle, last = P(("batch", "vocab")), P("vocab", "batch"), P(None, "batch", None), P(None, "batch")
    state = (split,) * 3 + (middle,) * 12 + (last,) * 6
    return jax.shard_map(
        functools.partial(shards, nb, nv),
        mesh=mesh,
        in_specs=(P("batch"), P("batch"), both, both, P("vocab"), P()) + state,
        out_specs=(P(), P()) + state,
        check_vma=False,
    )
```

```python
import functools
import math

import jax
import jax.numpy as jnp
from jax import lax
from jax.experimental import pallas as pl
from jax.experimental.pallas import tpu as pltpu
from jax.sharding import PartitionSpec as P

D = 768
H = 12
HD = 64
FF = 3072
NB = 256
SEG_BLOCKS = 4
SLOTS = SEG_BLOCKS - 2
SEQ_LEN = 1024
PICKS = 128
KEYS = SLOTS * NB + SEQ_LEN
BLK = 256
PAIR = 2 * HD
NPAIR = H // 2
EXTRA = 256
WIDE = (3 * D + EXTRA, D, FF, D)

NORM_EPS = 1e-05
MAX_NORM = 0.02
LEARN_RATE = 0.04
NORM_RATE = 0.5
BETA_ONE = 0.9
BETA_TWO = 0.999
ADAM_EPS = 1e-08
DECAY = 0.1
NEG_BIG = -1e30
BF = jnp.bfloat16
FL = jnp.float32
I32 = jnp.int32
MESH = pl.DeviceIdType.MESH
SD = jax.ShapeDtypeStruct
VM = pl.BlockSpec(memory_space=pltpu.VMEM)
SM = pl.BlockSpec(memory_space=pltpu.SMEM)
HB = pl.BlockSpec(memory_space=pl.ANY)
LIMIT = 62 * 2**20


def nn(a, b):
    return lax.dot_general(a, b, (((1,), (0,)), ((), ())), preferred_element_type=FL)


def nt(a, b):
    return lax.dot_general(a, b, (((1,), (1,)), ((), ())), preferred_element_type=FL)


def iota(shape, axis):
    return lax.broadcasted_iota(I32, shape, axis)


def lanes(start, size):
    return pl.ds(pl.multiple_of(start, 128), size)


def chunk_of(rows, want):
    return want if rows % want == 0 else rows


def run(kernel, outs, scratch, ins, name, collective=None, flops=0, moved=0, out_specs=None, in_specs=None):
    return pl.pallas_call(
        kernel,
        out_shape=outs,
        in_specs=in_specs if in_specs is not None else [VM] * len(ins),
        out_specs=out_specs if out_specs is not None else [VM] * len(outs),
        scratch_shapes=scratch,
        compiler_params=pltpu.CompilerParams(
            vmem_limit_bytes=LIMIT,
            collective_id=collective,
            has_side_effects=collective is not None,
        ),
        cost_estimate=pl.CostEstimate(flops=flops, bytes_accessed=moved, transcendentals=0),
        name=name,
    )(*ins)


def send(source, target, out_sem, in_sem, device):
    return pltpu.make_async_remote_copy(
        src_ref=source, dst_ref=target, send_sem=out_sem, recv_sem=in_sem, device_id=device, device_id_type=MESH
    )


def meet(axes):
    barrier = pltpu.get_barrier_semaphore()
    count = 0
    for axis, size in axes:
        me = lax.axis_index(axis)

        def greet(step, carry, axis=axis, size=size, me=me):
            pl.semaphore_signal(barrier, inc=1, device_id={axis: lax.rem(me + step, size)}, device_id_type=MESH)
            return carry

        lax.fori_loop(1, size, greet, 0)
        count += size - 1
    pl.semaphore_wait(barrier, count)


def each(start, stop, body):
    def step(index, carry):
        body(index)
        return carry

    lax.fori_loop(start, stop, step, 0)


def embed_kernel(
    nb, nv, cap, part, rows, first, split, *refs
):
    round_ref, tok_ref, words = refs[:3]
    shards, refs = (refs[3:5], refs[5:]) if first else ((), refs[3:])
    target_ref, refs = (refs[0], refs[1:]) if split else (None, refs)
    x_ref, ids_ref, place_ref, most_ref, tok_ref_all = refs[:5]
    wholes, refs = (refs[5:7], refs[7:]) if first else ((), refs[5:])
    (quarter_ref, target_all), refs = (refs[:2], refs[2:]) if split else ((None, None), refs)
    before, ranks, work, sent, got, spread, mixed, turned = refs[:8]
    tok_out, tok_in, row_out, row_in, mix_out, mix_in = refs[8:14]
    b, v = lax.axis_index("batch"), lax.axis_index("vocab")
    width = words.shape[0]
    shift = round_ref[0] * cap
    meet((("batch", nb), ("vocab", nv)))
    gather = WeightGather(nb, shards, wholes, *refs[14:19]) if first else None
    quarter_out, quarter_in, quarter_own, target_out, target_in = refs[19:24] if split else [None] * 5

    def tok_copy(step):
        return send(
            tok_ref, tok_ref_all.at[b], tok_out.at[step], tok_in.at[step], {"batch": lax.rem(b + step, nb)}
        )

    for step in range(1, nb):
        tok_copy(step).start()

    def target_copy(step):
        return send(
            target_ref, target_all.at[b], target_out.at[step], target_in.at[step], {"batch": lax.rem(b + step, nb)}
        )

    def quarter(owner):
        return words.at[:, lanes(owner * (words.shape[1] // nb), words.shape[1] // nb)]

    def quarter_copy(step):
        other = lax.rem(b + step, nb)
        place = quarter_ref.at[pl.ds(pl.multiple_of(b * width, 16), width), :]
        return send(quarter(other), place, quarter_out.at[step], quarter_in.at[step], {"batch": other})

    def quarter_keep():
        place = quarter_ref.at[pl.ds(pl.multiple_of(b * width, 16), width), :]
        return pltpu.make_async_copy(quarter(b), place, quarter_own.at[0])

    if split:
        target_all[b] = target_ref[...]
        for step in range(1, nb):
            target_copy(step).start()
    if first:
        gather.start()
    if split:
        quarter_keep().start()
    tok_ref_all[b] = tok_ref[...]
    before[...] = (iota((SEQ_LEN, SEQ_LEN), 0) < iota((SEQ_LEN, SEQ_LEN), 1)).astype(FL).astype(BF)
    for step in range(1, nb):
        tok_copy(step).wait()

    base = v * rows
    most = jnp.zeros((nv, 1), FL)
    for p in range(nb):
        ids = tok_ref_all[p]
        mine = (ids >= base) & (ids < base + rows)
        rank = nn(mine.astype(FL).astype(BF), before[...])
        ranks[p] = jnp.where(mine, rank.astype(I32) - shift, -1)
        for owner in range(nv):
            theirs = (ids >= owner * rows) & (ids < (owner + 1) * rows)
            most = jnp.maximum(most, jnp.sum(theirs.astype(FL), axis=1, keepdims=True))
    most_ref[0] = jnp.max(most).astype(I32)

    def row_copy(step):
        return send(
            sent.at[step], got.at[v], row_out.at[step], row_in.at[step], {"vocab": lax.rem(v + step, nv)}
        )

    def build(turn):
        step = lax.rem(turn, nv)
        dest = lax.rem(v + step, nv)
        found = []
        for p in range(nb):
            pick = (iota((cap, SEQ_LEN), 0) == ranks[p, pl.ds(dest, 1), :]).astype(FL).astype(BF)
            local = tok_ref_all[p, pl.ds(dest, 1), :] - base
            line = iota((8, SEQ_LEN), 0)
            high, low = lax.shift_right_arithmetic(local, 7), lax.bitwise_and(local, 127)
            digits = jnp.where(line == 0, high, jnp.where(line == 1, low, 0)).astype(FL).astype(BF)
            both = nt(pick, digits)
            found.append((both[:, 0:1] * 128.0 + both[:, 1:2]).astype(I32))
        index = jnp.concatenate(found, axis=0)
        ids_ref[dest] = index
        work[...] = jnp.zeros_like(work)

        def piece(j):
            hot = (index - j * part == iota((nb * cap, part), 1)).astype(FL).astype(BF)
            work[...] += nt(hot, words[:, lanes(j * part, part)])

        each(0, rows // part, piece)
        block = work[...].T.astype(BF)

        @pl.when(step > 0)
        def _():
            sent[step] = block
            row_copy(step).start()

        @pl.when(step == 0)
        def _():
            got[v] = block

    each(1, nv // 2 + 1, build)
    if first:
        gather.pass_on()
    if split:
        for step in range(1, nb):
            quarter_copy(step).start()
    each(nv // 2 + 1, nv + 1, build)

    keys = []
    for p in range(nb):
        ids = tok_ref_all[p, pl.ds(v, 1), :]
        owner = iota((nv, SEQ_LEN), 0)
        theirs = (ids >= owner * rows) & (ids < (owner + 1) * rows)
        rank = nn(theirs.astype(FL).astype(BF), before[...])
        place = jnp.sum(jnp.where(theirs, rank, 0.0), axis=0, keepdims=True).astype(I32) - shift
        holder = jnp.sum(jnp.where(theirs, owner.astype(FL), 0.0), axis=0, keepdims=True).astype(I32)
        line = iota((8, SEQ_LEN), 0)
        place_ref[p] = jnp.where(line == 0, holder, jnp.where(line == 1, place, 0))
        keys.append((holder, place))
        spread[p] = jnp.zeros((width, SEQ_LEN), FL)

    def take(turn):
        step = lax.rem(turn, nv)
        source = lax.rem(v - step + nv, nv)

        @pl.when(step > 0)
        def _():
            row_copy(step).wait()

        block = got[source]
        for p in range(nb):
            holder, place = keys[p]
            key = jnp.where(holder == source, place, -1)
            hot = (iota((cap, SEQ_LEN), 0) == key).astype(FL).astype(BF)
            spread[p] += nn(block[:, p * cap : (p + 1) * cap], hot)

    each(1, nv + 1, take)

    def mix_copy(step):
        return send(
            mixed.at[step], turned.at[b], mix_out.at[step], mix_in.at[step], {"batch": lax.rem(b + step, nb)}
        )

    for step in range(1, nb):
        mixed[step] = spread[lax.rem(b + step, nb)].astype(BF)
        mix_copy(step).start()
    turned[b] = spread[b].astype(BF)
    for step in range(1, nb):
        mix_copy(step).wait()
    x_ref[...] = turned[...].reshape(nb * width, SEQ_LEN).T
    if first:
        gather.finish()
    if split:
        quarter_keep().wait()
        for step in range(1, nb):
            target_copy(step).wait()
            quarter_copy(step).wait()


def weight_semaphores(count):
    return [pltpu.SemaphoreType.DMA((count,))] + [pltpu.SemaphoreType.DMA((count, 4))] * 4


class WeightGather:
    def __init__(self, nb, shards, wholes, own_sem, out_sem, in_sem, pair_out, pair_in):
        self.nb, self.shards, self.wholes = nb, shards, wholes
        self.own_sem, self.out_sem, self.in_sem, self.pair_out, self.pair_in = own_sem, out_sem, in_sem, pair_out, pair_in
        self.b, v = lax.axis_index("batch"), lax.axis_index("vocab")
        self.core = lax.rem(v, 2)
        self.sibling = {"vocab": v + 1 - 2 * self.core}

    def flip(self, bits):
        b = self.b
        low, high = lax.rem(b, 2), b // 2
        return (high if bits < 2 else 1 - high) * 2 + (low if bits % 2 == 0 else 1 - low)

    def place(self, w, owner, top, size):
        rows = self.shards[w].shape[0]
        first = pl.multiple_of(owner * rows + self.core * (rows // 2) + top, 16)
        return self.wholes[w].at[pl.ds(first, size), :]

    def routes(self, w):
        rows = self.shards[w].shape[0] // 2
        if self.nb == 4:
            half = rows // 2
            return [
                (self.b, 0, rows, self.flip(1), self.flip(1)),
                (self.b, 0, rows, self.flip(2), self.flip(2)),
                (self.flip(1), 0, half, self.flip(2), self.flip(3)),
                (self.flip(2), half, half, self.flip(1), self.flip(3)),
            ]
        others = [lax.rem(self.b + step, self.nb) for step in range(1, self.nb)]
        came = [lax.rem(self.b - step + self.nb, self.nb) for step in range(1, self.nb)]
        return [(self.b, 0, rows, other, source) for other, source in zip(others, came)]

    def own_copy(self, w):
        rows = self.shards[w].shape[0]
        first = pl.multiple_of(self.b * rows, 16)
        return pltpu.make_async_copy(self.shards[w], self.wholes[w].at[pl.ds(first, rows), :], self.own_sem.at[w])

    def copy(self, w, k):
        owner, top, size, device, _ = self.routes(w)[k]
        if self.nb == 4 and k >= 2:
            source = self.place(w, owner, top, size)
        else:
            source = self.shards[w].at[pl.ds(pl.multiple_of(self.core * size, 16), size), :]
        target = self.place(w, owner, top, size)
        return send(source, target, self.out_sem.at[w, k], self.in_sem.at[w, k], {"batch": device})

    def pair(self, w, k):
        _, top, size, _, arrived = self.routes(w)[k]
        ref = self.place(w, arrived, top, size)
        return send(ref, ref, self.pair_out.at[w, k], self.pair_in.at[w, k], self.sibling)

    def start(self):
        for w in range(len(self.shards)):
            for k in range(2 if self.nb == 4 else self.nb - 1):
                self.copy(w, k).start()
        for w in range(len(self.shards)):
            self.own_copy(w).start()

    def pass_on(self):
        if self.nb != 4:
            return
        for w in range(len(self.shards)):
            for k in range(2):
                self.copy(w, k).wait_recv()
                self.copy(w, k + 2).start()
                self.pair(w, k).start()

    def finish(self):
        for w in range(len(self.shards)):
            for k in range(2 if self.nb == 4 else 0, len(self.routes(w))):
                self.copy(w, k).wait_recv()
                self.pair(w, k).start()
        for w in range(len(self.shards)):
            self.own_copy(w).wait()
            for k in range(len(self.routes(w))):
                self.copy(w, k).wait_send()
                self.pair(w, k).wait()


def embed(nb, nv, cap, rows, turn, tok, table, shards=(), targets=None):
    width = table.shape[0]
    split = targets is not None
    part = chunk_of(rows, 640)
    count = nb * cap
    outs = [
        SD((SEQ_LEN, D), BF),
        SD((nv, count, 1), I32),
        SD((nb, 8, SEQ_LEN), I32),
        SD((1,), I32),
        SD((nb, nv, SEQ_LEN), I32),
    ]
    first = len(shards) > 0
    outs += [SD((nb * item.shape[0], item.shape[1]), BF) for item in shards]
    if split:
        outs += [SD((D, table.shape[1] // nb), BF), SD((nb, *targets.shape), I32)]
    dma = pltpu.SemaphoreType.DMA
    scratch = [
        pltpu.VMEM((SEQ_LEN, SEQ_LEN), BF),
        pltpu.VMEM((nb, nv, SEQ_LEN), I32),
        pltpu.VMEM((count, width), FL),
        pltpu.VMEM((nv, width, count), BF),
        pltpu.VMEM((nv, width, count), BF),
        pltpu.VMEM((nb, width, SEQ_LEN), FL),
        pltpu.VMEM((nb, width, SEQ_LEN), BF),
        pltpu.VMEM((nb, width, SEQ_LEN), BF),
        dma((nb,)), dma((nb,)), dma((nv,)), dma((nv,)), dma((nb,)), dma((nb,)),
    ]
    if first:
        scratch += weight_semaphores(len(shards))
    if split:
        scratch += [dma((nb,)), dma((nb,)), dma((1,)), dma((nb,)), dma((nb,))]
    extra = [targets] if split else []
    return run(
        functools.partial(embed_kernel, nb, nv, cap, part, rows, first, split), outs, scratch,
        [turn, tok, table, *shards, *extra],
        "embed" if first else "embed_more", 0 if first else 3,
        in_specs=[SM, VM, VM] + [VM] * len(shards) + [VM] * len(extra),
        out_specs=[VM] * 3 + [SM, VM] + [HB] * len(shards) + ([HB, VM] if split else []),
    )


class GradientSum:
    def __init__(self, nb, nv, grads, refs, totals=None, sums=None):
        self.nb, self.nv, self.grads, self.sums = nb, nv, grads, sums
        self.todo = [w for w, item in enumerate(grads) if item is not None]
        take = iter(refs)
        spread = lambda keys: {w: next(take) for w in keys}
        everything = range(len(grads))
        self.own, self.near, self.shard = spread(self.todo), spread(self.todo), spread(self.todo)
        if sums is not None:
            self.total = spread(self.todo)
            self.total.update(totals)
            self.bits, self.result = spread(everything), spread(everything)
        else:
            self.total = totals
        self.load_sem, self.pair_out, self.pair_in, self.mix_out, self.mix_in = (next(take) for _ in range(5))
        if sums is not None:
            (self.cut_out, self.cut_in, self.all_out, self.all_in, self.last_out, self.last_in,
             self.store_sem) = take
        self.b, v = lax.axis_index("batch"), lax.axis_index("vocab")
        self.core, self.chip, self.chips = lax.rem(v, 2), v // 2, nv // 2
        self.sibling = {"vocab": v + 1 - 2 * self.core}

    def half(self, w, core):
        cols = self.total[w].shape[1]
        return lanes(core * cols, cols)

    def load(self, w):
        return pltpu.make_async_copy(self.grads[w].at[:, self.half(w, self.core)], self.own[w], self.load_sem.at[w])

    def pair(self, w):
        source = self.grads[w].at[:, self.half(w, 1 - self.core)]
        return send(source, self.near[w], self.pair_out.at[w], self.pair_in.at[w], self.sibling)

    def start(self):
        for w in sorted(self.todo, reverse=True):
            self.pair(w).start()
            self.load(w).start()

    def mix(self, w, step):
        other = lax.rem(self.b + step, self.nb)
        rows = self.own[w].shape[0] // self.nb
        source = self.own[w].at[pl.ds(pl.multiple_of(other * rows, 16), rows), :]
        return send(source, self.shard[w].at[step], self.mix_out.at[w, step], self.mix_in.at[w, step], {"batch": other})

    def scatter(self, w):
        self.load(w).wait()
        self.pair(w).wait()
        rows = self.own[w].shape[0] // self.nb

        def add(i, w=w, rows=rows):
            cut = pl.ds(pl.multiple_of(i * rows, 16), rows)
            self.own[w][cut, :] = (self.own[w][cut, :].astype(FL) + self.near[w][cut, :].astype(FL)).astype(BF)

        each(0, self.nb, add)
        for step in range(1, self.nb):
            self.mix(w, step).start()

    def pieces(self, w):
        rows = self.total[w].shape[0]
        count = max(n for n in range(1, self.chips + 1) if rows % (16 * n) == 0)
        return count, rows // count

    def peer(self, step):
        other = lax.rem(self.chip + step, self.chips)
        return other, {"vocab": other * 2 + self.core}

    def cut(self, w, step):
        other, device = self.peer(step)
        size = self.pieces(w)[1]
        source = self.total[w].at[pl.ds(pl.multiple_of(other * size, 16), size), :]
        return send(source, self.bits[w].at[step], self.cut_out.at[w, step], self.cut_in.at[w, step], device)

    def back(self, w, step):
        size = self.pieces(w)[1]
        place = self.result[w].at[pl.ds(pl.multiple_of(self.chip * size, 16), size), :]
        return send(place, place, self.all_out.at[w, step], self.all_in.at[w, step], self.peer(step)[1])

    def back_recv(self, w, step):
        source = lax.rem(self.chip - step + self.chips, self.chips)
        size = self.pieces(w)[1]
        place = self.result[w].at[pl.ds(pl.multiple_of(source * size, 16), size), :]
        return send(place, place, self.all_out.at[w, step], self.all_in.at[w, step], self.peer(step)[1])

    def gather(self, w):
        rows = self.total[w].shape[0]
        for step in range(1, self.nb):
            self.mix(w, step).wait()
        here = pl.ds(pl.multiple_of(self.b * rows, 16), rows)
        value = self.own[w][here, :].astype(FL)
        for step in range(1, self.nb):
            value = value + self.shard[w][step].astype(FL)
        self.total[w][...] = value.astype(BF)

    def reduce(self, w):
        if w in self.todo:
            self.gather(w)
        count = self.pieces(w)[0]

        def go(step):
            @pl.when(self.peer(step)[0] < count)
            def _():
                self.cut(w, step).start()

        each(1, self.chips, go)

    def collect(self, w):
        count, size = self.pieces(w)
        mine = pl.ds(pl.multiple_of(self.chip * size, 16), size)

        @pl.when(self.chip < count)
        def _(w=w, mine=mine):
            def add(step, value):
                self.cut(w, step).wait_recv()
                return value + self.bits[w][step].astype(FL)

            value = lax.fori_loop(1, self.chips, add, self.total[w][mine, :].astype(FL))
            self.result[w][mine, :] = value.astype(BF)
            each(1, self.chips, lambda step: self.back(w, step).start())

        def sent(step, w=w, count=count):
            @pl.when(self.peer(step)[0] < count)
            def _():
                self.cut(w, step).wait_send()

        each(1, self.chips, sent)

    def last(self, w):
        return send(
            self.result[w], self.sums[w].at[:, self.half(w, self.core)], self.last_out.at[w], self.last_in.at[w], self.sibling
        )

    def store(self, w):
        return pltpu.make_async_copy(self.result[w], self.sums[w].at[:, self.half(w, self.core)], self.store_sem.at[w])

    def finish(self):
        for w in range(4):
            count = self.pieces(w)[0]

            def got(step, w=w, count=count):
                @pl.when(lax.rem(self.chip - step + self.chips, self.chips) < count)
                def _():
                    self.back_recv(w, step).wait_recv()

            each(1, self.chips, got)
            self.last(w).start()
            self.store(w).start()
        for w in range(4):
            count = self.pieces(w)[0]

            @pl.when(self.chip < count)
            def _(w=w):
                each(1, self.chips, lambda step: self.back(w, step).wait_send())

            self.store(w).wait()
            self.last(w).wait_send()
            other = self.sums[w].at[:, self.half(w, 1 - self.core)]
            send(other, other, self.last_out.at[w], self.last_in.at[w], self.sibling).wait_recv()


def gradient_scratch(nb, nv, shapes, todo, whole=True):
    chips = nv // 2
    halves = [(rows, cols // 2) for rows, cols in shapes]
    shards = [(rows // nb, cols) for rows, cols in halves]
    sizes = [rows // max(n for n in range(1, chips + 1) if rows % (16 * n) == 0) for rows, _ in shards]
    dma = pltpu.SemaphoreType.DMA
    count = len(shapes)
    refs = [pltpu.VMEM(halves[w], BF) for w in todo] * 2 + [pltpu.VMEM((nb, *shards[w]), BF) for w in todo]
    if whole:
        refs += [pltpu.VMEM(shards[w], BF) for w in todo]
        refs += [pltpu.VMEM((chips, size, item[1]), BF) for size, item in zip(sizes, shards)]
        refs += [pltpu.VMEM(item, BF) for item in shards]
    refs += [dma((count,)), dma((count,)), dma((count,)), dma((count, nb)), dma((count, nb))]
    if whole:
        refs += [dma((count, chips))] * 4 + [dma((count,))] * 3
    return refs


def unembed_kernel(nb, nv, cap, part, first, split, *refs):
    x_ref, ids_ref, place_ref = refs[:3]
    grads, refs = (refs[3:7], refs[7:]) if first else ((), refs[3:])
    if first:
        totals, grads = {2: grads[2]}, (grads[0], grads[1], None, grads[3])
    quarter_ref, refs = (refs[0], refs[1:]) if split else (None, refs)
    out_ref = refs[0]
    sums, refs = (refs[1:5], refs[5:]) if first else ((), refs[1:])
    dw_ref, refs = (refs[0], refs[1:]) if split else (None, refs)
    (quarter_out, quarter_in, quarter_own), refs = (refs[:3], refs[3:]) if split else ([None] * 3, refs)
    turned, parts, sent, got, mix_out, mix_in, row_out, row_in = refs[:8]
    layer = GradientSum(nb, nv, grads, refs[8:], totals, sums) if first else None
    b, v = lax.axis_index("batch"), lax.axis_index("vocab")
    width, rows = out_ref.shape
    meet((("batch", nb), ("vocab", nv)))
    turned[...] = x_ref[...].T.reshape(nb, width, SEQ_LEN)

    def mix_copy(step):
        other = lax.rem(b + step, nb)
        return send(turned.at[other], parts.at[b], mix_out.at[step], mix_in.at[step], {"batch": other})

    for step in range(1, nb):
        mix_copy(step).start()
    if first:
        layer.start()
        layer.reduce(2)
    parts[b] = turned[b]
    for step in range(1, nb):
        mix_copy(step).wait()

    def quarter_place():
        size = quarter_ref.shape[1]
        return dw_ref.at[:, lanes(b * size, size)]

    def quarter_copy(step):
        other = lax.rem(b + step, nb)
        source = quarter_ref.at[pl.ds(pl.multiple_of(other * width, 16), width), :]
        return send(source, quarter_place(), quarter_out.at[step], quarter_in.at[step], {"batch": other})

    def quarter_keep():
        source = quarter_ref.at[pl.ds(pl.multiple_of(b * width, 16), width), :]
        return pltpu.make_async_copy(source, quarter_place(), quarter_own.at[0])

    def row_copy(step):
        return send(
            sent.at[step], got.at[v], row_out.at[step], row_in.at[step], {"vocab": lax.rem(v + step, nv)}
        )

    def build(turn):
        step = lax.rem(turn, nv)
        owner = lax.rem(v + step, nv)
        blocks = []
        for p in range(nb):
            key = jnp.where(place_ref[p, 0:1, :] == owner, place_ref[p, 1:2, :], -1)
            hot = (iota((cap, SEQ_LEN), 0) == key).astype(FL).astype(BF)
            blocks.append(nt(parts[p], hot).astype(BF))
        block = jnp.concatenate(blocks, axis=1)

        @pl.when(step > 0)
        def _():
            sent[step] = block
            row_copy(step).start()

        @pl.when(step == 0)
        def _():
            got[v] = block

    if first:
        layer.scatter(3)
    each(1, nv // 2 + 1, build)
    if first:
        layer.collect(2)
    each(nv // 2 + 1, nv + 1, build)
    if first:
        layer.scatter(0)
    if split:
        quarter_keep().start()
    out_ref[...] = jnp.zeros_like(out_ref)

    def take(step):
        source = lax.rem(v - step + nv, nv)

        @pl.when(step > 0)
        def _():
            row_copy(step).wait()

        block, index = got[source], ids_ref[source]

        def piece(j):
            hot = (index - j * part == iota((nb * cap, part), 1)).astype(FL).astype(BF)
            out_ref[:, lanes(j * part, part)] += nn(block, hot)

        each(0, rows // part, piece)

    if first:
        quarter = nv // 4
        each(0, quarter, take)
        layer.reduce(3)
        layer.scatter(1)
        if split:
            for step in range(1, nb):
                quarter_copy(step).start()
        each(quarter, 2 * quarter, take)
        layer.reduce(0)
        each(2 * quarter, 3 * quarter, take)
        layer.collect(3)
        layer.reduce(1)
        each(3 * quarter, nv, take)
        layer.collect(0)
        layer.collect(1)
        layer.finish()
        if split:
            quarter_keep().wait()
            for step in range(1, nb):
                quarter_copy(step).wait()
    else:
        each(0, nv, take)


def unembed(nb, nv, cap, width, rows, grad, ids, place, grads=(), quarter=None):
    part = chunk_of(rows, 640)
    count = nb * cap
    dma = pltpu.SemaphoreType.DMA
    scratch = [
        pltpu.VMEM((nb, width, SEQ_LEN), BF),
        pltpu.VMEM((nb, width, SEQ_LEN), BF),
        pltpu.VMEM((nv, width, count), BF),
        pltpu.VMEM((nv, width, count), BF),
        dma((nb,)), dma((nb,)), dma((nv,)), dma((nv,)),
    ]
    first, split = len(grads) > 0, quarter is not None
    if split:
        scratch = [dma((nb,)), dma((nb,)), dma((1,))] + scratch
    if first:
        shapes = [item.shape if w != 2 else (nb * item.shape[0], 2 * item.shape[1]) for w, item in enumerate(grads)]
        scratch += gradient_scratch(nb, nv, shapes, (0, 1, 3))
    outs = [SD((width, rows), FL)] + [SD((item[0] // nb, item[1]), BF) for item in (shapes if first else ())]
    extra = [quarter] if split else []
    if split:
        outs.append(SD((width, nb * quarter.shape[1]), BF))
    return run(
        functools.partial(unembed_kernel, nb, nv, cap, part, first, split),
        outs,
        scratch,
        [grad, ids, place, *grads, *extra],
        "unembed" if first else "unembed_more",
        2 if first else 4,
        in_specs=[VM] * 3 + ([HB, HB, VM, HB] if first else []) + [VM] * len(extra),
        out_specs=[VM] + [HB] * (len(grads) + len(extra)),
    )


def later_slots(nv, cap, rows, every, turn):
    nb = every.shape[0]
    v = lax.axis_index("vocab")
    local = every - v * rows
    mine = (local >= 0) & (local < rows)
    rank = jnp.cumsum(mine.astype(I32), axis=-1) - 1 - turn * cap
    hot = (rank[:, :, None, :] == jnp.arange(cap)[None, None, :, None]) & mine[:, :, None, :]
    ids = jnp.sum(jnp.where(hot, local[:, :, None, :], 0), axis=-1)
    return jnp.transpose(ids, (1, 0, 2)).reshape(nv, nb * cap, 1)


def standard(value):
    centre = value - jnp.mean(value, axis=-1, keepdims=True)
    spread = jnp.mean(centre * centre, axis=-1, keepdims=True)
    scale = lax.rsqrt(spread + NORM_EPS)
    return centre * scale, scale


def norm_back(unit, scale, gain, upstream):
    inner = upstream * gain
    first = jnp.mean(inner, axis=-1, keepdims=True)
    second = jnp.mean(inner * unit, axis=-1, keepdims=True)
    grad = scale * (inner - first - unit * second)
    return grad, jnp.sum(upstream * unit, axis=0, keepdims=True), jnp.sum(upstream, axis=0, keepdims=True)


def head_lanes(value, head):
    lane = iota(value.shape, 1)
    keep = (lane < HD) if head == 0 else (lane >= HD)
    return jnp.where(keep, value, jnp.zeros_like(value))


def visible_keys(seg_ref, pos_ref):
    position = pos_ref[...]
    block = position // BLK
    marks = [seg_ref[:, i * BLK : i * BLK + 1] for i in range(SEQ_LEN // BLK)]
    segment = jnp.zeros_like(position)
    for i, mark in enumerate(marks):
        segment = jnp.where(block == i, mark, segment)
    row = iota((BLK, PICKS), 0)
    parts = [jnp.broadcast_to(segment == slot + 1, (NB, PICKS)) for slot in range(SLOTS)]
    parts += [(segment == mark) & (row + i * BLK <= position) for i, mark in enumerate(marks)]
    return parts


def masked(visible, scores):
    return jnp.concatenate(
        [jnp.where(keep, scores[i * BLK : (i + 1) * BLK, :], NEG_BIG) for i, keep in enumerate(visible)], axis=0
    )


def memory_weights(segments, slot):
    length = segments.shape[1]
    inside = (segments == slot).astype(FL)
    start = jnp.sum((segments < slot).astype(FL), axis=1, keepdims=True)
    count = jnp.sum(inside, axis=1, keepdims=True)
    times = (iota((1, length), 1).astype(FL) - start + 0.5) / jnp.maximum(count, 1.0)
    centres = (iota((NB, 1), 0).astype(FL) + 0.5) / NB
    offset = (times - centres) * NB
    basis = jnp.exp(-0.5 * offset * offset) * inside
    total = jnp.sum(basis, axis=1, keepdims=True) + (count == 0.0).astype(FL)
    return basis / total


def attend_kernel(
    nb, nv, x_ref, a_ref, seg_ref, pos_ref, p_ref, c_ref,
    hall_ref, kv_ref, q_ref, hq_ref, xq_ref, o_ref, lse_ref, norm_ref, mixt_ref, p_all, c_all, *sems,
):
    meet((("batch", nb), ("vocab", nv)))
    gather = WeightGather(nb, (p_ref, c_ref), (p_all, c_all), *sems)
    gather.start()
    norm_ref[...] = a_ref[:, 3 * D : 3 * D + 128].astype(FL).T[:8, :]
    gain, bias = norm_ref[0:1, :], norm_ref[3:4, :]

    def normalize(i):
        unit, _ = standard(x_ref[pl.ds(i * BLK, BLK), :].astype(FL))
        hall_ref[pl.ds(SLOTS * NB + i * BLK, BLK), :] = (unit * gain + bias).astype(BF)

    each(0, SEQ_LEN // BLK, normalize)
    normed = hall_ref[SLOTS * NB :, :]
    for slot in range(SLOTS):
        mixing = memory_weights(seg_ref[...], slot).astype(BF)
        hall_ref[slot * NB : (slot + 1) * NB, :] = nn(mixing, normed).astype(BF)
        mixt_ref[:, slot * NB : (slot + 1) * NB] = mixing.T

    def project(i):
        kv_ref[pl.ds(i * BLK, BLK), :] = nn(hall_ref[pl.ds(i * BLK, BLK), :], a_ref[:, D : 3 * D]).astype(BF)

    each(0, KEYS // BLK, project)
    pick = (pos_ref[...] == iota((SEQ_LEN, PICKS), 0)).astype(FL).astype(BF).T
    hq_ref[...] = nn(pick, normed).astype(BF)
    xq_ref[...] = nn(pick, x_ref[...])
    q_ref[...] = nn(hq_ref[...], a_ref[:, :D]).astype(BF)
    visible = visible_keys(seg_ref, pos_ref)

    def attend(p):
        keys = kv_ref[:, lanes(p * PAIR, PAIR)]
        values = kv_ref[:, lanes(D + p * PAIR, PAIR)].T
        queries = q_ref[:, lanes(p * PAIR, PAIR)] * HD ** (-0.5)
        outs = []
        for head in range(2):
            scores = masked(visible, nt(keys, head_lanes(queries, head)))
            peak = jnp.max(scores, axis=0, keepdims=True)
            expo = jnp.exp(scores - peak)
            total = jnp.sum(expo, axis=0, keepdims=True)
            probs = (expo * (1.0 / total)).astype(BF)
            outs.append(nn(values[head * HD : (head + 1) * HD, :], probs))
            lse_ref[p, head : head + 1, :] = peak + jnp.log(total)
        o_ref[:, lanes(p * PAIR, PAIR)] = jnp.concatenate(outs, axis=0).T.astype(BF)

    gather.pass_on()
    each(0, NPAIR, attend)
    gather.finish()


def feed_kernel(xq_ref, o_ref, p_ref, u_ref, c_ref, norm_ref, x1_ref, h2_ref, z_ref, act_ref, x2_ref, f_ref):
    x1 = xq_ref[...] + nn(o_ref[...], p_ref[...])
    x1_ref[...] = x1
    unit, _ = standard(x1)
    h2 = (unit * norm_ref[1:2, :] + norm_ref[4:5, :]).astype(BF)
    h2_ref[...] = h2
    x2_ref[...] = x1

    def piece(j):
        cut = lanes(j * D, D)
        z = nn(h2, u_ref[:, cut])
        z_ref[:, cut] = z
        act = jax.nn.gelu(z, approximate=True).astype(BF)
        act_ref[:, cut] = act
        x2_ref[...] += nn(act, c_ref[pl.ds(j * D, D), :])

    each(0, FF // D, piece)
    unit, _ = standard(x2_ref[...])
    f_ref[...] = (unit * norm_ref[2:3, :] + norm_ref[5:6, :]).astype(BF)


def feed_back_kernel(
    df_ref, x2_ref, x1_ref, h2_ref, z_ref, act_ref, o_ref, p_ref, u_ref, c_ref, norm_ref,
    dc_ref, du_ref, dp_ref, dx1_ref, do_ref, dnorm_ref, dh2,
):
    unit, scale = standard(x2_ref[...])
    dx2, gain_last, bias_last = norm_back(unit, scale, norm_ref[2:3, :], df_ref[...])
    dy = dx2.astype(BF)
    dh2[...] = jnp.zeros_like(dh2)
    h2t = h2_ref[...].T

    def piece(j):
        cut = lanes(j * D, D)
        dc_ref[pl.ds(j * D, D), :] = nn(act_ref[:, cut].T, dy).astype(BF)
        dact = nt(dy, c_ref[pl.ds(j * D, D), :])
        z = z_ref[:, cut]
        k = math.sqrt(2.0 / math.pi)
        t = jnp.tanh(k * (z + 0.044715 * z * z * z))
        slope = 0.5 * (1.0 + t) + 0.5 * z * (1.0 - t * t) * (k * (1.0 + 3 * 0.044715 * z * z))
        dz = (dact * slope).astype(BF)
        du_ref[:, cut] = nn(h2t, dz).astype(BF)
        dh2[...] += nt(dz, u_ref[:, cut])

    each(0, FF // D, piece)
    unit, scale = standard(x1_ref[...])
    dx1, gain_two, bias_two = norm_back(unit, scale, norm_ref[1:2, :], dh2[...])
    dx1 = dx1 + dx2
    dx1_ref[...] = dx1
    da = dx1.astype(BF)
    dp_ref[...] = nn(o_ref[...].T, da).astype(BF)
    do_ref[...] = nt(da, p_ref[...]).astype(BF)
    zero = jnp.zeros_like(gain_last)
    dnorm_ref[...] = jnp.concatenate([zero, gain_two, gain_last, zero, bias_two, bias_last, zero, zero], axis=0)


def attend_back_kernel(
    nb, nv, do_ref, q_ref, kv_ref, lse_ref, hall_ref, hq_ref, a_ref, x_ref, dx1_ref, mixt_ref, seg_ref, row_ref,
    norm_ref, dnorm_ref, du_ref, da_ref, dx_ref, du_sum, dkv, dq, hallt, dh, dxin, dmem, sel, *refs,
):
    meet((("batch", nb), ("vocab", nv)))
    layer = GradientSum(nb, nv, (du_ref,), refs, {0: du_sum})
    layer.start()
    visible = visible_keys(seg_ref, row_ref)

    def attend(p):
        cut = lanes(p * PAIR, PAIR)
        keys = kv_ref[:, cut]
        values = kv_ref[:, lanes(D + p * PAIR, PAIR)]
        turned = keys.T
        queries = q_ref[:, cut] * HD ** (-0.5)
        grads = do_ref[:, cut]
        outs = []
        dk = dv = None
        for head in range(2):
            own, grad = head_lanes(queries, head), head_lanes(grads, head)
            scores = masked(visible, nt(keys, own))
            probs = jnp.exp(scores - lse_ref[p, head : head + 1, :])
            dprobs = nt(values, grad)
            inner = jnp.sum(probs * dprobs, axis=0, keepdims=True)
            dscores = (probs * (dprobs - inner)).astype(BF)
            outs.append(nn(turned[head * HD : (head + 1) * HD, :], dscores))
            one, two = nn(dscores, own), nn(probs.astype(BF), grad)
            dk = one if head == 0 else dk + one
            dv = two if head == 0 else dv + two
        dq[:, cut] = (jnp.concatenate(outs, axis=0).T * HD ** (-0.5)).astype(BF)
        dkv[:, cut] = dk.astype(BF)
        dkv[:, lanes(D + p * PAIR, PAIR)] = dv.astype(BF)

    each(0, NPAIR // 2, attend)
    layer.scatter(0)
    each(NPAIR // 2, NPAIR, attend)
    da_ref[:, :D] = nn(hq_ref[...].T, dq[...]).astype(BF)

    def turn(i):
        hallt[:, lanes(i * BLK, BLK)] = hall_ref[pl.ds(i * BLK, BLK), :].T

    each(0, KEYS // BLK, turn)

    def weights(j):
        cut = lanes(j * BLK, BLK)
        da_ref[:, lanes(D + j * BLK, BLK)] = nn(hallt[...], dkv[:, cut]).astype(BF)

    each(0, 2 * D // BLK, weights)

    def memory(i):
        cut = pl.ds(i * BLK, BLK)
        dmem[cut, :] = nt(dkv[cut, :], a_ref[:, D : 3 * D]).astype(BF)

    each(0, SLOTS, memory)

    def local(i):
        cut = pl.ds(i * BLK, BLK)
        dh[cut, :] = nt(dkv[pl.ds(SLOTS * NB + i * BLK, BLK), :], a_ref[:, D : 3 * D]) + nn(mixt_ref[cut, :], dmem[...])

    each(0, SEQ_LEN // BLK, local)
    put = (row_ref[...] == iota((SEQ_LEN, PICKS), 0)).astype(FL).astype(BF)

    def scatter(target, value):
        for _ in range(3):
            part = value.astype(BF)
            value = value - part.astype(FL)

            def add(i, part=part):
                cut = pl.ds(i * BLK, BLK)
                target[cut, :] += nn(sel[cut, :], part)

            each(0, SEQ_LEN // BLK, add)

    sel[...] = put
    scatter(dh, nt(dq[...], a_ref[:, :D]))
    gain = norm_ref[0:1, :]
    da_rows = [jnp.zeros((1, D), FL), jnp.zeros((1, D), FL)]

    def finish(i, carry):
        cut = pl.ds(i * BLK, BLK)
        unit, scale = standard(x_ref[cut, :].astype(FL))
        grad, dgain, dbias = norm_back(unit, scale, gain, dh[cut, :])
        dxin[cut, :] = grad
        return carry[0] + dgain, carry[1] + dbias

    dgain, dbias = lax.fori_loop(0, SEQ_LEN // BLK, finish, tuple(da_rows))

    scatter(dxin, dx1_ref[...])
    dx_ref[...] = dxin[...].astype(BF)
    line = iota((8, D), 0)
    norms = dnorm_ref[...] + jnp.where(line == 0, dgain, jnp.where(line == 3, dbias, 0.0))
    tall = jnp.concatenate([norms, jnp.zeros((EXTRA - 8, D), FL)], axis=0)
    da_ref[:, 3 * D :] = tall.T.astype(BF)
    layer.gather(0)


def head_kernel(
    nb, nv, part, f_ref, w_ref, live_ref, target_ref, df_ref, dw_ref, loss_ref,
    fall, expo, block, mine, stats, ft, grad_sum, coef, df, half, far_got, out,
    near_out, near_in, far_out, far_in, stat_out, stat_in, pair_out, pair_in, sum_out, sum_in, dw_sem,
):
    v = lax.axis_index("vocab")
    rows = w_ref.shape[1]
    total_rows = nv * PICKS
    core, chip, chips = lax.rem(v, 2), v // 2, nv // 2
    sibling = {"vocab": v + 1 - 2 * core}
    base = v * rows
    pieces = rows // part
    depth = min(2, pieces)
    meet((("vocab", nv),))

    def peer(step):
        return {"vocab": lax.rem(chip + step, chips) * 2 + core}

    def far_copy(step):
        return send(f_ref, fall.at[v], far_out.at[step], far_in.at[step], peer(step))

    def near_copy(step):
        slot = lax.rem(chip - step + chips, chips) * 2 + core
        return send(fall.at[slot], fall.at[slot], near_out.at[step], near_in.at[step], sibling)

    fall[v] = f_ref[...]
    near_copy(0).start()
    each(1, chips, lambda step: far_copy(step).start())

    def logits(step):
        @pl.when(step > 0)
        def _():
            far_copy(step).wait_recv()
            near_copy(step).start()

        near_copy(step).wait_recv()
        source = lax.rem(chip - step + chips, chips)
        start = pl.multiple_of(source * 2 * PICKS, 2 * PICKS)
        features = fall[pl.ds(source * 2, 2)].reshape(2 * PICKS, D)
        target = target_ref[pl.ds(start, 2 * PICKS), :] - base

        def score(j, peak):
            cut = lanes(j * part, part)
            value = nn(features, w_ref[:, cut])
            block[:, cut] = value
            return jnp.maximum(
                peak, jnp.max(jnp.where(live_ref[0:1, cut] > 0, value, NEG_BIG), axis=1, keepdims=True)
            )

        peak = lax.fori_loop(0, pieces, score, jnp.full((2 * PICKS, 1), NEG_BIG, FL))

        def count(j, carry):
            total, picked, valid = carry
            cut = lanes(j * part, part)
            value = block[:, cut]
            live = live_ref[0:1, cut] > 0
            hot = target - j * part == iota((2 * PICKS, part), 1)
            e = jnp.where(live, jnp.exp(value - peak), 0.0)
            expo[pl.ds(start, 2 * PICKS), cut] = e.astype(BF)
            total = total + jnp.sum(e, axis=1, keepdims=True)
            picked = picked + jnp.sum(jnp.where(hot, value, 0.0), axis=1, keepdims=True)
            valid = valid + jnp.sum(jnp.where(hot & live, 1.0, 0.0), axis=1, keepdims=True)
            return total, picked, valid

        zero = jnp.zeros((2 * PICKS, 1), FL)
        total, picked, valid = lax.fori_loop(0, pieces, count, (zero, zero, zero))
        lane = iota((2 * PICKS, 128), 1)
        wide = jnp.where(lane == 0, peak, jnp.where(lane == 1, total, jnp.where(lane == 2, picked, valid)))
        mine[:, pl.ds(start, 2 * PICKS)] = wide.T[:8, :]

    each(0, chips, logits)

    def stat_copy(step):
        return send(mine, stats.at[v], stat_out.at[step], stat_in.at[step], {"vocab": lax.rem(v + step, nv)})

    each(1, nv, lambda step: stat_copy(step).start())
    stats[v] = mine[...]
    for i in range(total_rows // 256 if pieces > 1 else 0):
        ft[:, i * 256 : (i + 1) * 256] = fall[2 * i : 2 * i + 2].reshape(256, D).T
    each(1, nv, lambda step: stat_copy(step).wait())
    start = jnp.full((1, total_rows), NEG_BIG, FL)
    peak = lax.fori_loop(0, nv, lambda u, top: jnp.maximum(top, stats[u, 0:1, :]), start)

    def combine(u, carry):
        scale = jnp.exp(stats[u, 0:1, :] - peak)
        return (
            carry[0] + stats[u, 1:2, :] * scale, carry[1] + stats[u, 2:3, :], carry[2] + stats[u, 3:4, :],
        )

    zero = jnp.zeros((1, total_rows), FL)
    total, picked, valid = lax.fori_loop(0, nv, combine, (zero, zero, zero))
    lse = peak + jnp.log(jnp.maximum(total, 1e-37))
    weight = valid / (jnp.maximum(jnp.sum(valid, axis=1, keepdims=True), 1.0) * nb)
    loss = jnp.sum(weight * (lse - picked), axis=1, keepdims=True)
    loss_ref[...] = jnp.broadcast_to(loss, loss_ref.shape)
    alpha = weight * jnp.exp(mine[0:1, :] - lse)
    line = iota((128, 256), 0)
    for i in range(total_rows // 256):
        cut = slice(i * 256, (i + 1) * 256)
        coef[cut, :] = jnp.where(line == 0, alpha[:, cut], weight[:, cut]).T

    tall = min(total_rows, 1024 if pieces > 1 else 256)
    shards_tall = tall // PICKS
    df[...] = jnp.zeros_like(df)

    def out_copy(j):
        return pltpu.make_async_copy(
            out.at[lax.rem(j, depth)], dw_ref.at[:, lanes(j * part, part)], dw_sem.at[lax.rem(j, depth)]
        )

    def gradients(j):
        cut = lanes(j * part, part)
        words = w_ref[:, cut]

        @pl.when(j >= depth)
        def _():
            out_copy(j - depth).wait()

        def strip(t):
            start = t * tall if total_rows == tall else pl.multiple_of(t * tall, tall)
            here = pl.ds(start, tall)
            hot = target_ref[here, :] - base - j * part == iota((tall, part), 1)
            two = coef[here, :]
            value = two[:, 0:1] * expo[here, cut].astype(FL) - jnp.where(hot, two[:, 1:2], 0.0)
            dlogits = value.astype(BF)
            df[here, :] += nt(dlogits, words)
            if pieces > 1:
                turned = ft[:, pl.ds(start, tall)]
            else:
                turned = fall[pl.ds(t * shards_tall, shards_tall)].reshape(tall, D).T
            for r in range(0, D, D // 3):
                more = nn(turned[r : r + D // 3, :], dlogits)
                if total_rows == tall:
                    out[lax.rem(j, depth), r : r + D // 3, :] = more.astype(BF)
                else:
                    grad_sum[r : r + D // 3, :] += more

        if total_rows == tall:
            strip(0)
        else:
            grad_sum[...] = jnp.zeros_like(grad_sum)
            each(0, total_rows // tall, strip)
            for r in range(0, D, D // 3):
                out[lax.rem(j, depth), r : r + D // 3, :] = grad_sum[r : r + D // 3, :].astype(BF)
        out_copy(j).start()

    each(0, pieces, gradients)

    def shard(index):
        return pl.ds(pl.multiple_of(index * PICKS, PICKS), PICKS)

    def pair_copy(k):
        source = df.at[shard(2 * k + 1 - core), :] if pieces > 1 else fall.at[k]
        return send(source, half.at[k], pair_out.at[k], pair_in.at[k], sibling)

    near_copy(0).wait_send()

    def drain(step):
        far_copy(step).wait_send()
        near_copy(step).wait_send()

    each(1, chips, drain)

    def swap(k):
        if pieces == 1:
            fall[k] = df[shard(2 * k + 1 - core), :].astype(BF)
        pair_copy(k).start()

    each(0, chips, swap)

    def sum_copy(step):
        return send(fall.at[chips + step], far_got.at[step], sum_out.at[step], sum_in.at[step], peer(step))

    def pass_on(turn):
        step = lax.rem(turn, chips)
        k = lax.rem(chip + step, chips)
        pair_copy(k).wait()
        value = df[shard(2 * k + core), :] + half[k].astype(FL)

        @pl.when(step > 0)
        def _():
            fall[chips + step] = value.astype(BF)
            sum_copy(step).start()

        @pl.when(step == 0)
        def _():
            df_ref[...] = value

    each(1, chips + 1, pass_on)

    def collect(step):
        sum_copy(step).wait()
        df_ref[...] += far_got[step].astype(FL)

    each(1, chips, collect)
    for j in range(pieces - depth, pieces):
        out_copy(j).wait()


def head(nb, nv, features, words, live, targets):
    rows = words.shape[1]
    part = chunk_of(rows, 640)
    total_rows = nv * PICKS
    chips = nv // 2
    dma = pltpu.SemaphoreType.DMA
    scratch = [
        pltpu.VMEM((nv, PICKS, D), BF),
        pltpu.VMEM((total_rows, rows), BF),
        pltpu.VMEM((2 * PICKS, rows), FL),
        pltpu.VMEM((8, total_rows), FL),
        pltpu.VMEM((nv, 8, total_rows), FL),
        pltpu.VMEM((D, total_rows) if rows > part else (8, 128), BF),
        pltpu.VMEM((8, 128) if rows > part else (D, part), FL),
        pltpu.VMEM((total_rows, 128), FL),
        pltpu.VMEM((total_rows, D), FL),
        pltpu.VMEM((chips, PICKS, D), FL if rows > part else BF),
        pltpu.VMEM((chips, PICKS, D), BF),
        pltpu.VMEM((min(2, rows // part), D, part), BF),
        dma((chips,)), dma((chips,)), dma((chips,)), dma((chips,)), dma((nv,)), dma((nv,)),
        dma((chips,)), dma((chips,)), dma((chips,)), dma((chips,)), dma((2,)),
    ]
    return run(
        functools.partial(head_kernel, nb, nv, part),
        [SD((PICKS, D), FL), SD((D, rows), BF), SD((8, 128), FL)],
        scratch,
        [features, words, live, targets],
        "head",
        1,
        out_specs=[VM, HB, VM],
    )


def wide_head_kernel(
    nb, nv, block_rows, f_ref, w_ref, live_ref, target_ref, df_ref, dw_ref, loss_ref,
    fall, ft, expo, words_sum, mine, first_got, merged, second_got, tile, third_got, tiles, coef, group, half, handed, mix_got,
    far_sum, far_got,
    z_out, z_in, mix_out, mix_in, near_out, near_in, s_out, s_in, pair_out, pair_in, give_out, give_in, sum_out, sum_in,
):
    b, v = lax.axis_index("batch"), lax.axis_index("vocab")
    rows = w_ref.shape[1]
    core, chip, chips = lax.rem(v, 2), v // 2, nv // 2
    sibling = {"vocab": v + 1 - 2 * core}
    base = v * block_rows + b * rows
    live = live_ref[:, lanes(b * rows, rows)] > 0
    span = nv * PICKS
    meet((("batch", nb), ("vocab", nv)))

    def column(line):
        line = jnp.where(line < (v + 1) * block_rows, line - base, -1).astype(FL)
        return jnp.broadcast_to(line, (128, 2 * PICKS)).T[:, 0:1].astype(I32)

    def peer(step):
        return {"vocab": lax.rem(chip + step, chips) * 2 + core}

    def other(step):
        return {"batch": lax.rem(b + step, nb)}

    def flip(s):
        low, high = lax.rem(b, 2), b // 2
        return (high if s < 2 else 1 - high) * 2 + (low if s % 2 == 0 else 1 - low)

    def slot(s, k):
        return flip(s) * nv + lax.rem(chip - k + chips, chips) * 2 + core

    def z_copy(k):
        return send(f_ref, fall.at[b * nv + v], z_out.at[k], z_in.at[k], peer(k))

    def mix_copy(s, k, way=0):
        if s < 3:
            place, device = fall.at[slot(0, k)], flip(s)
        else:
            place, device = fall.at[slot(3 - way, k)], flip(way)
        return send(place, place, mix_out.at[k, s], mix_in.at[k, s], {"batch": device})

    near = [s for s in (1, 2) if s < nb]

    def near_copy(s, k):
        place = fall.at[slot(s, k)]
        return send(place, place, near_out.at[k, s], near_in.at[k, s], sibling)

    def arrive(s, k):
        if s == 0:

            @pl.when(k > 0)
            def _():
                z_copy(k).wait_recv()

            for t in near:
                mix_copy(t, k).start()
        else:
            mix_copy(s, k, 1).wait_recv()
        if nb == 4 and s in (1, 2):

            @pl.when(lax.rem(k, 2) == s - 1)
            def _():
                mix_copy(3, k, 3 - s).start()

        near_copy(s, k).start()

    fall[b * nv + v] = f_ref[...]
    each(1, chips, lambda k: z_copy(k).start())
    arrive(0, 0)

    def logits(s, k):
        near_copy(s, k).wait_recv()
        p, c = flip(s), lax.rem(chip - k + chips, chips)
        first = p * nv + c * 2
        start = pl.multiple_of(first * PICKS, 2 * PICKS)
        features = fall[pl.ds(first, 2)].reshape(2 * PICKS, D)
        ft[:, pl.ds(start, 2 * PICKS)] = features.T
        line = target_ref[p, :, pl.ds(pl.multiple_of(c * 2 * PICKS, 2 * PICKS), 2 * PICKS)]
        target = column(line)
        value = nn(features, w_ref[...])
        value = jnp.where(live, value, NEG_BIG)
        peak = jnp.maximum(jnp.max(value, axis=1, keepdims=True), 0.1 * NEG_BIG)
        e = jnp.exp(value - peak)
        expo[pl.ds(start, 2 * PICKS), :] = e.astype(BF)
        total = jnp.sum(e, axis=1, keepdims=True)
        picked = jnp.sum(jnp.where(target == iota((2 * PICKS, rows), 1), value, 0.0), axis=1, keepdims=True)
        lane = iota((2 * PICKS, 128), 1)
        wide = jnp.where(lane == 0, peak, jnp.where(lane == 1, total, picked)).T
        mine[c * 2, p] = wide[:8, :PICKS]
        mine[c * 2 + 1, p] = wide[:8, PICKS:]

    for s in range(nb):

        def one(k, s=s):
            @pl.when(k + 1 < chips)
            def _():
                arrive(s, k + 1)

            if s + 1 < nb:

                @pl.when(k + 1 == chips)
                def _():
                    arrive(s + 1, 0)

            logits(s, k)

        each(0, chips, one)

    def merge(read, count):
        peak = lax.fori_loop(
            0, count, lambda u, top: jnp.maximum(top, read(u)[0:1, :]), jnp.full((1, PICKS), NEG_BIG, FL)
        )

        def add(u, carry):
            one = read(u)
            return carry[0] + one[1:2, :] * jnp.exp(one[0:1, :] - peak), carry[1] + one[2:3, :]

        zero = jnp.zeros((1, PICKS), FL)
        return (peak, *lax.fori_loop(0, count, add, (zero, zero)))

    def tile_of(rows_of):
        line = iota((8, PICKS), 0)
        value = jnp.zeros((8, PICKS), FL)
        for i, row in enumerate(rows_of):
            value = jnp.where(line == i, row, value)
        return value

    def first_copy(t):
        u = lax.rem(v + t, nv)
        return send(mine.at[u], first_got.at[v], s_out.at[0, t], s_in.at[0, t], {"vocab": u})

    each(1, nv, lambda t: first_copy(t).start())
    first_got[v] = mine[v]
    each(1, nv, lambda t: first_copy(t).wait())
    for p in range(nb):
        merged[p] = tile_of(merge(lambda u, p=p: first_got[u, p], nv))

    def second_copy(t):
        return send(merged.at[lax.rem(b + t, nb)], second_got.at[b], s_out.at[1, t], s_in.at[1, t], other(t))

    each(1, nb, lambda t: second_copy(t).start())
    second_got[b] = merged[b]
    each(1, nb, lambda t: second_copy(t).wait())
    peak, total, picked = merge(lambda u: second_got[u], nb)
    valid = (picked > 0.5 * NEG_BIG).astype(FL)
    tile[...] = tile_of((peak + jnp.log(jnp.maximum(total, 1e-37)), picked, valid))

    def third_copy(t):
        return send(tile, third_got.at[b], s_out.at[2, t], s_in.at[2, t], other(t))

    each(1, nb, lambda t: third_copy(t).start())
    third_got[b] = tile[...]
    each(1, nb, lambda t: third_copy(t).wait())

    def last_copy(t):
        return send(third_got, tiles.at[v], s_out.at[3, t], s_in.at[3, t], {"vocab": lax.rem(v + t, nv)})

    each(1, nv, lambda t: last_copy(t).start())
    tiles[v] = third_got[...]
    each(1, nv, lambda t: last_copy(t).wait())

    def coefficients(p):
        count = lax.fori_loop(0, nv, lambda u, total: total + tiles[u, p, 2:3, :], jnp.zeros((1, PICKS), FL))
        share = 1.0 / (jnp.maximum(jnp.sum(count, axis=1, keepdims=True), 1.0) * nb)

        def spread(c, loss):
            rows_of = []
            for side in range(2):
                u = c * 2 + side
                lse, picked, valid = (tiles[u, p, i : i + 1, :] for i in range(3))
                weight = valid * share
                loss = loss + weight * (lse - picked)
                rows_of.append((weight * jnp.exp(mine[u, p, 0:1, :] - lse), weight))
            line = iota((128, 2 * PICKS), 0)
            alpha = jnp.concatenate([rows_of[0][0], rows_of[1][0]], axis=1)
            weight = jnp.concatenate([rows_of[0][1], rows_of[1][1]], axis=1)
            start = pl.multiple_of(p * span + c * 2 * PICKS, 2 * PICKS)
            coef[pl.ds(start, 2 * PICKS), :] = jnp.where(line == 0, alpha, weight).T
            return loss

        loss = lax.fori_loop(0, chips, spread, jnp.zeros((1, PICKS), FL))

        @pl.when(p == b)
        def _():
            loss_ref[...] = jnp.broadcast_to(jnp.sum(loss, axis=1, keepdims=True), loss_ref.shape)

    each(0, nb, coefficients)

    def shard(k, side):
        return pl.ds(pl.multiple_of((2 * k + side) * PICKS, PICKS), PICKS)

    def pair_copy(s, k):
        return send(handed.at[s, k], half.at[s, k], pair_out.at[s, k], pair_in.at[s, k], sibling)

    def give_copy(s, k):
        if s < 3:
            return send(handed.at[s, k], mix_got.at[s, k], give_out.at[s, k], give_in.at[s, k], {"batch": flip(s)})
        device = jnp.where(lax.rem(k, 2) == 0, flip(1), flip(2))
        return send(handed.at[3, k], mix_got.at[3, k], give_out.at[3, k], give_in.at[3, k], {"batch": device})

    def exchange(s):
        def add(k):
            pair_copy(s, k).wait()
            value = group[s % 2, shard(k, core), :] + half[s, k].astype(FL)
            handed[s, k] = value.astype(BF)
            if nb == 4 and s in (1, 2):

                @pl.when(lax.rem(k, 2) == 2 - s)
                def _():
                    give_copy(3, k).wait_recv()
                    handed[s, k] = (value + mix_got[3, k].astype(FL)).astype(BF)

            if s > 0:
                give_copy(s, k).start()

        each(0, chips, add)

    order = [3, 2, 1, 0] if nb == 4 else [1, 0]
    for turn, s in enumerate(order):
        p = flip(s)

        def strip(c, p=p):
            start = pl.multiple_of(p * span + c * 2 * PICKS, 2 * PICKS)
            here = pl.ds(start, 2 * PICKS)
            line = target_ref[p, :, pl.ds(pl.multiple_of(c * 2 * PICKS, 2 * PICKS), 2 * PICKS)]
            target = column(line)
            two = coef[here, :]
            hot = target == iota((2 * PICKS, rows), 1)
            value = two[:, 0:1] * expo[here, :].astype(FL) - jnp.where(hot, two[:, 1:2], 0.0)
            expo[here, :] = value.astype(BF)

        each(0, chips, strip)
        if turn > 0:
            exchange(order[turn - 1])

        def features_grad(i, p=p, s=s):
            here = pl.ds(pl.multiple_of(i * 512, 512), 512)
            group[s % 2, here, :] = nt(expo[pl.ds(pl.multiple_of(p * span + i * 512, 512), 512), :], w_ref[...])

        each(0, span // 512, features_grad)

        def swap(k, s=s):
            handed[s, k] = group[s % 2, shard(k, 1 - core), :].astype(BF)
            pair_copy(s, k).start()

        each(0, chips, swap)

    words_sum[...] = jnp.zeros_like(words_sum)

    def words_grad(i):
        cut = lanes(i * 512, 512)
        words_sum[...] += nn(ft[:, cut], expo[cut, :])

    strips = nb * span // 512
    each(0, 1, words_grad)
    exchange(0)
    each(1, strips // 2, words_grad)

    def total_of(k):
        value = handed[0, k].astype(FL)
        for s in near:
            give_copy(s, k).wait_recv()
            value = value + mix_got[s, k].astype(FL)
        return value

    def sum_copy(t):
        return send(far_sum.at[t], far_got.at[t], sum_out.at[t], sum_in.at[t], peer(t))

    def pass_on(t):
        far_sum[t] = total_of(lax.rem(chip + t, chips)).astype(BF)
        sum_copy(t).start()

    each(1, chips, pass_on)
    each(strips // 2, strips, words_grad)
    dw_ref[...] = words_sum[...].astype(BF)
    df_ref[...] = total_of(chip)

    def collect(t):
        sum_copy(t).wait()
        df_ref[...] += far_got[t].astype(FL)

    each(1, chips, collect)
    each(1, chips, lambda k: z_copy(k).wait_send())
    for s in range(nb):
        each(0, chips, lambda k, s=s: near_copy(s, k).wait_send())
        if s > 0:
            each(0, chips, lambda k, s=s: mix_copy(s, k, 1).wait_send())
            each(0, chips, lambda k, s=s: give_copy(s, k).wait_send())


def wide_head(nb, nv, block_rows, features, words, live, targets):
    rows = words.shape[1]
    tokens = nb * nv * PICKS
    chips = nv // 2
    dma = pltpu.SemaphoreType.DMA
    most = max(nb, nv)
    scratch = [
        pltpu.VMEM((nb * nv, PICKS, D), BF),
        pltpu.VMEM((D, tokens), BF),
        pltpu.VMEM((tokens, rows), BF),
        pltpu.VMEM((D, rows), FL),
        pltpu.VMEM((nv, nb, 8, PICKS), FL),
        pltpu.VMEM((nv, nb, 8, PICKS), FL),
        pltpu.VMEM((nb, 8, PICKS), FL),
        pltpu.VMEM((nb, 8, PICKS), FL),
        pltpu.VMEM((8, PICKS), FL),
        pltpu.VMEM((nb, 8, PICKS), FL),
        pltpu.VMEM((nv, nb, 8, PICKS), FL),
        pltpu.VMEM((tokens, 128), FL),
        pltpu.VMEM((2, nv * PICKS, D), FL),
        pltpu.VMEM((nb, chips, PICKS, D), BF),
        pltpu.VMEM((nb, chips, PICKS, D), BF),
        pltpu.VMEM((nb, chips, PICKS, D), BF),
        pltpu.VMEM((chips, PICKS, D), BF),
        pltpu.VMEM((chips, PICKS, D), BF),
        dma((chips,)), dma((chips,)), dma((chips, nb)), dma((chips, nb)), dma((chips, nb)), dma((chips, nb)),
        dma((4, most)), dma((4, most)), dma((nb, chips)), dma((nb, chips)), dma((nb, chips)), dma((nb, chips)),
        dma((chips,)), dma((chips,)),
    ]
    return run(
        functools.partial(wide_head_kernel, nb, nv, block_rows),
        [SD((PICKS, D), FL), SD((D, rows), BF), SD((8, 128), FL)],
        scratch,
        [features, words, live, targets],
        "wide_head",
        1,
    )


def norm_kernel(
    nb, nv, extra_ref, dw_ref, a_ref, p_ref, u_ref, c_ref, loss_ref, out_ref,
    mine, near, lines, vocab_out, vocab_in, batch_out, batch_in,
):
    b, v = lax.axis_index("batch"), lax.axis_index("vocab")
    meet((("batch", nb), ("vocab", nv)))

    def squares(refs, part):
        cols = refs[0].shape[1]

        def add(j, total):
            value = refs[0][:, lanes(j * part, part)].astype(FL)
            for ref in refs[1:]:
                value = value + ref[:, lanes(j * part, part)].astype(FL)
            return total + jnp.sum(value * value, axis=0, keepdims=True)

        line = lax.fori_loop(0, cols // part, add, jnp.zeros((1, part), FL))
        return jnp.sum(line, axis=1, keepdims=True)

    own = squares((extra_ref, dw_ref), chunk_of(extra_ref.shape[1], 640))
    layer = squares((a_ref,), 512) + squares((p_ref,), 384) + squares((u_ref,), 512) + squares((c_ref,), 384)
    own = own + jnp.where(v == 0, layer, jnp.zeros_like(layer))
    line = iota((8, 128), 0)
    mine[...] = jnp.where(line == 0, own, jnp.where((line == 1) & (v == 0), loss_ref[...], 0.0))

    def vocab_copy(step):
        return send(mine, near.at[v], vocab_out.at[step], vocab_in.at[step], {"vocab": lax.rem(v + step, nv)})

    each(1, nv, lambda step: vocab_copy(step).start())
    near[v] = mine[...]
    each(1, nv, lambda step: vocab_copy(step).wait())
    mine[...] = lax.fori_loop(0, nv, lambda u, total: total + near[u], jnp.zeros((8, 128), FL))

    def batch_copy(step):
        return send(mine, lines.at[b], batch_out.at[step], batch_in.at[step], {"batch": lax.rem(b + step, nb)})

    each(1, nb, lambda step: batch_copy(step).start())
    lines[b] = mine[...]
    each(1, nb, lambda step: batch_copy(step).wait())
    out_ref[...] = lax.fori_loop(0, nb, lambda u, total: total + lines[u], jnp.zeros((8, 128), FL))


def norm(nb, nv, extra, dw, sums, loss):
    dma = pltpu.SemaphoreType.DMA
    return run(
        functools.partial(norm_kernel, nb, nv),
        [SD((8, 128), FL)],
        [
            pltpu.VMEM((8, 128), FL), pltpu.VMEM((nv, 8, 128), FL), pltpu.VMEM((nb, 8, 128), FL),
            dma((nv,)), dma((nv,)), dma((nb,)), dma((nb,)),
        ],
        [extra, dw, *sums, loss],
        "norm",
        5,
    )[0]


def adamw(weight, moment, square, gradient, clip, count, decay, rate):
    gradient = gradient * clip
    moment = BETA_ONE * moment + (1 - BETA_ONE) * gradient
    square = BETA_TWO * square + (1 - BETA_TWO) * gradient * gradient
    fixed_moment = moment / (1 - BETA_ONE**count)
    fixed_square = square / (1 - BETA_TWO**count)
    weight = weight - rate * (fixed_moment / (jnp.sqrt(fixed_square) + ADAM_EPS) + decay * weight)
    return (weight, moment, square)


def slot_size(nv):
    mean = SEQ_LEN // nv
    return -(-(mean + int(5.5 * math.sqrt(mean))) // 32) * 32


def shards(
    nb, nv,
    tokens, targets, segments, counted, vocab_mask, step_count,
    table, table_moment, table_square,
    attend, attend_moment, attend_square,
    project, project_moment, project_square,
    expand, expand_moment, expand_square,
    contract, contract_moment, contract_square,
    gain, gain_moment, gain_square,
    shift, shift_moment, shift_square,
):
    rows, width = table.shape
    cap = slot_size(nv)
    table_t = table.T
    norms = jnp.concatenate([gain, shift], axis=0)
    packed = jnp.concatenate([attend[0], norms.T, jnp.zeros((width, EXTRA - 6), FL)], axis=1).astype(BF)
    pieces = (packed, project[0].astype(BF), expand[0].astype(BF), contract[0].astype(BF))
    split = nb * nv * PICKS <= 4096
    rounded = table_t.astype(BF)
    quarter = -(-rows // (nb * 128)) * 128
    if split:
        rounded = jnp.pad(rounded, ((0, 0), (0, nb * quarter - rows)))
    else:
        words = lax.all_gather(rounded, "batch", axis=0, tiled=True)

    seg_row, pos_row = segments[None, :], counted[None, :]
    tok = tokens.reshape(nv, SEQ_LEN)
    x, ids, place, most, every, a_all, u_all, *rest = embed(
        nb, nv, cap, rows, jnp.zeros((1,), I32), tok, rounded, (pieces[0], pieces[2]),
        targets[None, :] if split else None,
    )
    turns = (most[0] + cap - 1) // cap

    def more_rows(state):
        turn, total = state
        return turn + 1, total + embed(nb, nv, cap, rows, turn[None], tok, rounded)[0]

    x = lax.while_loop(lambda state: state[0] < turns, more_rows, (jnp.int32(1), x))[1]

    hall, kv, q, hq, xq, mixed, lse, norm_rows, mixing_t, p_all, c_all = run(
        functools.partial(attend_kernel, nb, nv),
        [
            SD((KEYS, D), BF), SD((KEYS, 2 * D), BF), SD((PICKS, D), BF), SD((PICKS, D), BF), SD((PICKS, D), FL),
            SD((PICKS, D), BF), SD((NPAIR, 2, PICKS), FL), SD((8, D), FL), SD((SEQ_LEN, SLOTS * NB), BF),
            SD((D, D), BF), SD((FF, D), BF),
        ],
        weight_semaphores(2),
        [x, a_all, seg_row, pos_row, pieces[1], pieces[3]],
        "attend", 6, flops=7 * 10**9, moved=20 * 10**6,
        out_specs=[VM] * 9 + [HB] * 2,
    )
    x1, h2, z, act, x2, features = run(
        feed_kernel,
        [
            SD((PICKS, D), FL), SD((PICKS, D), BF), SD((PICKS, FF), FL), SD((PICKS, FF), BF), SD((PICKS, D), FL),
            SD((PICKS, D), BF),
        ],
        [],
        [xq, mixed, p_all, u_all, c_all, norm_rows],
        "feed", flops=2 * 10**9, moved=15 * 10**6,
    )
    if split:
        live = jnp.pad(vocab_mask, (0, nb * quarter - rows))[None, :]
        df, dw, loss_block = wide_head(nb, nv, rows, features, rest[0], live, rest[1])
    else:
        df, dw, loss_block = head(nb, nv, features, words, vocab_mask[None, :], targets[:, None])
        dw_sum = lax.psum_scatter(dw, "batch", scatter_dimension=0, tiled=True)

    dc, du, dp, dx1, dmixed, dnorm = run(
        feed_back_kernel,
        [
            SD((FF, D), BF), SD((D, FF), BF), SD((D, D), BF), SD((PICKS, D), FL), SD((PICKS, D), BF), SD((8, D), FL),
        ],
        [pltpu.VMEM((PICKS, D), FL)],
        [df, x2, x1, h2, z, act, mixed, p_all, u_all, c_all, norm_rows],
        "feed_back", flops=4 * 10**9, moved=30 * 10**6,
    )
    da, dx, du_sum = run(
        functools.partial(attend_back_kernel, nb, nv),
        [SD((D, 3 * D + EXTRA), BF), SD((SEQ_LEN, D), BF), SD((width, FF // 2), BF)],
        [
            pltpu.VMEM((KEYS, 2 * D), BF), pltpu.VMEM((PICKS, D), BF), pltpu.VMEM((D, KEYS), BF),
            pltpu.VMEM((SEQ_LEN, D), FL), pltpu.VMEM((SEQ_LEN, D), FL), pltpu.VMEM((SLOTS * NB, D), BF),
            pltpu.VMEM((SEQ_LEN, PICKS), BF), *gradient_scratch(nb, nv, [du.shape], (0,), False),
        ],
        [dmixed, q, kv, lse, hall, hq, a_all, x, dx1, mixing_t, seg_row, pos_row, norm_rows, dnorm, du],
        "attend_back", 7, flops=12 * 10**9, moved=25 * 10**6,
        in_specs=[VM] * 14 + [HB],
    )
    extra, *sums = unembed(nb, nv, cap, width, rows, dx, ids, place, (da, dp, du_sum, dc), dw if split else None)
    if split:
        dw_sum = sums.pop()

    def more_grads(state):
        turn, total = state
        later = later_slots(nv, cap, rows, every, turn)
        return turn + 1, total + unembed(
            nb, nv, cap, width, rows, dx, later, place - jnp.array([0, 1, 0, 0, 0, 0, 0, 0], I32)[None, :, None] * (turn * cap)
        )[0]

    extra = lax.while_loop(lambda state: state[0] < turns, more_grads, (jnp.int32(1), extra))[1]

    totals = norm(nb, nv, extra, dw_sum, sums, loss_block)
    grad_table = dw_sum[:, :rows].astype(FL) + extra
    grad_a, grad_p, grad_u, grad_c = (item.astype(FL) for item in sums)
    grad_norms = grad_a[:, 3 * D : 3 * D + 6].T
    grad_a = grad_a[:, : 3 * D]
    squares, loss = totals[0, 0], totals[1, 0]
    gradient_norm = jnp.sqrt(squares)
    clip = jnp.minimum(1.0, MAX_NORM / (gradient_norm + 1e-06))
    count = step_count[0].astype(FL)

    def update(weight, moment, square, gradient, decay=DECAY, rate=LEARN_RATE):
        return adamw(weight, moment, square, gradient, clip, count, decay, rate)

    table_out = [item.T for item in update(table_t, table_moment.T, table_square.T, grad_table)]
    attend_out = update(attend, attend_moment, attend_square, grad_a[None])
    project_out = update(project, project_moment, project_square, grad_p[None])
    expand_out = update(expand, expand_moment, expand_square, grad_u[None])
    contract_out = update(contract, contract_moment, contract_square, grad_c[None])
    gain_out = update(gain, gain_moment, gain_square, grad_norms[:3], 0.0, NORM_RATE)
    shift_out = update(shift, shift_moment, shift_square, grad_norms[3:], 0.0, NORM_RATE)
    return (
        loss, gradient_norm, *table_out, *attend_out, *project_out, *expand_out, *contract_out, *gain_out, *shift_out,
    )


def solution(mesh):
    nb, nv = mesh.shape["batch"], mesh.shape["vocab"]
    both, split, middle, last = P(("batch", "vocab")), P("vocab", "batch"), P(None, "batch", None), P(None, "batch")
    state = (split,) * 3 + (middle,) * 12 + (last,) * 6
    return jax.shard_map(
        functools.partial(shards, nb, nv),
        mesh=mesh,
        in_specs=(P("batch"), P("batch"), both, both, P("vocab"), P()) + state,
        out_specs=(P(), P()) + state,
        check_vma=False,
    )
```

```python
import functools
import math

import jax
import jax.numpy as jnp
from jax import lax
from jax.experimental import pallas as pl
from jax.experimental.pallas import tpu as pltpu
from jax.sharding import PartitionSpec as P

D = 768
H = 12
HD = 64
FF = 3072
NB = 256
SEG_BLOCKS = 4
SLOTS = SEG_BLOCKS - 2
SEQ_LEN = 1024
PICKS = 128
KEYS = SLOTS * NB + SEQ_LEN
BLK = 256
PAIR = 2 * HD
NPAIR = H // 2
EXTRA = 256
WIDE = (3 * D + EXTRA, D, FF, D)

NORM_EPS = 1e-05
MAX_NORM = 0.02
LEARN_RATE = 0.04
NORM_RATE = 0.5
BETA_ONE = 0.9
BETA_TWO = 0.999
ADAM_EPS = 1e-08
DECAY = 0.1
NEG_BIG = -1e30
BF = jnp.bfloat16
FL = jnp.float32
I32 = jnp.int32
MESH = pl.DeviceIdType.MESH
SD = jax.ShapeDtypeStruct
VM = pl.BlockSpec(memory_space=pltpu.VMEM)
SM = pl.BlockSpec(memory_space=pltpu.SMEM)
HB = pl.BlockSpec(memory_space=pl.ANY)
LIMIT = 62 * 2**20


def nn(a, b):
    return lax.dot_general(a, b, (((1,), (0,)), ((), ())), preferred_element_type=FL)


def nt(a, b):
    return lax.dot_general(a, b, (((1,), (1,)), ((), ())), preferred_element_type=FL)


def iota(shape, axis):
    return lax.broadcasted_iota(I32, shape, axis)


def lanes(start, size):
    return pl.ds(pl.multiple_of(start, 128), size)


def chunk_of(rows, want):
    return want if rows % want == 0 else rows


def run(kernel, outs, scratch, ins, name, collective=None, flops=0, moved=0, out_specs=None, in_specs=None):
    return pl.pallas_call(
        kernel,
        out_shape=outs,
        in_specs=in_specs if in_specs is not None else [VM] * len(ins),
        out_specs=out_specs if out_specs is not None else [VM] * len(outs),
        scratch_shapes=scratch,
        compiler_params=pltpu.CompilerParams(
            vmem_limit_bytes=LIMIT,
            collective_id=collective,
            has_side_effects=collective is not None,
        ),
        cost_estimate=pl.CostEstimate(flops=flops, bytes_accessed=moved, transcendentals=0),
        name=name,
    )(*ins)


def send(source, target, out_sem, in_sem, device):
    return pltpu.make_async_remote_copy(
        src_ref=source, dst_ref=target, send_sem=out_sem, recv_sem=in_sem, device_id=device, device_id_type=MESH
    )


def meet(axes):
    barrier = pltpu.get_barrier_semaphore()
    count = 0
    for axis, size in axes:
        me = lax.axis_index(axis)

        def greet(step, carry, axis=axis, size=size, me=me):
            pl.semaphore_signal(barrier, inc=1, device_id={axis: lax.rem(me + step, size)}, device_id_type=MESH)
            return carry

        lax.fori_loop(1, size, greet, 0)
        count += size - 1
    pl.semaphore_wait(barrier, count)


def each(start, stop, body):
    def step(index, carry):
        body(index)
        return carry

    lax.fori_loop(start, stop, step, 0)


def embed_kernel(
    nb, nv, cap, part, rows, first, split, *refs
):
    round_ref, tok_ref, words = refs[:3]
    shards, refs = (refs[3:5], refs[5:]) if first else ((), refs[3:])
    target_ref, refs = (refs[0], refs[1:]) if split else (None, refs)
    x_ref, ids_ref, place_ref, most_ref, tok_ref_all = refs[:5]
    wholes, refs = (refs[5:7], refs[7:]) if first else ((), refs[5:])
    (quarter_ref, target_all), refs = (refs[:2], refs[2:]) if split else ((None, None), refs)
    before, ranks, work, sent, got, spread, mixed, turned = refs[:8]
    tok_out, tok_in, row_out, row_in, mix_out, mix_in = refs[8:14]
    b, v = lax.axis_index("batch"), lax.axis_index("vocab")
    width = words.shape[0]
    shift = round_ref[0] * cap
    meet((("batch", nb), ("vocab", nv)))
    gather = WeightGather(nb, shards, wholes, *refs[14:19]) if first else None
    quarter_out, quarter_in, quarter_own, target_out, target_in = refs[19:24] if split else [None] * 5

    def tok_copy(step):
        return send(
            tok_ref, tok_ref_all.at[b], tok_out.at[step], tok_in.at[step], {"batch": lax.rem(b + step, nb)}
        )

    for step in range(1, nb):
        tok_copy(step).start()

    def target_copy(step):
        return send(
            target_ref, target_all.at[b], target_out.at[step], target_in.at[step], {"batch": lax.rem(b + step, nb)}
        )

    def quarter(owner):
        return words.at[:, lanes(owner * (words.shape[1] // nb), words.shape[1] // nb)]

    def quarter_copy(step):
        other = lax.rem(b + step, nb)
        place = quarter_ref.at[pl.ds(pl.multiple_of(b * width, 16), width), :]
        return send(quarter(other), place, quarter_out.at[step], quarter_in.at[step], {"batch": other})

    def quarter_keep():
        place = quarter_ref.at[pl.ds(pl.multiple_of(b * width, 16), width), :]
        return pltpu.make_async_copy(quarter(b), place, quarter_own.at[0])

    if split:
        target_all[b] = target_ref[...]
        for step in range(1, nb):
            target_copy(step).start()
    if first:
        gather.start()
    if split:
        quarter_keep().start()
    tok_ref_all[b] = tok_ref[...]
    before[...] = (iota((SEQ_LEN, SEQ_LEN), 0) < iota((SEQ_LEN, SEQ_LEN), 1)).astype(FL).astype(BF)
    for step in range(1, nb):
        tok_copy(step).wait()

    base = v * rows
    most = jnp.zeros((nv, 1), FL)
    for p in range(nb):
        ids = tok_ref_all[p]
        mine = (ids >= base) & (ids < base + rows)
        rank = nn(mine.astype(FL).astype(BF), before[...])
        ranks[p] = jnp.where(mine, rank.astype(I32) - shift, -1)
        for owner in range(nv):
            theirs = (ids >= owner * rows) & (ids < (owner + 1) * rows)
            most = jnp.maximum(most, jnp.sum(theirs.astype(FL), axis=1, keepdims=True))
    most_ref[0] = jnp.max(most).astype(I32)

    def row_copy(step):
        return send(
            sent.at[step], got.at[v], row_out.at[step], row_in.at[step], {"vocab": lax.rem(v + step, nv)}
        )

    def build(turn):
        step = lax.rem(turn, nv)
        dest = lax.rem(v + step, nv)
        found = []
        for p in range(nb):
            pick = (iota((cap, SEQ_LEN), 0) == ranks[p, pl.ds(dest, 1), :]).astype(FL).astype(BF)
            local = tok_ref_all[p, pl.ds(dest, 1), :] - base
            line = iota((8, SEQ_LEN), 0)
            high, low = lax.shift_right_arithmetic(local, 7), lax.bitwise_and(local, 127)
            digits = jnp.where(line == 0, high, jnp.where(line == 1, low, 0)).astype(FL).astype(BF)
            both = nt(pick, digits)
            found.append((both[:, 0:1] * 128.0 + both[:, 1:2]).astype(I32))
        index = jnp.concatenate(found, axis=0)
        ids_ref[dest] = index
        work[...] = jnp.zeros_like(work)

        def piece(j):
            hot = (index - j * part == iota((nb * cap, part), 1)).astype(FL).astype(BF)
            work[...] += nt(hot, words[:, lanes(j * part, part)])

        each(0, rows // part, piece)
        block = work[...].T.astype(BF)

        @pl.when(step > 0)
        def _():
            sent[step] = block
            row_copy(step).start()

        @pl.when(step == 0)
        def _():
            got[v] = block

    each(1, nv // 2 + 1, build)
    if first:
        gather.pass_on()
    if split:
        for step in range(1, nb):
            quarter_copy(step).start()
    each(nv // 2 + 1, nv + 1, build)

    keys = []
    for p in range(nb):
        ids = tok_ref_all[p, pl.ds(v, 1), :]
        owner = iota((nv, SEQ_LEN), 0)
        theirs = (ids >= owner * rows) & (ids < (owner + 1) * rows)
        rank = nn(theirs.astype(FL).astype(BF), before[...])
        place = jnp.sum(jnp.where(theirs, rank, 0.0), axis=0, keepdims=True).astype(I32) - shift
        holder = jnp.sum(jnp.where(theirs, owner.astype(FL), 0.0), axis=0, keepdims=True).astype(I32)
        line = iota((8, SEQ_LEN), 0)
        place_ref[p] = jnp.where(line == 0, holder, jnp.where(line == 1, place, 0))
        keys.append((holder, place))
        spread[p] = jnp.zeros((width, SEQ_LEN), FL)

    def take(turn):
        step = lax.rem(turn, nv)
        source = lax.rem(v - step + nv, nv)

        @pl.when(step > 0)
        def _():
            row_copy(step).wait()

        block = got[source]
        for p in range(nb):
            holder, place = keys[p]
            key = jnp.where(holder == source, place, -1)
            hot = (iota((cap, SEQ_LEN), 0) == key).astype(FL).astype(BF)
            spread[p] += nn(block[:, p * cap : (p + 1) * cap], hot)

    each(1, nv + 1, take)

    def mix_copy(step):
        return send(
            mixed.at[step], turned.at[b], mix_out.at[step], mix_in.at[step], {"batch": lax.rem(b + step, nb)}
        )

    for step in range(1, nb):
        mixed[step] = spread[lax.rem(b + step, nb)].astype(BF)
        mix_copy(step).start()
    turned[b] = spread[b].astype(BF)
    for step in range(1, nb):
        mix_copy(step).wait()
    x_ref[...] = turned[...].reshape(nb * width, SEQ_LEN).T
    if first:
        gather.finish()
    if split:
        quarter_keep().wait()
        for step in range(1, nb):
            target_copy(step).wait()
            quarter_copy(step).wait()


def weight_semaphores(count):
    return [pltpu.SemaphoreType.DMA((count,))] + [pltpu.SemaphoreType.DMA((count, 4))] * 4


class WeightGather:
    def __init__(self, nb, shards, wholes, own_sem, out_sem, in_sem, pair_out, pair_in):
        self.nb, self.shards, self.wholes = nb, shards, wholes
        self.own_sem, self.out_sem, self.in_sem, self.pair_out, self.pair_in = own_sem, out_sem, in_sem, pair_out, pair_in
        self.b, v = lax.axis_index("batch"), lax.axis_index("vocab")
        self.core = lax.rem(v, 2)
        self.sibling = {"vocab": v + 1 - 2 * self.core}

    def flip(self, bits):
        b = self.b
        low, high = lax.rem(b, 2), b // 2
        return (high if bits < 2 else 1 - high) * 2 + (low if bits % 2 == 0 else 1 - low)

    def place(self, w, owner, top, size):
        rows = self.shards[w].shape[0]
        first = pl.multiple_of(owner * rows + self.core * (rows // 2) + top, 16)
        return self.wholes[w].at[pl.ds(first, size), :]

    def routes(self, w):
        rows = self.shards[w].shape[0] // 2
        if self.nb == 4:
            half = rows // 2
            return [
                (self.b, 0, rows, self.flip(1), self.flip(1)),
                (self.b, 0, rows, self.flip(2), self.flip(2)),
                (self.flip(1), 0, half, self.flip(2), self.flip(3)),
                (self.flip(2), half, half, self.flip(1), self.flip(3)),
            ]
        others = [lax.rem(self.b + step, self.nb) for step in range(1, self.nb)]
        came = [lax.rem(self.b - step + self.nb, self.nb) for step in range(1, self.nb)]
        return [(self.b, 0, rows, other, source) for other, source in zip(others, came)]

    def own_copy(self, w):
        rows = self.shards[w].shape[0]
        first = pl.multiple_of(self.b * rows, 16)
        return pltpu.make_async_copy(self.shards[w], self.wholes[w].at[pl.ds(first, rows), :], self.own_sem.at[w])

    def copy(self, w, k):
        owner, top, size, device, _ = self.routes(w)[k]
        if self.nb == 4 and k >= 2:
            source = self.place(w, owner, top, size)
        else:
            source = self.shards[w].at[pl.ds(pl.multiple_of(self.core * size, 16), size), :]
        target = self.place(w, owner, top, size)
        return send(source, target, self.out_sem.at[w, k], self.in_sem.at[w, k], {"batch": device})

    def pair(self, w, k):
        _, top, size, _, arrived = self.routes(w)[k]
        ref = self.place(w, arrived, top, size)
        return send(ref, ref, self.pair_out.at[w, k], self.pair_in.at[w, k], self.sibling)

    def start(self):
        for w in range(len(self.shards)):
            for k in range(2 if self.nb == 4 else self.nb - 1):
                self.copy(w, k).start()
        for w in range(len(self.shards)):
            self.own_copy(w).start()

    def pass_on(self):
        if self.nb != 4:
            return
        for w in range(len(self.shards)):
            for k in range(2):
                self.copy(w, k).wait_recv()
                self.copy(w, k + 2).start()
                self.pair(w, k).start()

    def finish(self):
        for w in range(len(self.shards)):
            for k in range(2 if self.nb == 4 else 0, len(self.routes(w))):
                self.copy(w, k).wait_recv()
                self.pair(w, k).start()
        for w in range(len(self.shards)):
            self.own_copy(w).wait()
            for k in range(len(self.routes(w))):
                self.copy(w, k).wait_send()
                self.pair(w, k).wait()


def embed(nb, nv, cap, rows, turn, tok, table, shards=(), targets=None):
    width = table.shape[0]
    split = targets is not None
    part = chunk_of(rows, 640)
    count = nb * cap
    outs = [
        SD((SEQ_LEN, D), BF),
        SD((nv, count, 1), I32),
        SD((nb, 8, SEQ_LEN), I32),
        SD((1,), I32),
        SD((nb, nv, SEQ_LEN), I32),
    ]
    first = len(shards) > 0
    outs += [SD((nb * item.shape[0], item.shape[1]), BF) for item in shards]
    if split:
        outs += [SD((D, table.shape[1] // nb), BF), SD((nb, *targets.shape), I32)]
    dma = pltpu.SemaphoreType.DMA
    scratch = [
        pltpu.VMEM((SEQ_LEN, SEQ_LEN), BF),
        pltpu.VMEM((nb, nv, SEQ_LEN), I32),
        pltpu.VMEM((count, width), FL),
        pltpu.VMEM((nv, width, count), BF),
        pltpu.VMEM((nv, width, count), BF),
        pltpu.VMEM((nb, width, SEQ_LEN), FL),
        pltpu.VMEM((nb, width, SEQ_LEN), BF),
        pltpu.VMEM((nb, width, SEQ_LEN), BF),
        dma((nb,)), dma((nb,)), dma((nv,)), dma((nv,)), dma((nb,)), dma((nb,)),
    ]
    if first:
        scratch += weight_semaphores(len(shards))
    if split:
        scratch += [dma((nb,)), dma((nb,)), dma((1,)), dma((nb,)), dma((nb,))]
    extra = [targets] if split else []
    return run(
        functools.partial(embed_kernel, nb, nv, cap, part, rows, first, split), outs, scratch,
        [turn, tok, table, *shards, *extra],
        "embed" if first else "embed_more", 0 if first else 3,
        in_specs=[SM, VM, VM] + [VM] * len(shards) + [VM] * len(extra),
        out_specs=[VM] * 3 + [SM, VM] + [HB] * len(shards) + ([HB, VM] if split else []),
    )


class GradientSum:
    def __init__(self, nb, nv, grads, refs, totals=None, sums=None):
        self.nb, self.nv, self.grads, self.sums = nb, nv, grads, sums
        self.todo = [w for w, item in enumerate(grads) if item is not None]
        take = iter(refs)
        spread = lambda keys: {w: next(take) for w in keys}
        everything = range(len(grads))
        self.own, self.near, self.shard = spread(self.todo), spread(self.todo), spread(self.todo)
        if sums is not None:
            self.total = spread(self.todo)
            self.total.update(totals)
            self.bits, self.result = spread(everything), spread(everything)
        else:
            self.total = totals
        self.load_sem, self.pair_out, self.pair_in, self.mix_out, self.mix_in = (next(take) for _ in range(5))
        if sums is not None:
            (self.cut_out, self.cut_in, self.all_out, self.all_in, self.last_out, self.last_in,
             self.store_sem) = take
        self.b, v = lax.axis_index("batch"), lax.axis_index("vocab")
        self.core, self.chip, self.chips = lax.rem(v, 2), v // 2, nv // 2
        self.sibling = {"vocab": v + 1 - 2 * self.core}

    def half(self, w, core):
        cols = self.total[w].shape[1]
        return lanes(core * cols, cols)

    def load(self, w):
        return pltpu.make_async_copy(self.grads[w].at[:, self.half(w, self.core)], self.own[w], self.load_sem.at[w])

    def pair(self, w):
        source = self.grads[w].at[:, self.half(w, 1 - self.core)]
        return send(source, self.near[w], self.pair_out.at[w], self.pair_in.at[w], self.sibling)

    def start(self):
        for w in sorted(self.todo, reverse=True):
            self.pair(w).start()
            self.load(w).start()

    def mix(self, w, step):
        other = lax.rem(self.b + step, self.nb)
        rows = self.own[w].shape[0] // self.nb
        source = self.own[w].at[pl.ds(pl.multiple_of(other * rows, 16), rows), :]
        return send(source, self.shard[w].at[step], self.mix_out.at[w, step], self.mix_in.at[w, step], {"batch": other})

    def scatter(self, w):
        self.load(w).wait()
        self.pair(w).wait()
        rows = self.own[w].shape[0] // self.nb

        def add(i, w=w, rows=rows):
            cut = pl.ds(pl.multiple_of(i * rows, 16), rows)
            self.own[w][cut, :] = (self.own[w][cut, :].astype(FL) + self.near[w][cut, :].astype(FL)).astype(BF)

        each(0, self.nb, add)
        for step in range(1, self.nb):
            self.mix(w, step).start()

    def pieces(self, w):
        rows = self.total[w].shape[0]
        count = max(n for n in range(1, self.chips + 1) if rows % (16 * n) == 0)
        return count, rows // count

    def peer(self, step):
        other = lax.rem(self.chip + step, self.chips)
        return other, {"vocab": other * 2 + self.core}

    def cut(self, w, step):
        other, device = self.peer(step)
        size = self.pieces(w)[1]
        source = self.total[w].at[pl.ds(pl.multiple_of(other * size, 16), size), :]
        return send(source, self.bits[w].at[step], self.cut_out.at[w, step], self.cut_in.at[w, step], device)

    def back(self, w, step):
        size = self.pieces(w)[1]
        place = self.result[w].at[pl.ds(pl.multiple_of(self.chip * size, 16), size), :]
        return send(place, place, self.all_out.at[w, step], self.all_in.at[w, step], self.peer(step)[1])

    def back_recv(self, w, step):
        source = lax.rem(self.chip - step + self.chips, self.chips)
        size = self.pieces(w)[1]
        place = self.result[w].at[pl.ds(pl.multiple_of(source * size, 16), size), :]
        return send(place, place, self.all_out.at[w, step], self.all_in.at[w, step], self.peer(step)[1])

    def gather(self, w):
        rows = self.total[w].shape[0]
        for step in range(1, self.nb):
            self.mix(w, step).wait()
        here = pl.ds(pl.multiple_of(self.b * rows, 16), rows)
        value = self.own[w][here, :].astype(FL)
        for step in range(1, self.nb):
            value = value + self.shard[w][step].astype(FL)
        self.total[w][...] = value.astype(BF)

    def reduce(self, w):
        if w in self.todo:
            self.gather(w)
        count = self.pieces(w)[0]

        def go(step):
            @pl.when(self.peer(step)[0] < count)
            def _():
                self.cut(w, step).start()

        each(1, self.chips, go)

    def collect(self, w):
        count, size = self.pieces(w)
        mine = pl.ds(pl.multiple_of(self.chip * size, 16), size)

        @pl.when(self.chip < count)
        def _(w=w, mine=mine):
            def add(step, value):
                self.cut(w, step).wait_recv()
                return value + self.bits[w][step].astype(FL)

            value = lax.fori_loop(1, self.chips, add, self.total[w][mine, :].astype(FL))
            self.result[w][mine, :] = value.astype(BF)
            each(1, self.chips, lambda step: self.back(w, step).start())

        def sent(step, w=w, count=count):
            @pl.when(self.peer(step)[0] < count)
            def _():
                self.cut(w, step).wait_send()

        each(1, self.chips, sent)

    def last(self, w):
        return send(
            self.result[w], self.sums[w].at[:, self.half(w, self.core)], self.last_out.at[w], self.last_in.at[w], self.sibling
        )

    def store(self, w):
        return pltpu.make_async_copy(self.result[w], self.sums[w].at[:, self.half(w, self.core)], self.store_sem.at[w])

    def finish(self):
        for w in range(4):
            count = self.pieces(w)[0]

            def got(step, w=w, count=count):
                @pl.when(lax.rem(self.chip - step + self.chips, self.chips) < count)
                def _():
                    self.back_recv(w, step).wait_recv()

            each(1, self.chips, got)
            self.last(w).start()
            self.store(w).start()
        for w in range(4):
            count = self.pieces(w)[0]

            @pl.when(self.chip < count)
            def _(w=w):
                each(1, self.chips, lambda step: self.back(w, step).wait_send())

            self.store(w).wait()
            self.last(w).wait_send()
            other = self.sums[w].at[:, self.half(w, 1 - self.core)]
            send(other, other, self.last_out.at[w], self.last_in.at[w], self.sibling).wait_recv()


def gradient_scratch(nb, nv, shapes, todo, whole=True):
    chips = nv // 2
    halves = [(rows, cols // 2) for rows, cols in shapes]
    shards = [(rows // nb, cols) for rows, cols in halves]
    sizes = [rows // max(n for n in range(1, chips + 1) if rows % (16 * n) == 0) for rows, _ in shards]
    dma = pltpu.SemaphoreType.DMA
    count = len(shapes)
    refs = [pltpu.VMEM(halves[w], BF) for w in todo] * 2 + [pltpu.VMEM((nb, *shards[w]), BF) for w in todo]
    if whole:
        refs += [pltpu.VMEM(shards[w], BF) for w in todo]
        refs += [pltpu.VMEM((chips, size, item[1]), BF) for size, item in zip(sizes, shards)]
        refs += [pltpu.VMEM(item, BF) for item in shards]
    refs += [dma((count,)), dma((count,)), dma((count,)), dma((count, nb)), dma((count, nb))]
    if whole:
        refs += [dma((count, chips))] * 4 + [dma((count,))] * 3
    return refs


def squares(refs, part):
    cols = min(ref.shape[1] for ref in refs)

    def add(j, total):
        value = refs[0][:, lanes(j * part, part)].astype(FL)
        for ref in refs[1:]:
            value = value + ref[:, lanes(j * part, part)].astype(FL)
        return total + jnp.sum(value * value, axis=0, keepdims=True)

    line = lax.fori_loop(0, cols // part, add, jnp.zeros((1, part), FL))
    return jnp.sum(line, axis=1, keepdims=True)


def add_up(nb, nv, own, loss_ref, out_ref, mine, near, lines, vocab_out, vocab_in, batch_out, batch_in):
    b, v = lax.axis_index("batch"), lax.axis_index("vocab")
    line = iota((8, 128), 0)
    mine[...] = jnp.where(line == 0, own, jnp.where((line == 1) & (v == 0), loss_ref[...], 0.0))

    def vocab_copy(step):
        return send(mine, near.at[v], vocab_out.at[step], vocab_in.at[step], {"vocab": lax.rem(v + step, nv)})

    each(1, nv, lambda step: vocab_copy(step).start())
    near[v] = mine[...]
    each(1, nv, lambda step: vocab_copy(step).wait())
    mine[...] = lax.fori_loop(0, nv, lambda u, total: total + near[u], jnp.zeros((8, 128), FL))

    def batch_copy(step):
        return send(mine, lines.at[b], batch_out.at[step], batch_in.at[step], {"batch": lax.rem(b + step, nb)})

    each(1, nb, lambda step: batch_copy(step).start())
    lines[b] = mine[...]
    each(1, nb, lambda step: batch_copy(step).wait())
    out_ref[...] = lax.fori_loop(0, nb, lambda u, total: total + lines[u], jnp.zeros((8, 128), FL))


def add_up_scratch(nb, nv):
    dma = pltpu.SemaphoreType.DMA
    tiles = [pltpu.VMEM((8, 128), FL), pltpu.VMEM((nv, 8, 128), FL), pltpu.VMEM((nb, 8, 128), FL)]
    return tiles + [dma((nv,)), dma((nv,)), dma((nb,)), dma((nb,))]


def norm_kernel(nb, nv, extra_ref, dw_ref, a_ref, p_ref, u_ref, c_ref, loss_ref, out_ref, *scratch):
    meet((("batch", nb), ("vocab", nv)))
    own = squares((extra_ref, dw_ref), chunk_of(extra_ref.shape[1], 640))
    layer = squares((a_ref,), 512) + squares((p_ref,), 384) + squares((u_ref,), 512) + squares((c_ref,), 384)
    own = own + jnp.where(lax.axis_index("vocab") == 0, layer, jnp.zeros_like(layer))
    add_up(nb, nv, own, loss_ref, out_ref, *scratch)


def unembed_kernel(nb, nv, cap, part, first, split, *refs):
    x_ref, ids_ref, place_ref = refs[:3]
    grads, refs = (refs[3:7], refs[7:]) if first else ((), refs[3:])
    if first:
        totals, grads = {2: grads[2]}, (grads[0], grads[1], None, grads[3])
    (quarter_ref, loss_ref), refs = (refs[:2], refs[2:]) if split else ((None, None), refs)
    out_ref = refs[0]
    sums, refs = (refs[1:5], refs[5:]) if first else ((), refs[1:])
    (dw_ref, total_ref, rows_ref), refs = (refs[:3], refs[3:]) if split else ([None] * 3, refs)
    (quarter_out, quarter_in, quarter_own), refs = (refs[:3], refs[3:]) if split else ([None] * 3, refs)
    (strip, strip_sem, *sum_refs), refs = (refs[:9], refs[9:]) if split else ([None] * 2, refs)
    turned, parts, sent, got, mix_out, mix_in, row_out, row_in = refs[:8]
    layer = GradientSum(nb, nv, grads, refs[8:], totals, sums) if first else None
    b, v = lax.axis_index("batch"), lax.axis_index("vocab")
    width, rows = out_ref.shape
    meet((("batch", nb), ("vocab", nv)))
    turned[...] = x_ref[...].T.reshape(nb, width, SEQ_LEN)

    def mix_copy(step):
        other = lax.rem(b + step, nb)
        return send(turned.at[other], parts.at[b], mix_out.at[step], mix_in.at[step], {"batch": other})

    for step in range(1, nb):
        mix_copy(step).start()
    if first:
        layer.start()
        layer.reduce(2)
    parts[b] = turned[b]
    for step in range(1, nb):
        mix_copy(step).wait()

    def quarter_place():
        size = quarter_ref.shape[1]
        return dw_ref.at[:, lanes(b * size, size)]

    def quarter_copy(step):
        other = lax.rem(b + step, nb)
        source = quarter_ref.at[pl.ds(pl.multiple_of(other * width, 16), width), :]
        return send(source, quarter_place(), quarter_out.at[step], quarter_in.at[step], {"batch": other})

    def quarter_keep():
        source = quarter_ref.at[pl.ds(pl.multiple_of(b * width, 16), width), :]
        return pltpu.make_async_copy(source, quarter_place(), quarter_own.at[0])

    def row_copy(step):
        return send(
            sent.at[step], got.at[v], row_out.at[step], row_in.at[step], {"vocab": lax.rem(v + step, nv)}
        )

    def build(turn):
        step = lax.rem(turn, nv)
        owner = lax.rem(v + step, nv)
        blocks = []
        for p in range(nb):
            key = jnp.where(place_ref[p, 0:1, :] == owner, place_ref[p, 1:2, :], -1)
            hot = (iota((cap, SEQ_LEN), 0) == key).astype(FL).astype(BF)
            blocks.append(nt(parts[p], hot).astype(BF))
        block = jnp.concatenate(blocks, axis=1)

        @pl.when(step > 0)
        def _():
            sent[step] = block
            row_copy(step).start()

        @pl.when(step == 0)
        def _():
            got[v] = block

    if first:
        layer.scatter(3)
    each(1, nv // 2 + 1, build)
    if first:
        layer.collect(2)
    each(nv // 2 + 1, nv + 1, build)
    if first:
        layer.scatter(0)
    if split:
        quarter_keep().start()
    out_ref[...] = jnp.zeros_like(out_ref)

    def take(step):
        source = lax.rem(v - step + nv, nv)

        @pl.when(step > 0)
        def _():
            row_copy(step).wait()

        block, index = got[source], ids_ref[source]

        def piece(j):
            hot = (index - j * part == iota((nb * cap, part), 1)).astype(FL).astype(BF)
            out_ref[:, lanes(j * part, part)] += nn(block, hot)

        each(0, rows // part, piece)

    if first:
        quarter = nv // 4
        each(0, quarter, take)
        layer.reduce(3)
        layer.scatter(1)
        if split:
            for step in range(1, nb):
                quarter_copy(step).start()
        each(quarter, 2 * quarter, take)
        layer.reduce(0)
        each(2 * quarter, 3 * quarter, take)
        layer.collect(3)
        layer.reduce(1)
        each(3 * quarter, nv, take)
        layer.collect(0)
        layer.collect(1)
        layer.finish()
        if split:
            quarter_keep().wait()
            for step in range(1, nb):
                quarter_copy(step).wait()
            rows_copy = pltpu.make_async_copy(sums[0].at[:, lanes(3 * D, 128)], strip, strip_sem.at[0])
            rows_copy.start()
            layer_squares = jnp.zeros((1, 1), FL)
            for w in range(4):
                cols = layer.result[w].shape[1]
                layer_squares += squares((layer.result[w],), max(n for n in (640, 512, 384, 128) if cols % n == 0))
            own = squares((out_ref, dw_ref), part)
            own = own + jnp.where(v < 2, layer_squares, 0.0)
            add_up(nb, nv, own, loss_ref, total_ref, *sum_refs)
            rows_copy.wait()
            rows_ref[...] = strip[...].astype(FL).T[:8, :]
    else:
        each(0, nv, take)


def unembed(nb, nv, cap, width, rows, grad, ids, place, grads=(), quarter=None, loss=None):
    part = chunk_of(rows, 640)
    count = nb * cap
    dma = pltpu.SemaphoreType.DMA
    scratch = [
        pltpu.VMEM((nb, width, SEQ_LEN), BF),
        pltpu.VMEM((nb, width, SEQ_LEN), BF),
        pltpu.VMEM((nv, width, count), BF),
        pltpu.VMEM((nv, width, count), BF),
        dma((nb,)), dma((nb,)), dma((nv,)), dma((nv,)),
    ]
    first, split = len(grads) > 0, quarter is not None
    if split:
        strip = [pltpu.VMEM((width, 128), BF), dma((1,))]
        scratch = [dma((nb,)), dma((nb,)), dma((1,))] + strip + add_up_scratch(nb, nv) + scratch
    if first:
        shapes = [item.shape if w != 2 else (nb * item.shape[0], 2 * item.shape[1]) for w, item in enumerate(grads)]
        scratch += gradient_scratch(nb, nv, shapes, (0, 1, 3))
    outs = [SD((width, rows), FL)] + [SD((item[0] // nb, item[1]), BF) for item in (shapes if first else ())]
    extra = [quarter, loss] if split else []
    if split:
        outs += [SD((width, nb * quarter.shape[1]), BF), SD((8, 128), FL), SD((8, width), FL)]
    return run(
        functools.partial(unembed_kernel, nb, nv, cap, part, first, split),
        outs,
        scratch,
        [grad, ids, place, *grads, *extra],
        "unembed" if first else "unembed_more",
        2 if first else 4,
        in_specs=[VM] * 3 + ([HB, HB, VM, HB] if first else []) + [VM] * len(extra),
        out_specs=[VM] + [HB] * len(grads) + ([VM] * 3 if split else []),
    )


def later_slots(nv, cap, rows, every, turn):
    nb = every.shape[0]
    v = lax.axis_index("vocab")
    local = every - v * rows
    mine = (local >= 0) & (local < rows)
    rank = jnp.cumsum(mine.astype(I32), axis=-1) - 1 - turn * cap
    hot = (rank[:, :, None, :] == jnp.arange(cap)[None, None, :, None]) & mine[:, :, None, :]
    ids = jnp.sum(jnp.where(hot, local[:, :, None, :], 0), axis=-1)
    return jnp.transpose(ids, (1, 0, 2)).reshape(nv, nb * cap, 1)


def standard(value):
    centre = value - jnp.mean(value, axis=-1, keepdims=True)
    spread = jnp.mean(centre * centre, axis=-1, keepdims=True)
    scale = lax.rsqrt(spread + NORM_EPS)
    return centre * scale, scale


def norm_back(unit, scale, gain, upstream):
    inner = upstream * gain
    first = jnp.mean(inner, axis=-1, keepdims=True)
    second = jnp.mean(inner * unit, axis=-1, keepdims=True)
    grad = scale * (inner - first - unit * second)
    return grad, jnp.sum(upstream * unit, axis=0, keepdims=True), jnp.sum(upstream, axis=0, keepdims=True)


def head_lanes(value, head):
    lane = iota(value.shape, 1)
    keep = (lane < HD) if head == 0 else (lane >= HD)
    return jnp.where(keep, value, jnp.zeros_like(value))


def visible_keys(seg_ref, pos_ref):
    position = pos_ref[...]
    block = position // BLK
    marks = [seg_ref[:, i * BLK : i * BLK + 1] for i in range(SEQ_LEN // BLK)]
    segment = jnp.zeros_like(position)
    for i, mark in enumerate(marks):
        segment = jnp.where(block == i, mark, segment)
    row = iota((BLK, PICKS), 0)
    parts = [jnp.broadcast_to(segment == slot + 1, (NB, PICKS)) for slot in range(SLOTS)]
    parts += [(segment == mark) & (row + i * BLK <= position) for i, mark in enumerate(marks)]
    return parts


def masked(visible, scores):
    return jnp.concatenate(
        [jnp.where(keep, scores[i * BLK : (i + 1) * BLK, :], NEG_BIG) for i, keep in enumerate(visible)], axis=0
    )


def memory_weights(segments, slot):
    length = segments.shape[1]
    inside = (segments == slot).astype(FL)
    start = jnp.sum((segments < slot).astype(FL), axis=1, keepdims=True)
    count = jnp.sum(inside, axis=1, keepdims=True)
    times = (iota((1, length), 1).astype(FL) - start + 0.5) / jnp.maximum(count, 1.0)
    centres = (iota((NB, 1), 0).astype(FL) + 0.5) / NB
    offset = (times - centres) * NB
    basis = jnp.exp(-0.5 * offset * offset) * inside
    total = jnp.sum(basis, axis=1, keepdims=True) + (count == 0.0).astype(FL)
    return basis / total


def attend_kernel(
    nb, nv, x_ref, a_ref, seg_ref, pos_ref, p_ref, c_ref,
    hall_ref, kv_ref, q_ref, hq_ref, xq_ref, o_ref, lse_ref, norm_ref, mixt_ref, p_all, c_all, *sems,
):
    meet((("batch", nb), ("vocab", nv)))
    gather = WeightGather(nb, (p_ref, c_ref), (p_all, c_all), *sems)
    gather.start()
    norm_ref[...] = a_ref[:, 3 * D : 3 * D + 128].astype(FL).T[:8, :]
    gain, bias = norm_ref[0:1, :], norm_ref[3:4, :]

    def normalize(i):
        unit, _ = standard(x_ref[pl.ds(i * BLK, BLK), :].astype(FL))
        hall_ref[pl.ds(SLOTS * NB + i * BLK, BLK), :] = (unit * gain + bias).astype(BF)

    each(0, SEQ_LEN // BLK, normalize)
    normed = hall_ref[SLOTS * NB :, :]
    for slot in range(SLOTS):
        mixing = memory_weights(seg_ref[...], slot).astype(BF)
        hall_ref[slot * NB : (slot + 1) * NB, :] = nn(mixing, normed).astype(BF)
        mixt_ref[:, slot * NB : (slot + 1) * NB] = mixing.T

    def project(i):
        kv_ref[pl.ds(i * BLK, BLK), :] = nn(hall_ref[pl.ds(i * BLK, BLK), :], a_ref[:, D : 3 * D]).astype(BF)

    each(0, KEYS // BLK, project)
    pick = (pos_ref[...] == iota((SEQ_LEN, PICKS), 0)).astype(FL).astype(BF).T
    hq_ref[...] = nn(pick, normed).astype(BF)
    xq_ref[...] = nn(pick, x_ref[...])
    q_ref[...] = nn(hq_ref[...], a_ref[:, :D]).astype(BF)
    visible = visible_keys(seg_ref, pos_ref)

    def attend(p):
        keys = kv_ref[:, lanes(p * PAIR, PAIR)]
        values = kv_ref[:, lanes(D + p * PAIR, PAIR)].T
        queries = q_ref[:, lanes(p * PAIR, PAIR)] * HD ** (-0.5)
        outs = []
        for head in range(2):
            scores = masked(visible, nt(keys, head_lanes(queries, head)))
            peak = jnp.max(scores, axis=0, keepdims=True)
            expo = jnp.exp(scores - peak)
            total = jnp.sum(expo, axis=0, keepdims=True)
            probs = (expo * (1.0 / total)).astype(BF)
            outs.append(nn(values[head * HD : (head + 1) * HD, :], probs))
            lse_ref[p, head : head + 1, :] = peak + jnp.log(total)
        o_ref[:, lanes(p * PAIR, PAIR)] = jnp.concatenate(outs, axis=0).T.astype(BF)

    gather.pass_on()
    each(0, NPAIR, attend)
    gather.finish()


def feed_kernel(xq_ref, o_ref, p_ref, u_ref, c_ref, norm_ref, x1_ref, h2_ref, z_ref, act_ref, x2_ref, f_ref):
    x1 = xq_ref[...] + nn(o_ref[...], p_ref[...])
    x1_ref[...] = x1
    unit, _ = standard(x1)
    h2 = (unit * norm_ref[1:2, :] + norm_ref[4:5, :]).astype(BF)
    h2_ref[...] = h2
    x2_ref[...] = x1

    def piece(j):
        cut = lanes(j * D, D)
        z = nn(h2, u_ref[:, cut])
        z_ref[:, cut] = z
        act = jax.nn.gelu(z, approximate=True).astype(BF)
        act_ref[:, cut] = act
        x2_ref[...] += nn(act, c_ref[pl.ds(j * D, D), :])

    each(0, FF // D, piece)
    unit, _ = standard(x2_ref[...])
    f_ref[...] = (unit * norm_ref[2:3, :] + norm_ref[5:6, :]).astype(BF)


def feed_back_kernel(
    df_ref, x2_ref, x1_ref, h2_ref, z_ref, act_ref, o_ref, p_ref, u_ref, c_ref, norm_ref,
    dc_ref, du_ref, dp_ref, dx1_ref, do_ref, dnorm_ref, dh2,
):
    unit, scale = standard(x2_ref[...])
    dx2, gain_last, bias_last = norm_back(unit, scale, norm_ref[2:3, :], df_ref[...])
    dy = dx2.astype(BF)
    dh2[...] = jnp.zeros_like(dh2)
    h2t = h2_ref[...].T

    def piece(j):
        cut = lanes(j * D, D)
        dc_ref[pl.ds(j * D, D), :] = nn(act_ref[:, cut].T, dy).astype(BF)
        dact = nt(dy, c_ref[pl.ds(j * D, D), :])
        z = z_ref[:, cut]
        k = math.sqrt(2.0 / math.pi)
        t = jnp.tanh(k * (z + 0.044715 * z * z * z))
        slope = 0.5 * (1.0 + t) + 0.5 * z * (1.0 - t * t) * (k * (1.0 + 3 * 0.044715 * z * z))
        dz = (dact * slope).astype(BF)
        du_ref[:, cut] = nn(h2t, dz).astype(BF)
        dh2[...] += nt(dz, u_ref[:, cut])

    each(0, FF // D, piece)
    unit, scale = standard(x1_ref[...])
    dx1, gain_two, bias_two = norm_back(unit, scale, norm_ref[1:2, :], dh2[...])
    dx1 = dx1 + dx2
    dx1_ref[...] = dx1
    da = dx1.astype(BF)
    dp_ref[...] = nn(o_ref[...].T, da).astype(BF)
    do_ref[...] = nt(da, p_ref[...]).astype(BF)
    zero = jnp.zeros_like(gain_last)
    dnorm_ref[...] = jnp.concatenate([zero, gain_two, gain_last, zero, bias_two, bias_last, zero, zero], axis=0)


def attend_back_kernel(
    nb, nv, do_ref, q_ref, kv_ref, lse_ref, hall_ref, hq_ref, a_ref, x_ref, dx1_ref, mixt_ref, seg_ref, row_ref,
    norm_ref, dnorm_ref, du_ref, da_ref, dx_ref, du_sum, dkv, dq, hallt, dh, dxin, dmem, sel, *refs,
):
    meet((("batch", nb), ("vocab", nv)))
    layer = GradientSum(nb, nv, (du_ref,), refs, {0: du_sum})
    layer.start()
    visible = visible_keys(seg_ref, row_ref)

    def attend(p):
        cut = lanes(p * PAIR, PAIR)
        keys = kv_ref[:, cut]
        values = kv_ref[:, lanes(D + p * PAIR, PAIR)]
        turned = keys.T
        queries = q_ref[:, cut] * HD ** (-0.5)
        grads = do_ref[:, cut]
        outs = []
        dk = dv = None
        for head in range(2):
            own, grad = head_lanes(queries, head), head_lanes(grads, head)
            scores = masked(visible, nt(keys, own))
            probs = jnp.exp(scores - lse_ref[p, head : head + 1, :])
            dprobs = nt(values, grad)
            inner = jnp.sum(probs * dprobs, axis=0, keepdims=True)
            dscores = (probs * (dprobs - inner)).astype(BF)
            outs.append(nn(turned[head * HD : (head + 1) * HD, :], dscores))
            one, two = nn(dscores, own), nn(probs.astype(BF), grad)
            dk = one if head == 0 else dk + one
            dv = two if head == 0 else dv + two
        dq[:, cut] = (jnp.concatenate(outs, axis=0).T * HD ** (-0.5)).astype(BF)
        dkv[:, cut] = dk.astype(BF)
        dkv[:, lanes(D + p * PAIR, PAIR)] = dv.astype(BF)

    each(0, NPAIR // 2, attend)
    layer.scatter(0)
    each(NPAIR // 2, NPAIR, attend)
    da_ref[:, :D] = nn(hq_ref[...].T, dq[...]).astype(BF)

    def turn(i):
        hallt[:, lanes(i * BLK, BLK)] = hall_ref[pl.ds(i * BLK, BLK), :].T

    each(0, KEYS // BLK, turn)

    def weights(j):
        cut = lanes(j * BLK, BLK)
        da_ref[:, lanes(D + j * BLK, BLK)] = nn(hallt[...], dkv[:, cut]).astype(BF)

    each(0, 2 * D // BLK, weights)

    def memory(i):
        cut = pl.ds(i * BLK, BLK)
        dmem[cut, :] = nt(dkv[cut, :], a_ref[:, D : 3 * D]).astype(BF)

    each(0, SLOTS, memory)

    def local(i):
        cut = pl.ds(i * BLK, BLK)
        dh[cut, :] = nt(dkv[pl.ds(SLOTS * NB + i * BLK, BLK), :], a_ref[:, D : 3 * D]) + nn(mixt_ref[cut, :], dmem[...])

    each(0, SEQ_LEN // BLK, local)
    put = (row_ref[...] == iota((SEQ_LEN, PICKS), 0)).astype(FL).astype(BF)

    def scatter(target, value):
        for _ in range(3):
            part = value.astype(BF)
            value = value - part.astype(FL)

            def add(i, part=part):
                cut = pl.ds(i * BLK, BLK)
                target[cut, :] += nn(sel[cut, :], part)

            each(0, SEQ_LEN // BLK, add)

    sel[...] = put
    scatter(dh, nt(dq[...], a_ref[:, :D]))
    gain = norm_ref[0:1, :]
    da_rows = [jnp.zeros((1, D), FL), jnp.zeros((1, D), FL)]

    def finish(i, carry):
        cut = pl.ds(i * BLK, BLK)
        unit, scale = standard(x_ref[cut, :].astype(FL))
        grad, dgain, dbias = norm_back(unit, scale, gain, dh[cut, :])
        dxin[cut, :] = grad
        return carry[0] + dgain, carry[1] + dbias

    dgain, dbias = lax.fori_loop(0, SEQ_LEN // BLK, finish, tuple(da_rows))

    scatter(dxin, dx1_ref[...])
    dx_ref[...] = dxin[...].astype(BF)
    line = iota((8, D), 0)
    norms = dnorm_ref[...] + jnp.where(line == 0, dgain, jnp.where(line == 3, dbias, 0.0))
    tall = jnp.concatenate([norms, jnp.zeros((EXTRA - 8, D), FL)], axis=0)
    da_ref[:, 3 * D :] = tall.T.astype(BF)
    layer.gather(0)


def head_kernel(
    nb, nv, part, f_ref, w_ref, live_ref, target_ref, df_ref, dw_ref, loss_ref,
    fall, expo, block, mine, stats, ft, grad_sum, coef, df, half, far_got, out,
    near_out, near_in, far_out, far_in, stat_out, stat_in, pair_out, pair_in, sum_out, sum_in, dw_sem,
):
    v = lax.axis_index("vocab")
    rows = w_ref.shape[1]
    total_rows = nv * PICKS
    core, chip, chips = lax.rem(v, 2), v // 2, nv // 2
    sibling = {"vocab": v + 1 - 2 * core}
    base = v * rows
    pieces = rows // part
    depth = min(2, pieces)
    meet((("vocab", nv),))

    def peer(step):
        return {"vocab": lax.rem(chip + step, chips) * 2 + core}

    def far_copy(step):
        return send(f_ref, fall.at[v], far_out.at[step], far_in.at[step], peer(step))

    def near_copy(step):
        slot = lax.rem(chip - step + chips, chips) * 2 + core
        return send(fall.at[slot], fall.at[slot], near_out.at[step], near_in.at[step], sibling)

    fall[v] = f_ref[...]
    near_copy(0).start()
    each(1, chips, lambda step: far_copy(step).start())

    def logits(step):
        @pl.when(step > 0)
        def _():
            far_copy(step).wait_recv()
            near_copy(step).start()

        near_copy(step).wait_recv()
        source = lax.rem(chip - step + chips, chips)
        start = pl.multiple_of(source * 2 * PICKS, 2 * PICKS)
        features = fall[pl.ds(source * 2, 2)].reshape(2 * PICKS, D)
        target = target_ref[pl.ds(start, 2 * PICKS), :] - base

        def score(j, peak):
            cut = lanes(j * part, part)
            value = nn(features, w_ref[:, cut])
            block[:, cut] = value
            return jnp.maximum(
                peak, jnp.max(jnp.where(live_ref[0:1, cut] > 0, value, NEG_BIG), axis=1, keepdims=True)
            )

        peak = lax.fori_loop(0, pieces, score, jnp.full((2 * PICKS, 1), NEG_BIG, FL))

        def count(j, carry):
            total, picked, valid = carry
            cut = lanes(j * part, part)
            value = block[:, cut]
            live = live_ref[0:1, cut] > 0
            hot = target - j * part == iota((2 * PICKS, part), 1)
            e = jnp.where(live, jnp.exp(value - peak), 0.0)
            expo[pl.ds(start, 2 * PICKS), cut] = e.astype(BF)
            total = total + jnp.sum(e, axis=1, keepdims=True)
            picked = picked + jnp.sum(jnp.where(hot, value, 0.0), axis=1, keepdims=True)
            valid = valid + jnp.sum(jnp.where(hot & live, 1.0, 0.0), axis=1, keepdims=True)
            return total, picked, valid

        zero = jnp.zeros((2 * PICKS, 1), FL)
        total, picked, valid = lax.fori_loop(0, pieces, count, (zero, zero, zero))
        lane = iota((2 * PICKS, 128), 1)
        wide = jnp.where(lane == 0, peak, jnp.where(lane == 1, total, jnp.where(lane == 2, picked, valid)))
        mine[:, pl.ds(start, 2 * PICKS)] = wide.T[:8, :]

    each(0, chips, logits)

    def stat_copy(step):
        return send(mine, stats.at[v], stat_out.at[step], stat_in.at[step], {"vocab": lax.rem(v + step, nv)})

    each(1, nv, lambda step: stat_copy(step).start())
    stats[v] = mine[...]
    for i in range(total_rows // 256 if pieces > 1 else 0):
        ft[:, i * 256 : (i + 1) * 256] = fall[2 * i : 2 * i + 2].reshape(256, D).T
    each(1, nv, lambda step: stat_copy(step).wait())
    start = jnp.full((1, total_rows), NEG_BIG, FL)
    peak = lax.fori_loop(0, nv, lambda u, top: jnp.maximum(top, stats[u, 0:1, :]), start)

    def combine(u, carry):
        scale = jnp.exp(stats[u, 0:1, :] - peak)
        return (
            carry[0] + stats[u, 1:2, :] * scale, carry[1] + stats[u, 2:3, :], carry[2] + stats[u, 3:4, :],
        )

    zero = jnp.zeros((1, total_rows), FL)
    total, picked, valid = lax.fori_loop(0, nv, combine, (zero, zero, zero))
    lse = peak + jnp.log(jnp.maximum(total, 1e-37))
    weight = valid / (jnp.maximum(jnp.sum(valid, axis=1, keepdims=True), 1.0) * nb)
    loss = jnp.sum(weight * (lse - picked), axis=1, keepdims=True)
    loss_ref[...] = jnp.broadcast_to(loss, loss_ref.shape)
    alpha = weight * jnp.exp(mine[0:1, :] - lse)
    line = iota((128, 256), 0)
    for i in range(total_rows // 256):
        cut = slice(i * 256, (i + 1) * 256)
        coef[cut, :] = jnp.where(line == 0, alpha[:, cut], weight[:, cut]).T

    tall = min(total_rows, 1024 if pieces > 1 else 256)
    shards_tall = tall // PICKS
    df[...] = jnp.zeros_like(df)

    def out_copy(j):
        return pltpu.make_async_copy(
            out.at[lax.rem(j, depth)], dw_ref.at[:, lanes(j * part, part)], dw_sem.at[lax.rem(j, depth)]
        )

    def gradients(j):
        cut = lanes(j * part, part)
        words = w_ref[:, cut]

        @pl.when(j >= depth)
        def _():
            out_copy(j - depth).wait()

        def strip(t):
            start = t * tall if total_rows == tall else pl.multiple_of(t * tall, tall)
            here = pl.ds(start, tall)
            hot = target_ref[here, :] - base - j * part == iota((tall, part), 1)
            two = coef[here, :]
            value = two[:, 0:1] * expo[here, cut].astype(FL) - jnp.where(hot, two[:, 1:2], 0.0)
            dlogits = value.astype(BF)
            df[here, :] += nt(dlogits, words)
            if pieces > 1:
                turned = ft[:, pl.ds(start, tall)]
            else:
                turned = fall[pl.ds(t * shards_tall, shards_tall)].reshape(tall, D).T
            for r in range(0, D, D // 3):
                more = nn(turned[r : r + D // 3, :], dlogits)
                if total_rows == tall:
                    out[lax.rem(j, depth), r : r + D // 3, :] = more.astype(BF)
                else:
                    grad_sum[r : r + D // 3, :] += more

        if total_rows == tall:
            strip(0)
        else:
            grad_sum[...] = jnp.zeros_like(grad_sum)
            each(0, total_rows // tall, strip)
            for r in range(0, D, D // 3):
                out[lax.rem(j, depth), r : r + D // 3, :] = grad_sum[r : r + D // 3, :].astype(BF)
        out_copy(j).start()

    each(0, pieces, gradients)

    def shard(index):
        return pl.ds(pl.multiple_of(index * PICKS, PICKS), PICKS)

    def pair_copy(k):
        source = df.at[shard(2 * k + 1 - core), :] if pieces > 1 else fall.at[k]
        return send(source, half.at[k], pair_out.at[k], pair_in.at[k], sibling)

    near_copy(0).wait_send()

    def drain(step):
        far_copy(step).wait_send()
        near_copy(step).wait_send()

    each(1, chips, drain)

    def swap(k):
        if pieces == 1:
            fall[k] = df[shard(2 * k + 1 - core), :].astype(BF)
        pair_copy(k).start()

    each(0, chips, swap)

    def sum_copy(step):
        return send(fall.at[chips + step], far_got.at[step], sum_out.at[step], sum_in.at[step], peer(step))

    def pass_on(turn):
        step = lax.rem(turn, chips)
        k = lax.rem(chip + step, chips)
        pair_copy(k).wait()
        value = df[shard(2 * k + core), :] + half[k].astype(FL)

        @pl.when(step > 0)
        def _():
            fall[chips + step] = value.astype(BF)
            sum_copy(step).start()

        @pl.when(step == 0)
        def _():
            df_ref[...] = value

    each(1, chips + 1, pass_on)

    def collect(step):
        sum_copy(step).wait()
        df_ref[...] += far_got[step].astype(FL)

    each(1, chips, collect)
    for j in range(pieces - depth, pieces):
        out_copy(j).wait()


def head(nb, nv, features, words, live, targets):
    rows = words.shape[1]
    part = chunk_of(rows, 640)
    total_rows = nv * PICKS
    chips = nv // 2
    dma = pltpu.SemaphoreType.DMA
    scratch = [
        pltpu.VMEM((nv, PICKS, D), BF),
        pltpu.VMEM((total_rows, rows), BF),
        pltpu.VMEM((2 * PICKS, rows), FL),
        pltpu.VMEM((8, total_rows), FL),
        pltpu.VMEM((nv, 8, total_rows), FL),
        pltpu.VMEM((D, total_rows) if rows > part else (8, 128), BF),
        pltpu.VMEM((8, 128) if rows > part else (D, part), FL),
        pltpu.VMEM((total_rows, 128), FL),
        pltpu.VMEM((total_rows, D), FL),
        pltpu.VMEM((chips, PICKS, D), FL if rows > part else BF),
        pltpu.VMEM((chips, PICKS, D), BF),
        pltpu.VMEM((min(2, rows // part), D, part), BF),
        dma((chips,)), dma((chips,)), dma((chips,)), dma((chips,)), dma((nv,)), dma((nv,)),
        dma((chips,)), dma((chips,)), dma((chips,)), dma((chips,)), dma((2,)),
    ]
    return run(
        functools.partial(head_kernel, nb, nv, part),
        [SD((PICKS, D), FL), SD((D, rows), BF), SD((8, 128), FL)],
        scratch,
        [features, words, live, targets],
        "head",
        1,
        out_specs=[VM, HB, VM],
    )


def wide_head_kernel(
    nb, nv, block_rows, f_ref, w_ref, live_ref, target_ref, df_ref, dw_ref, loss_ref,
    fall, ft, expo, words_sum, mine, first_got, merged, second_got, tile, third_got, tiles, coef, group, half, handed, mix_got,
    far_sum, far_got,
    z_out, z_in, mix_out, mix_in, near_out, near_in, s_out, s_in, pair_out, pair_in, give_out, give_in, sum_out, sum_in,
):
    b, v = lax.axis_index("batch"), lax.axis_index("vocab")
    rows = w_ref.shape[1]
    core, chip, chips = lax.rem(v, 2), v // 2, nv // 2
    sibling = {"vocab": v + 1 - 2 * core}
    base = v * block_rows + b * rows
    live = live_ref[:, lanes(b * rows, rows)] > 0
    span = nv * PICKS
    meet((("batch", nb), ("vocab", nv)))

    def column(line):
        line = jnp.where(line < (v + 1) * block_rows, line - base, -1).astype(FL)
        return jnp.broadcast_to(line, (128, 2 * PICKS)).T[:, 0:1].astype(I32)

    def peer(step):
        return {"vocab": lax.rem(chip + step, chips) * 2 + core}

    def other(step):
        return {"batch": lax.rem(b + step, nb)}

    def flip(s):
        low, high = lax.rem(b, 2), b // 2
        return (high if s < 2 else 1 - high) * 2 + (low if s % 2 == 0 else 1 - low)

    def slot(s, k):
        return flip(s) * nv + lax.rem(chip - k + chips, chips) * 2 + core

    def z_copy(k):
        return send(f_ref, fall.at[b * nv + v], z_out.at[k], z_in.at[k], peer(k))

    def mix_copy(s, k, way=0):
        if s < 3:
            place, device = fall.at[slot(0, k)], flip(s)
        else:
            place, device = fall.at[slot(3 - way, k)], flip(way)
        return send(place, place, mix_out.at[k, s], mix_in.at[k, s], {"batch": device})

    near = [s for s in (1, 2) if s < nb]

    def near_copy(s, k):
        place = fall.at[slot(s, k)]
        return send(place, place, near_out.at[k, s], near_in.at[k, s], sibling)

    def arrive(s, k):
        if s == 0:

            @pl.when(k > 0)
            def _():
                z_copy(k).wait_recv()

            for t in near:
                mix_copy(t, k).start()
        else:
            mix_copy(s, k, 1).wait_recv()
        if nb == 4 and s in (1, 2):

            @pl.when(lax.rem(k, 2) == s - 1)
            def _():
                mix_copy(3, k, 3 - s).start()

        near_copy(s, k).start()

    fall[b * nv + v] = f_ref[...]
    each(1, chips, lambda k: z_copy(k).start())
    arrive(0, 0)

    def logits(s, k):
        near_copy(s, k).wait_recv()
        p, c = flip(s), lax.rem(chip - k + chips, chips)
        first = p * nv + c * 2
        start = pl.multiple_of(first * PICKS, 2 * PICKS)
        features = fall[pl.ds(first, 2)].reshape(2 * PICKS, D)
        ft[:, pl.ds(start, 2 * PICKS)] = features.T
        line = target_ref[p, :, pl.ds(pl.multiple_of(c * 2 * PICKS, 2 * PICKS), 2 * PICKS)]
        target = column(line)
        value = nn(features, w_ref[...])
        value = jnp.where(live, value, NEG_BIG)
        peak = jnp.maximum(jnp.max(value, axis=1, keepdims=True), 0.1 * NEG_BIG)
        e = jnp.exp(value - peak)
        expo[pl.ds(start, 2 * PICKS), :] = e.astype(BF)
        total = jnp.sum(e, axis=1, keepdims=True)
        picked = jnp.sum(jnp.where(target == iota((2 * PICKS, rows), 1), value, 0.0), axis=1, keepdims=True)
        lane = iota((2 * PICKS, 128), 1)
        wide = jnp.where(lane == 0, peak, jnp.where(lane == 1, total, picked)).T
        mine[c * 2, p] = wide[:8, :PICKS]
        mine[c * 2 + 1, p] = wide[:8, PICKS:]

    for s in range(nb):

        def one(k, s=s):
            @pl.when(k + 1 < chips)
            def _():
                arrive(s, k + 1)

            if s + 1 < nb:

                @pl.when(k + 1 == chips)
                def _():
                    arrive(s + 1, 0)

            logits(s, k)

        each(0, chips, one)

    def merge(read, count):
        peak = lax.fori_loop(
            0, count, lambda u, top: jnp.maximum(top, read(u)[0:1, :]), jnp.full((1, PICKS), NEG_BIG, FL)
        )

        def add(u, carry):
            one = read(u)
            return carry[0] + one[1:2, :] * jnp.exp(one[0:1, :] - peak), carry[1] + one[2:3, :]

        zero = jnp.zeros((1, PICKS), FL)
        return (peak, *lax.fori_loop(0, count, add, (zero, zero)))

    def tile_of(rows_of):
        line = iota((8, PICKS), 0)
        value = jnp.zeros((8, PICKS), FL)
        for i, row in enumerate(rows_of):
            value = jnp.where(line == i, row, value)
        return value

    def first_copy(t):
        u = lax.rem(v + t, nv)
        return send(mine.at[u], first_got.at[v], s_out.at[0, t], s_in.at[0, t], {"vocab": u})

    each(1, nv, lambda t: first_copy(t).start())
    first_got[v] = mine[v]
    each(1, nv, lambda t: first_copy(t).wait())
    for p in range(nb):
        merged[p] = tile_of(merge(lambda u, p=p: first_got[u, p], nv))

    def second_copy(t):
        return send(merged.at[lax.rem(b + t, nb)], second_got.at[b], s_out.at[1, t], s_in.at[1, t], other(t))

    each(1, nb, lambda t: second_copy(t).start())
    second_got[b] = merged[b]
    each(1, nb, lambda t: second_copy(t).wait())
    peak, total, picked = merge(lambda u: second_got[u], nb)
    valid = (picked > 0.5 * NEG_BIG).astype(FL)
    tile[...] = tile_of((peak + jnp.log(jnp.maximum(total, 1e-37)), picked, valid))

    def third_copy(t):
        return send(tile, third_got.at[b], s_out.at[2, t], s_in.at[2, t], other(t))

    each(1, nb, lambda t: third_copy(t).start())
    third_got[b] = tile[...]
    each(1, nb, lambda t: third_copy(t).wait())

    def last_copy(t):
        return send(third_got, tiles.at[v], s_out.at[3, t], s_in.at[3, t], {"vocab": lax.rem(v + t, nv)})

    each(1, nv, lambda t: last_copy(t).start())
    tiles[v] = third_got[...]
    each(1, nv, lambda t: last_copy(t).wait())

    def coefficients(p):
        count = lax.fori_loop(0, nv, lambda u, total: total + tiles[u, p, 2:3, :], jnp.zeros((1, PICKS), FL))
        share = 1.0 / (jnp.maximum(jnp.sum(count, axis=1, keepdims=True), 1.0) * nb)

        def spread(c, loss):
            rows_of = []
            for side in range(2):
                u = c * 2 + side
                lse, picked, valid = (tiles[u, p, i : i + 1, :] for i in range(3))
                weight = valid * share
                loss = loss + weight * (lse - picked)
                rows_of.append((weight * jnp.exp(mine[u, p, 0:1, :] - lse), weight))
            line = iota((128, 2 * PICKS), 0)
            alpha = jnp.concatenate([rows_of[0][0], rows_of[1][0]], axis=1)
            weight = jnp.concatenate([rows_of[0][1], rows_of[1][1]], axis=1)
            start = pl.multiple_of(p * span + c * 2 * PICKS, 2 * PICKS)
            coef[pl.ds(start, 2 * PICKS), :] = jnp.where(line == 0, alpha, weight).T
            return loss

        loss = lax.fori_loop(0, chips, spread, jnp.zeros((1, PICKS), FL))

        @pl.when(p == b)
        def _():
            loss_ref[...] = jnp.broadcast_to(jnp.sum(loss, axis=1, keepdims=True), loss_ref.shape)

    each(0, nb, coefficients)

    def shard(k, side):
        return pl.ds(pl.multiple_of((2 * k + side) * PICKS, PICKS), PICKS)

    def pair_copy(s, k):
        return send(handed.at[s, k], half.at[s, k], pair_out.at[s, k], pair_in.at[s, k], sibling)

    def give_copy(s, k):
        if s < 3:
            return send(handed.at[s, k], mix_got.at[s, k], give_out.at[s, k], give_in.at[s, k], {"batch": flip(s)})
        device = jnp.where(lax.rem(k, 2) == 0, flip(1), flip(2))
        return send(handed.at[3, k], mix_got.at[3, k], give_out.at[3, k], give_in.at[3, k], {"batch": device})

    def exchange(s):
        def add(k):
            pair_copy(s, k).wait()
            value = group[s % 2, shard(k, core), :] + half[s, k].astype(FL)
            handed[s, k] = value.astype(BF)
            if nb == 4 and s in (1, 2):

                @pl.when(lax.rem(k, 2) == 2 - s)
                def _():
                    give_copy(3, k).wait_recv()
                    handed[s, k] = (value + mix_got[3, k].astype(FL)).astype(BF)

            if s > 0:
                give_copy(s, k).start()

        each(0, chips, add)

    order = [3, 2, 1, 0] if nb == 4 else [1, 0]
    for turn, s in enumerate(order):
        p = flip(s)

        def strip(c, p=p):
            start = pl.multiple_of(p * span + c * 2 * PICKS, 2 * PICKS)
            here = pl.ds(start, 2 * PICKS)
            line = target_ref[p, :, pl.ds(pl.multiple_of(c * 2 * PICKS, 2 * PICKS), 2 * PICKS)]
            target = column(line)
            two = coef[here, :]
            hot = target == iota((2 * PICKS, rows), 1)
            value = two[:, 0:1] * expo[here, :].astype(FL) - jnp.where(hot, two[:, 1:2], 0.0)
            expo[here, :] = value.astype(BF)

        each(0, chips, strip)
        if turn > 0:
            exchange(order[turn - 1])

        def features_grad(i, p=p, s=s):
            here = pl.ds(pl.multiple_of(i * 512, 512), 512)
            group[s % 2, here, :] = nt(expo[pl.ds(pl.multiple_of(p * span + i * 512, 512), 512), :], w_ref[...])

        each(0, span // 512, features_grad)

        def swap(k, s=s):
            handed[s, k] = group[s % 2, shard(k, 1 - core), :].astype(BF)
            pair_copy(s, k).start()

        each(0, chips, swap)

    words_sum[...] = jnp.zeros_like(words_sum)

    def words_grad(i):
        cut = lanes(i * 512, 512)
        words_sum[...] += nn(ft[:, cut], expo[cut, :])

    strips = nb * span // 512
    each(0, 1, words_grad)
    exchange(0)
    each(1, strips // 2, words_grad)

    def total_of(k):
        value = handed[0, k].astype(FL)
        for s in near:
            give_copy(s, k).wait_recv()
            value = value + mix_got[s, k].astype(FL)
        return value

    def sum_copy(t):
        return send(far_sum.at[t], far_got.at[t], sum_out.at[t], sum_in.at[t], peer(t))

    def pass_on(t):
        far_sum[t] = total_of(lax.rem(chip + t, chips)).astype(BF)
        sum_copy(t).start()

    each(1, chips, pass_on)
    each(strips // 2, strips, words_grad)
    dw_ref[...] = words_sum[...].astype(BF)
    df_ref[...] = total_of(chip)

    def collect(t):
        sum_copy(t).wait()
        df_ref[...] += far_got[t].astype(FL)

    each(1, chips, collect)
    each(1, chips, lambda k: z_copy(k).wait_send())
    for s in range(nb):
        each(0, chips, lambda k, s=s: near_copy(s, k).wait_send())
        if s > 0:
            each(0, chips, lambda k, s=s: mix_copy(s, k, 1).wait_send())
            each(0, chips, lambda k, s=s: give_copy(s, k).wait_send())


def wide_head(nb, nv, block_rows, features, words, live, targets):
    rows = words.shape[1]
    tokens = nb * nv * PICKS
    chips = nv // 2
    dma = pltpu.SemaphoreType.DMA
    most = max(nb, nv)
    scratch = [
        pltpu.VMEM((nb * nv, PICKS, D), BF),
        pltpu.VMEM((D, tokens), BF),
        pltpu.VMEM((tokens, rows), BF),
        pltpu.VMEM((D, rows), FL),
        pltpu.VMEM((nv, nb, 8, PICKS), FL),
        pltpu.VMEM((nv, nb, 8, PICKS), FL),
        pltpu.VMEM((nb, 8, PICKS), FL),
        pltpu.VMEM((nb, 8, PICKS), FL),
        pltpu.VMEM((8, PICKS), FL),
        pltpu.VMEM((nb, 8, PICKS), FL),
        pltpu.VMEM((nv, nb, 8, PICKS), FL),
        pltpu.VMEM((tokens, 128), FL),
        pltpu.VMEM((2, nv * PICKS, D), FL),
        pltpu.VMEM((nb, chips, PICKS, D), BF),
        pltpu.VMEM((nb, chips, PICKS, D), BF),
        pltpu.VMEM((nb, chips, PICKS, D), BF),
        pltpu.VMEM((chips, PICKS, D), BF),
        pltpu.VMEM((chips, PICKS, D), BF),
        dma((chips,)), dma((chips,)), dma((chips, nb)), dma((chips, nb)), dma((chips, nb)), dma((chips, nb)),
        dma((4, most)), dma((4, most)), dma((nb, chips)), dma((nb, chips)), dma((nb, chips)), dma((nb, chips)),
        dma((chips,)), dma((chips,)),
    ]
    return run(
        functools.partial(wide_head_kernel, nb, nv, block_rows),
        [SD((PICKS, D), FL), SD((D, rows), BF), SD((8, 128), FL)],
        scratch,
        [features, words, live, targets],
        "wide_head",
        1,
    )


def norm(nb, nv, extra, dw, sums, loss):
    return run(
        functools.partial(norm_kernel, nb, nv), [SD((8, 128), FL)], add_up_scratch(nb, nv),
        [extra, dw, *sums, loss], "norm", 5,
    )[0]


def adamw(weight, moment, square, gradient, clip, count, decay, rate):
    gradient = gradient * clip
    moment = BETA_ONE * moment + (1 - BETA_ONE) * gradient
    square = BETA_TWO * square + (1 - BETA_TWO) * gradient * gradient
    fixed_moment = moment / (1 - BETA_ONE**count)
    fixed_square = square / (1 - BETA_TWO**count)
    weight = weight - rate * (fixed_moment / (jnp.sqrt(fixed_square) + ADAM_EPS) + decay * weight)
    return (weight, moment, square)


def slot_size(nv):
    mean = SEQ_LEN // nv
    return -(-(mean + int(5.5 * math.sqrt(mean))) // 32) * 32


def shards(
    nb, nv,
    tokens, targets, segments, counted, vocab_mask, step_count,
    table, table_moment, table_square,
    attend, attend_moment, attend_square,
    project, project_moment, project_square,
    expand, expand_moment, expand_square,
    contract, contract_moment, contract_square,
    gain, gain_moment, gain_square,
    shift, shift_moment, shift_square,
):
    rows, width = table.shape
    cap = slot_size(nv)
    table_t = table.T
    norms = jnp.concatenate([gain, shift], axis=0)
    packed = jnp.concatenate([attend[0], norms.T, jnp.zeros((width, EXTRA - 6), FL)], axis=1).astype(BF)
    pieces = (packed, project[0].astype(BF), expand[0].astype(BF), contract[0].astype(BF))
    split = nb * nv * PICKS <= 4096
    rounded = table_t.astype(BF)
    quarter = -(-rows // (nb * 128)) * 128
    if split:
        rounded = jnp.pad(rounded, ((0, 0), (0, nb * quarter - rows)))
    else:
        words = lax.all_gather(rounded, "batch", axis=0, tiled=True)

    seg_row, pos_row = segments[None, :], counted[None, :]
    tok = tokens.reshape(nv, SEQ_LEN)
    x, ids, place, most, every, a_all, u_all, *rest = embed(
        nb, nv, cap, rows, jnp.zeros((1,), I32), tok, rounded, (pieces[0], pieces[2]),
        targets[None, :] if split else None,
    )
    turns = (most[0] + cap - 1) // cap

    def more_rows(state):
        turn, total = state
        return turn + 1, total + embed(nb, nv, cap, rows, turn[None], tok, rounded)[0]

    x = lax.while_loop(lambda state: state[0] < turns, more_rows, (jnp.int32(1), x))[1]

    hall, kv, q, hq, xq, mixed, lse, norm_rows, mixing_t, p_all, c_all = run(
        functools.partial(attend_kernel, nb, nv),
        [
            SD((KEYS, D), BF), SD((KEYS, 2 * D), BF), SD((PICKS, D), BF), SD((PICKS, D), BF), SD((PICKS, D), FL),
            SD((PICKS, D), BF), SD((NPAIR, 2, PICKS), FL), SD((8, D), FL), SD((SEQ_LEN, SLOTS * NB), BF),
            SD((D, D), BF), SD((FF, D), BF),
        ],
        weight_semaphores(2),
        [x, a_all, seg_row, pos_row, pieces[1], pieces[3]],
        "attend", 6, flops=7 * 10**9, moved=20 * 10**6,
        out_specs=[VM] * 9 + [HB] * 2,
    )
    x1, h2, z, act, x2, features = run(
        feed_kernel,
        [
            SD((PICKS, D), FL), SD((PICKS, D), BF), SD((PICKS, FF), FL), SD((PICKS, FF), BF), SD((PICKS, D), FL),
            SD((PICKS, D), BF),
        ],
        [],
        [xq, mixed, p_all, u_all, c_all, norm_rows],
        "feed", flops=2 * 10**9, moved=15 * 10**6,
    )
    if split:
        live = jnp.pad(vocab_mask, (0, nb * quarter - rows))[None, :]
        df, dw, loss_block = wide_head(nb, nv, rows, features, rest[0], live, rest[1])
    else:
        df, dw, loss_block = head(nb, nv, features, words, vocab_mask[None, :], targets[:, None])
        dw_sum = lax.psum_scatter(dw, "batch", scatter_dimension=0, tiled=True)

    dc, du, dp, dx1, dmixed, dnorm = run(
        feed_back_kernel,
        [
            SD((FF, D), BF), SD((D, FF), BF), SD((D, D), BF), SD((PICKS, D), FL), SD((PICKS, D), BF), SD((8, D), FL),
        ],
        [pltpu.VMEM((PICKS, D), FL)],
        [df, x2, x1, h2, z, act, mixed, p_all, u_all, c_all, norm_rows],
        "feed_back", flops=4 * 10**9, moved=30 * 10**6,
    )
    da, dx, du_sum = run(
        functools.partial(attend_back_kernel, nb, nv),
        [SD((D, 3 * D + EXTRA), BF), SD((SEQ_LEN, D), BF), SD((width, FF // 2), BF)],
        [
            pltpu.VMEM((KEYS, 2 * D), BF), pltpu.VMEM((PICKS, D), BF), pltpu.VMEM((D, KEYS), BF),
            pltpu.VMEM((SEQ_LEN, D), FL), pltpu.VMEM((SEQ_LEN, D), FL), pltpu.VMEM((SLOTS * NB, D), BF),
            pltpu.VMEM((SEQ_LEN, PICKS), BF), *gradient_scratch(nb, nv, [du.shape], (0,), False),
        ],
        [dmixed, q, kv, lse, hall, hq, a_all, x, dx1, mixing_t, seg_row, pos_row, norm_rows, dnorm, du],
        "attend_back", 7, flops=12 * 10**9, moved=25 * 10**6,
        in_specs=[VM] * 14 + [HB],
    )
    extra, *sums = unembed(nb, nv, cap, width, rows, dx, ids, place, (da, dp, du_sum, dc), *((dw, loss_block) if split else ()))
    if split:
        *sums, dw_sum, totals, norm_grads = sums

    def more_grads(state):
        turn, total = state
        later = later_slots(nv, cap, rows, every, turn)
        return turn + 1, total + unembed(
            nb, nv, cap, width, rows, dx, later, place - jnp.array([0, 1, 0, 0, 0, 0, 0, 0], I32)[None, :, None] * (turn * cap)
        )[0]

    extra = lax.while_loop(lambda state: state[0] < turns, more_grads, (jnp.int32(1), extra))[1]

    if split:
        totals = lax.cond(
            turns > 1, lambda: norm(nb, nv, extra, dw_sum, sums, loss_block), lambda: totals
        )
    else:
        totals = norm(nb, nv, extra, dw_sum, sums, loss_block)
    grad_table = dw_sum[:, :rows].astype(FL) + extra
    grad_a, grad_p, grad_u, grad_c = (item.astype(FL) for item in sums)
    grad_norms = norm_grads if split else grad_a[:, 3 * D : 3 * D + 6].T
    grad_a = grad_a[:, : 3 * D]
    squares, loss = totals[0, 0], totals[1, 0]
    gradient_norm = jnp.sqrt(squares)
    clip = jnp.minimum(1.0, MAX_NORM / (gradient_norm + 1e-06))
    count = step_count[0].astype(FL)

    def update(weight, moment, square, gradient, decay=DECAY, rate=LEARN_RATE):
        return adamw(weight, moment, square, gradient, clip, count, decay, rate)

    table_out = [item.T for item in update(table_t, table_moment.T, table_square.T, grad_table)]
    attend_out = update(attend, attend_moment, attend_square, grad_a[None])
    project_out = update(project, project_moment, project_square, grad_p[None])
    expand_out = update(expand, expand_moment, expand_square, grad_u[None])
    contract_out = update(contract, contract_moment, contract_square, grad_c[None])
    gain_out = update(gain, gain_moment, gain_square, grad_norms[:3], 0.0, NORM_RATE)
    shift_out = update(shift, shift_moment, shift_square, grad_norms[3:6], 0.0, NORM_RATE)
    return (
        loss, gradient_norm, *table_out, *attend_out, *project_out, *expand_out, *contract_out, *gain_out, *shift_out,
    )


def solution(mesh):
    nb, nv = mesh.shape["batch"], mesh.shape["vocab"]
    both, split, middle, last = P(("batch", "vocab")), P("vocab", "batch"), P(None, "batch", None), P(None, "batch")
    state = (split,) * 3 + (middle,) * 12 + (last,) * 6
    return jax.shard_map(
        functools.partial(shards, nb, nv),
        mesh=mesh,
        in_specs=(P("batch"), P("batch"), both, both, P("vocab"), P()) + state,
        out_specs=(P(), P()) + state,
        check_vma=False,
    )
```

```python
import functools
import math

import jax
import jax.numpy as jnp
from jax import lax
from jax.experimental import pallas as pl
from jax.experimental.pallas import tpu as pltpu
from jax.sharding import PartitionSpec as P

D = 768
H = 12
HD = 64
FF = 3072
NB = 256
SEG_BLOCKS = 4
SLOTS = SEG_BLOCKS - 2
SEQ_LEN = 1024
PICKS = 128
KEYS = SLOTS * NB + SEQ_LEN
BLK = 256
PAIR = 2 * HD
NPAIR = H // 2
EXTRA = 256
WIDE = (3 * D + EXTRA, D, FF, D)

NORM_EPS = 1e-05
MAX_NORM = 0.02
LEARN_RATE = 0.04
NORM_RATE = 0.5
BETA_ONE = 0.9
BETA_TWO = 0.999
ADAM_EPS = 1e-08
DECAY = 0.1
NEG_BIG = -1e30
BF = jnp.bfloat16
FL = jnp.float32
I32 = jnp.int32
MESH = pl.DeviceIdType.MESH
SD = jax.ShapeDtypeStruct
VM = pl.BlockSpec(memory_space=pltpu.VMEM)
SM = pl.BlockSpec(memory_space=pltpu.SMEM)
HB = pl.BlockSpec(memory_space=pl.ANY)
LIMIT = 62 * 2**20


def nn(a, b):
    return lax.dot_general(a, b, (((1,), (0,)), ((), ())), preferred_element_type=FL)


def nt(a, b):
    return lax.dot_general(a, b, (((1,), (1,)), ((), ())), preferred_element_type=FL)


def iota(shape, axis):
    return lax.broadcasted_iota(I32, shape, axis)


def lanes(start, size):
    return pl.ds(pl.multiple_of(start, 128), size)


def chunk_of(rows, want):
    return want if rows % want == 0 else rows


def run(kernel, outs, scratch, ins, name, collective=None, flops=0, moved=0, out_specs=None, in_specs=None):
    return pl.pallas_call(
        kernel,
        out_shape=outs,
        in_specs=in_specs if in_specs is not None else [VM] * len(ins),
        out_specs=out_specs if out_specs is not None else [VM] * len(outs),
        scratch_shapes=scratch,
        compiler_params=pltpu.CompilerParams(
            vmem_limit_bytes=LIMIT,
            collective_id=collective,
            has_side_effects=collective is not None,
        ),
        cost_estimate=pl.CostEstimate(flops=flops, bytes_accessed=moved, transcendentals=0),
        name=name,
    )(*ins)


def send(source, target, out_sem, in_sem, device):
    return pltpu.make_async_remote_copy(
        src_ref=source, dst_ref=target, send_sem=out_sem, recv_sem=in_sem, device_id=device, device_id_type=MESH
    )


def meet(axes):
    barrier = pltpu.get_barrier_semaphore()
    count = 0
    for axis, size in axes:
        me = lax.axis_index(axis)

        def greet(step, carry, axis=axis, size=size, me=me):
            pl.semaphore_signal(barrier, inc=1, device_id={axis: lax.rem(me + step, size)}, device_id_type=MESH)
            return carry

        lax.fori_loop(1, size, greet, 0)
        count += size - 1
    pl.semaphore_wait(barrier, count)


def each(start, stop, body):
    def step(index, carry):
        body(index)
        return carry

    lax.fori_loop(start, stop, step, 0)


def embed_kernel(
    nb, nv, cap, part, rows, first, split, *refs
):
    round_ref, tok_ref, words = refs[:3]
    shards, refs = (refs[3:5], refs[5:]) if first else ((), refs[3:])
    target_ref, refs = (refs[0], refs[1:]) if split else (None, refs)
    x_ref, ids_ref, place_ref, most_ref, tok_ref_all = refs[:5]
    wholes, refs = (refs[5:7], refs[7:]) if first else ((), refs[5:])
    (quarter_ref, target_all), refs = (refs[:2], refs[2:]) if split else ((None, None), refs)
    before, ranks, work, sent, got, spread, mixed, turned = refs[:8]
    tok_out, tok_in, row_out, row_in, mix_out, mix_in = refs[8:14]
    b, v = lax.axis_index("batch"), lax.axis_index("vocab")
    width = words.shape[0]
    shift = round_ref[0] * cap
    meet((("batch", nb), ("vocab", nv)))
    gather = WeightGather(nb, shards, wholes, *refs[14:19]) if first else None
    quarter_out, quarter_in, quarter_own, target_out, target_in = refs[19:24] if split else [None] * 5

    def tok_copy(step):
        return send(
            tok_ref, tok_ref_all.at[b], tok_out.at[step], tok_in.at[step], {"batch": lax.rem(b + step, nb)}
        )

    for step in range(1, nb):
        tok_copy(step).start()

    def target_copy(step):
        return send(
            target_ref, target_all.at[b], target_out.at[step], target_in.at[step], {"batch": lax.rem(b + step, nb)}
        )

    def quarter(owner):
        return words.at[:, lanes(owner * (words.shape[1] // nb), words.shape[1] // nb)]

    def quarter_copy(step):
        other = lax.rem(b + step, nb)
        place = quarter_ref.at[pl.ds(pl.multiple_of(b * width, 16), width), :]
        return send(quarter(other), place, quarter_out.at[step], quarter_in.at[step], {"batch": other})

    def quarter_keep():
        place = quarter_ref.at[pl.ds(pl.multiple_of(b * width, 16), width), :]
        return pltpu.make_async_copy(quarter(b), place, quarter_own.at[0])

    if split:
        target_all[b] = target_ref[...]
        for step in range(1, nb):
            target_copy(step).start()
    if first:
        gather.start()
    if split:
        quarter_keep().start()
    tok_ref_all[b] = tok_ref[...]
    before[...] = (iota((SEQ_LEN, SEQ_LEN), 0) < iota((SEQ_LEN, SEQ_LEN), 1)).astype(FL).astype(BF)
    for step in range(1, nb):
        tok_copy(step).wait()

    base = v * rows
    most = jnp.zeros((nv, 1), FL)
    for p in range(nb):
        ids = tok_ref_all[p]
        mine = (ids >= base) & (ids < base + rows)
        rank = nn(mine.astype(FL).astype(BF), before[...])
        ranks[p] = jnp.where(mine, rank.astype(I32) - shift, -1)
        for owner in range(nv):
            theirs = (ids >= owner * rows) & (ids < (owner + 1) * rows)
            most = jnp.maximum(most, jnp.sum(theirs.astype(FL), axis=1, keepdims=True))
    most_ref[0] = jnp.max(most).astype(I32)

    def row_copy(step):
        return send(
            sent.at[step], got.at[v], row_out.at[step], row_in.at[step], {"vocab": lax.rem(v + step, nv)}
        )

    def build(turn):
        step = lax.rem(turn, nv)
        dest = lax.rem(v + step, nv)
        found = []
        for p in range(nb):
            pick = (iota((cap, SEQ_LEN), 0) == ranks[p, pl.ds(dest, 1), :]).astype(FL).astype(BF)
            local = tok_ref_all[p, pl.ds(dest, 1), :] - base
            line = iota((8, SEQ_LEN), 0)
            high, low = lax.shift_right_arithmetic(local, 7), lax.bitwise_and(local, 127)
            digits = jnp.where(line == 0, high, jnp.where(line == 1, low, 0)).astype(FL).astype(BF)
            both = nt(pick, digits)
            found.append((both[:, 0:1] * 128.0 + both[:, 1:2]).astype(I32))
        index = jnp.concatenate(found, axis=0)
        ids_ref[dest] = index
        work[...] = jnp.zeros_like(work)

        def piece(j):
            hot = (index - j * part == iota((nb * cap, part), 1)).astype(FL).astype(BF)
            work[...] += nt(hot, words[:, lanes(j * part, part)])

        each(0, rows // part, piece)
        block = work[...].T.astype(BF)

        @pl.when(step > 0)
        def _():
            sent[step] = block
            row_copy(step).start()

        @pl.when(step == 0)
        def _():
            got[v] = block

    each(1, nv // 2 + 1, build)
    if first:
        gather.pass_on()
    if split:
        for step in range(1, nb):
            quarter_copy(step).start()
    each(nv // 2 + 1, nv + 1, build)

    keys = []
    for p in range(nb):
        ids = tok_ref_all[p, pl.ds(v, 1), :]
        owner = iota((nv, SEQ_LEN), 0)
        theirs = (ids >= owner * rows) & (ids < (owner + 1) * rows)
        rank = nn(theirs.astype(FL).astype(BF), before[...])
        place = jnp.sum(jnp.where(theirs, rank, 0.0), axis=0, keepdims=True).astype(I32) - shift
        holder = jnp.sum(jnp.where(theirs, owner.astype(FL), 0.0), axis=0, keepdims=True).astype(I32)
        line = iota((8, SEQ_LEN), 0)
        place_ref[p] = jnp.where(line == 0, holder, jnp.where(line == 1, place, 0))
        keys.append((holder, place))
        spread[p] = jnp.zeros((width, SEQ_LEN), FL)

    def take(turn):
        step = lax.rem(turn, nv)
        source = lax.rem(v - step + nv, nv)

        @pl.when(step > 0)
        def _():
            row_copy(step).wait()

        block = got[source]
        for p in range(nb):
            holder, place = keys[p]
            key = jnp.where(holder == source, place, -1)
            hot = (iota((cap, SEQ_LEN), 0) == key).astype(FL).astype(BF)
            spread[p] += nn(block[:, p * cap : (p + 1) * cap], hot)

    each(1, nv + 1, take)

    def mix_copy(step):
        return send(
            mixed.at[step], turned.at[b], mix_out.at[step], mix_in.at[step], {"batch": lax.rem(b + step, nb)}
        )

    for step in range(1, nb):
        mixed[step] = spread[lax.rem(b + step, nb)].astype(BF)
        mix_copy(step).start()
    turned[b] = spread[b].astype(BF)
    for step in range(1, nb):
        mix_copy(step).wait()
    x_ref[...] = turned[...].reshape(nb * width, SEQ_LEN).T
    if first:
        gather.last_hop()
        for w in range(len(shards)):
            gather.finish(w)
    if split:
        quarter_keep().wait()
        for step in range(1, nb):
            target_copy(step).wait()
            quarter_copy(step).wait()


def weight_semaphores(count):
    return [pltpu.SemaphoreType.DMA((count,))] + [pltpu.SemaphoreType.DMA((count, 4))] * 4


class WeightGather:
    def __init__(self, nb, shards, wholes, own_sem, out_sem, in_sem, pair_out, pair_in):
        self.nb, self.shards, self.wholes = nb, shards, wholes
        self.own_sem, self.out_sem, self.in_sem, self.pair_out, self.pair_in = own_sem, out_sem, in_sem, pair_out, pair_in
        self.b, v = lax.axis_index("batch"), lax.axis_index("vocab")
        self.core = lax.rem(v, 2)
        self.sibling = {"vocab": v + 1 - 2 * self.core}

    def flip(self, bits):
        b = self.b
        low, high = lax.rem(b, 2), b // 2
        return (high if bits < 2 else 1 - high) * 2 + (low if bits % 2 == 0 else 1 - low)

    def place(self, w, owner, top, size):
        rows = self.shards[w].shape[0]
        first = pl.multiple_of(owner * rows + self.core * (rows // 2) + top, 16)
        return self.wholes[w].at[pl.ds(first, size), :]

    def routes(self, w):
        rows = self.shards[w].shape[0] // 2
        if self.nb == 4:
            half = rows // 2
            return [
                (self.b, 0, rows, self.flip(1), self.flip(1)),
                (self.b, 0, rows, self.flip(2), self.flip(2)),
                (self.flip(1), 0, half, self.flip(2), self.flip(3)),
                (self.flip(2), half, half, self.flip(1), self.flip(3)),
            ]
        others = [lax.rem(self.b + step, self.nb) for step in range(1, self.nb)]
        came = [lax.rem(self.b - step + self.nb, self.nb) for step in range(1, self.nb)]
        return [(self.b, 0, rows, other, source) for other, source in zip(others, came)]

    def own_copy(self, w):
        rows = self.shards[w].shape[0]
        first = pl.multiple_of(self.b * rows, 16)
        return pltpu.make_async_copy(self.shards[w], self.wholes[w].at[pl.ds(first, rows), :], self.own_sem.at[w])

    def copy(self, w, k):
        owner, top, size, device, _ = self.routes(w)[k]
        if self.nb == 4 and k >= 2:
            source = self.place(w, owner, top, size)
        else:
            source = self.shards[w].at[pl.ds(pl.multiple_of(self.core * size, 16), size), :]
        target = self.place(w, owner, top, size)
        return send(source, target, self.out_sem.at[w, k], self.in_sem.at[w, k], {"batch": device})

    def pair(self, w, k):
        _, top, size, _, arrived = self.routes(w)[k]
        ref = self.place(w, arrived, top, size)
        return send(ref, ref, self.pair_out.at[w, k], self.pair_in.at[w, k], self.sibling)

    def start(self):
        for w in range(len(self.shards)):
            for k in range(2 if self.nb == 4 else self.nb - 1):
                self.copy(w, k).start()
        for w in range(len(self.shards)):
            self.own_copy(w).start()

    def pass_on(self):
        if self.nb != 4:
            return
        for w in range(len(self.shards)):
            for k in range(2):
                self.copy(w, k).wait_recv()
                self.copy(w, k + 2).start()
                self.pair(w, k).start()

    def last_hop(self):
        for w in range(len(self.shards)):
            for k in range(2 if self.nb == 4 else 0, len(self.routes(w))):
                self.copy(w, k).wait_recv()
                self.pair(w, k).start()

    def finish(self, w):
        self.own_copy(w).wait()
        for k in range(len(self.routes(w))):
            self.copy(w, k).wait_send()
            self.pair(w, k).wait()


def embed(nb, nv, cap, rows, turn, tok, table, shards=(), targets=None):
    width = table.shape[0]
    split = targets is not None
    part = chunk_of(rows, 640)
    count = nb * cap
    outs = [
        SD((SEQ_LEN, D), BF),
        SD((nv, count, 1), I32),
        SD((nb, 8, SEQ_LEN), I32),
        SD((1,), I32),
        SD((nb, nv, SEQ_LEN), I32),
    ]
    first = len(shards) > 0
    outs += [SD((nb * item.shape[0], item.shape[1]), BF) for item in shards]
    if split:
        outs += [SD((D, table.shape[1] // nb), BF), SD((nb, *targets.shape), I32)]
    dma = pltpu.SemaphoreType.DMA
    scratch = [
        pltpu.VMEM((SEQ_LEN, SEQ_LEN), BF),
        pltpu.VMEM((nb, nv, SEQ_LEN), I32),
        pltpu.VMEM((count, width), FL),
        pltpu.VMEM((nv, width, count), BF),
        pltpu.VMEM((nv, width, count), BF),
        pltpu.VMEM((nb, width, SEQ_LEN), FL),
        pltpu.VMEM((nb, width, SEQ_LEN), BF),
        pltpu.VMEM((nb, width, SEQ_LEN), BF),
        dma((nb,)), dma((nb,)), dma((nv,)), dma((nv,)), dma((nb,)), dma((nb,)),
    ]
    if first:
        scratch += weight_semaphores(len(shards))
    if split:
        scratch += [dma((nb,)), dma((nb,)), dma((1,)), dma((nb,)), dma((nb,))]
    extra = [targets] if split else []
    return run(
        functools.partial(embed_kernel, nb, nv, cap, part, rows, first, split), outs, scratch,
        [turn, tok, table, *shards, *extra],
        "embed" if first else "embed_more", 0 if first else 3,
        in_specs=[SM, VM, VM] + [VM] * len(shards) + [VM] * len(extra),
        out_specs=[VM] * 3 + [SM, VM] + [HB] * len(shards) + ([HB, VM] if split else []),
    )


class GradientSum:
    def __init__(self, nb, nv, grads, refs, totals=None, sums=None):
        self.nb, self.nv, self.grads, self.sums = nb, nv, grads, sums
        self.todo = [w for w, item in enumerate(grads) if item is not None]
        take = iter(refs)
        spread = lambda keys: {w: next(take) for w in keys}
        everything = range(len(grads))
        self.own, self.near, self.shard = spread(self.todo), spread(self.todo), spread(self.todo)
        if sums is not None:
            self.total = spread(self.todo)
            self.total.update(totals)
            self.bits, self.result = spread(everything), spread(everything)
        else:
            self.total = totals
        self.load_sem, self.pair_out, self.pair_in, self.mix_out, self.mix_in = (next(take) for _ in range(5))
        if sums is not None:
            (self.cut_out, self.cut_in, self.all_out, self.all_in, self.last_out, self.last_in,
             self.store_sem) = take
        self.b, v = lax.axis_index("batch"), lax.axis_index("vocab")
        self.core, self.chip, self.chips = lax.rem(v, 2), v // 2, nv // 2
        self.sibling = {"vocab": v + 1 - 2 * self.core}

    def half(self, w, core):
        cols = self.total[w].shape[1]
        return lanes(core * cols, cols)

    def load(self, w):
        return pltpu.make_async_copy(self.grads[w].at[:, self.half(w, self.core)], self.own[w], self.load_sem.at[w])

    def pair(self, w):
        source = self.grads[w].at[:, self.half(w, 1 - self.core)]
        return send(source, self.near[w], self.pair_out.at[w], self.pair_in.at[w], self.sibling)

    def start(self):
        for w in sorted(self.todo, reverse=True):
            self.pair(w).start()
            self.load(w).start()

    def flip(self, bits):
        low, high = lax.rem(self.b, 2), self.b // 2
        return (high if bits < 2 else 1 - high) * 2 + (low if bits % 2 == 0 else 1 - low)

    def rows_of(self, w, owner, top, size):
        rows = self.own[w].shape[0] // self.nb
        return pl.ds(pl.multiple_of(owner * rows + top, 16), size)

    def mix(self, w, step):
        rows = self.own[w].shape[0] // self.nb
        other = self.flip(step) if self.nb == 4 else lax.rem(self.b + step, self.nb)
        source = self.own[w].at[self.rows_of(w, other, 0, rows), :]
        return send(source, self.shard[w].at[step], self.mix_out.at[w, step], self.mix_in.at[w, step], {"batch": other})

    def corner(self, w, way):
        half = self.own[w].shape[0] // self.nb // 2
        cut = pl.ds((way - 1) * half, half)
        source = self.own[w].at[self.rows_of(w, self.flip(3), (way - 1) * half, half), :]
        at = 3 * (way - 1)
        return send(
            source, self.shard[w].at[3, cut, :], self.mix_out.at[w, at], self.mix_in.at[w, at], {"batch": self.flip(way)}
        )

    def relay(self, w):
        if self.nb != 4:
            return
        half = self.own[w].shape[0] // self.nb // 2
        for way in (1, 2):
            self.corner(w, way).wait()
            cut = pl.ds((way - 1) * half, half)
            here = self.rows_of(w, self.flip(3 - way), (way - 1) * half, half)
            self.own[w][here, :] = (self.own[w][here, :].astype(FL) + self.shard[w][3, cut, :].astype(FL)).astype(BF)
        for step in (1, 2):
            self.mix(w, step).start()

    def steps(self):
        return (1, 2) if self.nb == 4 else range(1, self.nb)

    def scatter(self, w):
        self.load(w).wait()
        self.pair(w).wait()
        rows = self.own[w].shape[0] // self.nb

        def add(i, w=w, rows=rows):
            cut = pl.ds(pl.multiple_of(i * rows, 16), rows)
            self.own[w][cut, :] = (self.own[w][cut, :].astype(FL) + self.near[w][cut, :].astype(FL)).astype(BF)

        each(0, self.nb, add)
        if self.nb == 4:
            for way in (1, 2):
                self.corner(w, way).start()
        else:
            for step in self.steps():
                self.mix(w, step).start()

    def pieces(self, w):
        rows = self.total[w].shape[0]
        count = max(n for n in range(1, self.chips + 1) if rows % (16 * n) == 0)
        return count, rows // count

    def peer(self, step):
        other = lax.rem(self.chip + step, self.chips)
        return other, {"vocab": other * 2 + self.core}

    def cut(self, w, step):
        other, device = self.peer(step)
        size = self.pieces(w)[1]
        source = self.total[w].at[pl.ds(pl.multiple_of(other * size, 16), size), :]
        return send(source, self.bits[w].at[step], self.cut_out.at[w, step], self.cut_in.at[w, step], device)

    def back(self, w, step):
        size = self.pieces(w)[1]
        place = self.result[w].at[pl.ds(pl.multiple_of(self.chip * size, 16), size), :]
        return send(place, place, self.all_out.at[w, step], self.all_in.at[w, step], self.peer(step)[1])

    def back_recv(self, w, step):
        source = lax.rem(self.chip - step + self.chips, self.chips)
        size = self.pieces(w)[1]
        place = self.result[w].at[pl.ds(pl.multiple_of(source * size, 16), size), :]
        return send(place, place, self.all_out.at[w, step], self.all_in.at[w, step], self.peer(step)[1])

    def gather(self, w):
        rows = self.total[w].shape[0]
        for step in self.steps():
            self.mix(w, step).wait()
        here = pl.ds(pl.multiple_of(self.b * rows, 16), rows)
        value = self.own[w][here, :].astype(FL)
        for step in self.steps():
            value = value + self.shard[w][step].astype(FL)
        self.total[w][...] = value.astype(BF)

    def reduce(self, w):
        if w in self.todo:
            self.gather(w)
        count = self.pieces(w)[0]

        def go(step):
            @pl.when(self.peer(step)[0] < count)
            def _():
                self.cut(w, step).start()

        each(1, self.chips, go)

    def collect(self, w):
        count, size = self.pieces(w)
        mine = pl.ds(pl.multiple_of(self.chip * size, 16), size)

        @pl.when(self.chip < count)
        def _(w=w, mine=mine):
            def add(step, value):
                self.cut(w, step).wait_recv()
                return value + self.bits[w][step].astype(FL)

            value = lax.fori_loop(1, self.chips, add, self.total[w][mine, :].astype(FL))
            self.result[w][mine, :] = value.astype(BF)
            each(1, self.chips, lambda step: self.back(w, step).start())

        def sent(step, w=w, count=count):
            @pl.when(self.peer(step)[0] < count)
            def _():
                self.cut(w, step).wait_send()

        each(1, self.chips, sent)

    def last(self, w):
        return send(
            self.result[w], self.sums[w].at[:, self.half(w, self.core)], self.last_out.at[w], self.last_in.at[w], self.sibling
        )

    def store(self, w):
        return pltpu.make_async_copy(self.result[w], self.sums[w].at[:, self.half(w, self.core)], self.store_sem.at[w])

    def finish(self):
        for w in range(4):
            count = self.pieces(w)[0]

            def got(step, w=w, count=count):
                @pl.when(lax.rem(self.chip - step + self.chips, self.chips) < count)
                def _():
                    self.back_recv(w, step).wait_recv()

            each(1, self.chips, got)
            self.last(w).start()
            self.store(w).start()
        for w in range(4):
            count = self.pieces(w)[0]

            @pl.when(self.chip < count)
            def _(w=w):
                each(1, self.chips, lambda step: self.back(w, step).wait_send())

            self.store(w).wait()
            self.last(w).wait_send()
            other = self.sums[w].at[:, self.half(w, 1 - self.core)]
            send(other, other, self.last_out.at[w], self.last_in.at[w], self.sibling).wait_recv()


def gradient_scratch(nb, nv, shapes, todo, whole=True):
    chips = nv // 2
    halves = [(rows, cols // 2) for rows, cols in shapes]
    shards = [(rows // nb, cols) for rows, cols in halves]
    sizes = [rows // max(n for n in range(1, chips + 1) if rows % (16 * n) == 0) for rows, _ in shards]
    dma = pltpu.SemaphoreType.DMA
    count = len(shapes)
    refs = [pltpu.VMEM(halves[w], BF) for w in todo] * 2 + [pltpu.VMEM((nb, *shards[w]), BF) for w in todo]
    if whole:
        refs += [pltpu.VMEM(shards[w], BF) for w in todo]
        refs += [pltpu.VMEM((chips, size, item[1]), BF) for size, item in zip(sizes, shards)]
        refs += [pltpu.VMEM(item, BF) for item in shards]
    refs += [dma((count,)), dma((count,)), dma((count,)), dma((count, nb)), dma((count, nb))]
    if whole:
        refs += [dma((count, chips))] * 4 + [dma((count,))] * 3
    return refs


def squares(refs, part):
    cols = min(ref.shape[1] for ref in refs)

    def add(j, total):
        value = refs[0][:, lanes(j * part, part)].astype(FL)
        for ref in refs[1:]:
            value = value + ref[:, lanes(j * part, part)].astype(FL)
        return total + jnp.sum(value * value, axis=0, keepdims=True)

    line = lax.fori_loop(0, cols // part, add, jnp.zeros((1, part), FL))
    return jnp.sum(line, axis=1, keepdims=True)


def add_up(nb, nv, own, loss_ref, out_ref, mine, near, lines, vocab_out, vocab_in, batch_out, batch_in):
    b, v = lax.axis_index("batch"), lax.axis_index("vocab")
    line = iota((8, 128), 0)
    mine[...] = jnp.where(line == 0, own, jnp.where((line == 1) & (v == 0), loss_ref[...], 0.0))

    def vocab_copy(step):
        return send(mine, near.at[v], vocab_out.at[step], vocab_in.at[step], {"vocab": lax.rem(v + step, nv)})

    each(1, nv, lambda step: vocab_copy(step).start())
    near[v] = mine[...]
    each(1, nv, lambda step: vocab_copy(step).wait())
    mine[...] = lax.fori_loop(0, nv, lambda u, total: total + near[u], jnp.zeros((8, 128), FL))

    def batch_copy(step):
        return send(mine, lines.at[b], batch_out.at[step], batch_in.at[step], {"batch": lax.rem(b + step, nb)})

    each(1, nb, lambda step: batch_copy(step).start())
    lines[b] = mine[...]
    each(1, nb, lambda step: batch_copy(step).wait())
    out_ref[...] = lax.fori_loop(0, nb, lambda u, total: total + lines[u], jnp.zeros((8, 128), FL))


def add_up_scratch(nb, nv):
    dma = pltpu.SemaphoreType.DMA
    tiles = [pltpu.VMEM((8, 128), FL), pltpu.VMEM((nv, 8, 128), FL), pltpu.VMEM((nb, 8, 128), FL)]
    return tiles + [dma((nv,)), dma((nv,)), dma((nb,)), dma((nb,))]


def norm_kernel(nb, nv, extra_ref, dw_ref, a_ref, p_ref, u_ref, c_ref, loss_ref, out_ref, *scratch):
    meet((("batch", nb), ("vocab", nv)))
    own = squares((extra_ref, dw_ref), chunk_of(extra_ref.shape[1], 640))
    layer = squares((a_ref,), 512) + squares((p_ref,), 384) + squares((u_ref,), 512) + squares((c_ref,), 384)
    own = own + jnp.where(lax.axis_index("vocab") == 0, layer, jnp.zeros_like(layer))
    add_up(nb, nv, own, loss_ref, out_ref, *scratch)


def unembed_kernel(nb, nv, cap, part, first, split, *refs):
    x_ref, ids_ref, place_ref = refs[:3]
    grads, refs = (refs[3:7], refs[7:]) if first else ((), refs[3:])
    if first:
        totals, grads = {2: grads[2]}, (grads[0], grads[1], None, grads[3])
    (quarter_ref, loss_ref), refs = (refs[:2], refs[2:]) if split else ((None, None), refs)
    out_ref = refs[0]
    sums, refs = (refs[1:5], refs[5:]) if first else ((), refs[1:])
    (dw_ref, total_ref, rows_ref), refs = (refs[:3], refs[3:]) if split else ([None] * 3, refs)
    (quarter_out, quarter_in, quarter_own), refs = (refs[:3], refs[3:]) if split else ([None] * 3, refs)
    (strip, strip_sem, *sum_refs), refs = (refs[:9], refs[9:]) if split else ([None] * 2, refs)
    turned, parts, sent, got, mix_out, mix_in, row_out, row_in = refs[:8]
    layer = GradientSum(nb, nv, grads, refs[8:], totals, sums) if first else None
    b, v = lax.axis_index("batch"), lax.axis_index("vocab")
    width, rows = out_ref.shape
    meet((("batch", nb), ("vocab", nv)))
    turned[...] = x_ref[...].T.reshape(nb, width, SEQ_LEN)

    def mix_copy(step):
        other = lax.rem(b + step, nb)
        return send(turned.at[other], parts.at[b], mix_out.at[step], mix_in.at[step], {"batch": other})

    for step in range(1, nb):
        mix_copy(step).start()
    if first:
        layer.start()
        layer.reduce(2)
    parts[b] = turned[b]
    for step in range(1, nb):
        mix_copy(step).wait()

    def quarter_place():
        size = quarter_ref.shape[1]
        return dw_ref.at[:, lanes(b * size, size)]

    def quarter_copy(step):
        other = lax.rem(b + step, nb)
        source = quarter_ref.at[pl.ds(pl.multiple_of(other * width, 16), width), :]
        return send(source, quarter_place(), quarter_out.at[step], quarter_in.at[step], {"batch": other})

    def quarter_keep():
        source = quarter_ref.at[pl.ds(pl.multiple_of(b * width, 16), width), :]
        return pltpu.make_async_copy(source, quarter_place(), quarter_own.at[0])

    def row_copy(step):
        return send(
            sent.at[step], got.at[v], row_out.at[step], row_in.at[step], {"vocab": lax.rem(v + step, nv)}
        )

    def build(turn):
        step = lax.rem(turn, nv)
        owner = lax.rem(v + step, nv)
        blocks = []
        for p in range(nb):
            key = jnp.where(place_ref[p, 0:1, :] == owner, place_ref[p, 1:2, :], -1)
            hot = (iota((cap, SEQ_LEN), 0) == key).astype(FL).astype(BF)
            blocks.append(nt(parts[p], hot).astype(BF))
        block = jnp.concatenate(blocks, axis=1)

        @pl.when(step > 0)
        def _():
            sent[step] = block
            row_copy(step).start()

        @pl.when(step == 0)
        def _():
            got[v] = block

    if first:
        layer.scatter(3)
    each(1, nv // 2 + 1, build)
    if first:
        layer.relay(3)
        layer.collect(2)
    each(nv // 2 + 1, nv + 1, build)
    if first:
        layer.scatter(0)
    if split:
        quarter_keep().start()
    out_ref[...] = jnp.zeros_like(out_ref)

    def take(step):
        source = lax.rem(v - step + nv, nv)

        @pl.when(step > 0)
        def _():
            row_copy(step).wait()

        block, index = got[source], ids_ref[source]

        def piece(j):
            hot = (index - j * part == iota((nb * cap, part), 1)).astype(FL).astype(BF)
            out_ref[:, lanes(j * part, part)] += nn(block, hot)

        each(0, rows // part, piece)

    if first:
        quarter = nv // 4
        each(0, quarter, take)
        layer.relay(0)
        layer.reduce(3)
        layer.scatter(1)
        if split:
            for step in range(1, nb):
                quarter_copy(step).start()
        each(quarter, 2 * quarter, take)
        layer.relay(1)
        layer.reduce(0)
        each(2 * quarter, 3 * quarter, take)
        layer.collect(3)
        layer.reduce(1)
        each(3 * quarter, nv, take)
        layer.collect(0)
        layer.collect(1)
        layer.finish()
        if split:
            quarter_keep().wait()
            for step in range(1, nb):
                quarter_copy(step).wait()
            rows_copy = pltpu.make_async_copy(sums[0].at[:, lanes(3 * D, 128)], strip, strip_sem.at[0])
            rows_copy.start()
            layer_squares = jnp.zeros((1, 1), FL)
            for w in range(4):
                cols = layer.result[w].shape[1]
                layer_squares += squares((layer.result[w],), max(n for n in (640, 512, 384, 128) if cols % n == 0))
            own = squares((out_ref, dw_ref), part)
            own = own + jnp.where(v < 2, layer_squares, 0.0)
            add_up(nb, nv, own, loss_ref, total_ref, *sum_refs)
            rows_copy.wait()
            rows_ref[...] = strip[...].astype(FL).T[:8, :]
    else:
        each(0, nv, take)


def unembed(nb, nv, cap, width, rows, grad, ids, place, grads=(), quarter=None, loss=None):
    part = chunk_of(rows, 640)
    count = nb * cap
    dma = pltpu.SemaphoreType.DMA
    scratch = [
        pltpu.VMEM((nb, width, SEQ_LEN), BF),
        pltpu.VMEM((nb, width, SEQ_LEN), BF),
        pltpu.VMEM((nv, width, count), BF),
        pltpu.VMEM((nv, width, count), BF),
        dma((nb,)), dma((nb,)), dma((nv,)), dma((nv,)),
    ]
    first, split = len(grads) > 0, quarter is not None
    if split:
        strip = [pltpu.VMEM((width, 128), BF), dma((1,))]
        scratch = [dma((nb,)), dma((nb,)), dma((1,))] + strip + add_up_scratch(nb, nv) + scratch
    if first:
        shapes = [item.shape if w != 2 else (nb * item.shape[0], 2 * item.shape[1]) for w, item in enumerate(grads)]
        scratch += gradient_scratch(nb, nv, shapes, (0, 1, 3))
    outs = [SD((width, rows), FL)] + [SD((item[0] // nb, item[1]), BF) for item in (shapes if first else ())]
    extra = [quarter, loss] if split else []
    if split:
        outs += [SD((width, nb * quarter.shape[1]), BF), SD((8, 128), FL), SD((8, width), FL)]
    return run(
        functools.partial(unembed_kernel, nb, nv, cap, part, first, split),
        outs,
        scratch,
        [grad, ids, place, *grads, *extra],
        "unembed" if first else "unembed_more",
        2 if first else 4,
        in_specs=[VM] * 3 + ([HB, HB, VM, HB] if first else []) + [VM] * len(extra),
        out_specs=[VM] + [HB] * len(grads) + ([VM] * 3 if split else []),
    )


def later_slots(nv, cap, rows, every, turn):
    nb = every.shape[0]
    v = lax.axis_index("vocab")
    local = every - v * rows
    mine = (local >= 0) & (local < rows)
    rank = jnp.cumsum(mine.astype(I32), axis=-1) - 1 - turn * cap
    hot = (rank[:, :, None, :] == jnp.arange(cap)[None, None, :, None]) & mine[:, :, None, :]
    ids = jnp.sum(jnp.where(hot, local[:, :, None, :], 0), axis=-1)
    return jnp.transpose(ids, (1, 0, 2)).reshape(nv, nb * cap, 1)


def standard(value):
    centre = value - jnp.mean(value, axis=-1, keepdims=True)
    spread = jnp.mean(centre * centre, axis=-1, keepdims=True)
    scale = lax.rsqrt(spread + NORM_EPS)
    return centre * scale, scale


def norm_back(unit, scale, gain, upstream):
    inner = upstream * gain
    first = jnp.mean(inner, axis=-1, keepdims=True)
    second = jnp.mean(inner * unit, axis=-1, keepdims=True)
    grad = scale * (inner - first - unit * second)
    return grad, jnp.sum(upstream * unit, axis=0, keepdims=True), jnp.sum(upstream, axis=0, keepdims=True)


def head_lanes(value, head):
    lane = iota(value.shape, 1)
    keep = (lane < HD) if head == 0 else (lane >= HD)
    return jnp.where(keep, value, jnp.zeros_like(value))


def visible_keys(seg_ref, pos_ref):
    position = pos_ref[...]
    block = position // BLK
    marks = [seg_ref[:, i * BLK : i * BLK + 1] for i in range(SEQ_LEN // BLK)]
    segment = jnp.zeros_like(position)
    for i, mark in enumerate(marks):
        segment = jnp.where(block == i, mark, segment)
    row = iota((BLK, PICKS), 0)
    parts = [jnp.broadcast_to(segment == slot + 1, (NB, PICKS)) for slot in range(SLOTS)]
    parts += [(segment == mark) & (row + i * BLK <= position) for i, mark in enumerate(marks)]
    return parts


def masked(visible, scores):
    return jnp.concatenate(
        [jnp.where(keep, scores[i * BLK : (i + 1) * BLK, :], NEG_BIG) for i, keep in enumerate(visible)], axis=0
    )


def memory_weights(segments, slot):
    length = segments.shape[1]
    inside = (segments == slot).astype(FL)
    start = jnp.sum((segments < slot).astype(FL), axis=1, keepdims=True)
    count = jnp.sum(inside, axis=1, keepdims=True)
    times = (iota((1, length), 1).astype(FL) - start + 0.5) / jnp.maximum(count, 1.0)
    centres = (iota((NB, 1), 0).astype(FL) + 0.5) / NB
    offset = (times - centres) * NB
    basis = jnp.exp(-0.5 * offset * offset) * inside
    total = jnp.sum(basis, axis=1, keepdims=True) + (count == 0.0).astype(FL)
    return basis / total


def attend_kernel(
    nb, nv, x_ref, a_ref, seg_ref, pos_ref, p_ref, c_ref, u_ref,
    hall_ref, kv_ref, q_ref, hq_ref, o_ref, lse_ref, norm_ref, mixt_ref, p_all, c_all,
    x1_ref, h2_ref, z_ref, act_ref, x2_ref, f_ref, *sems,
):
    meet((("batch", nb), ("vocab", nv)))
    gather = WeightGather(nb, (p_ref, c_ref), (p_all, c_all), *sems)
    gather.start()
    norm_ref[...] = a_ref[:, 3 * D : 3 * D + 128].astype(FL).T[:8, :]
    gain, bias = norm_ref[0:1, :], norm_ref[3:4, :]

    def normalize(i):
        unit, _ = standard(x_ref[pl.ds(i * BLK, BLK), :].astype(FL))
        hall_ref[pl.ds(SLOTS * NB + i * BLK, BLK), :] = (unit * gain + bias).astype(BF)

    each(0, SEQ_LEN // BLK, normalize)
    normed = hall_ref[SLOTS * NB :, :]
    for slot in range(SLOTS):
        mixing = memory_weights(seg_ref[...], slot).astype(BF)
        hall_ref[slot * NB : (slot + 1) * NB, :] = nn(mixing, normed).astype(BF)
        mixt_ref[:, slot * NB : (slot + 1) * NB] = mixing.T

    def project(i):
        kv_ref[pl.ds(i * BLK, BLK), :] = nn(hall_ref[pl.ds(i * BLK, BLK), :], a_ref[:, D : 3 * D]).astype(BF)

    each(0, KEYS // BLK, project)
    pick = (pos_ref[...] == iota((SEQ_LEN, PICKS), 0)).astype(FL).astype(BF).T
    hq_ref[...] = nn(pick, normed).astype(BF)
    x1_ref[...] = nn(pick, x_ref[...])
    q_ref[...] = nn(hq_ref[...], a_ref[:, :D]).astype(BF)
    visible = visible_keys(seg_ref, pos_ref)

    def attend(p):
        keys = kv_ref[:, lanes(p * PAIR, PAIR)]
        values = kv_ref[:, lanes(D + p * PAIR, PAIR)].T
        queries = q_ref[:, lanes(p * PAIR, PAIR)] * HD ** (-0.5)
        outs = []
        for head in range(2):
            scores = masked(visible, nt(keys, head_lanes(queries, head)))
            peak = jnp.max(scores, axis=0, keepdims=True)
            expo = jnp.exp(scores - peak)
            total = jnp.sum(expo, axis=0, keepdims=True)
            probs = (expo * (1.0 / total)).astype(BF)
            outs.append(nn(values[head * HD : (head + 1) * HD, :], probs))
            lse_ref[p, head : head + 1, :] = peak + jnp.log(total)
        o_ref[:, lanes(p * PAIR, PAIR)] = jnp.concatenate(outs, axis=0).T.astype(BF)

    gather.pass_on()
    each(0, NPAIR, attend)
    gather.last_hop()
    gather.finish(0)
    x1 = x1_ref[...] + nn(o_ref[...], p_all[...])
    x1_ref[...] = x1
    unit, _ = standard(x1)
    h2 = (unit * norm_ref[1:2, :] + norm_ref[4:5, :]).astype(BF)
    h2_ref[...] = h2
    x2_ref[...] = x1

    def expand(j):
        cut = lanes(j * D, D)
        z = nn(h2, u_ref[:, cut])
        z_ref[:, cut] = z
        act_ref[:, cut] = jax.nn.gelu(z, approximate=True).astype(BF)

    each(0, FF // D, expand)
    gather.finish(1)

    def contract(j):
        x2_ref[...] += nn(act_ref[:, lanes(j * D, D)], c_all[pl.ds(j * D, D), :])

    each(0, FF // D, contract)
    unit, _ = standard(x2_ref[...])
    f_ref[...] = (unit * norm_ref[2:3, :] + norm_ref[5:6, :]).astype(BF)


def feed_back_kernel(
    df_ref, x2_ref, x1_ref, h2_ref, z_ref, act_ref, o_ref, p_ref, u_ref, c_ref, norm_ref,
    dc_ref, du_ref, dp_ref, dx1_ref, do_ref, dnorm_ref, dh2,
):
    unit, scale = standard(x2_ref[...])
    dx2, gain_last, bias_last = norm_back(unit, scale, norm_ref[2:3, :], df_ref[...])
    dy = dx2.astype(BF)
    dh2[...] = jnp.zeros_like(dh2)
    h2t = h2_ref[...].T

    def piece(j):
        cut = lanes(j * D, D)
        dc_ref[pl.ds(j * D, D), :] = nn(act_ref[:, cut].T, dy).astype(BF)
        dact = nt(dy, c_ref[pl.ds(j * D, D), :])
        z = z_ref[:, cut]
        k = math.sqrt(2.0 / math.pi)
        t = jnp.tanh(k * (z + 0.044715 * z * z * z))
        slope = 0.5 * (1.0 + t) + 0.5 * z * (1.0 - t * t) * (k * (1.0 + 3 * 0.044715 * z * z))
        dz = (dact * slope).astype(BF)
        du_ref[:, cut] = nn(h2t, dz).astype(BF)
        dh2[...] += nt(dz, u_ref[:, cut])

    each(0, FF // D, piece)
    unit, scale = standard(x1_ref[...])
    dx1, gain_two, bias_two = norm_back(unit, scale, norm_ref[1:2, :], dh2[...])
    dx1 = dx1 + dx2
    dx1_ref[...] = dx1
    da = dx1.astype(BF)
    dp_ref[...] = nn(o_ref[...].T, da).astype(BF)
    do_ref[...] = nt(da, p_ref[...]).astype(BF)
    zero = jnp.zeros_like(gain_last)
    dnorm_ref[...] = jnp.concatenate([zero, gain_two, gain_last, zero, bias_two, bias_last, zero, zero], axis=0)


def attend_back_kernel(
    nb, nv, do_ref, q_ref, kv_ref, lse_ref, hall_ref, hq_ref, a_ref, x_ref, dx1_ref, mixt_ref, seg_ref, row_ref,
    norm_ref, dnorm_ref, du_ref, da_ref, dx_ref, du_sum, dkv, dq, hallt, dh, dxin, dmem, sel, *refs,
):
    meet((("batch", nb), ("vocab", nv)))
    layer = GradientSum(nb, nv, (du_ref,), refs, {0: du_sum})
    layer.start()
    visible = visible_keys(seg_ref, row_ref)

    def attend(p):
        cut = lanes(p * PAIR, PAIR)
        keys = kv_ref[:, cut]
        values = kv_ref[:, lanes(D + p * PAIR, PAIR)]
        turned = keys.T
        queries = q_ref[:, cut] * HD ** (-0.5)
        grads = do_ref[:, cut]
        outs = []
        dk = dv = None
        for head in range(2):
            own, grad = head_lanes(queries, head), head_lanes(grads, head)
            scores = masked(visible, nt(keys, own))
            probs = jnp.exp(scores - lse_ref[p, head : head + 1, :])
            dprobs = nt(values, grad)
            inner = jnp.sum(probs * dprobs, axis=0, keepdims=True)
            dscores = (probs * (dprobs - inner)).astype(BF)
            outs.append(nn(turned[head * HD : (head + 1) * HD, :], dscores))
            one, two = nn(dscores, own), nn(probs.astype(BF), grad)
            dk = one if head == 0 else dk + one
            dv = two if head == 0 else dv + two
        dq[:, cut] = (jnp.concatenate(outs, axis=0).T * HD ** (-0.5)).astype(BF)
        dkv[:, cut] = dk.astype(BF)
        dkv[:, lanes(D + p * PAIR, PAIR)] = dv.astype(BF)

    each(0, NPAIR // 2, attend)
    layer.scatter(0)
    each(NPAIR // 2, NPAIR, attend)
    layer.relay(0)
    da_ref[:, :D] = nn(hq_ref[...].T, dq[...]).astype(BF)

    def turn(i):
        hallt[:, lanes(i * BLK, BLK)] = hall_ref[pl.ds(i * BLK, BLK), :].T

    each(0, KEYS // BLK, turn)

    def weights(j):
        cut = lanes(j * BLK, BLK)
        da_ref[:, lanes(D + j * BLK, BLK)] = nn(hallt[...], dkv[:, cut]).astype(BF)

    each(0, 2 * D // BLK, weights)

    def memory(i):
        cut = pl.ds(i * BLK, BLK)
        dmem[cut, :] = nt(dkv[cut, :], a_ref[:, D : 3 * D]).astype(BF)

    each(0, SLOTS, memory)

    def local(i):
        cut = pl.ds(i * BLK, BLK)
        dh[cut, :] = nt(dkv[pl.ds(SLOTS * NB + i * BLK, BLK), :], a_ref[:, D : 3 * D]) + nn(mixt_ref[cut, :], dmem[...])

    each(0, SEQ_LEN // BLK, local)
    put = (row_ref[...] == iota((SEQ_LEN, PICKS), 0)).astype(FL).astype(BF)

    def scatter(target, value):
        for _ in range(3):
            part = value.astype(BF)
            value = value - part.astype(FL)

            def add(i, part=part):
                cut = pl.ds(i * BLK, BLK)
                target[cut, :] += nn(sel[cut, :], part)

            each(0, SEQ_LEN // BLK, add)

    sel[...] = put
    scatter(dh, nt(dq[...], a_ref[:, :D]))
    gain = norm_ref[0:1, :]
    da_rows = [jnp.zeros((1, D), FL), jnp.zeros((1, D), FL)]

    def finish(i, carry):
        cut = pl.ds(i * BLK, BLK)
        unit, scale = standard(x_ref[cut, :].astype(FL))
        grad, dgain, dbias = norm_back(unit, scale, gain, dh[cut, :])
        dxin[cut, :] = grad
        return carry[0] + dgain, carry[1] + dbias

    dgain, dbias = lax.fori_loop(0, SEQ_LEN // BLK, finish, tuple(da_rows))

    scatter(dxin, dx1_ref[...])
    dx_ref[...] = dxin[...].astype(BF)
    line = iota((8, D), 0)
    norms = dnorm_ref[...] + jnp.where(line == 0, dgain, jnp.where(line == 3, dbias, 0.0))
    tall = jnp.concatenate([norms, jnp.zeros((EXTRA - 8, D), FL)], axis=0)
    da_ref[:, 3 * D :] = tall.T.astype(BF)
    layer.gather(0)


def head_kernel(
    nb, nv, part, f_ref, w_ref, live_ref, target_ref, df_ref, dw_ref, loss_ref,
    fall, expo, block, mine, stats, ft, grad_sum, coef, df, half, far_got, out,
    near_out, near_in, far_out, far_in, stat_out, stat_in, pair_out, pair_in, sum_out, sum_in, dw_sem,
):
    v = lax.axis_index("vocab")
    rows = w_ref.shape[1]
    total_rows = nv * PICKS
    core, chip, chips = lax.rem(v, 2), v // 2, nv // 2
    sibling = {"vocab": v + 1 - 2 * core}
    base = v * rows
    pieces = rows // part
    depth = min(2, pieces)
    meet((("vocab", nv),))

    def peer(step):
        return {"vocab": lax.rem(chip + step, chips) * 2 + core}

    def far_copy(step):
        return send(f_ref, fall.at[v], far_out.at[step], far_in.at[step], peer(step))

    def near_copy(step):
        slot = lax.rem(chip - step + chips, chips) * 2 + core
        return send(fall.at[slot], fall.at[slot], near_out.at[step], near_in.at[step], sibling)

    fall[v] = f_ref[...]
    near_copy(0).start()
    each(1, chips, lambda step: far_copy(step).start())

    def logits(step):
        @pl.when(step > 0)
        def _():
            far_copy(step).wait_recv()
            near_copy(step).start()

        near_copy(step).wait_recv()
        source = lax.rem(chip - step + chips, chips)
        start = pl.multiple_of(source * 2 * PICKS, 2 * PICKS)
        features = fall[pl.ds(source * 2, 2)].reshape(2 * PICKS, D)
        target = target_ref[pl.ds(start, 2 * PICKS), :] - base

        def score(j, peak):
            cut = lanes(j * part, part)
            value = nn(features, w_ref[:, cut])
            block[:, cut] = value
            return jnp.maximum(
                peak, jnp.max(jnp.where(live_ref[0:1, cut] > 0, value, NEG_BIG), axis=1, keepdims=True)
            )

        peak = lax.fori_loop(0, pieces, score, jnp.full((2 * PICKS, 1), NEG_BIG, FL))

        def count(j, carry):
            total, picked, valid = carry
            cut = lanes(j * part, part)
            value = block[:, cut]
            live = live_ref[0:1, cut] > 0
            hot = target - j * part == iota((2 * PICKS, part), 1)
            e = jnp.where(live, jnp.exp(value - peak), 0.0)
            expo[pl.ds(start, 2 * PICKS), cut] = e.astype(BF)
            total = total + jnp.sum(e, axis=1, keepdims=True)
            picked = picked + jnp.sum(jnp.where(hot, value, 0.0), axis=1, keepdims=True)
            valid = valid + jnp.sum(jnp.where(hot & live, 1.0, 0.0), axis=1, keepdims=True)
            return total, picked, valid

        zero = jnp.zeros((2 * PICKS, 1), FL)
        total, picked, valid = lax.fori_loop(0, pieces, count, (zero, zero, zero))
        lane = iota((2 * PICKS, 128), 1)
        wide = jnp.where(lane == 0, peak, jnp.where(lane == 1, total, jnp.where(lane == 2, picked, valid)))
        mine[:, pl.ds(start, 2 * PICKS)] = wide.T[:8, :]

    each(0, chips, logits)

    def stat_copy(step):
        return send(mine, stats.at[v], stat_out.at[step], stat_in.at[step], {"vocab": lax.rem(v + step, nv)})

    each(1, nv, lambda step: stat_copy(step).start())
    stats[v] = mine[...]
    for i in range(total_rows // 256 if pieces > 1 else 0):
        ft[:, i * 256 : (i + 1) * 256] = fall[2 * i : 2 * i + 2].reshape(256, D).T
    each(1, nv, lambda step: stat_copy(step).wait())
    start = jnp.full((1, total_rows), NEG_BIG, FL)
    peak = lax.fori_loop(0, nv, lambda u, top: jnp.maximum(top, stats[u, 0:1, :]), start)

    def combine(u, carry):
        scale = jnp.exp(stats[u, 0:1, :] - peak)
        return (
            carry[0] + stats[u, 1:2, :] * scale, carry[1] + stats[u, 2:3, :], carry[2] + stats[u, 3:4, :],
        )

    zero = jnp.zeros((1, total_rows), FL)
    total, picked, valid = lax.fori_loop(0, nv, combine, (zero, zero, zero))
    lse = peak + jnp.log(jnp.maximum(total, 1e-37))
    weight = valid / (jnp.maximum(jnp.sum(valid, axis=1, keepdims=True), 1.0) * nb)
    loss = jnp.sum(weight * (lse - picked), axis=1, keepdims=True)
    loss_ref[...] = jnp.broadcast_to(loss, loss_ref.shape)
    alpha = weight * jnp.exp(mine[0:1, :] - lse)
    line = iota((128, 256), 0)
    for i in range(total_rows // 256):
        cut = slice(i * 256, (i + 1) * 256)
        coef[cut, :] = jnp.where(line == 0, alpha[:, cut], weight[:, cut]).T

    tall = min(total_rows, 1024 if pieces > 1 else 256)
    shards_tall = tall // PICKS
    df[...] = jnp.zeros_like(df)

    def out_copy(j):
        return pltpu.make_async_copy(
            out.at[lax.rem(j, depth)], dw_ref.at[:, lanes(j * part, part)], dw_sem.at[lax.rem(j, depth)]
        )

    def gradients(j):
        cut = lanes(j * part, part)
        words = w_ref[:, cut]

        @pl.when(j >= depth)
        def _():
            out_copy(j - depth).wait()

        def strip(t):
            start = t * tall if total_rows == tall else pl.multiple_of(t * tall, tall)
            here = pl.ds(start, tall)
            hot = target_ref[here, :] - base - j * part == iota((tall, part), 1)
            two = coef[here, :]
            value = two[:, 0:1] * expo[here, cut].astype(FL) - jnp.where(hot, two[:, 1:2], 0.0)
            dlogits = value.astype(BF)
            df[here, :] += nt(dlogits, words)
            if pieces > 1:
                turned = ft[:, pl.ds(start, tall)]
            else:
                turned = fall[pl.ds(t * shards_tall, shards_tall)].reshape(tall, D).T
            for r in range(0, D, D // 3):
                more = nn(turned[r : r + D // 3, :], dlogits)
                if total_rows == tall:
                    out[lax.rem(j, depth), r : r + D // 3, :] = more.astype(BF)
                else:
                    grad_sum[r : r + D // 3, :] += more

        if total_rows == tall:
            strip(0)
        else:
            grad_sum[...] = jnp.zeros_like(grad_sum)
            each(0, total_rows // tall, strip)
            for r in range(0, D, D // 3):
                out[lax.rem(j, depth), r : r + D // 3, :] = grad_sum[r : r + D // 3, :].astype(BF)
        out_copy(j).start()

    each(0, pieces, gradients)

    def shard(index):
        return pl.ds(pl.multiple_of(index * PICKS, PICKS), PICKS)

    def pair_copy(k):
        source = df.at[shard(2 * k + 1 - core), :] if pieces > 1 else fall.at[k]
        return send(source, half.at[k], pair_out.at[k], pair_in.at[k], sibling)

    near_copy(0).wait_send()

    def drain(step):
        far_copy(step).wait_send()
        near_copy(step).wait_send()

    each(1, chips, drain)

    def swap(k):
        if pieces == 1:
            fall[k] = df[shard(2 * k + 1 - core), :].astype(BF)
        pair_copy(k).start()

    each(0, chips, swap)

    def sum_copy(step):
        return send(fall.at[chips + step], far_got.at[step], sum_out.at[step], sum_in.at[step], peer(step))

    def pass_on(turn):
        step = lax.rem(turn, chips)
        k = lax.rem(chip + step, chips)
        pair_copy(k).wait()
        value = df[shard(2 * k + core), :] + half[k].astype(FL)

        @pl.when(step > 0)
        def _():
            fall[chips + step] = value.astype(BF)
            sum_copy(step).start()

        @pl.when(step == 0)
        def _():
            df_ref[...] = value

    each(1, chips + 1, pass_on)

    def collect(step):
        sum_copy(step).wait()
        df_ref[...] += far_got[step].astype(FL)

    each(1, chips, collect)
    for j in range(pieces - depth, pieces):
        out_copy(j).wait()


def head(nb, nv, features, words, live, targets):
    rows = words.shape[1]
    part = chunk_of(rows, 640)
    total_rows = nv * PICKS
    chips = nv // 2
    dma = pltpu.SemaphoreType.DMA
    scratch = [
        pltpu.VMEM((nv, PICKS, D), BF),
        pltpu.VMEM((total_rows, rows), BF),
        pltpu.VMEM((2 * PICKS, rows), FL),
        pltpu.VMEM((8, total_rows), FL),
        pltpu.VMEM((nv, 8, total_rows), FL),
        pltpu.VMEM((D, total_rows) if rows > part else (8, 128), BF),
        pltpu.VMEM((8, 128) if rows > part else (D, part), FL),
        pltpu.VMEM((total_rows, 128), FL),
        pltpu.VMEM((total_rows, D), FL),
        pltpu.VMEM((chips, PICKS, D), FL if rows > part else BF),
        pltpu.VMEM((chips, PICKS, D), BF),
        pltpu.VMEM((min(2, rows // part), D, part), BF),
        dma((chips,)), dma((chips,)), dma((chips,)), dma((chips,)), dma((nv,)), dma((nv,)),
        dma((chips,)), dma((chips,)), dma((chips,)), dma((chips,)), dma((2,)),
    ]
    return run(
        functools.partial(head_kernel, nb, nv, part),
        [SD((PICKS, D), FL), SD((D, rows), BF), SD((8, 128), FL)],
        scratch,
        [features, words, live, targets],
        "head",
        1,
        out_specs=[VM, HB, VM],
    )


def wide_head_kernel(
    nb, nv, block_rows, f_ref, w_ref, live_ref, target_ref, df_ref, dw_ref, loss_ref,
    fall, ft, expo, words_sum, mine, first_got, merged, second_got, tile, third_got, tiles, coef, group, half, handed, mix_got,
    far_sum, far_got,
    z_out, z_in, mix_out, mix_in, near_out, near_in, s_out, s_in, pair_out, pair_in, give_out, give_in, sum_out, sum_in,
):
    b, v = lax.axis_index("batch"), lax.axis_index("vocab")
    rows = w_ref.shape[1]
    core, chip, chips = lax.rem(v, 2), v // 2, nv // 2
    sibling = {"vocab": v + 1 - 2 * core}
    base = v * block_rows + b * rows
    live = live_ref[:, lanes(b * rows, rows)] > 0
    span = nv * PICKS
    meet((("batch", nb), ("vocab", nv)))

    def column(line):
        line = jnp.where(line < (v + 1) * block_rows, line - base, -1).astype(FL)
        return jnp.broadcast_to(line, (128, 2 * PICKS)).T[:, 0:1].astype(I32)

    def peer(step):
        return {"vocab": lax.rem(chip + step, chips) * 2 + core}

    def other(step):
        return {"batch": lax.rem(b + step, nb)}

    def flip(s):
        low, high = lax.rem(b, 2), b // 2
        return (high if s < 2 else 1 - high) * 2 + (low if s % 2 == 0 else 1 - low)

    def slot(s, k):
        return flip(s) * nv + lax.rem(chip - k + chips, chips) * 2 + core

    def z_copy(k):
        return send(f_ref, fall.at[b * nv + v], z_out.at[k], z_in.at[k], peer(k))

    def mix_copy(s, k, way=0):
        if s < 3:
            place, device = fall.at[slot(0, k)], flip(s)
        else:
            place, device = fall.at[slot(3 - way, k)], flip(way)
        return send(place, place, mix_out.at[k, s], mix_in.at[k, s], {"batch": device})

    near = [s for s in (1, 2) if s < nb]

    def near_copy(s, k):
        place = fall.at[slot(s, k)]
        return send(place, place, near_out.at[k, s], near_in.at[k, s], sibling)

    def arrive(s, k):
        if s == 0:

            @pl.when(k > 0)
            def _():
                z_copy(k).wait_recv()

            for t in near:
                mix_copy(t, k).start()
        else:
            mix_copy(s, k, 1).wait_recv()
        if nb == 4 and s in (1, 2):

            @pl.when(lax.rem(k, 2) == s - 1)
            def _():
                mix_copy(3, k, 3 - s).start()

        near_copy(s, k).start()

    fall[b * nv + v] = f_ref[...]
    each(1, chips, lambda k: z_copy(k).start())
    arrive(0, 0)

    def logits(s, k):
        near_copy(s, k).wait_recv()
        p, c = flip(s), lax.rem(chip - k + chips, chips)
        first = p * nv + c * 2
        start = pl.multiple_of(first * PICKS, 2 * PICKS)
        features = fall[pl.ds(first, 2)].reshape(2 * PICKS, D)
        ft[:, pl.ds(start, 2 * PICKS)] = features.T
        line = target_ref[p, :, pl.ds(pl.multiple_of(c * 2 * PICKS, 2 * PICKS), 2 * PICKS)]
        target = column(line)
        value = nn(features, w_ref[...])
        value = jnp.where(live, value, NEG_BIG)
        peak = jnp.maximum(jnp.max(value, axis=1, keepdims=True), 0.1 * NEG_BIG)
        e = jnp.exp(value - peak)
        expo[pl.ds(start, 2 * PICKS), :] = e.astype(BF)
        total = jnp.sum(e, axis=1, keepdims=True)
        picked = jnp.sum(jnp.where(target == iota((2 * PICKS, rows), 1), value, 0.0), axis=1, keepdims=True)
        lane = iota((2 * PICKS, 128), 1)
        wide = jnp.where(lane == 0, peak, jnp.where(lane == 1, total, picked)).T
        mine[c * 2, p] = wide[:8, :PICKS]
        mine[c * 2 + 1, p] = wide[:8, PICKS:]

    for s in range(nb):

        def one(k, s=s):
            @pl.when(k + 1 < chips)
            def _():
                arrive(s, k + 1)

            if s + 1 < nb:

                @pl.when(k + 1 == chips)
                def _():
                    arrive(s + 1, 0)

            logits(s, k)

        each(0, chips, one)

    def merge(read, count):
        peak = lax.fori_loop(
            0, count, lambda u, top: jnp.maximum(top, read(u)[0:1, :]), jnp.full((1, PICKS), NEG_BIG, FL)
        )

        def add(u, carry):
            one = read(u)
            return carry[0] + one[1:2, :] * jnp.exp(one[0:1, :] - peak), carry[1] + one[2:3, :]

        zero = jnp.zeros((1, PICKS), FL)
        return (peak, *lax.fori_loop(0, count, add, (zero, zero)))

    def tile_of(rows_of):
        line = iota((8, PICKS), 0)
        value = jnp.zeros((8, PICKS), FL)
        for i, row in enumerate(rows_of):
            value = jnp.where(line == i, row, value)
        return value

    def first_copy(t):
        u = lax.rem(v + t, nv)
        return send(mine.at[u], first_got.at[v], s_out.at[0, t], s_in.at[0, t], {"vocab": u})

    each(1, nv, lambda t: first_copy(t).start())
    first_got[v] = mine[v]
    each(1, nv, lambda t: first_copy(t).wait())
    for p in range(nb):
        merged[p] = tile_of(merge(lambda u, p=p: first_got[u, p], nv))

    def second_copy(t):
        return send(merged.at[lax.rem(b + t, nb)], second_got.at[b], s_out.at[1, t], s_in.at[1, t], other(t))

    each(1, nb, lambda t: second_copy(t).start())
    second_got[b] = merged[b]
    each(1, nb, lambda t: second_copy(t).wait())
    peak, total, picked = merge(lambda u: second_got[u], nb)
    valid = (picked > 0.5 * NEG_BIG).astype(FL)
    tile[...] = tile_of((peak + jnp.log(jnp.maximum(total, 1e-37)), picked, valid))

    def third_copy(t):
        return send(tile, third_got.at[b], s_out.at[2, t], s_in.at[2, t], other(t))

    each(1, nb, lambda t: third_copy(t).start())
    third_got[b] = tile[...]
    each(1, nb, lambda t: third_copy(t).wait())

    def last_copy(t):
        return send(third_got, tiles.at[v], s_out.at[3, t], s_in.at[3, t], {"vocab": lax.rem(v + t, nv)})

    each(1, nv, lambda t: last_copy(t).start())
    tiles[v] = third_got[...]
    each(1, nv, lambda t: last_copy(t).wait())

    def coefficients(p):
        count = lax.fori_loop(0, nv, lambda u, total: total + tiles[u, p, 2:3, :], jnp.zeros((1, PICKS), FL))
        share = 1.0 / (jnp.maximum(jnp.sum(count, axis=1, keepdims=True), 1.0) * nb)

        def spread(c, loss):
            rows_of = []
            for side in range(2):
                u = c * 2 + side
                lse, picked, valid = (tiles[u, p, i : i + 1, :] for i in range(3))
                weight = valid * share
                loss = loss + weight * (lse - picked)
                rows_of.append((weight * jnp.exp(mine[u, p, 0:1, :] - lse), weight))
            line = iota((128, 2 * PICKS), 0)
            alpha = jnp.concatenate([rows_of[0][0], rows_of[1][0]], axis=1)
            weight = jnp.concatenate([rows_of[0][1], rows_of[1][1]], axis=1)
            start = pl.multiple_of(p * span + c * 2 * PICKS, 2 * PICKS)
            coef[pl.ds(start, 2 * PICKS), :] = jnp.where(line == 0, alpha, weight).T
            return loss

        loss = lax.fori_loop(0, chips, spread, jnp.zeros((1, PICKS), FL))

        @pl.when(p == b)
        def _():
            loss_ref[...] = jnp.broadcast_to(jnp.sum(loss, axis=1, keepdims=True), loss_ref.shape)

    each(0, nb, coefficients)

    def shard(k, side):
        return pl.ds(pl.multiple_of((2 * k + side) * PICKS, PICKS), PICKS)

    def pair_copy(s, k):
        return send(handed.at[s, k], half.at[s, k], pair_out.at[s, k], pair_in.at[s, k], sibling)

    def give_copy(s, k):
        if s < 3:
            return send(handed.at[s, k], mix_got.at[s, k], give_out.at[s, k], give_in.at[s, k], {"batch": flip(s)})
        device = jnp.where(lax.rem(k, 2) == 0, flip(1), flip(2))
        return send(handed.at[3, k], mix_got.at[3, k], give_out.at[3, k], give_in.at[3, k], {"batch": device})

    def exchange(s):
        def add(k):
            pair_copy(s, k).wait()
            value = group[s % 2, shard(k, core), :] + half[s, k].astype(FL)
            handed[s, k] = value.astype(BF)
            if nb == 4 and s in (1, 2):

                @pl.when(lax.rem(k, 2) == 2 - s)
                def _():
                    give_copy(3, k).wait_recv()
                    handed[s, k] = (value + mix_got[3, k].astype(FL)).astype(BF)

            if s > 0:
                give_copy(s, k).start()

        each(0, chips, add)

    order = [3, 2, 1, 0] if nb == 4 else [1, 0]
    for turn, s in enumerate(order):
        p = flip(s)

        def strip(c, p=p):
            start = pl.multiple_of(p * span + c * 2 * PICKS, 2 * PICKS)
            here = pl.ds(start, 2 * PICKS)
            line = target_ref[p, :, pl.ds(pl.multiple_of(c * 2 * PICKS, 2 * PICKS), 2 * PICKS)]
            target = column(line)
            two = coef[here, :]
            hot = target == iota((2 * PICKS, rows), 1)
            value = two[:, 0:1] * expo[here, :].astype(FL) - jnp.where(hot, two[:, 1:2], 0.0)
            expo[here, :] = value.astype(BF)

        each(0, chips, strip)
        if turn > 0:
            exchange(order[turn - 1])

        def features_grad(i, p=p, s=s):
            here = pl.ds(pl.multiple_of(i * 512, 512), 512)
            group[s % 2, here, :] = nt(expo[pl.ds(pl.multiple_of(p * span + i * 512, 512), 512), :], w_ref[...])

        each(0, span // 512, features_grad)

        def swap(k, s=s):
            handed[s, k] = group[s % 2, shard(k, 1 - core), :].astype(BF)
            pair_copy(s, k).start()

        each(0, chips, swap)

    words_sum[...] = jnp.zeros_like(words_sum)

    def words_grad(i):
        cut = lanes(i * 512, 512)
        words_sum[...] += nn(ft[:, cut], expo[cut, :])

    strips = nb * span // 512
    each(0, 1, words_grad)
    exchange(0)
    each(1, strips // 2, words_grad)

    def total_of(k):
        value = handed[0, k].astype(FL)
        for s in near:
            give_copy(s, k).wait_recv()
            value = value + mix_got[s, k].astype(FL)
        return value

    def sum_copy(t):
        return send(far_sum.at[t], far_got.at[t], sum_out.at[t], sum_in.at[t], peer(t))

    def pass_on(t):
        far_sum[t] = total_of(lax.rem(chip + t, chips)).astype(BF)
        sum_copy(t).start()

    each(1, chips, pass_on)
    each(strips // 2, strips, words_grad)
    dw_ref[...] = words_sum[...].astype(BF)
    df_ref[...] = total_of(chip)

    def collect(t):
        sum_copy(t).wait()
        df_ref[...] += far_got[t].astype(FL)

    each(1, chips, collect)
    each(1, chips, lambda k: z_copy(k).wait_send())
    for s in range(nb):
        each(0, chips, lambda k, s=s: near_copy(s, k).wait_send())
        if s > 0:
            each(0, chips, lambda k, s=s: mix_copy(s, k, 1).wait_send())
            each(0, chips, lambda k, s=s: give_copy(s, k).wait_send())


def wide_head(nb, nv, block_rows, features, words, live, targets):
    rows = words.shape[1]
    tokens = nb * nv * PICKS
    chips = nv // 2
    dma = pltpu.SemaphoreType.DMA
    most = max(nb, nv)
    scratch = [
        pltpu.VMEM((nb * nv, PICKS, D), BF),
        pltpu.VMEM((D, tokens), BF),
        pltpu.VMEM((tokens, rows), BF),
        pltpu.VMEM((D, rows), FL),
        pltpu.VMEM((nv, nb, 8, PICKS), FL),
        pltpu.VMEM((nv, nb, 8, PICKS), FL),
        pltpu.VMEM((nb, 8, PICKS), FL),
        pltpu.VMEM((nb, 8, PICKS), FL),
        pltpu.VMEM((8, PICKS), FL),
        pltpu.VMEM((nb, 8, PICKS), FL),
        pltpu.VMEM((nv, nb, 8, PICKS), FL),
        pltpu.VMEM((tokens, 128), FL),
        pltpu.VMEM((2, nv * PICKS, D), FL),
        pltpu.VMEM((nb, chips, PICKS, D), BF),
        pltpu.VMEM((nb, chips, PICKS, D), BF),
        pltpu.VMEM((nb, chips, PICKS, D), BF),
        pltpu.VMEM((chips, PICKS, D), BF),
        pltpu.VMEM((chips, PICKS, D), BF),
        dma((chips,)), dma((chips,)), dma((chips, nb)), dma((chips, nb)), dma((chips, nb)), dma((chips, nb)),
        dma((4, most)), dma((4, most)), dma((nb, chips)), dma((nb, chips)), dma((nb, chips)), dma((nb, chips)),
        dma((chips,)), dma((chips,)),
    ]
    return run(
        functools.partial(wide_head_kernel, nb, nv, block_rows),
        [SD((PICKS, D), FL), SD((D, rows), BF), SD((8, 128), FL)],
        scratch,
        [features, words, live, targets],
        "wide_head",
        1,
    )


def norm(nb, nv, extra, dw, sums, loss):
    return run(
        functools.partial(norm_kernel, nb, nv), [SD((8, 128), FL)], add_up_scratch(nb, nv),
        [extra, dw, *sums, loss], "norm", 5,
    )[0]


def adamw(weight, moment, square, gradient, clip, count, decay, rate):
    gradient = gradient * clip
    moment = BETA_ONE * moment + (1 - BETA_ONE) * gradient
    square = BETA_TWO * square + (1 - BETA_TWO) * gradient * gradient
    fixed_moment = moment / (1 - BETA_ONE**count)
    fixed_square = square / (1 - BETA_TWO**count)
    weight = weight - rate * (fixed_moment / (jnp.sqrt(fixed_square) + ADAM_EPS) + decay * weight)
    return (weight, moment, square)


def slot_size(nv):
    mean = SEQ_LEN // nv
    return -(-(mean + int(5.5 * math.sqrt(mean))) // 32) * 32


def shards(
    nb, nv,
    tokens, targets, segments, counted, vocab_mask, step_count,
    table, table_moment, table_square,
    attend, attend_moment, attend_square,
    project, project_moment, project_square,
    expand, expand_moment, expand_square,
    contract, contract_moment, contract_square,
    gain, gain_moment, gain_square,
    shift, shift_moment, shift_square,
):
    rows, width = table.shape
    cap = slot_size(nv)
    table_t = table.T
    norms = jnp.concatenate([gain, shift], axis=0)
    packed = jnp.concatenate([attend[0], norms.T, jnp.zeros((width, EXTRA - 6), FL)], axis=1).astype(BF)
    pieces = (packed, project[0].astype(BF), expand[0].astype(BF), contract[0].astype(BF))
    split = nb * nv * PICKS <= 4096
    rounded = table_t.astype(BF)
    quarter = -(-rows // (nb * 128)) * 128
    if split:
        rounded = jnp.pad(rounded, ((0, 0), (0, nb * quarter - rows)))
    else:
        words = lax.all_gather(rounded, "batch", axis=0, tiled=True)

    seg_row, pos_row = segments[None, :], counted[None, :]
    tok = tokens.reshape(nv, SEQ_LEN)
    x, ids, place, most, every, a_all, u_all, *rest = embed(
        nb, nv, cap, rows, jnp.zeros((1,), I32), tok, rounded, (pieces[0], pieces[2]),
        targets[None, :] if split else None,
    )
    turns = (most[0] + cap - 1) // cap

    def more_rows(state):
        turn, total = state
        return turn + 1, total + embed(nb, nv, cap, rows, turn[None], tok, rounded)[0]

    x = lax.while_loop(lambda state: state[0] < turns, more_rows, (jnp.int32(1), x))[1]

    hall, kv, q, hq, mixed, lse, norm_rows, mixing_t, p_all, c_all, x1, h2, z, act, x2, features = run(
        functools.partial(attend_kernel, nb, nv),
        [
            SD((KEYS, D), BF), SD((KEYS, 2 * D), BF), SD((PICKS, D), BF), SD((PICKS, D), BF),
            SD((PICKS, D), BF), SD((NPAIR, 2, PICKS), FL), SD((8, D), FL), SD((SEQ_LEN, SLOTS * NB), BF),
            SD((D, D), BF), SD((FF, D), BF),
            SD((PICKS, D), FL), SD((PICKS, D), BF), SD((PICKS, FF), FL), SD((PICKS, FF), BF), SD((PICKS, D), FL),
            SD((PICKS, D), BF),
        ],
        weight_semaphores(2),
        [x, a_all, seg_row, pos_row, pieces[1], pieces[3], u_all],
        "attend", 6, flops=9 * 10**9, moved=30 * 10**6,
    )
    if split:
        live = jnp.pad(vocab_mask, (0, nb * quarter - rows))[None, :]
        df, dw, loss_block = wide_head(nb, nv, rows, features, rest[0], live, rest[1])
    else:
        df, dw, loss_block = head(nb, nv, features, words, vocab_mask[None, :], targets[:, None])
        dw_sum = lax.psum_scatter(dw, "batch", scatter_dimension=0, tiled=True)

    dc, du, dp, dx1, dmixed, dnorm = run(
        feed_back_kernel,
        [
            SD((FF, D), BF), SD((D, FF), BF), SD((D, D), BF), SD((PICKS, D), FL), SD((PICKS, D), BF), SD((8, D), FL),
        ],
        [pltpu.VMEM((PICKS, D), FL)],
        [df, x2, x1, h2, z, act, mixed, p_all, u_all, c_all, norm_rows],
        "feed_back", flops=4 * 10**9, moved=30 * 10**6,
    )
    da, dx, du_sum = run(
        functools.partial(attend_back_kernel, nb, nv),
        [SD((D, 3 * D + EXTRA), BF), SD((SEQ_LEN, D), BF), SD((width, FF // 2), BF)],
        [
            pltpu.VMEM((KEYS, 2 * D), BF), pltpu.VMEM((PICKS, D), BF), pltpu.VMEM((D, KEYS), BF),
            pltpu.VMEM((SEQ_LEN, D), FL), pltpu.VMEM((SEQ_LEN, D), FL), pltpu.VMEM((SLOTS * NB, D), BF),
            pltpu.VMEM((SEQ_LEN, PICKS), BF), *gradient_scratch(nb, nv, [du.shape], (0,), False),
        ],
        [dmixed, q, kv, lse, hall, hq, a_all, x, dx1, mixing_t, seg_row, pos_row, norm_rows, dnorm, du],
        "attend_back", 7, flops=12 * 10**9, moved=25 * 10**6,
        in_specs=[VM] * 14 + [HB],
    )
    extra, *sums = unembed(nb, nv, cap, width, rows, dx, ids, place, (da, dp, du_sum, dc), *((dw, loss_block) if split else ()))
    if split:
        *sums, dw_sum, totals, norm_grads = sums

    def more_grads(state):
        turn, total = state
        later = later_slots(nv, cap, rows, every, turn)
        return turn + 1, total + unembed(
            nb, nv, cap, width, rows, dx, later, place - jnp.array([0, 1, 0, 0, 0, 0, 0, 0], I32)[None, :, None] * (turn * cap)
        )[0]

    extra = lax.while_loop(lambda state: state[0] < turns, more_grads, (jnp.int32(1), extra))[1]

    if split:
        totals = lax.cond(
            turns > 1, lambda: norm(nb, nv, extra, dw_sum, sums, loss_block), lambda: totals
        )
    else:
        totals = norm(nb, nv, extra, dw_sum, sums, loss_block)
    grad_table = dw_sum[:, :rows].astype(FL) + extra
    grad_a, grad_p, grad_u, grad_c = (item.astype(FL) for item in sums)
    grad_norms = norm_grads if split else grad_a[:, 3 * D : 3 * D + 6].T
    grad_a = grad_a[:, : 3 * D]
    squares, loss = totals[0, 0], totals[1, 0]
    gradient_norm = jnp.sqrt(squares)
    clip = jnp.minimum(1.0, MAX_NORM / (gradient_norm + 1e-06))
    count = step_count[0].astype(FL)

    def update(weight, moment, square, gradient, decay=DECAY, rate=LEARN_RATE):
        return adamw(weight, moment, square, gradient, clip, count, decay, rate)

    table_out = [item.T for item in update(table_t, table_moment.T, table_square.T, grad_table)]
    attend_out = update(attend, attend_moment, attend_square, grad_a[None])
    project_out = update(project, project_moment, project_square, grad_p[None])
    expand_out = update(expand, expand_moment, expand_square, grad_u[None])
    contract_out = update(contract, contract_moment, contract_square, grad_c[None])
    gain_out = update(gain, gain_moment, gain_square, grad_norms[:3], 0.0, NORM_RATE)
    shift_out = update(shift, shift_moment, shift_square, grad_norms[3:6], 0.0, NORM_RATE)
    return (
        loss, gradient_norm, *table_out, *attend_out, *project_out, *expand_out, *contract_out, *gain_out, *shift_out,
    )


def solution(mesh):
    nb, nv = mesh.shape["batch"], mesh.shape["vocab"]
    both, split, middle, last = P(("batch", "vocab")), P("vocab", "batch"), P(None, "batch", None), P(None, "batch")
    state = (split,) * 3 + (middle,) * 12 + (last,) * 6
    return jax.shard_map(
        functools.partial(shards, nb, nv),
        mesh=mesh,
        in_specs=(P("batch"), P("batch"), both, both, P("vocab"), P()) + state,
        out_specs=(P(), P()) + state,
        check_vma=False,
    )
```

```python
import functools
import math

import jax
import jax.numpy as jnp
from jax import lax
from jax.experimental import pallas as pl
from jax.experimental.pallas import tpu as pltpu
from jax.sharding import PartitionSpec as P

D = 768
H = 12
HD = 64
FF = 3072
NB = 256
SEG_BLOCKS = 4
SLOTS = SEG_BLOCKS - 2
SEQ_LEN = 1024
PICKS = 128
KEYS = SLOTS * NB + SEQ_LEN
BLK = 256
PAIR = 2 * HD
NPAIR = H // 2
EXTRA = 256
WIDE = (3 * D + EXTRA, D, FF, D)

NORM_EPS = 1e-05
MAX_NORM = 0.02
LEARN_RATE = 0.04
NORM_RATE = 0.5
BETA_ONE = 0.9
BETA_TWO = 0.999
ADAM_EPS = 1e-08
DECAY = 0.1
NEG_BIG = -1e30
BF = jnp.bfloat16
FL = jnp.float32
I32 = jnp.int32
MESH = pl.DeviceIdType.MESH
SD = jax.ShapeDtypeStruct
VM = pl.BlockSpec(memory_space=pltpu.VMEM)
SM = pl.BlockSpec(memory_space=pltpu.SMEM)
HB = pl.BlockSpec(memory_space=pl.ANY)
LIMIT = 62 * 2**20


def nn(a, b):
    return lax.dot_general(a, b, (((1,), (0,)), ((), ())), preferred_element_type=FL)


def nt(a, b):
    return lax.dot_general(a, b, (((1,), (1,)), ((), ())), preferred_element_type=FL)


def iota(shape, axis):
    return lax.broadcasted_iota(I32, shape, axis)


def lanes(start, size):
    return pl.ds(pl.multiple_of(start, 128), size)


def chunk_of(rows, want):
    return want if rows % want == 0 else rows


def run(kernel, outs, scratch, ins, name, collective=None, flops=0, moved=0, out_specs=None, in_specs=None):
    return pl.pallas_call(
        kernel,
        out_shape=outs,
        in_specs=in_specs if in_specs is not None else [VM] * len(ins),
        out_specs=out_specs if out_specs is not None else [VM] * len(outs),
        scratch_shapes=scratch,
        compiler_params=pltpu.CompilerParams(
            vmem_limit_bytes=LIMIT,
            collective_id=collective,
            has_side_effects=collective is not None,
        ),
        cost_estimate=pl.CostEstimate(flops=flops, bytes_accessed=moved, transcendentals=0),
        name=name,
    )(*ins)


def send(source, target, out_sem, in_sem, device):
    return pltpu.make_async_remote_copy(
        src_ref=source, dst_ref=target, send_sem=out_sem, recv_sem=in_sem, device_id=device, device_id_type=MESH
    )


def meet(axes):
    barrier = pltpu.get_barrier_semaphore()
    count = 0
    for axis, size in axes:
        me = lax.axis_index(axis)

        def greet(step, carry, axis=axis, size=size, me=me):
            pl.semaphore_signal(barrier, inc=1, device_id={axis: lax.rem(me + step, size)}, device_id_type=MESH)
            return carry

        lax.fori_loop(1, size, greet, 0)
        count += size - 1
    pl.semaphore_wait(barrier, count)


def each(start, stop, body):
    def step(index, carry):
        body(index)
        return carry

    lax.fori_loop(start, stop, step, 0)


def embed_kernel(
    nb, nv, cap, part, rows, first, split, *refs
):
    round_ref, tok_ref, words = refs[:3]
    shards, refs = (refs[3:5], refs[5:]) if first else ((), refs[3:])
    target_ref, refs = (refs[0], refs[1:]) if split else (None, refs)
    x_ref, ids_ref, place_ref, most_ref, tok_ref_all = refs[:5]
    wholes, refs = (refs[5:7], refs[7:]) if first else ((), refs[5:])
    (quarter_ref, target_all), refs = (refs[:2], refs[2:]) if split else ((None, None), refs)
    before, ranks, work, sent, got, spread, mixed, turned = refs[:8]
    tok_out, tok_in, row_out, row_in, mix_out, mix_in = refs[8:14]
    b, v = lax.axis_index("batch"), lax.axis_index("vocab")
    width = words.shape[0]
    shift = round_ref[0] * cap
    meet((("batch", nb), ("vocab", nv)))
    gather = WeightGather(nb, shards, wholes, *refs[14:19]) if first else None
    quarter_out, quarter_in, quarter_own, target_out, target_in = refs[19:24] if split else [None] * 5

    def tok_copy(step):
        return send(
            tok_ref, tok_ref_all.at[b], tok_out.at[step], tok_in.at[step], {"batch": lax.rem(b + step, nb)}
        )

    for step in range(1, nb):
        tok_copy(step).start()

    def target_copy(step):
        return send(
            target_ref, target_all.at[b], target_out.at[step], target_in.at[step], {"batch": lax.rem(b + step, nb)}
        )

    def quarter(owner):
        return words.at[:, lanes(owner * (words.shape[1] // nb), words.shape[1] // nb)]

    def quarter_copy(step):
        other = lax.rem(b + step, nb)
        place = quarter_ref.at[pl.ds(pl.multiple_of(b * width, 16), width), :]
        return send(quarter(other), place, quarter_out.at[step], quarter_in.at[step], {"batch": other})

    def quarter_keep():
        place = quarter_ref.at[pl.ds(pl.multiple_of(b * width, 16), width), :]
        return pltpu.make_async_copy(quarter(b), place, quarter_own.at[0])

    if split:
        target_all[b] = target_ref[...]
        for step in range(1, nb):
            target_copy(step).start()
    if first:
        gather.start()
    if split:
        quarter_keep().start()
    tok_ref_all[b] = tok_ref[...]
    before[...] = (iota((SEQ_LEN, SEQ_LEN), 0) < iota((SEQ_LEN, SEQ_LEN), 1)).astype(FL).astype(BF)
    for step in range(1, nb):
        tok_copy(step).wait()

    base = v * rows
    most = jnp.zeros((nv, 1), FL)
    for p in range(nb):
        ids = tok_ref_all[p]
        mine = (ids >= base) & (ids < base + rows)
        rank = nn(mine.astype(FL).astype(BF), before[...])
        ranks[p] = jnp.where(mine, rank.astype(I32) - shift, -1)
        for owner in range(nv):
            theirs = (ids >= owner * rows) & (ids < (owner + 1) * rows)
            most = jnp.maximum(most, jnp.sum(theirs.astype(FL), axis=1, keepdims=True))
    most_ref[0] = jnp.max(most).astype(I32)

    def row_copy(step):
        return send(
            sent.at[step], got.at[v], row_out.at[step], row_in.at[step], {"vocab": lax.rem(v + step, nv)}
        )

    def build(turn):
        step = lax.rem(turn, nv)
        dest = lax.rem(v + step, nv)
        found = []
        for p in range(nb):
            pick = (iota((cap, SEQ_LEN), 0) == ranks[p, pl.ds(dest, 1), :]).astype(FL).astype(BF)
            local = tok_ref_all[p, pl.ds(dest, 1), :] - base
            line = iota((8, SEQ_LEN), 0)
            high, low = lax.shift_right_arithmetic(local, 7), lax.bitwise_and(local, 127)
            digits = jnp.where(line == 0, high, jnp.where(line == 1, low, 0)).astype(FL).astype(BF)
            both = nt(pick, digits)
            found.append((both[:, 0:1] * 128.0 + both[:, 1:2]).astype(I32))
        index = jnp.concatenate(found, axis=0)
        ids_ref[dest] = index
        work[...] = jnp.zeros_like(work)

        def piece(j):
            hot = (index - j * part == iota((nb * cap, part), 1)).astype(FL).astype(BF)
            work[...] += nt(hot, words[:, lanes(j * part, part)])

        each(0, rows // part, piece)
        block = work[...].T.astype(BF)

        @pl.when(step > 0)
        def _():
            sent[step] = block
            row_copy(step).start()

        @pl.when(step == 0)
        def _():
            got[v] = block

    each(1, nv // 2 + 1, build)
    if first:
        gather.pass_on()
    if split:
        for step in range(1, nb):
            quarter_copy(step).start()
    each(nv // 2 + 1, nv + 1, build)

    keys = []
    for p in range(nb):
        ids = tok_ref_all[p, pl.ds(v, 1), :]
        owner = iota((nv, SEQ_LEN), 0)
        theirs = (ids >= owner * rows) & (ids < (owner + 1) * rows)
        rank = nn(theirs.astype(FL).astype(BF), before[...])
        place = jnp.sum(jnp.where(theirs, rank, 0.0), axis=0, keepdims=True).astype(I32) - shift
        holder = jnp.sum(jnp.where(theirs, owner.astype(FL), 0.0), axis=0, keepdims=True).astype(I32)
        line = iota((8, SEQ_LEN), 0)
        place_ref[p] = jnp.where(line == 0, holder, jnp.where(line == 1, place, 0))
        keys.append((holder, place))
        spread[p] = jnp.zeros((width, SEQ_LEN), FL)

    def take(turn):
        step = lax.rem(turn, nv)
        source = lax.rem(v - step + nv, nv)

        @pl.when(step > 0)
        def _():
            row_copy(step).wait()

        block = got[source]
        for p in range(nb):
            holder, place = keys[p]
            key = jnp.where(holder == source, place, -1)
            hot = (iota((cap, SEQ_LEN), 0) == key).astype(FL).astype(BF)
            spread[p] += nn(block[:, p * cap : (p + 1) * cap], hot)

    each(1, nv + 1, take)

    def mix_copy(step):
        return send(
            mixed.at[step], turned.at[b], mix_out.at[step], mix_in.at[step], {"batch": lax.rem(b + step, nb)}
        )

    for step in range(1, nb):
        mixed[step] = spread[lax.rem(b + step, nb)].astype(BF)
        mix_copy(step).start()
    turned[b] = spread[b].astype(BF)
    for step in range(1, nb):
        mix_copy(step).wait()
    x_ref[...] = turned[...].reshape(nb * width, SEQ_LEN).T
    if first:
        gather.last_hop()
        for w in range(len(shards)):
            gather.finish(w)
    if split:
        quarter_keep().wait()
        for step in range(1, nb):
            target_copy(step).wait()
            quarter_copy(step).wait()


def weight_semaphores(count):
    return [pltpu.SemaphoreType.DMA((count,))] + [pltpu.SemaphoreType.DMA((count, 4))] * 4


class WeightGather:
    def __init__(self, nb, shards, wholes, own_sem, out_sem, in_sem, pair_out, pair_in):
        self.nb, self.shards, self.wholes = nb, shards, wholes
        self.own_sem, self.out_sem, self.in_sem, self.pair_out, self.pair_in = own_sem, out_sem, in_sem, pair_out, pair_in
        self.b, v = lax.axis_index("batch"), lax.axis_index("vocab")
        self.core = lax.rem(v, 2)
        self.sibling = {"vocab": v + 1 - 2 * self.core}

    def flip(self, bits):
        b = self.b
        low, high = lax.rem(b, 2), b // 2
        return (high if bits < 2 else 1 - high) * 2 + (low if bits % 2 == 0 else 1 - low)

    def place(self, w, owner, top, size):
        rows = self.shards[w].shape[0]
        first = pl.multiple_of(owner * rows + self.core * (rows // 2) + top, 16)
        return self.wholes[w].at[pl.ds(first, size), :]

    def routes(self, w):
        rows = self.shards[w].shape[0] // 2
        if self.nb == 4:
            half = rows // 2
            return [
                (self.b, 0, rows, self.flip(1), self.flip(1)),
                (self.b, 0, rows, self.flip(2), self.flip(2)),
                (self.flip(1), 0, half, self.flip(2), self.flip(3)),
                (self.flip(2), half, half, self.flip(1), self.flip(3)),
            ]
        others = [lax.rem(self.b + step, self.nb) for step in range(1, self.nb)]
        came = [lax.rem(self.b - step + self.nb, self.nb) for step in range(1, self.nb)]
        return [(self.b, 0, rows, other, source) for other, source in zip(others, came)]

    def own_copy(self, w):
        rows = self.shards[w].shape[0]
        first = pl.multiple_of(self.b * rows, 16)
        return pltpu.make_async_copy(self.shards[w], self.wholes[w].at[pl.ds(first, rows), :], self.own_sem.at[w])

    def copy(self, w, k):
        owner, top, size, device, _ = self.routes(w)[k]
        if self.nb == 4 and k >= 2:
            source = self.place(w, owner, top, size)
        else:
            source = self.shards[w].at[pl.ds(pl.multiple_of(self.core * size, 16), size), :]
        target = self.place(w, owner, top, size)
        return send(source, target, self.out_sem.at[w, k], self.in_sem.at[w, k], {"batch": device})

    def pair(self, w, k):
        _, top, size, _, arrived = self.routes(w)[k]
        ref = self.place(w, arrived, top, size)
        return send(ref, ref, self.pair_out.at[w, k], self.pair_in.at[w, k], self.sibling)

    def start(self):
        for w in range(len(self.shards)):
            for k in range(2 if self.nb == 4 else self.nb - 1):
                self.copy(w, k).start()
        for w in range(len(self.shards)):
            self.own_copy(w).start()

    def pass_on(self):
        if self.nb != 4:
            return
        for w in range(len(self.shards)):
            for k in range(2):
                self.copy(w, k).wait_recv()
                self.copy(w, k + 2).start()
                self.pair(w, k).start()

    def last_hop(self):
        for w in range(len(self.shards)):
            for k in range(2 if self.nb == 4 else 0, len(self.routes(w))):
                self.copy(w, k).wait_recv()
                self.pair(w, k).start()

    def finish(self, w):
        self.own_copy(w).wait()
        for k in range(len(self.routes(w))):
            self.copy(w, k).wait_send()
            self.pair(w, k).wait()


def embed(nb, nv, cap, rows, turn, tok, table, shards=(), targets=None):
    width = table.shape[0]
    split = targets is not None
    part = chunk_of(rows, 640)
    count = nb * cap
    outs = [
        SD((SEQ_LEN, D), BF),
        SD((nv, count, 1), I32),
        SD((nb, 8, SEQ_LEN), I32),
        SD((1,), I32),
        SD((nb, nv, SEQ_LEN), I32),
    ]
    first = len(shards) > 0
    outs += [SD((nb * item.shape[0], item.shape[1]), BF) for item in shards]
    if split:
        outs += [SD((D, table.shape[1] // nb), BF), SD((nb, *targets.shape), I32)]
    dma = pltpu.SemaphoreType.DMA
    scratch = [
        pltpu.VMEM((SEQ_LEN, SEQ_LEN), BF),
        pltpu.VMEM((nb, nv, SEQ_LEN), I32),
        pltpu.VMEM((count, width), FL),
        pltpu.VMEM((nv, width, count), BF),
        pltpu.VMEM((nv, width, count), BF),
        pltpu.VMEM((nb, width, SEQ_LEN), FL),
        pltpu.VMEM((nb, width, SEQ_LEN), BF),
        pltpu.VMEM((nb, width, SEQ_LEN), BF),
        dma((nb,)), dma((nb,)), dma((nv,)), dma((nv,)), dma((nb,)), dma((nb,)),
    ]
    if first:
        scratch += weight_semaphores(len(shards))
    if split:
        scratch += [dma((nb,)), dma((nb,)), dma((1,)), dma((nb,)), dma((nb,))]
    extra = [targets] if split else []
    return run(
        functools.partial(embed_kernel, nb, nv, cap, part, rows, first, split), outs, scratch,
        [turn, tok, table, *shards, *extra],
        "embed" if first else "embed_more", 0 if first else 3,
        in_specs=[SM, VM, VM] + [VM] * len(shards) + [VM] * len(extra),
        out_specs=[VM] * 3 + [SM, VM] + [HB] * len(shards) + ([HB, VM] if split else []),
    )


class GradientSum:
    def __init__(self, nb, nv, grads, refs, totals=None, sums=None):
        self.nb, self.nv, self.grads, self.sums = nb, nv, grads, sums
        self.todo = [w for w, item in enumerate(grads) if item is not None]
        take = iter(refs)
        spread = lambda keys: {w: next(take) for w in keys}
        everything = range(len(grads))
        self.own, self.near, self.shard = spread(self.todo), spread(self.todo), spread(self.todo)
        if sums is not None:
            self.total = spread(self.todo)
            self.total.update(totals)
            self.bits, self.result = spread(everything), spread(everything)
        else:
            self.total = totals
        self.load_sem, self.pair_out, self.pair_in, self.mix_out, self.mix_in = (next(take) for _ in range(5))
        if sums is not None:
            (self.cut_out, self.cut_in, self.all_out, self.all_in, self.last_out, self.last_in,
             self.store_sem) = take
        self.b, v = lax.axis_index("batch"), lax.axis_index("vocab")
        self.core, self.chip, self.chips = lax.rem(v, 2), v // 2, nv // 2
        self.sibling = {"vocab": v + 1 - 2 * self.core}

    def half(self, w, core):
        cols = self.total[w].shape[1]
        return lanes(core * cols, cols)

    def load(self, w):
        return pltpu.make_async_copy(self.grads[w].at[:, self.half(w, self.core)], self.own[w], self.load_sem.at[w])

    def pair(self, w):
        source = self.grads[w].at[:, self.half(w, 1 - self.core)]
        return send(source, self.near[w], self.pair_out.at[w], self.pair_in.at[w], self.sibling)

    def start(self):
        for w in sorted(self.todo, reverse=True):
            self.pair(w).start()
            self.load(w).start()

    def mix(self, w, step):
        other = lax.rem(self.b + step, self.nb)
        rows = self.own[w].shape[0] // self.nb
        source = self.own[w].at[pl.ds(pl.multiple_of(other * rows, 16), rows), :]
        return send(source, self.shard[w].at[step], self.mix_out.at[w, step], self.mix_in.at[w, step], {"batch": other})

    def scatter(self, w):
        self.load(w).wait()
        self.pair(w).wait()
        rows = self.own[w].shape[0] // self.nb

        def add(i, w=w, rows=rows):
            cut = pl.ds(pl.multiple_of(i * rows, 16), rows)
            self.own[w][cut, :] = (self.own[w][cut, :].astype(FL) + self.near[w][cut, :].astype(FL)).astype(BF)

        each(0, self.nb, add)
        for step in range(1, self.nb):
            self.mix(w, step).start()

    def pieces(self, w):
        rows = self.total[w].shape[0]
        count = max(n for n in range(1, self.chips + 1) if rows % (16 * n) == 0)
        return count, rows // count

    def peer(self, step):
        other = lax.rem(self.chip + step, self.chips)
        return other, {"vocab": other * 2 + self.core}

    def cut(self, w, step):
        other, device = self.peer(step)
        size = self.pieces(w)[1]
        source = self.total[w].at[pl.ds(pl.multiple_of(other * size, 16), size), :]
        return send(source, self.bits[w].at[step], self.cut_out.at[w, step], self.cut_in.at[w, step], device)

    def back(self, w, step):
        size = self.pieces(w)[1]
        place = self.result[w].at[pl.ds(pl.multiple_of(self.chip * size, 16), size), :]
        return send(place, place, self.all_out.at[w, step], self.all_in.at[w, step], self.peer(step)[1])

    def back_recv(self, w, step):
        source = lax.rem(self.chip - step + self.chips, self.chips)
        size = self.pieces(w)[1]
        place = self.result[w].at[pl.ds(pl.multiple_of(source * size, 16), size), :]
        return send(place, place, self.all_out.at[w, step], self.all_in.at[w, step], self.peer(step)[1])

    def gather(self, w):
        rows = self.total[w].shape[0]
        for step in range(1, self.nb):
            self.mix(w, step).wait()
        here = pl.ds(pl.multiple_of(self.b * rows, 16), rows)
        value = self.own[w][here, :].astype(FL)
        for step in range(1, self.nb):
            value = value + self.shard[w][step].astype(FL)
        self.total[w][...] = value.astype(BF)

    def reduce(self, w):
        if w in self.todo:
            self.gather(w)
        count = self.pieces(w)[0]

        def go(step):
            @pl.when(self.peer(step)[0] < count)
            def _():
                self.cut(w, step).start()

        each(1, self.chips, go)

    def collect(self, w):
        count, size = self.pieces(w)
        mine = pl.ds(pl.multiple_of(self.chip * size, 16), size)

        @pl.when(self.chip < count)
        def _(w=w, mine=mine):
            def add(step, value):
                self.cut(w, step).wait_recv()
                return value + self.bits[w][step].astype(FL)

            value = lax.fori_loop(1, self.chips, add, self.total[w][mine, :].astype(FL))
            self.result[w][mine, :] = value.astype(BF)
            each(1, self.chips, lambda step: self.back(w, step).start())

        def sent(step, w=w, count=count):
            @pl.when(self.peer(step)[0] < count)
            def _():
                self.cut(w, step).wait_send()

        each(1, self.chips, sent)

    def last(self, w):
        return send(
            self.result[w], self.sums[w].at[:, self.half(w, self.core)], self.last_out.at[w], self.last_in.at[w], self.sibling
        )

    def store(self, w):
        return pltpu.make_async_copy(self.result[w], self.sums[w].at[:, self.half(w, self.core)], self.store_sem.at[w])

    def finish(self):
        for w in range(4):
            count = self.pieces(w)[0]

            def got(step, w=w, count=count):
                @pl.when(lax.rem(self.chip - step + self.chips, self.chips) < count)
                def _():
                    self.back_recv(w, step).wait_recv()

            each(1, self.chips, got)
            self.last(w).start()
            self.store(w).start()
        for w in range(4):
            count = self.pieces(w)[0]

            @pl.when(self.chip < count)
            def _(w=w):
                each(1, self.chips, lambda step: self.back(w, step).wait_send())

            self.store(w).wait()
            self.last(w).wait_send()
            other = self.sums[w].at[:, self.half(w, 1 - self.core)]
            send(other, other, self.last_out.at[w], self.last_in.at[w], self.sibling).wait_recv()


def gradient_scratch(nb, nv, shapes, todo, whole=True):
    chips = nv // 2
    halves = [(rows, cols // 2) for rows, cols in shapes]
    shards = [(rows // nb, cols) for rows, cols in halves]
    sizes = [rows // max(n for n in range(1, chips + 1) if rows % (16 * n) == 0) for rows, _ in shards]
    dma = pltpu.SemaphoreType.DMA
    count = len(shapes)
    refs = [pltpu.VMEM(halves[w], BF) for w in todo] * 2 + [pltpu.VMEM((nb, *shards[w]), BF) for w in todo]
    if whole:
        refs += [pltpu.VMEM(shards[w], BF) for w in todo]
        refs += [pltpu.VMEM((chips, size, item[1]), BF) for size, item in zip(sizes, shards)]
        refs += [pltpu.VMEM(item, BF) for item in shards]
    refs += [dma((count,)), dma((count,)), dma((count,)), dma((count, nb)), dma((count, nb))]
    if whole:
        refs += [dma((count, chips))] * 4 + [dma((count,))] * 3
    return refs


def squares(refs, part):
    cols = min(ref.shape[1] for ref in refs)

    def add(j, total):
        value = refs[0][:, lanes(j * part, part)].astype(FL)
        for ref in refs[1:]:
            value = value + ref[:, lanes(j * part, part)].astype(FL)
        return total + jnp.sum(value * value, axis=0, keepdims=True)

    line = lax.fori_loop(0, cols // part, add, jnp.zeros((1, part), FL))
    return jnp.sum(line, axis=1, keepdims=True)


def add_up(nb, nv, own, loss_ref, out_ref, mine, near, lines, vocab_out, vocab_in, batch_out, batch_in):
    b, v = lax.axis_index("batch"), lax.axis_index("vocab")
    line = iota((8, 128), 0)
    mine[...] = jnp.where(line == 0, own, jnp.where((line == 1) & (v == 0), loss_ref[...], 0.0))

    def vocab_copy(step):
        return send(mine, near.at[v], vocab_out.at[step], vocab_in.at[step], {"vocab": lax.rem(v + step, nv)})

    each(1, nv, lambda step: vocab_copy(step).start())
    near[v] = mine[...]
    each(1, nv, lambda step: vocab_copy(step).wait())
    mine[...] = lax.fori_loop(0, nv, lambda u, total: total + near[u], jnp.zeros((8, 128), FL))

    def batch_copy(step):
        return send(mine, lines.at[b], batch_out.at[step], batch_in.at[step], {"batch": lax.rem(b + step, nb)})

    each(1, nb, lambda step: batch_copy(step).start())
    lines[b] = mine[...]
    each(1, nb, lambda step: batch_copy(step).wait())
    out_ref[...] = lax.fori_loop(0, nb, lambda u, total: total + lines[u], jnp.zeros((8, 128), FL))


def add_up_scratch(nb, nv):
    dma = pltpu.SemaphoreType.DMA
    tiles = [pltpu.VMEM((8, 128), FL), pltpu.VMEM((nv, 8, 128), FL), pltpu.VMEM((nb, 8, 128), FL)]
    return tiles + [dma((nv,)), dma((nv,)), dma((nb,)), dma((nb,))]


def norm_kernel(nb, nv, extra_ref, dw_ref, a_ref, p_ref, u_ref, c_ref, loss_ref, out_ref, *scratch):
    meet((("batch", nb), ("vocab", nv)))
    own = squares((extra_ref, dw_ref), chunk_of(extra_ref.shape[1], 640))
    layer = squares((a_ref,), 512) + squares((p_ref,), 384) + squares((u_ref,), 512) + squares((c_ref,), 384)
    own = own + jnp.where(lax.axis_index("vocab") == 0, layer, jnp.zeros_like(layer))
    add_up(nb, nv, own, loss_ref, out_ref, *scratch)


def unembed_kernel(nb, nv, cap, part, first, split, *refs):
    x_ref, ids_ref, place_ref = refs[:3]
    grads, refs = (refs[3:7], refs[7:]) if first else ((), refs[3:])
    if first:
        totals, grads = {2: grads[2]}, (grads[0], grads[1], None, grads[3])
    (quarter_ref, loss_ref), refs = (refs[:2], refs[2:]) if split else ((None, None), refs)
    out_ref = refs[0]
    sums, refs = (refs[1:5], refs[5:]) if first else ((), refs[1:])
    (dw_ref, total_ref, rows_ref), refs = (refs[:3], refs[3:]) if split else ([None] * 3, refs)
    (quarter_out, quarter_in, quarter_own), refs = (refs[:3], refs[3:]) if split else ([None] * 3, refs)
    (strip, strip_sem, *sum_refs), refs = (refs[:9], refs[9:]) if split else ([None] * 2, refs)
    turned, parts, sent, got, mix_out, mix_in, row_out, row_in = refs[:8]
    layer = GradientSum(nb, nv, grads, refs[8:], totals, sums) if first else None
    b, v = lax.axis_index("batch"), lax.axis_index("vocab")
    width, rows = out_ref.shape
    meet((("batch", nb), ("vocab", nv)))
    turned[...] = x_ref[...].T.reshape(nb, width, SEQ_LEN)

    def mix_copy(step):
        other = lax.rem(b + step, nb)
        return send(turned.at[other], parts.at[b], mix_out.at[step], mix_in.at[step], {"batch": other})

    for step in range(1, nb):
        mix_copy(step).start()
    if first:
        layer.start()
        layer.reduce(2)
    parts[b] = turned[b]
    for step in range(1, nb):
        mix_copy(step).wait()

    def quarter_place():
        size = quarter_ref.shape[1]
        return dw_ref.at[:, lanes(b * size, size)]

    def quarter_copy(step):
        other = lax.rem(b + step, nb)
        source = quarter_ref.at[pl.ds(pl.multiple_of(other * width, 16), width), :]
        return send(source, quarter_place(), quarter_out.at[step], quarter_in.at[step], {"batch": other})

    def quarter_keep():
        source = quarter_ref.at[pl.ds(pl.multiple_of(b * width, 16), width), :]
        return pltpu.make_async_copy(source, quarter_place(), quarter_own.at[0])

    def row_copy(step):
        return send(
            sent.at[step], got.at[v], row_out.at[step], row_in.at[step], {"vocab": lax.rem(v + step, nv)}
        )

    def build(turn):
        step = lax.rem(turn, nv)
        owner = lax.rem(v + step, nv)
        blocks = []
        for p in range(nb):
            key = jnp.where(place_ref[p, 0:1, :] == owner, place_ref[p, 1:2, :], -1)
            hot = (iota((cap, SEQ_LEN), 0) == key).astype(FL).astype(BF)
            blocks.append(nt(parts[p], hot).astype(BF))
        block = jnp.concatenate(blocks, axis=1)

        @pl.when(step > 0)
        def _():
            sent[step] = block
            row_copy(step).start()

        @pl.when(step == 0)
        def _():
            got[v] = block

    if first:
        layer.scatter(3)
    each(1, nv // 2 + 1, build)
    if first:
        layer.collect(2)
    each(nv // 2 + 1, nv + 1, build)
    if first:
        layer.scatter(0)
    if split:
        quarter_keep().start()
    out_ref[...] = jnp.zeros_like(out_ref)

    def take(step):
        source = lax.rem(v - step + nv, nv)

        @pl.when(step > 0)
        def _():
            row_copy(step).wait()

        block, index = got[source], ids_ref[source]

        def piece(j):
            hot = (index - j * part == iota((nb * cap, part), 1)).astype(FL).astype(BF)
            out_ref[:, lanes(j * part, part)] += nn(block, hot)

        each(0, rows // part, piece)

    if first:
        quarter = nv // 4
        each(0, quarter, take)
        layer.reduce(3)
        layer.scatter(1)
        if split:
            for step in range(1, nb):
                quarter_copy(step).start()
        each(quarter, 2 * quarter, take)
        layer.reduce(0)
        each(2 * quarter, 3 * quarter, take)
        layer.collect(3)
        layer.reduce(1)
        each(3 * quarter, nv, take)
        layer.collect(0)
        layer.collect(1)
        layer.finish()
        if split:
            quarter_keep().wait()
            for step in range(1, nb):
                quarter_copy(step).wait()
            rows_copy = pltpu.make_async_copy(sums[0].at[:, lanes(3 * D, 128)], strip, strip_sem.at[0])
            rows_copy.start()
            layer_squares = jnp.zeros((1, 1), FL)
            for w in range(4):
                cols = layer.result[w].shape[1]
                layer_squares += squares((layer.result[w],), max(n for n in (640, 512, 384, 128) if cols % n == 0))
            own = squares((out_ref, dw_ref), part)
            own = own + jnp.where(v < 2, layer_squares, 0.0)
            add_up(nb, nv, own, loss_ref, total_ref, *sum_refs)
            rows_copy.wait()
            rows_ref[...] = strip[...].astype(FL).T[:8, :]
    else:
        each(0, nv, take)


def unembed(nb, nv, cap, width, rows, grad, ids, place, grads=(), quarter=None, loss=None):
    part = chunk_of(rows, 640)
    count = nb * cap
    dma = pltpu.SemaphoreType.DMA
    scratch = [
        pltpu.VMEM((nb, width, SEQ_LEN), BF),
        pltpu.VMEM((nb, width, SEQ_LEN), BF),
        pltpu.VMEM((nv, width, count), BF),
        pltpu.VMEM((nv, width, count), BF),
        dma((nb,)), dma((nb,)), dma((nv,)), dma((nv,)),
    ]
    first, split = len(grads) > 0, quarter is not None
    if split:
        strip = [pltpu.VMEM((width, 128), BF), dma((1,))]
        scratch = [dma((nb,)), dma((nb,)), dma((1,))] + strip + add_up_scratch(nb, nv) + scratch
    if first:
        shapes = [item.shape if w != 2 else (nb * item.shape[0], 2 * item.shape[1]) for w, item in enumerate(grads)]
        scratch += gradient_scratch(nb, nv, shapes, (0, 1, 3))
    outs = [SD((width, rows), FL)] + [SD((item[0] // nb, item[1]), BF) for item in (shapes if first else ())]
    extra = [quarter, loss] if split else []
    if split:
        outs += [SD((width, nb * quarter.shape[1]), BF), SD((8, 128), FL), SD((8, width), FL)]
    return run(
        functools.partial(unembed_kernel, nb, nv, cap, part, first, split),
        outs,
        scratch,
        [grad, ids, place, *grads, *extra],
        "unembed" if first else "unembed_more",
        2 if first else 4,
        in_specs=[VM] * 3 + ([HB, HB, VM, HB] if first else []) + [VM] * len(extra),
        out_specs=[VM] + [HB] * len(grads) + ([VM] * 3 if split else []),
    )


def later_slots(nv, cap, rows, every, turn):
    nb = every.shape[0]
    v = lax.axis_index("vocab")
    local = every - v * rows
    mine = (local >= 0) & (local < rows)
    rank = jnp.cumsum(mine.astype(I32), axis=-1) - 1 - turn * cap
    hot = (rank[:, :, None, :] == jnp.arange(cap)[None, None, :, None]) & mine[:, :, None, :]
    ids = jnp.sum(jnp.where(hot, local[:, :, None, :], 0), axis=-1)
    return jnp.transpose(ids, (1, 0, 2)).reshape(nv, nb * cap, 1)


def standard(value):
    centre = value - jnp.mean(value, axis=-1, keepdims=True)
    spread = jnp.mean(centre * centre, axis=-1, keepdims=True)
    scale = lax.rsqrt(spread + NORM_EPS)
    return centre * scale, scale


def norm_back(unit, scale, gain, upstream):
    inner = upstream * gain
    first = jnp.mean(inner, axis=-1, keepdims=True)
    second = jnp.mean(inner * unit, axis=-1, keepdims=True)
    grad = scale * (inner - first - unit * second)
    return grad, jnp.sum(upstream * unit, axis=0, keepdims=True), jnp.sum(upstream, axis=0, keepdims=True)


def head_lanes(value, head):
    lane = iota(value.shape, 1)
    keep = (lane < HD) if head == 0 else (lane >= HD)
    return jnp.where(keep, value, jnp.zeros_like(value))


def visible_keys(seg_ref, pos_ref):
    position = pos_ref[...]
    block = position // BLK
    marks = [seg_ref[:, i * BLK : i * BLK + 1] for i in range(SEQ_LEN // BLK)]
    segment = jnp.zeros_like(position)
    for i, mark in enumerate(marks):
        segment = jnp.where(block == i, mark, segment)
    row = iota((BLK, PICKS), 0)
    parts = [jnp.broadcast_to(segment == slot + 1, (NB, PICKS)) for slot in range(SLOTS)]
    parts += [(segment == mark) & (row + i * BLK <= position) for i, mark in enumerate(marks)]
    return parts


def masked(visible, scores):
    return jnp.concatenate(
        [jnp.where(keep, scores[i * BLK : (i + 1) * BLK, :], NEG_BIG) for i, keep in enumerate(visible)], axis=0
    )


def memory_weights(segments, slot):
    length = segments.shape[1]
    inside = (segments == slot).astype(FL)
    start = jnp.sum((segments < slot).astype(FL), axis=1, keepdims=True)
    count = jnp.sum(inside, axis=1, keepdims=True)
    times = (iota((1, length), 1).astype(FL) - start + 0.5) / jnp.maximum(count, 1.0)
    centres = (iota((NB, 1), 0).astype(FL) + 0.5) / NB
    offset = (times - centres) * NB
    basis = jnp.exp(-0.5 * offset * offset) * inside
    total = jnp.sum(basis, axis=1, keepdims=True) + (count == 0.0).astype(FL)
    return basis / total


def attend_kernel(
    nb, nv, x_ref, a_ref, seg_ref, pos_ref, p_ref, c_ref, u_ref,
    hall_ref, kv_ref, q_ref, hq_ref, o_ref, lse_ref, norm_ref, mixt_ref, p_all, c_all,
    x1_ref, h2_ref, z_ref, act_ref, x2_ref, f_ref, *sems,
):
    meet((("batch", nb), ("vocab", nv)))
    gather = WeightGather(nb, (p_ref, c_ref), (p_all, c_all), *sems)
    gather.start()
    norm_ref[...] = a_ref[:, 3 * D : 3 * D + 128].astype(FL).T[:8, :]
    gain, bias = norm_ref[0:1, :], norm_ref[3:4, :]

    def normalize(i):
        unit, _ = standard(x_ref[pl.ds(i * BLK, BLK), :].astype(FL))
        hall_ref[pl.ds(SLOTS * NB + i * BLK, BLK), :] = (unit * gain + bias).astype(BF)

    each(0, SEQ_LEN // BLK, normalize)
    normed = hall_ref[SLOTS * NB :, :]
    for slot in range(SLOTS):
        mixing = memory_weights(seg_ref[...], slot).astype(BF)
        hall_ref[slot * NB : (slot + 1) * NB, :] = nn(mixing, normed).astype(BF)
        mixt_ref[:, slot * NB : (slot + 1) * NB] = mixing.T

    def project(i):
        kv_ref[pl.ds(i * BLK, BLK), :] = nn(hall_ref[pl.ds(i * BLK, BLK), :], a_ref[:, D : 3 * D]).astype(BF)

    each(0, KEYS // BLK, project)
    pick = (pos_ref[...] == iota((SEQ_LEN, PICKS), 0)).astype(FL).astype(BF).T
    hq_ref[...] = nn(pick, normed).astype(BF)
    x1_ref[...] = nn(pick, x_ref[...])
    q_ref[...] = nn(hq_ref[...], a_ref[:, :D]).astype(BF)
    visible = visible_keys(seg_ref, pos_ref)

    def attend(p):
        keys = kv_ref[:, lanes(p * PAIR, PAIR)]
        values = kv_ref[:, lanes(D + p * PAIR, PAIR)].T
        queries = q_ref[:, lanes(p * PAIR, PAIR)] * HD ** (-0.5)
        outs = []
        for head in range(2):
            scores = masked(visible, nt(keys, head_lanes(queries, head)))
            peak = jnp.max(scores, axis=0, keepdims=True)
            expo = jnp.exp(scores - peak)
            total = jnp.sum(expo, axis=0, keepdims=True)
            probs = (expo * (1.0 / total)).astype(BF)
            outs.append(nn(values[head * HD : (head + 1) * HD, :], probs))
            lse_ref[p, head : head + 1, :] = peak + jnp.log(total)
        o_ref[:, lanes(p * PAIR, PAIR)] = jnp.concatenate(outs, axis=0).T.astype(BF)

    gather.pass_on()
    each(0, NPAIR, attend)
    gather.last_hop()
    gather.finish(0)
    x1 = x1_ref[...] + nn(o_ref[...], p_all[...])
    x1_ref[...] = x1
    unit, _ = standard(x1)
    h2 = (unit * norm_ref[1:2, :] + norm_ref[4:5, :]).astype(BF)
    h2_ref[...] = h2
    x2_ref[...] = x1

    def expand(j):
        cut = lanes(j * D, D)
        z = nn(h2, u_ref[:, cut])
        z_ref[:, cut] = z
        act_ref[:, cut] = jax.nn.gelu(z, approximate=True).astype(BF)

    each(0, FF // D, expand)
    gather.finish(1)

    def contract(j):
        x2_ref[...] += nn(act_ref[:, lanes(j * D, D)], c_all[pl.ds(j * D, D), :])

    each(0, FF // D, contract)
    unit, _ = standard(x2_ref[...])
    f_ref[...] = (unit * norm_ref[2:3, :] + norm_ref[5:6, :]).astype(BF)


def feed_back_kernel(
    df_ref, x2_ref, x1_ref, h2_ref, z_ref, act_ref, o_ref, p_ref, u_ref, c_ref, norm_ref,
    dc_ref, du_ref, dp_ref, dx1_ref, do_ref, dnorm_ref, dh2,
):
    unit, scale = standard(x2_ref[...])
    dx2, gain_last, bias_last = norm_back(unit, scale, norm_ref[2:3, :], df_ref[...])
    dy = dx2.astype(BF)
    dh2[...] = jnp.zeros_like(dh2)
    h2t = h2_ref[...].T

    def piece(j):
        cut = lanes(j * D, D)
        dc_ref[pl.ds(j * D, D), :] = nn(act_ref[:, cut].T, dy).astype(BF)
        dact = nt(dy, c_ref[pl.ds(j * D, D), :])
        z = z_ref[:, cut]
        k = math.sqrt(2.0 / math.pi)
        t = jnp.tanh(k * (z + 0.044715 * z * z * z))
        slope = 0.5 * (1.0 + t) + 0.5 * z * (1.0 - t * t) * (k * (1.0 + 3 * 0.044715 * z * z))
        dz = (dact * slope).astype(BF)
        du_ref[:, cut] = nn(h2t, dz).astype(BF)
        dh2[...] += nt(dz, u_ref[:, cut])

    each(0, FF // D, piece)
    unit, scale = standard(x1_ref[...])
    dx1, gain_two, bias_two = norm_back(unit, scale, norm_ref[1:2, :], dh2[...])
    dx1 = dx1 + dx2
    dx1_ref[...] = dx1
    da = dx1.astype(BF)
    dp_ref[...] = nn(o_ref[...].T, da).astype(BF)
    do_ref[...] = nt(da, p_ref[...]).astype(BF)
    zero = jnp.zeros_like(gain_last)
    dnorm_ref[...] = jnp.concatenate([zero, gain_two, gain_last, zero, bias_two, bias_last, zero, zero], axis=0)


def attend_back_kernel(
    nb, nv, do_ref, q_ref, kv_ref, lse_ref, hall_ref, hq_ref, a_ref, x_ref, dx1_ref, mixt_ref, seg_ref, row_ref,
    norm_ref, dnorm_ref, du_ref, da_ref, dx_ref, du_sum, dkv, dq, hallt, dh, dxin, dmem, sel, *refs,
):
    meet((("batch", nb), ("vocab", nv)))
    layer = GradientSum(nb, nv, (du_ref,), refs, {0: du_sum})
    layer.start()
    visible = visible_keys(seg_ref, row_ref)

    def attend(p):
        cut = lanes(p * PAIR, PAIR)
        keys = kv_ref[:, cut]
        values = kv_ref[:, lanes(D + p * PAIR, PAIR)]
        turned = keys.T
        queries = q_ref[:, cut] * HD ** (-0.5)
        grads = do_ref[:, cut]
        outs = []
        dk = dv = None
        for head in range(2):
            own, grad = head_lanes(queries, head), head_lanes(grads, head)
            scores = masked(visible, nt(keys, own))
            probs = jnp.exp(scores - lse_ref[p, head : head + 1, :])
            dprobs = nt(values, grad)
            inner = jnp.sum(probs * dprobs, axis=0, keepdims=True)
            dscores = (probs * (dprobs - inner)).astype(BF)
            outs.append(nn(turned[head * HD : (head + 1) * HD, :], dscores))
            one, two = nn(dscores, own), nn(probs.astype(BF), grad)
            dk = one if head == 0 else dk + one
            dv = two if head == 0 else dv + two
        dq[:, cut] = (jnp.concatenate(outs, axis=0).T * HD ** (-0.5)).astype(BF)
        dkv[:, cut] = dk.astype(BF)
        dkv[:, lanes(D + p * PAIR, PAIR)] = dv.astype(BF)

    each(0, NPAIR // 2, attend)
    layer.scatter(0)
    each(NPAIR // 2, NPAIR, attend)
    da_ref[:, :D] = nn(hq_ref[...].T, dq[...]).astype(BF)

    def turn(i):
        hallt[:, lanes(i * BLK, BLK)] = hall_ref[pl.ds(i * BLK, BLK), :].T

    each(0, KEYS // BLK, turn)

    def weights(j):
        cut = lanes(j * BLK, BLK)
        da_ref[:, lanes(D + j * BLK, BLK)] = nn(hallt[...], dkv[:, cut]).astype(BF)

    each(0, 2 * D // BLK, weights)

    def memory(i):
        cut = pl.ds(i * BLK, BLK)
        dmem[cut, :] = nt(dkv[cut, :], a_ref[:, D : 3 * D]).astype(BF)

    each(0, SLOTS, memory)

    def local(i):
        cut = pl.ds(i * BLK, BLK)
        dh[cut, :] = nt(dkv[pl.ds(SLOTS * NB + i * BLK, BLK), :], a_ref[:, D : 3 * D]) + nn(mixt_ref[cut, :], dmem[...])

    each(0, SEQ_LEN // BLK, local)
    put = (row_ref[...] == iota((SEQ_LEN, PICKS), 0)).astype(FL).astype(BF)

    def scatter(target, value):
        for _ in range(3):
            part = value.astype(BF)
            value = value - part.astype(FL)

            def add(i, part=part):
                cut = pl.ds(i * BLK, BLK)
                target[cut, :] += nn(sel[cut, :], part)

            each(0, SEQ_LEN // BLK, add)

    sel[...] = put
    scatter(dh, nt(dq[...], a_ref[:, :D]))
    gain = norm_ref[0:1, :]
    da_rows = [jnp.zeros((1, D), FL), jnp.zeros((1, D), FL)]

    def finish(i, carry):
        cut = pl.ds(i * BLK, BLK)
        unit, scale = standard(x_ref[cut, :].astype(FL))
        grad, dgain, dbias = norm_back(unit, scale, gain, dh[cut, :])
        dxin[cut, :] = grad
        return carry[0] + dgain, carry[1] + dbias

    dgain, dbias = lax.fori_loop(0, SEQ_LEN // BLK, finish, tuple(da_rows))

    scatter(dxin, dx1_ref[...])
    dx_ref[...] = dxin[...].astype(BF)
    line = iota((8, D), 0)
    norms = dnorm_ref[...] + jnp.where(line == 0, dgain, jnp.where(line == 3, dbias, 0.0))
    tall = jnp.concatenate([norms, jnp.zeros((EXTRA - 8, D), FL)], axis=0)
    da_ref[:, 3 * D :] = tall.T.astype(BF)
    layer.gather(0)


def head_kernel(
    nb, nv, part, f_ref, w_ref, live_ref, target_ref, df_ref, dw_ref, loss_ref,
    fall, expo, block, mine, stats, ft, grad_sum, coef, df, half, far_got, out,
    near_out, near_in, far_out, far_in, stat_out, stat_in, pair_out, pair_in, sum_out, sum_in, dw_sem,
):
    v = lax.axis_index("vocab")
    rows = w_ref.shape[1]
    total_rows = nv * PICKS
    core, chip, chips = lax.rem(v, 2), v // 2, nv // 2
    sibling = {"vocab": v + 1 - 2 * core}
    base = v * rows
    pieces = rows // part
    depth = min(2, pieces)
    meet((("vocab", nv),))

    def peer(step):
        return {"vocab": lax.rem(chip + step, chips) * 2 + core}

    def far_copy(step):
        return send(f_ref, fall.at[v], far_out.at[step], far_in.at[step], peer(step))

    def near_copy(step):
        slot = lax.rem(chip - step + chips, chips) * 2 + core
        return send(fall.at[slot], fall.at[slot], near_out.at[step], near_in.at[step], sibling)

    fall[v] = f_ref[...]
    near_copy(0).start()
    each(1, chips, lambda step: far_copy(step).start())

    def logits(step):
        @pl.when(step > 0)
        def _():
            far_copy(step).wait_recv()
            near_copy(step).start()

        near_copy(step).wait_recv()
        source = lax.rem(chip - step + chips, chips)
        start = pl.multiple_of(source * 2 * PICKS, 2 * PICKS)
        features = fall[pl.ds(source * 2, 2)].reshape(2 * PICKS, D)
        target = target_ref[pl.ds(start, 2 * PICKS), :] - base

        def score(j, peak):
            cut = lanes(j * part, part)
            value = nn(features, w_ref[:, cut])
            block[:, cut] = value
            return jnp.maximum(
                peak, jnp.max(jnp.where(live_ref[0:1, cut] > 0, value, NEG_BIG), axis=1, keepdims=True)
            )

        peak = lax.fori_loop(0, pieces, score, jnp.full((2 * PICKS, 1), NEG_BIG, FL))

        def count(j, carry):
            total, picked, valid = carry
            cut = lanes(j * part, part)
            value = block[:, cut]
            live = live_ref[0:1, cut] > 0
            hot = target - j * part == iota((2 * PICKS, part), 1)
            e = jnp.where(live, jnp.exp(value - peak), 0.0)
            expo[pl.ds(start, 2 * PICKS), cut] = e.astype(BF)
            total = total + jnp.sum(e, axis=1, keepdims=True)
            picked = picked + jnp.sum(jnp.where(hot, value, 0.0), axis=1, keepdims=True)
            valid = valid + jnp.sum(jnp.where(hot & live, 1.0, 0.0), axis=1, keepdims=True)
            return total, picked, valid

        zero = jnp.zeros((2 * PICKS, 1), FL)
        total, picked, valid = lax.fori_loop(0, pieces, count, (zero, zero, zero))
        lane = iota((2 * PICKS, 128), 1)
        wide = jnp.where(lane == 0, peak, jnp.where(lane == 1, total, jnp.where(lane == 2, picked, valid)))
        mine[:, pl.ds(start, 2 * PICKS)] = wide.T[:8, :]

    each(0, chips, logits)

    def stat_copy(step):
        return send(mine, stats.at[v], stat_out.at[step], stat_in.at[step], {"vocab": lax.rem(v + step, nv)})

    each(1, nv, lambda step: stat_copy(step).start())
    stats[v] = mine[...]
    for i in range(total_rows // 256 if pieces > 1 else 0):
        ft[:, i * 256 : (i + 1) * 256] = fall[2 * i : 2 * i + 2].reshape(256, D).T
    each(1, nv, lambda step: stat_copy(step).wait())
    start = jnp.full((1, total_rows), NEG_BIG, FL)
    peak = lax.fori_loop(0, nv, lambda u, top: jnp.maximum(top, stats[u, 0:1, :]), start)

    def combine(u, carry):
        scale = jnp.exp(stats[u, 0:1, :] - peak)
        return (
            carry[0] + stats[u, 1:2, :] * scale, carry[1] + stats[u, 2:3, :], carry[2] + stats[u, 3:4, :],
        )

    zero = jnp.zeros((1, total_rows), FL)
    total, picked, valid = lax.fori_loop(0, nv, combine, (zero, zero, zero))
    lse = peak + jnp.log(jnp.maximum(total, 1e-37))
    weight = valid / (jnp.maximum(jnp.sum(valid, axis=1, keepdims=True), 1.0) * nb)
    loss = jnp.sum(weight * (lse - picked), axis=1, keepdims=True)
    loss_ref[...] = jnp.broadcast_to(loss, loss_ref.shape)
    alpha = weight * jnp.exp(mine[0:1, :] - lse)
    line = iota((128, 256), 0)
    for i in range(total_rows // 256):
        cut = slice(i * 256, (i + 1) * 256)
        coef[cut, :] = jnp.where(line == 0, alpha[:, cut], weight[:, cut]).T

    tall = min(total_rows, 1024 if pieces > 1 else 256)
    shards_tall = tall // PICKS
    df[...] = jnp.zeros_like(df)

    def out_copy(j):
        return pltpu.make_async_copy(
            out.at[lax.rem(j, depth)], dw_ref.at[:, lanes(j * part, part)], dw_sem.at[lax.rem(j, depth)]
        )

    def gradients(j):
        cut = lanes(j * part, part)
        words = w_ref[:, cut]

        @pl.when(j >= depth)
        def _():
            out_copy(j - depth).wait()

        def strip(t):
            start = t * tall if total_rows == tall else pl.multiple_of(t * tall, tall)
            here = pl.ds(start, tall)
            hot = target_ref[here, :] - base - j * part == iota((tall, part), 1)
            two = coef[here, :]
            value = two[:, 0:1] * expo[here, cut].astype(FL) - jnp.where(hot, two[:, 1:2], 0.0)
            dlogits = value.astype(BF)
            df[here, :] += nt(dlogits, words)
            if pieces > 1:
                turned = ft[:, pl.ds(start, tall)]
            else:
                turned = fall[pl.ds(t * shards_tall, shards_tall)].reshape(tall, D).T
            for r in range(0, D, D // 3):
                more = nn(turned[r : r + D // 3, :], dlogits)
                if total_rows == tall:
                    out[lax.rem(j, depth), r : r + D // 3, :] = more.astype(BF)
                else:
                    grad_sum[r : r + D // 3, :] += more

        if total_rows == tall:
            strip(0)
        else:
            grad_sum[...] = jnp.zeros_like(grad_sum)
            each(0, total_rows // tall, strip)
            for r in range(0, D, D // 3):
                out[lax.rem(j, depth), r : r + D // 3, :] = grad_sum[r : r + D // 3, :].astype(BF)
        out_copy(j).start()

    each(0, pieces, gradients)

    def shard(index):
        return pl.ds(pl.multiple_of(index * PICKS, PICKS), PICKS)

    def pair_copy(k):
        source = df.at[shard(2 * k + 1 - core), :] if pieces > 1 else fall.at[k]
        return send(source, half.at[k], pair_out.at[k], pair_in.at[k], sibling)

    near_copy(0).wait_send()

    def drain(step):
        far_copy(step).wait_send()
        near_copy(step).wait_send()

    each(1, chips, drain)

    def swap(k):
        if pieces == 1:
            fall[k] = df[shard(2 * k + 1 - core), :].astype(BF)
        pair_copy(k).start()

    each(0, chips, swap)

    def sum_copy(step):
        return send(fall.at[chips + step], far_got.at[step], sum_out.at[step], sum_in.at[step], peer(step))

    def pass_on(turn):
        step = lax.rem(turn, chips)
        k = lax.rem(chip + step, chips)
        pair_copy(k).wait()
        value = df[shard(2 * k + core), :] + half[k].astype(FL)

        @pl.when(step > 0)
        def _():
            fall[chips + step] = value.astype(BF)
            sum_copy(step).start()

        @pl.when(step == 0)
        def _():
            df_ref[...] = value

    each(1, chips + 1, pass_on)

    def collect(step):
        sum_copy(step).wait()
        df_ref[...] += far_got[step].astype(FL)

    each(1, chips, collect)
    for j in range(pieces - depth, pieces):
        out_copy(j).wait()


def head(nb, nv, features, words, live, targets):
    rows = words.shape[1]
    part = chunk_of(rows, 640)
    total_rows = nv * PICKS
    chips = nv // 2
    dma = pltpu.SemaphoreType.DMA
    scratch = [
        pltpu.VMEM((nv, PICKS, D), BF),
        pltpu.VMEM((total_rows, rows), BF),
        pltpu.VMEM((2 * PICKS, rows), FL),
        pltpu.VMEM((8, total_rows), FL),
        pltpu.VMEM((nv, 8, total_rows), FL),
        pltpu.VMEM((D, total_rows) if rows > part else (8, 128), BF),
        pltpu.VMEM((8, 128) if rows > part else (D, part), FL),
        pltpu.VMEM((total_rows, 128), FL),
        pltpu.VMEM((total_rows, D), FL),
        pltpu.VMEM((chips, PICKS, D), FL if rows > part else BF),
        pltpu.VMEM((chips, PICKS, D), BF),
        pltpu.VMEM((min(2, rows // part), D, part), BF),
        dma((chips,)), dma((chips,)), dma((chips,)), dma((chips,)), dma((nv,)), dma((nv,)),
        dma((chips,)), dma((chips,)), dma((chips,)), dma((chips,)), dma((2,)),
    ]
    return run(
        functools.partial(head_kernel, nb, nv, part),
        [SD((PICKS, D), FL), SD((D, rows), BF), SD((8, 128), FL)],
        scratch,
        [features, words, live, targets],
        "head",
        1,
        out_specs=[VM, HB, VM],
    )


def wide_head_kernel(
    nb, nv, block_rows, f_ref, w_ref, live_ref, target_ref, df_ref, dw_ref, loss_ref,
    fall, ft, expo, words_sum, mine, first_got, merged, second_got, tile, third_got, tiles, coef, group, half, handed, mix_got,
    far_sum, far_got,
    z_out, z_in, mix_out, mix_in, near_out, near_in, s_out, s_in, pair_out, pair_in, give_out, give_in, sum_out, sum_in,
):
    b, v = lax.axis_index("batch"), lax.axis_index("vocab")
    rows = w_ref.shape[1]
    core, chip, chips = lax.rem(v, 2), v // 2, nv // 2
    sibling = {"vocab": v + 1 - 2 * core}
    base = v * block_rows + b * rows
    live = live_ref[:, lanes(b * rows, rows)] > 0
    span = nv * PICKS
    meet((("batch", nb), ("vocab", nv)))

    def column(line):
        line = jnp.where(line < (v + 1) * block_rows, line - base, -1).astype(FL)
        return jnp.broadcast_to(line, (128, 2 * PICKS)).T[:, 0:1].astype(I32)

    def peer(step):
        return {"vocab": lax.rem(chip + step, chips) * 2 + core}

    def other(step):
        return {"batch": lax.rem(b + step, nb)}

    def flip(s):
        low, high = lax.rem(b, 2), b // 2
        return (high if s < 2 else 1 - high) * 2 + (low if s % 2 == 0 else 1 - low)

    def slot(s, k):
        return flip(s) * nv + lax.rem(chip - k + chips, chips) * 2 + core

    def z_copy(k):
        return send(f_ref, fall.at[b * nv + v], z_out.at[k], z_in.at[k], peer(k))

    def mix_copy(s, k, way=0):
        if s < 3:
            place, device = fall.at[slot(0, k)], flip(s)
        else:
            place, device = fall.at[slot(3 - way, k)], flip(way)
        return send(place, place, mix_out.at[k, s], mix_in.at[k, s], {"batch": device})

    near = [s for s in (1, 2) if s < nb]

    def near_copy(s, k):
        place = fall.at[slot(s, k)]
        return send(place, place, near_out.at[k, s], near_in.at[k, s], sibling)

    def arrive(s, k):
        if s == 0:

            @pl.when(k > 0)
            def _():
                z_copy(k).wait_recv()

            for t in near:
                mix_copy(t, k).start()
        else:
            mix_copy(s, k, 1).wait_recv()
        if nb == 4 and s in (1, 2):

            @pl.when(lax.rem(k, 2) == s - 1)
            def _():
                mix_copy(3, k, 3 - s).start()

        near_copy(s, k).start()

    fall[b * nv + v] = f_ref[...]
    each(1, chips, lambda k: z_copy(k).start())
    arrive(0, 0)

    def logits(s, k):
        near_copy(s, k).wait_recv()
        p, c = flip(s), lax.rem(chip - k + chips, chips)
        first = p * nv + c * 2
        start = pl.multiple_of(first * PICKS, 2 * PICKS)
        features = fall[pl.ds(first, 2)].reshape(2 * PICKS, D)
        ft[:, pl.ds(start, 2 * PICKS)] = features.T
        line = target_ref[p, :, pl.ds(pl.multiple_of(c * 2 * PICKS, 2 * PICKS), 2 * PICKS)]
        target = column(line)
        value = nn(features, w_ref[...])
        value = jnp.where(live, value, NEG_BIG)
        peak = jnp.maximum(jnp.max(value, axis=1, keepdims=True), 0.1 * NEG_BIG)
        e = jnp.exp(value - peak)
        expo[pl.ds(start, 2 * PICKS), :] = e.astype(BF)
        total = jnp.sum(e, axis=1, keepdims=True)
        picked = jnp.sum(jnp.where(target == iota((2 * PICKS, rows), 1), value, 0.0), axis=1, keepdims=True)
        lane = iota((2 * PICKS, 128), 1)
        wide = jnp.where(lane == 0, peak, jnp.where(lane == 1, total, picked)).T
        mine[c * 2, p] = wide[:8, :PICKS]
        mine[c * 2 + 1, p] = wide[:8, PICKS:]

    for s in range(nb):

        def one(k, s=s):
            @pl.when(k + 1 < chips)
            def _():
                arrive(s, k + 1)

            if s + 1 < nb:

                @pl.when(k + 1 == chips)
                def _():
                    arrive(s + 1, 0)

            logits(s, k)

        each(0, chips, one)

    def merge(read, count):
        peak = lax.fori_loop(
            0, count, lambda u, top: jnp.maximum(top, read(u)[0:1, :]), jnp.full((1, PICKS), NEG_BIG, FL)
        )

        def add(u, carry):
            one = read(u)
            return carry[0] + one[1:2, :] * jnp.exp(one[0:1, :] - peak), carry[1] + one[2:3, :]

        zero = jnp.zeros((1, PICKS), FL)
        return (peak, *lax.fori_loop(0, count, add, (zero, zero)))

    def tile_of(rows_of):
        line = iota((8, PICKS), 0)
        value = jnp.zeros((8, PICKS), FL)
        for i, row in enumerate(rows_of):
            value = jnp.where(line == i, row, value)
        return value

    def first_copy(t):
        u = lax.rem(v + t, nv)
        return send(mine.at[u], first_got.at[v], s_out.at[0, t], s_in.at[0, t], {"vocab": u})

    each(1, nv, lambda t: first_copy(t).start())
    first_got[v] = mine[v]
    each(1, nv, lambda t: first_copy(t).wait())
    for p in range(nb):
        merged[p] = tile_of(merge(lambda u, p=p: first_got[u, p], nv))

    def second_copy(t):
        return send(merged.at[lax.rem(b + t, nb)], second_got.at[b], s_out.at[1, t], s_in.at[1, t], other(t))

    each(1, nb, lambda t: second_copy(t).start())
    second_got[b] = merged[b]
    each(1, nb, lambda t: second_copy(t).wait())
    peak, total, picked = merge(lambda u: second_got[u], nb)
    valid = (picked > 0.5 * NEG_BIG).astype(FL)
    tile[...] = tile_of((peak + jnp.log(jnp.maximum(total, 1e-37)), picked, valid))

    def third_copy(t):
        return send(tile, third_got.at[b], s_out.at[2, t], s_in.at[2, t], other(t))

    each(1, nb, lambda t: third_copy(t).start())
    third_got[b] = tile[...]
    each(1, nb, lambda t: third_copy(t).wait())

    def last_copy(t):
        return send(third_got, tiles.at[v], s_out.at[3, t], s_in.at[3, t], {"vocab": lax.rem(v + t, nv)})

    each(1, nv, lambda t: last_copy(t).start())
    tiles[v] = third_got[...]
    each(1, nv, lambda t: last_copy(t).wait())

    def coefficients(p):
        count = lax.fori_loop(0, nv, lambda u, total: total + tiles[u, p, 2:3, :], jnp.zeros((1, PICKS), FL))
        share = 1.0 / (jnp.maximum(jnp.sum(count, axis=1, keepdims=True), 1.0) * nb)

        def spread(c, loss):
            rows_of = []
            for side in range(2):
                u = c * 2 + side
                lse, picked, valid = (tiles[u, p, i : i + 1, :] for i in range(3))
                weight = valid * share
                loss = loss + weight * (lse - picked)
                rows_of.append((weight * jnp.exp(mine[u, p, 0:1, :] - lse), weight))
            line = iota((128, 2 * PICKS), 0)
            alpha = jnp.concatenate([rows_of[0][0], rows_of[1][0]], axis=1)
            weight = jnp.concatenate([rows_of[0][1], rows_of[1][1]], axis=1)
            start = pl.multiple_of(p * span + c * 2 * PICKS, 2 * PICKS)
            coef[pl.ds(start, 2 * PICKS), :] = jnp.where(line == 0, alpha, weight).T
            return loss

        loss = lax.fori_loop(0, chips, spread, jnp.zeros((1, PICKS), FL))

        @pl.when(p == b)
        def _():
            loss_ref[...] = jnp.broadcast_to(jnp.sum(loss, axis=1, keepdims=True), loss_ref.shape)

    each(0, nb, coefficients)

    def shard(k, side):
        return pl.ds(pl.multiple_of((2 * k + side) * PICKS, PICKS), PICKS)

    def pair_copy(s, k):
        return send(handed.at[s, k], half.at[s, k], pair_out.at[s, k], pair_in.at[s, k], sibling)

    def give_copy(s, k):
        if s < 3:
            return send(handed.at[s, k], mix_got.at[s, k], give_out.at[s, k], give_in.at[s, k], {"batch": flip(s)})
        device = jnp.where(lax.rem(k, 2) == 0, flip(1), flip(2))
        return send(handed.at[3, k], mix_got.at[3, k], give_out.at[3, k], give_in.at[3, k], {"batch": device})

    def exchange(s):
        def add(k):
            pair_copy(s, k).wait()
            value = group[s % 2, shard(k, core), :] + half[s, k].astype(FL)
            handed[s, k] = value.astype(BF)
            if nb == 4 and s in (1, 2):

                @pl.when(lax.rem(k, 2) == 2 - s)
                def _():
                    give_copy(3, k).wait_recv()
                    handed[s, k] = (value + mix_got[3, k].astype(FL)).astype(BF)

            if s > 0:
                give_copy(s, k).start()

        each(0, chips, add)

    order = [3, 2, 1, 0] if nb == 4 else [1, 0]
    for turn, s in enumerate(order):
        p = flip(s)

        def strip(c, p=p):
            start = pl.multiple_of(p * span + c * 2 * PICKS, 2 * PICKS)
            here = pl.ds(start, 2 * PICKS)
            line = target_ref[p, :, pl.ds(pl.multiple_of(c * 2 * PICKS, 2 * PICKS), 2 * PICKS)]
            target = column(line)
            two = coef[here, :]
            hot = target == iota((2 * PICKS, rows), 1)
            value = two[:, 0:1] * expo[here, :].astype(FL) - jnp.where(hot, two[:, 1:2], 0.0)
            expo[here, :] = value.astype(BF)

        each(0, chips, strip)
        if turn > 0:
            exchange(order[turn - 1])

        def features_grad(i, p=p, s=s):
            here = pl.ds(pl.multiple_of(i * 512, 512), 512)
            group[s % 2, here, :] = nt(expo[pl.ds(pl.multiple_of(p * span + i * 512, 512), 512), :], w_ref[...])

        each(0, span // 512, features_grad)

        def swap(k, s=s):
            handed[s, k] = group[s % 2, shard(k, 1 - core), :].astype(BF)
            pair_copy(s, k).start()

        each(0, chips, swap)

    words_sum[...] = jnp.zeros_like(words_sum)

    def words_grad(i):
        cut = lanes(i * 512, 512)
        words_sum[...] += nn(ft[:, cut], expo[cut, :])

    strips = nb * span // 512
    each(0, 1, words_grad)
    exchange(0)
    each(1, strips // 2, words_grad)

    def total_of(k):
        value = handed[0, k].astype(FL)
        for s in near:
            give_copy(s, k).wait_recv()
            value = value + mix_got[s, k].astype(FL)
        return value

    def sum_copy(t):
        return send(far_sum.at[t], far_got.at[t], sum_out.at[t], sum_in.at[t], peer(t))

    def pass_on(t):
        far_sum[t] = total_of(lax.rem(chip + t, chips)).astype(BF)
        sum_copy(t).start()

    each(1, chips, pass_on)
    each(strips // 2, strips, words_grad)
    dw_ref[...] = words_sum[...].astype(BF)
    df_ref[...] = total_of(chip)

    def collect(t):
        sum_copy(t).wait()
        df_ref[...] += far_got[t].astype(FL)

    each(1, chips, collect)
    each(1, chips, lambda k: z_copy(k).wait_send())
    for s in range(nb):
        each(0, chips, lambda k, s=s: near_copy(s, k).wait_send())
        if s > 0:
            each(0, chips, lambda k, s=s: mix_copy(s, k, 1).wait_send())
            each(0, chips, lambda k, s=s: give_copy(s, k).wait_send())


def wide_head(nb, nv, block_rows, features, words, live, targets):
    rows = words.shape[1]
    tokens = nb * nv * PICKS
    chips = nv // 2
    dma = pltpu.SemaphoreType.DMA
    most = max(nb, nv)
    scratch = [
        pltpu.VMEM((nb * nv, PICKS, D), BF),
        pltpu.VMEM((D, tokens), BF),
        pltpu.VMEM((tokens, rows), BF),
        pltpu.VMEM((D, rows), FL),
        pltpu.VMEM((nv, nb, 8, PICKS), FL),
        pltpu.VMEM((nv, nb, 8, PICKS), FL),
        pltpu.VMEM((nb, 8, PICKS), FL),
        pltpu.VMEM((nb, 8, PICKS), FL),
        pltpu.VMEM((8, PICKS), FL),
        pltpu.VMEM((nb, 8, PICKS), FL),
        pltpu.VMEM((nv, nb, 8, PICKS), FL),
        pltpu.VMEM((tokens, 128), FL),
        pltpu.VMEM((2, nv * PICKS, D), FL),
        pltpu.VMEM((nb, chips, PICKS, D), BF),
        pltpu.VMEM((nb, chips, PICKS, D), BF),
        pltpu.VMEM((nb, chips, PICKS, D), BF),
        pltpu.VMEM((chips, PICKS, D), BF),
        pltpu.VMEM((chips, PICKS, D), BF),
        dma((chips,)), dma((chips,)), dma((chips, nb)), dma((chips, nb)), dma((chips, nb)), dma((chips, nb)),
        dma((4, most)), dma((4, most)), dma((nb, chips)), dma((nb, chips)), dma((nb, chips)), dma((nb, chips)),
        dma((chips,)), dma((chips,)),
    ]
    return run(
        functools.partial(wide_head_kernel, nb, nv, block_rows),
        [SD((PICKS, D), FL), SD((D, rows), BF), SD((8, 128), FL)],
        scratch,
        [features, words, live, targets],
        "wide_head",
        1,
    )


def norm(nb, nv, extra, dw, sums, loss):
    return run(
        functools.partial(norm_kernel, nb, nv), [SD((8, 128), FL)], add_up_scratch(nb, nv),
        [extra, dw, *sums, loss], "norm", 5,
    )[0]


def adamw(weight, moment, square, gradient, clip, count, decay, rate):
    gradient = gradient * clip
    moment = BETA_ONE * moment + (1 - BETA_ONE) * gradient
    square = BETA_TWO * square + (1 - BETA_TWO) * gradient * gradient
    fixed_moment = moment / (1 - BETA_ONE**count)
    fixed_square = square / (1 - BETA_TWO**count)
    weight = weight - rate * (fixed_moment / (jnp.sqrt(fixed_square) + ADAM_EPS) + decay * weight)
    return (weight, moment, square)


def slot_size(nv):
    mean = SEQ_LEN // nv
    return -(-(mean + int(5.5 * math.sqrt(mean))) // 32) * 32


def shards(
    nb, nv,
    tokens, targets, segments, counted, vocab_mask, step_count,
    table, table_moment, table_square,
    attend, attend_moment, attend_square,
    project, project_moment, project_square,
    expand, expand_moment, expand_square,
    contract, contract_moment, contract_square,
    gain, gain_moment, gain_square,
    shift, shift_moment, shift_square,
):
    rows, width = table.shape
    cap = slot_size(nv)
    table_t = table.T
    norms = jnp.concatenate([gain, shift], axis=0)
    packed = jnp.concatenate([attend[0], norms.T, jnp.zeros((width, EXTRA - 6), FL)], axis=1).astype(BF)
    pieces = (packed, project[0].astype(BF), expand[0].astype(BF), contract[0].astype(BF))
    split = nb * nv * PICKS <= 4096
    rounded = table_t.astype(BF)
    quarter = -(-rows // (nb * 128)) * 128
    if split:
        rounded = jnp.pad(rounded, ((0, 0), (0, nb * quarter - rows)))
    else:
        words = lax.all_gather(rounded, "batch", axis=0, tiled=True)

    seg_row, pos_row = segments[None, :], counted[None, :]
    tok = tokens.reshape(nv, SEQ_LEN)
    x, ids, place, most, every, a_all, u_all, *rest = embed(
        nb, nv, cap, rows, jnp.zeros((1,), I32), tok, rounded, (pieces[0], pieces[2]),
        targets[None, :] if split else None,
    )
    turns = (most[0] + cap - 1) // cap

    def more_rows(state):
        turn, total = state
        return turn + 1, total + embed(nb, nv, cap, rows, turn[None], tok, rounded)[0]

    x = lax.while_loop(lambda state: state[0] < turns, more_rows, (jnp.int32(1), x))[1]

    hall, kv, q, hq, mixed, lse, norm_rows, mixing_t, p_all, c_all, x1, h2, z, act, x2, features = run(
        functools.partial(attend_kernel, nb, nv),
        [
            SD((KEYS, D), BF), SD((KEYS, 2 * D), BF), SD((PICKS, D), BF), SD((PICKS, D), BF),
            SD((PICKS, D), BF), SD((NPAIR, 2, PICKS), FL), SD((8, D), FL), SD((SEQ_LEN, SLOTS * NB), BF),
            SD((D, D), BF), SD((FF, D), BF),
            SD((PICKS, D), FL), SD((PICKS, D), BF), SD((PICKS, FF), FL), SD((PICKS, FF), BF), SD((PICKS, D), FL),
            SD((PICKS, D), BF),
        ],
        weight_semaphores(2),
        [x, a_all, seg_row, pos_row, pieces[1], pieces[3], u_all],
        "attend", 6, flops=9 * 10**9, moved=30 * 10**6,
    )
    if split:
        live = jnp.pad(vocab_mask, (0, nb * quarter - rows))[None, :]
        df, dw, loss_block = wide_head(nb, nv, rows, features, rest[0], live, rest[1])
    else:
        df, dw, loss_block = head(nb, nv, features, words, vocab_mask[None, :], targets[:, None])
        dw_sum = lax.psum_scatter(dw, "batch", scatter_dimension=0, tiled=True)

    dc, du, dp, dx1, dmixed, dnorm = run(
        feed_back_kernel,
        [
            SD((FF, D), BF), SD((D, FF), BF), SD((D, D), BF), SD((PICKS, D), FL), SD((PICKS, D), BF), SD((8, D), FL),
        ],
        [pltpu.VMEM((PICKS, D), FL)],
        [df, x2, x1, h2, z, act, mixed, p_all, u_all, c_all, norm_rows],
        "feed_back", flops=4 * 10**9, moved=30 * 10**6,
    )
    da, dx, du_sum = run(
        functools.partial(attend_back_kernel, nb, nv),
        [SD((D, 3 * D + EXTRA), BF), SD((SEQ_LEN, D), BF), SD((width, FF // 2), BF)],
        [
            pltpu.VMEM((KEYS, 2 * D), BF), pltpu.VMEM((PICKS, D), BF), pltpu.VMEM((D, KEYS), BF),
            pltpu.VMEM((SEQ_LEN, D), FL), pltpu.VMEM((SEQ_LEN, D), FL), pltpu.VMEM((SLOTS * NB, D), BF),
            pltpu.VMEM((SEQ_LEN, PICKS), BF), *gradient_scratch(nb, nv, [du.shape], (0,), False),
        ],
        [dmixed, q, kv, lse, hall, hq, a_all, x, dx1, mixing_t, seg_row, pos_row, norm_rows, dnorm, du],
        "attend_back", 7, flops=12 * 10**9, moved=25 * 10**6,
        in_specs=[VM] * 14 + [HB],
    )
    extra, *sums = unembed(nb, nv, cap, width, rows, dx, ids, place, (da, dp, du_sum, dc), *((dw, loss_block) if split else ()))
    if split:
        *sums, dw_sum, totals, norm_grads = sums

    def more_grads(state):
        turn, total = state
        later = later_slots(nv, cap, rows, every, turn)
        return turn + 1, total + unembed(
            nb, nv, cap, width, rows, dx, later, place - jnp.array([0, 1, 0, 0, 0, 0, 0, 0], I32)[None, :, None] * (turn * cap)
        )[0]

    extra = lax.while_loop(lambda state: state[0] < turns, more_grads, (jnp.int32(1), extra))[1]

    if split:
        totals = lax.cond(
            turns > 1, lambda: norm(nb, nv, extra, dw_sum, sums, loss_block), lambda: totals
        )
    else:
        totals = norm(nb, nv, extra, dw_sum, sums, loss_block)
    grad_table = dw_sum[:, :rows].astype(FL) + extra
    grad_a, grad_p, grad_u, grad_c = (item.astype(FL) for item in sums)
    grad_norms = norm_grads if split else grad_a[:, 3 * D : 3 * D + 6].T
    grad_a = grad_a[:, : 3 * D]
    squares, loss = totals[0, 0], totals[1, 0]
    gradient_norm = jnp.sqrt(squares)
    clip = jnp.minimum(1.0, MAX_NORM / (gradient_norm + 1e-06))
    count = step_count[0].astype(FL)

    def update(weight, moment, square, gradient, decay=DECAY, rate=LEARN_RATE):
        return adamw(weight, moment, square, gradient, clip, count, decay, rate)

    table_out = [item.T for item in update(table_t, table_moment.T, table_square.T, grad_table)]
    attend_out = update(attend, attend_moment, attend_square, grad_a[None])
    project_out = update(project, project_moment, project_square, grad_p[None])
    expand_out = update(expand, expand_moment, expand_square, grad_u[None])
    contract_out = update(contract, contract_moment, contract_square, grad_c[None])
    gain_out = update(gain, gain_moment, gain_square, grad_norms[:3], 0.0, NORM_RATE)
    shift_out = update(shift, shift_moment, shift_square, grad_norms[3:6], 0.0, NORM_RATE)
    return (
        loss, gradient_norm, *table_out, *attend_out, *project_out, *expand_out, *contract_out, *gain_out, *shift_out,
    )


def solution(mesh):
    nb, nv = mesh.shape["batch"], mesh.shape["vocab"]
    both, split, middle, last = P(("batch", "vocab")), P("vocab", "batch"), P(None, "batch", None), P(None, "batch")
    state = (split,) * 3 + (middle,) * 12 + (last,) * 6
    return jax.shard_map(
        functools.partial(shards, nb, nv),
        mesh=mesh,
        in_specs=(P("batch"), P("batch"), both, both, P("vocab"), P()) + state,
        out_specs=(P(), P()) + state,
        check_vma=False,
    )
```
